32 devices in a mesh: seq: 8 (over z, x), fsdp: 4 (over y, core).
Axes of the slice: x: 2, y: 2, z: 4, core: 2. Of those that a mesh axis runs over, the one named last changes fastest.
Arguments:
- tokens: bfloat16 [8, 1024, 1536], P('fsdp', 'seq'), may hold values from -6 to 6
- segments: int32 [8, 1024], P('fsdp'), may hold values from 0 to 7, never falling along the last dimension, each value on 1 to 512 neighbouring positions
- gain_in: float32 [1536], replicated, may hold values from 0.5 to 1.5
- w_in: bfloat16 [1536, 6448], P(('seq', 'fsdp')), may hold values from -0.15625 to 0.15625
- conv_w: float32 [4, 3328], replicated, may hold values from -3 to 3
- conv_b: float32 [3328], replicated, may hold values from -3 to 3
- dt_bias: float32 [48], replicated, may hold values from -6 to -1
- a_log: float32 [48], replicated, may hold values from 0 to 2.5
- skip: float32 [48], replicated, may hold values from 0.5 to 1.5
- gain_out: float32 [3072], replicated, may hold values from 0.5 to 1.5
- w_out: bfloat16 [3072, 1536], P(('seq', 'fsdp')), may hold values from -0.109375 to 0.109375
- cotangent: bfloat16 [8, 1024, 1536], P('fsdp', 'seq'), may hold values from -6 to 6
Outputs:
- mixed: bfloat16 [8, 1024, 1536], P('fsdp', 'seq')
- tokens_grad: float32 [8, 1024, 1536], P('fsdp', 'seq')
- gain_in_grad: float32 [1536], replicated
- w_in_grad: float32 [1536, 6448], P(('seq', 'fsdp'))
- conv_w_grad: float32 [4, 3328], replicated
- conv_b_grad: float32 [3328], replicated
- dt_bias_grad: float32 [48], replicated
- a_log_grad: float32 [48], replicated
- skip_grad: float32 [48], replicated
- gain_out_grad: float32 [3072], replicated
- w_out_grad: float32 [3072, 1536], P(('seq', 'fsdp'))
The draws below stay inside these ranges and needn't reach their ends.
Inputs may be any that keep to these rules, and one draw needn't show every extreme that they name: `segments`: document numbers never fall along a sequence and start at 0; each document spans 1 to 512 tokens, one exactly 512.
All inputs are finite; a program needn't handle non-finite values.
Results may differ from the reference program's by a relative error of at most 0.0098.
Values may be sent and summed in bfloat16 or wider, within the bound.
A program may use at most 320 MiB of HBM per device.

```python
import math
import jax
import jax.numpy as jnp
import numpy as np
from jax import lax

D = 1536
HEADS = 48
HEAD_DIM = 64
STATE = 128
KERNEL = 4
STRETCH = 256
INNER = 3072
CHANNELS = 3328
PROJ = 6448
LEN = 1024
SEQS = 8
DOC_MOST = 512
DOCS = 8


def level_of(key, extent, cuts, least, high):
    def one(position, shards_of):
        heights = jax.random.uniform(jax.random.fold_in(jax.random.fold_in(key, 6), position), (shards_of,), jnp.float32, least / len(cuts), high / len(cuts))
        return jnp.repeat(jnp.exp(heights), extent[position] // shards_of).reshape((-1,) + (1,) * (len(extent) - position - 1))

    factor_of = one(*cuts[0])
    for cut in cuts[1:]:
        factor_of = factor_of * one(*cut)
    return factor_of


def split_up(number_of, total, most, lean):
    portions = [(1 << 20) // math.isqrt(rank ** lean) + 1 for rank in range(2, number_of + 1)]
    rest, holding = total - most - (number_of - 1), [1] * (number_of - 1)
    while rest > 0:
        free = [i for i in range(number_of - 1) if holding[i] < most]
        whole, budget = sum([portions[i] for i in free]), rest
        for i in free:
            addition = min(most - holding[i], max(1, budget * portions[i] // whole), rest)
            holding[i] = holding[i] + addition
            rest = rest - addition
    return np.array([most] + holding)


def uneven(own_key, count, total, reach, lean):
    if count == 2:
        one = jax.random.randint(own_key, (), max(1, total - reach), min(reach, total - 1) + 1)
        return jnp.stack([one, total - one])
    sizes = jnp.asarray(split_up(count, total, reach, lean), jnp.int32)
    couples = (count - 1) // 2
    source_of, taker = sizes[1:1 + 2 * couples:2], sizes[2:2 + 2 * couples:2]
    slack = jnp.minimum(source_of - 1, reach - taker)
    moved = jax.random.randint(jax.random.fold_in(own_key, 1), (couples,), 0, 1 << 20) % (slack + 1)
    sizes = sizes.at[1:1 + 2 * couples:2].set(source_of - moved).at[2:2 + 2 * couples:2].set(taker + moved)
    return sizes[jax.random.permutation(jax.random.fold_in(own_key, 2), count)]


def centred(rng, extent, scale, bound, cuts=(), kind=jnp.bfloat16):
    loudness = level_of(rng, extent, cuts, -0.22, 0.18) if cuts else 1.0
    drawn = jax.random.normal(rng, extent, jnp.float32) * scale * loudness
    return jnp.minimum(jnp.maximum(drawn, -bound), bound).astype(kind)


def setup_inputs(seed: int = 0) -> dict:
    arg_keys = jax.random.split(jax.random.key(seed), 13)
    return {
        "tokens": centred(arg_keys[0], (SEQS, LEN, D), 1.0, 6.0, ((0, 4), (1, 8))),
        "segments": jax.vmap(lambda own: jnp.searchsorted(jnp.cumsum(uneven(own, DOCS, LEN, DOC_MOST, 2)), jnp.arange(LEN), side="right"))(jax.random.split(arg_keys[1], SEQS)).reshape((SEQS, LEN)).astype(jnp.int32),
        "gain_in": jnp.clip(1.0 + 0.1 * jax.random.normal(arg_keys[2], (D,), jnp.float32), 0.5, 1.5),
        "w_in": centred(arg_keys[3], (D, PROJ), D ** -0.5, 0.15625, ((0, 32),)),
        "conv_w": centred(arg_keys[4], (KERNEL, CHANNELS), KERNEL ** -0.5, 3.0, (), jnp.float32),
        "conv_b": centred(arg_keys[5], (CHANNELS,), 0.5, 3.0, (), jnp.float32),
        "dt_bias": jnp.clip(jax.random.uniform(arg_keys[6], (HEADS,), jnp.float32, -6.0, -1.0), -6.0, -1.0),
        "a_log": jnp.clip(jax.random.uniform(arg_keys[7], (HEADS,), jnp.float32, 0.0, 2.5), 0.0, 2.5),
        "skip": jnp.clip(jax.random.uniform(arg_keys[8], (HEADS,), jnp.float32, 0.5, 1.5), 0.5, 1.5),
        "gain_out": jnp.clip(1.0 + 0.1 * jax.random.normal(arg_keys[9], (INNER,), jnp.float32), 0.5, 1.5),
        "w_out": centred(arg_keys[10], (INNER, D), INNER ** -0.5, 0.109375, ((0, 32),)),
        "cotangent": centred(arg_keys[11], (SEQS, LEN, D), 1.0, 6.0, ((0, 4), (1, 8))),
    }


EPSILON = 1e-05
HIGHEST = lax.Precision.HIGHEST

@jax.custom_vjp
def low(v):
    return lax.optimization_barrier(v.astype(jnp.bfloat16)).astype(jnp.float32)

@jax.custom_vjp
def low_back(v):
    return v

def low_keep(v):
    return (low(v), None)

def low_pass(kept, grad):
    return (grad,)

def back_keep(v):
    return (v, None)

def back_low(kept, grad):
    return (low(grad),)
low.defvjp(low_keep, low_pass)
low_back.defvjp(back_keep, back_low)

def norm_rows(values, gain):
    return values * lax.rsqrt(lax.optimization_barrier(jnp.mean(values * values, axis=-1, keepdims=True)) + EPSILON) * gain

def causal_conv(values, seg, weight, bias):
    total = bias + weight[KERNEL - 1] * values
    for offset in range(1, KERNEL):
        shifted = jnp.concatenate([jnp.zeros((offset, values.shape[1]), values.dtype), values[:-offset]], axis=0)
        earlier = jnp.concatenate([jnp.full((offset,), -1, jnp.int32), seg[:-offset]], axis=0)
        keep_mask = (earlier == seg)[:, None]
        total = total + weight[KERNEL - 1 - offset] * jnp.where(keep_mask, shifted, 0.0)
    return total

def state_mix(values, b_in, c_in, dt_raw, seg, dt_bias, a_log, skip):
    length = values.shape[0]
    head_count = dt_raw.shape[1]
    blocks = length // STRETCH
    step_size = jax.nn.softplus(dt_raw + dt_bias)
    rates = step_size * -jnp.exp(a_log)
    values_heads = values.reshape(length, head_count, HEAD_DIM)
    order = jnp.arange(STRETCH)
    causal = order[:, None] >= order[None, :]

    def one_block(carried, pieces):
        memory, prev_seg = carried
        x_blk, b_blk, c_blk, dt_blk, rate_blk, seg_blk = pieces
        cumul = jnp.cumsum(rate_blk, axis=0)
        same = causal & (seg_blk[:, None] == seg_blk[None, :])
        spans = cumul.T[:, :, None] - cumul.T[:, None, :]
        decays = jnp.where(same[None], jnp.exp(jnp.where(same[None], spans, 0.0)), 0.0)
        scores = jnp.dot(c_blk, b_blk.T, precision=HIGHEST)
        mixing = decays * scores[None] * dt_blk.T[:, None, :]
        inside = jnp.einsum('hts,shp->thp', mixing, x_blk, precision=HIGHEST)
        carry_on = jnp.where(seg_blk == prev_seg, 1.0, 0.0).astype(jnp.float32)
        entry = jnp.exp(cumul) * carry_on[:, None]
        outside = jnp.einsum('tn,hpn->thp', c_blk, memory, precision=HIGHEST) * entry[:, :, None]
        last_seg = seg_blk[-1]
        to_end = jnp.where((seg_blk == last_seg)[:, None], jnp.exp(cumul[-1][None, :] - cumul), 0.0) * dt_blk
        fresh = jnp.einsum('sh,shp,sn->hpn', to_end, x_blk, b_blk, precision=HIGHEST)
        kept_old = jnp.where(last_seg == prev_seg, 1.0, 0.0).astype(jnp.float32)
        memory = memory * (jnp.exp(cumul[-1]) * kept_old)[:, None, None] + fresh
        return ((memory, last_seg), inside + outside)
    pieces = (values_heads.reshape(blocks, STRETCH, head_count, HEAD_DIM), b_in.reshape(blocks, STRETCH, b_in.shape[1]), c_in.reshape(blocks, STRETCH, c_in.shape[1]), step_size.reshape(blocks, STRETCH, head_count), rates.reshape(blocks, STRETCH, head_count), seg.reshape(blocks, STRETCH))
    start = (jnp.zeros((head_count, HEAD_DIM, b_in.shape[1]), jnp.float32), jnp.array(-1, jnp.int32))
    final_state, outputs = lax.scan(jax.checkpoint(one_block), start, pieces)
    result = outputs.reshape(length, head_count, HEAD_DIM) + values_heads * skip[None, :, None]
    return result.reshape(length, head_count * HEAD_DIM)

def mix_layer(xbc, dt_raw, seg, conv_w, conv_b, dt_bias, a_log, skip):
    act = jax.nn.silu(causal_conv(xbc, seg, conv_w, conv_b))
    width = xbc.shape[1] - 2 * STATE
    return state_mix(act[:, :width], act[:, width:width + STATE], act[:, width + STATE:], dt_raw, seg, dt_bias, a_log, skip)

def forward(rows, seg, gain_in, w_in, conv_w, conv_b, dt_bias, a_log, skip, gain_out, w_out):
    normed = low(norm_rows(rows, gain_in))
    projected = low(low_back(jnp.dot(normed, w_in, precision=HIGHEST)))
    gate = projected[:, :INNER]
    xbc = projected[:, INNER:INNER + CHANNELS]
    dt_raw = projected[:, INNER + CHANNELS:]
    mixed_heads = mix_layer(xbc, dt_raw, seg, conv_w, conv_b, dt_bias, a_log, skip)
    mixed_heads = low(low_back(mixed_heads))
    gated = low(norm_rows(mixed_heads * jax.nn.silu(gate), gain_out))
    return rows + jnp.dot(gated, w_out, precision=HIGHEST)

def reference(tokens, segments, gain_in, w_in, conv_w, conv_b, dt_bias, a_log, skip, gain_out, w_out, cotangent):
    params = (gain_in.astype(jnp.float32), w_in.astype(jnp.float32), conv_w.astype(jnp.float32), conv_b.astype(jnp.float32), dt_bias.astype(jnp.float32), a_log.astype(jnp.float32), skip.astype(jnp.float32), gain_out.astype(jnp.float32), w_out.astype(jnp.float32))

    def one_sequence(totals, pieces):
        rows, seg, grad_rows = pieces

        def layer(inputs, *weights):
            return forward(inputs, seg, *weights)
        result, pull = jax.vjp(layer, rows.astype(jnp.float32), *params)
        grads = pull(grad_rows.astype(jnp.float32))
        totals = tuple((left + right for left, right in zip(totals, grads[1:])))
        return (totals, (result.astype(jnp.bfloat16), grads[0]))
    start = tuple((jnp.zeros_like(param) for param in params))
    totals, (outputs, input_grads) = lax.scan(one_sequence, start, (tokens, segments, cotangent))
    return (outputs, input_grads, totals[0], totals[1], totals[2], totals[3], totals[4], totals[5], totals[6], totals[7], totals[8])
```

```python
import functools

import jax
import jax.numpy as jnp
from jax import lax
from jax.experimental import pallas as pl
from jax.experimental.pallas import tpu as pltpu
from jax.sharding import PartitionSpec as P

D = 1536
HEADS = 48
HEAD_DIM = 64
STATE = 128
KERNEL = 4
INNER = 3072
LANES = 128
HALO = 16
EPSILON = 1e-05
F32 = jnp.float32
BF16 = jnp.bfloat16


def mm(a, b):
    return jnp.dot(a.astype(BF16), b.astype(BF16), preferred_element_type=F32)


def mm_tr(a, b):
    return lax.dot_general(
        a.astype(BF16), b.astype(BF16), (((1,), (1,)), ((), ())), preferred_element_type=F32
    )


def tr_mm(a, b):
    return lax.dot_general(
        a.astype(BF16), b.astype(BF16), (((0,), (0,)), ((), ())), preferred_element_type=F32
    )


def pieces(a, count):
    out = []
    for _ in range(count - 1):
        part = a.astype(BF16)
        out.append(part)
        a = a - part.astype(F32)
    out.append(a.astype(BF16))
    return out


def ones_mm(ones, a, count):
    return sum(jnp.dot(ones, part, preferred_element_type=F32) for part in pieces(a, count))


def mm_ones(a, ones, count):
    return sum(jnp.dot(part, ones, preferred_element_type=F32) for part in pieces(a, count))


def mm_ones_tr(a, ones, count):
    return sum(
        lax.dot_general(part, ones, (((1,), (1,)), ((), ())), preferred_element_type=F32)
        for part in pieces(a, count)
    )


def iota(shape, dim):
    return lax.broadcasted_iota(jnp.int32, shape, dim)


def softplus(v):
    return jnp.maximum(v, 0.0) + jnp.log1p(jnp.exp(-jnp.abs(v)))


def sigmoid(v):
    return 1.0 / (1.0 + jnp.exp(-v))


def causal_conv(ext, current, halo, weight, bias, offset):
    length = current.shape[0]
    ext[0:HALO, :] = halo
    ext[HALO : HALO + length, :] = current
    total = bias + weight[KERNEL - 1 : KERNEL, :] * current
    for back in range(1, KERNEL):
        shifted = jnp.where(offset >= back, ext[pl.ds(HALO - back, length), :], 0.0)
        total = total + weight[KERNEL - 1 - back : KERNEL - back, :] * shifted
    return total


def head_tiles(width):
    out = []
    for start in range(0, width, LANES):
        size = min(LANES, width - start)
        heads = [start // HEAD_DIM + i for i in range(size // HEAD_DIM)]
        out.append((start, size, heads))
    return out


def masked_heads(tile, heads):
    if len(heads) == 1:
        return tile
    lane = iota(tile.shape, 1) // HEAD_DIM
    return jnp.concatenate(
        [jnp.where(lane == i, tile, jnp.zeros_like(tile)) for i in range(len(heads))], axis=0
    )


def expander(width):
    return (iota((LANES, width), 1) // HEAD_DIM == iota((LANES, width), 0)).astype(BF16)


def chunk_common(x, xh, tail, tailh, offset, params, ext_x, ext_t, width):
    wx, bx, wt, bt, heads_p = params
    length = x.shape[0]
    conv_x = causal_conv(ext_x, x.astype(F32), xh.astype(F32), wx, bx, offset)
    conv_t = causal_conv(
        ext_t,
        tail[:, : 2 * STATE].astype(F32),
        tailh[:, : 2 * STATE].astype(F32),
        wt,
        bt,
        offset,
    )
    raw = tail[:, 2 * STATE :].astype(F32) + heads_p[0:1, :]
    step = softplus(raw)
    decay_rate = jnp.exp(heads_p[1:2, :])
    rate = -step * decay_rate
    tril = (iota((length, length), 0) >= iota((length, length), 1)).astype(BF16)
    cumul = ones_mm(tril, rate, 3)
    spread = expander(width)
    row = iota((length, 1), 0)
    entry = jnp.where(offset > row.astype(F32), jnp.exp(cumul), 0.0)
    last_off = offset[length - 1 : length, :]
    same_last = row.astype(F32) >= (length - 1) - last_off
    to_end = jnp.where(same_last, jnp.exp(cumul[length - 1 : length, :] - cumul), 0.0)
    step_x = mm_ones(step, spread, 2)
    entry_x = mm_ones(entry, spread, 2)
    end_x = mm_ones(to_end, spread, 2)
    return conv_x, conv_t, raw, step, rate, decay_rate, cumul, spread, step_x, entry_x, end_x


def forward_kernel(
    x_ref, xh_ref, tail_ref, tailh_ref, off_ref, wx_ref, bx_ref, wt_ref, bt_ref, hp_ref, skip_ref,
    y_ref, state_ref, memory, ext_x, ext_t,
):
    seqs, length, width = x_ref.shape[1:]

    @pl.when(pl.program_id(0) == 0)
    def _():
        memory[...] = jnp.zeros_like(memory)

    params = (wx_ref[...], bx_ref[...], wt_ref[...], bt_ref[...], hp_ref[...])
    for q in range(seqs):
        offset = off_ref[0, q]
        conv_x, conv_t, _, _, _, _, cumul, _, step_x, entry_x, end_x = chunk_common(
            x_ref[0, q], xh_ref[0, q], tail_ref[0, q], tailh_ref[0, q], offset, params,
            ext_x.at[q], ext_t.at[q], width,
        )
        xs = conv_x * sigmoid(conv_x)
        act_t = conv_t * sigmoid(conv_t)
        bs = act_t[:, :STATE].astype(BF16)
        cs = act_t[:, STATE:].astype(BF16)
        scaled = xs * step_x
        scores = mm_tr(cs, bs)
        gap = iota((length, length), 0) - iota((length, length), 1)
        same = (gap >= 0) & (gap.astype(F32) <= offset)
        cumul_t = cumul.T
        old = memory[q]
        old_low = old.astype(BF16)
        state_ref[0, q] = old_low
        outside = mm(cs, old_low) * entry_x + skip_ref[...] * xs
        for start, size, heads in head_tiles(width):
            mixing = []
            for head in heads:
                spans = cumul[:, head : head + 1] - cumul_t[head : head + 1, :]
                decays = jnp.exp(jnp.where(same, spans, -1e30))
                mixing.append((decays * scores).astype(BF16))
            tile = masked_heads(scaled[:, start : start + size].astype(BF16), heads)
            mix = mixing[0] if len(heads) == 1 else jnp.concatenate(mixing, axis=1)
            inside = jnp.dot(mix, tile, preferred_element_type=F32)
            y_ref[0, q, :, start : start + size] = (
                inside + outside[:, start : start + size]
            ).astype(BF16)
        fresh = tr_mm(bs, scaled * end_x)
        memory[q] = old * entry_x[length - 1 : length, :] + fresh


def backward_kernel(
    x_ref, xh_ref, tail_ref, tailh_ref, off_ref, offr_ref, rem_ref, dy_ref, state_ref,
    wx_ref, bx_ref, wt_ref, bt_ref, hp_ref, skip_ref,
    dx_ref, dtail_ref, gx_ref, gt_ref, gh_ref,
    memory, ext_x, ext_t, next_x, next_t,
):
    seqs, length, width = x_ref.shape[1:]

    @pl.when(pl.program_id(0) == 0)
    def _():
        memory[...] = jnp.zeros_like(memory)
        gx_ref[...] = jnp.zeros_like(gx_ref)
        gt_ref[...] = jnp.zeros_like(gt_ref)
        gh_ref[...] = jnp.zeros_like(gh_ref)
        next_x[:, length:, :] = jnp.zeros_like(next_x[:, length:, :])
        next_t[:, length:, :] = jnp.zeros_like(next_t[:, length:, :])

    params = (wx_ref[...], bx_ref[...], wt_ref[...], bt_ref[...], hp_ref[...])
    for q in range(seqs):
        offset = off_ref[0, q]
        conv_x, conv_t, raw, step, rate, decay_rate, cumul, spread, step_x, entry_x, end_x = (
            chunk_common(
                x_ref[0, q], xh_ref[0, q], tail_ref[0, q], tailh_ref[0, q], offset, params,
                ext_x.at[q], ext_t.at[q], width,
            )
        )
        sig_x = sigmoid(conv_x)
        xs = conv_x * sig_x
        slope_x = sig_x + xs * (1.0 - sig_x)
        sig_t = sigmoid(conv_t)
        act_t = conv_t * sig_t
        slope_t = sig_t + act_t * (1.0 - sig_t)
        bs = act_t[:, :STATE].astype(BF16)
        cs = act_t[:, STATE:].astype(BF16)
        scaled = xs * step_x
        scaled_low = scaled.astype(BF16)
        dy_low = dy_ref[0, q]
        dy = dy_low.astype(F32)
        scores = mm_tr(bs, cs)
        rows, cols = iota((length, length), 0), iota((length, length), 1)
        gap = cols - rows
        same = (gap >= 0) & (gap.astype(F32) <= offr_ref[0, q])
        strict = gap > 0
        upper = (rows >= cols).astype(BF16)
        cumul_t = cumul.T
        old = state_ref[0, q]
        grad_state = memory[q]
        state_low = grad_state.astype(BF16)
        grad_scores = jnp.zeros((length, length), F32)
        grad_scaled = []
        inside_rows = []
        for start, size, heads in head_tiles(width):
            dy_tile = masked_heads(dy_low[:, start : start + size], heads)
            grad_mix = mm_tr(scaled_low[:, start : start + size], dy_tile)
            mixing = []
            for place, head in enumerate(heads):
                spans = cumul_t[head : head + 1, :] - cumul[:, head : head + 1]
                decays = jnp.exp(jnp.where(same, spans, -1e30))
                weighted = grad_mix[:, place * length : (place + 1) * length] * decays
                grad_scores = grad_scores + weighted
                mixing.append((decays * scores).astype(BF16))
                terms = jnp.where(strict, weighted * scores, 0.0).astype(BF16)
                sums = jnp.dot(terms, upper, preferred_element_type=F32)
                inside_rows.append(
                    jnp.sum(jnp.where(strict, sums, 0.0), axis=0, keepdims=True)
                )
            mix = mixing[0] if len(heads) == 1 else jnp.concatenate(mixing, axis=1)
            grad_scaled.append(jnp.dot(mix, dy_tile, preferred_element_type=F32))
        inside_rows.append(jnp.zeros((LANES - len(inside_rows), length), F32))
        inside = jnp.concatenate(inside_rows, axis=0).T
        from_end = mm(bs, state_low) * end_x
        grad_scaled = jnp.concatenate(grad_scaled, axis=1) + from_end
        entry_dy = dy * entry_x
        entry_dy_low = entry_dy.astype(BF16)
        out_terms = mm(cs, old) * entry_dy
        end_terms = scaled * from_end
        grad_step = mm_ones_tr(xs * grad_scaled, spread, 2)
        out_terms = mm_ones_tr(out_terms, spread, 2)
        end_terms = mm_ones_tr(end_terms, spread, 2)
        keep_row = entry_x[length - 1 : length, :]
        carried = jnp.sum(grad_state * old.astype(F32), axis=0, keepdims=True) * keep_row
        carried = mm_ones_tr(jnp.broadcast_to(carried, (8, width)), spread, 2)[0:1, :]
        triu = (cols >= rows).astype(BF16)
        below = (rows > cols).astype(BF16)
        grad_rate = inside + ones_mm(triu, out_terms, 2) + ones_mm(below, end_terms, 2) + carried
        grad_step = grad_step - decay_rate * grad_rate
        grad_raw = grad_step * sigmoid(raw)
        grad_scores_low = grad_scores.astype(BF16)
        grad_b = mm(grad_scores_low, cs) + mm_tr(scaled * end_x, state_low)
        grad_c = tr_mm(grad_scores_low, bs) + mm_tr(entry_dy_low, old)
        memory[q] = grad_state * keep_row + tr_mm(cs, entry_dy_low)
        conv_grad_x = (skip_ref[...] * dy + step_x * grad_scaled) * slope_x
        conv_grad_t = jnp.concatenate([grad_b, grad_c], axis=1) * slope_t

        remain = rem_ref[0, q]
        for grad, ext, nxt, weight, out, sums, cols_of in (
            (conv_grad_x, ext_x.at[q], next_x.at[q], params[0], dx_ref, gx_ref, width),
            (conv_grad_t, ext_t.at[q], next_t.at[q], params[2], dtail_ref, gt_ref, 2 * STATE),
        ):
            current = ext[pl.ds(HALO, length), :]
            sums[KERNEL : KERNEL + 1, :] += jnp.sum(grad, axis=0, keepdims=True)
            sums[KERNEL - 1 : KERNEL, :] += jnp.sum(grad * current, axis=0, keepdims=True)
            nxt[0:length, :] = grad
            total = weight[KERNEL - 1 : KERNEL, :] * grad
            for back in range(1, KERNEL):
                tap = KERNEL - 1 - back
                shifted = jnp.where(offset >= back, ext[pl.ds(HALO - back, length), :], 0.0)
                sums[tap : tap + 1, :] += jnp.sum(grad * shifted, axis=0, keepdims=True)
                ahead = jnp.where(remain >= back, nxt[pl.ds(back, length), :], 0.0)
                total = total + weight[tap : tap + 1, :] * ahead
            nxt[length:, :] = grad[0:HALO, :]
            out[0, q, :, :cols_of] = total.astype(BF16)
        gx_ref[KERNEL + 1 : KERNEL + 2, :] += jnp.sum(dy * xs, axis=0, keepdims=True)
        dtail_ref[0, q, :, 2 * STATE :] = grad_raw.astype(BF16)
        gh_ref[0:1, :] += jnp.sum(grad_raw, axis=0, keepdims=True)
        gh_ref[1:2, :] += jnp.sum(grad_rate * rate, axis=0, keepdims=True)


def whole_spec(shape):
    return pl.BlockSpec(shape, lambda i: (0,) * len(shape))


def forward_mix(x, tail, off_col, wx, bx, wt, bt, heads_p, skip_x):
    steps, seqs, length, width = x.shape
    wide = tail.shape[3]

    def block(cols):
        return pl.BlockSpec((1, seqs, length, cols), lambda i: (i, 0, 0, 0))

    def before(cols):
        return pl.BlockSpec(
            (1, seqs, HALO, cols), lambda i: (jnp.maximum(i - 1, 0), 0, length // HALO - 1, 0)
        )

    return pl.pallas_call(
        forward_kernel,
        grid=(steps,),
        in_specs=[
            block(width), before(width), block(wide), before(wide), block(1),
            whole_spec(wx.shape), whole_spec(bx.shape), whole_spec(wt.shape), whole_spec(bt.shape),
            whole_spec(heads_p.shape), whole_spec(skip_x.shape),
        ],
        out_specs=[
            block(width),
            pl.BlockSpec((1, seqs, STATE, width), lambda i: (i, 0, 0, 0)),
        ],
        out_shape=[
            jax.ShapeDtypeStruct(x.shape, BF16),
            jax.ShapeDtypeStruct((steps, seqs, STATE, width), BF16),
        ],
        scratch_shapes=[
            pltpu.VMEM((seqs, STATE, width), F32),
            pltpu.VMEM((seqs, HALO + length, width), F32),
            pltpu.VMEM((seqs, HALO + length, 2 * STATE), F32),
        ],
        compiler_params=pltpu.CompilerParams(
            dimension_semantics=("arbitrary",), vmem_limit_bytes=32 << 20
        ),
        cost_estimate=pl.CostEstimate(
            flops=steps * seqs * 150_000_000, transcendentals=0, bytes_accessed=8_000_000
        ),
        name="mix_forward",
    )(x, x, tail, tail, off_col, wx, bx, wt, bt, heads_p, skip_x)


def backward_mix(x, tail, off_col, off_row, rem_col, dy, states, wx, bx, wt, bt, heads_p, skip_x):
    steps, seqs, length, width = x.shape
    wide = tail.shape[3]

    def block(cols):
        return pl.BlockSpec((1, seqs, length, cols), lambda i: (steps - 1 - i, 0, 0, 0))

    def before(cols):
        return pl.BlockSpec(
            (1, seqs, HALO, cols),
            lambda i: (jnp.maximum(steps - 2 - i, 0), 0, length // HALO - 1, 0),
        )

    return pl.pallas_call(
        backward_kernel,
        grid=(steps,),
        in_specs=[
            block(width), before(width), block(wide), before(wide), block(1),
            pl.BlockSpec((1, seqs, 1, length), lambda i: (steps - 1 - i, 0, 0, 0)),
            block(1), block(width),
            pl.BlockSpec((1, seqs, STATE, width), lambda i: (steps - 1 - i, 0, 0, 0)),
            whole_spec(wx.shape), whole_spec(bx.shape), whole_spec(wt.shape), whole_spec(bt.shape),
            whole_spec(heads_p.shape), whole_spec(skip_x.shape),
        ],
        out_specs=[
            block(width), block(wide),
            whole_spec((8, width)), whole_spec((8, 2 * STATE)), whole_spec((8, LANES)),
        ],
        out_shape=[
            jax.ShapeDtypeStruct(x.shape, BF16),
            jax.ShapeDtypeStruct(tail.shape, BF16),
            jax.ShapeDtypeStruct((8, width), F32),
            jax.ShapeDtypeStruct((8, 2 * STATE), F32),
            jax.ShapeDtypeStruct((8, LANES), F32),
        ],
        scratch_shapes=[
            pltpu.VMEM((seqs, STATE, width), F32),
            pltpu.VMEM((seqs, HALO + length, width), F32),
            pltpu.VMEM((seqs, HALO + length, 2 * STATE), F32),
            pltpu.VMEM((seqs, length + HALO, width), F32),
            pltpu.VMEM((seqs, length + HALO, 2 * STATE), F32),
        ],
        compiler_params=pltpu.CompilerParams(
            dimension_semantics=("arbitrary",), vmem_limit_bytes=40 << 20
        ),
        cost_estimate=pl.CostEstimate(
            flops=steps * seqs * 400_000_000, transcendentals=0, bytes_accessed=12_000_000
        ),
        name="mix_backward",
    )(x, x, tail, tail, off_col, off_row, rem_col, dy, states, wx, bx, wt, bt, heads_p, skip_x)


def chunked(per_token, steps, length):
    return per_token.reshape(per_token.shape[0], steps, length).transpose(1, 0, 2)


def spread_last(piece, start, whole):
    zeros_full = jnp.zeros(piece.shape[:-1] + (whole,), F32)
    return lax.dynamic_update_slice_in_dim(zeros_full, piece, start, piece.ndim - 1)


def local(
    tokens, segments, gain_in, w_in, conv_w, conv_b, dt_bias, a_log, skip, gain_out, w_out,
    cotangent,
):
    steps = lax.axis_size("seq")
    shards = lax.axis_size("fsdp")
    rank = lax.axis_index("seq")
    seqs, length, _ = tokens.shape
    width = INNER // steps
    heads = HEADS // steps
    rows_in = w_in.shape[0]

    def mine(array, size):
        return lax.dynamic_slice_in_dim(array, rank * size, size, array.ndim - 1)

    wide = tokens.astype(F32)
    scale_in = lax.rsqrt(jnp.mean(wide * wide, axis=-1, keepdims=True) + EPSILON)
    normed = (wide * scale_in * gain_in).astype(BF16)
    h_all = lax.all_gather(normed, "seq", axis=0)
    cot_all = lax.all_gather(cotangent, "seq", axis=0)

    zx_local = w_in[:, : 2 * INNER].reshape(rows_in, 2, steps, width).transpose(2, 0, 1, 3)
    zx_local = zx_local.reshape(steps, rows_in, 2 * width)
    zx = lax.all_to_all(zx_local, "seq", split_axis=0, concat_axis=0, tiled=True)
    zx = lax.all_gather(zx, "fsdp", axis=1, tiled=True).reshape(D, 2 * width)
    tail_w = lax.all_gather(w_in[:, 2 * INNER :], ("seq", "fsdp"), axis=0, tiled=True)
    tail_w = jnp.concatenate(
        [
            tail_w[:, : 2 * STATE],
            mine(tail_w[:, 2 * STATE :], heads),
            jnp.zeros((D, LANES - heads), BF16),
        ],
        axis=1,
    )
    out_w = lax.all_gather(w_out, "fsdp", axis=0, tiled=True)
    w_z, w_x = zx[:, :width], zx[:, width:]

    total = steps * length
    index = lax.broadcasted_iota(jnp.int32, (seqs, total), 1)
    starts = jnp.concatenate(
        [jnp.ones((seqs, 1), bool), segments[:, 1:] != segments[:, :-1]], axis=1
    )
    first = lax.cummax(jnp.where(starts, index, 0), axis=1)
    ends = jnp.concatenate([starts[:, 1:], jnp.ones((seqs, 1), bool)], axis=1)
    last = lax.cummin(jnp.where(ends, index, total), axis=1, reverse=True)
    off = chunked((index - first).astype(F32), steps, length)
    rem = chunked((last - index).astype(F32), steps, length)
    off_col, off_row, rem_col = off[..., None], off[:, :, None, :], rem[..., None]

    wx, bx = mine(conv_w[:, :INNER], width), mine(conv_b[None, :INNER], width)
    wt, bt = conv_w[:, INNER:], conv_b[None, INNER:]
    heads_p = jnp.stack([mine(dt_bias, heads), mine(a_log, heads)])
    heads_p = jnp.pad(heads_p, ((0, 6), (0, LANES - heads)))
    skip_x = jnp.repeat(mine(skip, heads), HEAD_DIM)[None]
    gain_mine = mine(gain_out, width)

    def dot(a, b):
        return lax.dot_general(a, b, (((3,), (0,)), ((), ())), preferred_element_type=F32)

    def dot_tr(a, b):
        return lax.dot_general(a, b, (((3,), (1,)), ((), ())), preferred_element_type=F32)

    def dot_tokens(a, b):
        dims = (0, 1, 2)
        return lax.dot_general(a, b, ((dims, dims), ((), ())), preferred_element_type=F32)

    z = dot(h_all, w_z).astype(BF16)
    x = dot(h_all, w_x).astype(BF16)
    tail = dot(h_all, tail_w).astype(BF16)
    y, states = forward_mix(x, tail, off_col, wx, bx, wt, bt, heads_p, skip_x)

    grad_yn = dot_tr(cot_all, out_w)
    z_wide, y_wide = z.astype(F32), y.astype(F32)
    sig = sigmoid(z_wide)
    silu_z = z_wide * sig
    gated = y_wide * silu_z
    sums = jnp.stack(
        [
            jnp.sum(gated * gated, axis=-1),
            jnp.sum(grad_yn * gain_mine * gated, axis=-1),
        ]
    )
    sums = lax.psum(sums, "seq")
    scale = lax.rsqrt(sums[0] / INNER + EPSILON)[..., None]
    slope = sums[1][..., None] * (scale * scale * scale / INNER)
    y_normed = (gated * scale * gain_mine).astype(BF16)
    mixed_part = dot(y_normed, out_w).astype(BF16)
    mixed = lax.psum_scatter(mixed_part, "seq", scatter_dimension=0)
    mixed = (wide + mixed.astype(F32)).astype(BF16)
    out_part = dot_tokens(y_normed, cot_all)
    w_out_grad = lax.psum_scatter(out_part, "fsdp", scatter_dimension=0, tiled=True)
    gain_out_part = jnp.sum(grad_yn * gated * scale, axis=(0, 1, 2))
    grad_gated = scale * gain_mine * grad_yn - gated * slope
    dy = (grad_gated * silu_z).astype(BF16)
    dz = (grad_gated * y_wide * (sig + silu_z * (1.0 - sig))).astype(BF16)

    dx, dtail, sums_x, sums_t, sums_h = backward_mix(
        x, tail, off_col, off_row, rem_col, dy, states, wx, bx, wt, bt, heads_p, skip_x
    )

    grad_h = (dot_tr(dz, w_z) + dot_tr(dx, w_x) + dot_tr(dtail, tail_w)).astype(BF16)
    grad_h = lax.psum_scatter(grad_h, "seq", scatter_dimension=0).astype(F32)
    part_z = dot_tokens(h_all, dz)
    part_x = dot_tokens(h_all, dx)
    part_t = dot_tokens(h_all, dtail)
    part = jnp.concatenate([part_z, part_x, part_t[:, 2 * STATE : 2 * STATE + heads]], axis=1)
    part = part.reshape(steps, shards, rows_in, 2 * width + heads)
    part = lax.psum_scatter(part, "fsdp", scatter_dimension=1)
    part = lax.all_to_all(part.astype(BF16), "seq", split_axis=0, concat_axis=0, tiled=True)
    part = part.astype(F32)
    bc_grad = lax.psum_scatter(
        part_t[:, : 2 * STATE], ("seq", "fsdp"), scatter_dimension=0, tiled=True
    )

    def columns(start, size):
        piece = part[:, :, start : start + size].transpose(1, 0, 2)
        return piece.reshape(rows_in, steps * size)

    w_in_grad = jnp.concatenate(
        [columns(0, width), columns(width, width), bc_grad, columns(2 * width, heads)], axis=1
    )

    scaled = grad_h * gain_in
    unit = wide * scale_in
    tokens_grad = cotangent.astype(F32) + scale_in * (
        scaled - unit * jnp.mean(scaled * unit, axis=-1, keepdims=True)
    )
    gain_in_part = jnp.sum(grad_h * unit, axis=(0, 1))

    skip_part = jnp.sum(sums_x[KERNEL + 1].reshape(heads, HEAD_DIM), axis=-1)
    reduced = lax.psum(
        (
            gain_in_part,
            spread_last(gain_out_part, rank * width, INNER),
            spread_last(sums_x[: KERNEL + 1], rank * width, INNER),
            sums_t[: KERNEL + 1],
            spread_last(sums_h[0, :heads], rank * heads, HEADS),
            spread_last(sums_h[1, :heads], rank * heads, HEADS),
            spread_last(skip_part, rank * heads, HEADS),
        ),
        ("seq", "fsdp"),
    )
    conv_grads = jnp.concatenate([reduced[2], reduced[3]], axis=1)
    return (
        mixed, tokens_grad, reduced[0], w_in_grad, conv_grads[:KERNEL], conv_grads[KERNEL],
        reduced[4], reduced[5], reduced[6], reduced[1], w_out_grad,
    )


def solution(mesh):
    by_token = P("fsdp", "seq", None)
    by_row = P(("seq", "fsdp"), None)
    placed = (
        by_token, P("fsdp", None), P(), by_row, P(), P(), P(), P(), P(), P(), by_row, by_token,
    )
    return jax.shard_map(
        local,
        mesh=mesh,
        in_specs=placed,
        out_specs=(by_token, by_token, P(), by_row, P(), P(), P(), P(), P(), P(), by_row),
        check_vma=False,
    )
```

```python
import functools

import jax
import jax.numpy as jnp
import numpy as np
from jax import lax
from jax.experimental import pallas as pl
from jax.experimental.pallas import tpu as pltpu
from jax.sharding import PartitionSpec as P

D = 1536
HEADS = 48
HEAD_DIM = 64
STATE = 128
KERNEL = 4
INNER = 3072
LANES = 128
HALO = 16
EPSILON = 1e-05
F32 = jnp.float32
BF16 = jnp.bfloat16


def mm(a, b):
    return jnp.dot(a.astype(BF16), b.astype(BF16), preferred_element_type=F32)


def mm_tr(a, b):
    return lax.dot_general(
        a.astype(BF16), b.astype(BF16), (((1,), (1,)), ((), ())), preferred_element_type=F32
    )


def tr_mm(a, b):
    return lax.dot_general(
        a.astype(BF16), b.astype(BF16), (((0,), (0,)), ((), ())), preferred_element_type=F32
    )


def pieces(a, count):
    out = []
    for _ in range(count - 1):
        part = a.astype(BF16)
        out.append(part)
        a = a - part.astype(F32)
    out.append(a.astype(BF16))
    return out


def ones_mm(ones, a, count):
    return sum(jnp.dot(ones, part, preferred_element_type=F32) for part in pieces(a, count))


def mm_ones(a, ones, count):
    return sum(jnp.dot(part, ones, preferred_element_type=F32) for part in pieces(a, count))


def mm_ones_tr(a, ones, count):
    return sum(
        lax.dot_general(part, ones, (((1,), (1,)), ((), ())), preferred_element_type=F32)
        for part in pieces(a, count)
    )


def iota(shape, dim):
    return lax.broadcasted_iota(jnp.int32, shape, dim)


def softplus(v):
    return jnp.maximum(v, 0.0) + jnp.log1p(jnp.exp(-jnp.abs(v)))


def sigmoid(v):
    return 1.0 / (1.0 + jnp.exp(-v))


def causal_conv(ext, current, halo, weight, bias, offset):
    length = current.shape[0]
    ext[0:HALO, :] = halo
    ext[HALO : HALO + length, :] = current
    total = bias + weight[KERNEL - 1 : KERNEL, :] * current
    for back in range(1, KERNEL):
        shifted = jnp.where(offset >= back, ext[pl.ds(HALO - back, length), :], 0.0)
        total = total + weight[KERNEL - 1 - back : KERNEL - back, :] * shifted
    return total


def head_tiles(width):
    out = []
    for start in range(0, width, LANES):
        size = min(LANES, width - start)
        heads = [start // HEAD_DIM + i for i in range(size // HEAD_DIM)]
        out.append((start, size, heads))
    return out


def masked_heads(tile, heads):
    if len(heads) == 1:
        return tile
    lane = iota(tile.shape, 1) // HEAD_DIM
    return jnp.concatenate(
        [jnp.where(lane == i, tile, jnp.zeros_like(tile)) for i in range(len(heads))], axis=0
    )


def expander(width):
    return (iota((LANES, width), 1) // HEAD_DIM == iota((LANES, width), 0)).astype(BF16)


def chunk_common(x, xh, tail, tailh, offset, params, ext_x, ext_t, width):
    wx, bx, wt, bt, heads_p = params
    length = x.shape[0]
    conv_x = causal_conv(ext_x, x.astype(F32), xh.astype(F32), wx, bx, offset)
    conv_t = causal_conv(
        ext_t,
        tail[:, : 2 * STATE].astype(F32),
        tailh[:, : 2 * STATE].astype(F32),
        wt,
        bt,
        offset,
    )
    raw = tail[:, 2 * STATE :].astype(F32) + heads_p[0:1, :]
    step = softplus(raw)
    decay_rate = jnp.exp(heads_p[1:2, :])
    rate = -step * decay_rate
    tril = (iota((length, length), 0) >= iota((length, length), 1)).astype(BF16)
    cumul = ones_mm(tril, rate, 3)
    spread = expander(width)
    row = iota((length, 1), 0)
    entry = jnp.where(offset > row.astype(F32), jnp.exp(cumul), 0.0)
    last_off = offset[length - 1 : length, :]
    same_last = row.astype(F32) >= (length - 1) - last_off
    to_end = jnp.where(same_last, jnp.exp(cumul[length - 1 : length, :] - cumul), 0.0)
    step_x = mm_ones(step, spread, 2)
    entry_x = mm_ones(entry, spread, 2)
    end_x = mm_ones(to_end, spread, 2)
    return conv_x, conv_t, raw, step, rate, decay_rate, cumul, spread, step_x, entry_x, end_x


def forward_kernel(order_ref, *refs, seqs):
    del order_ref
    per_seq, refs = refs[: 5 * seqs], refs[5 * seqs :]
    (wx_ref, bx_ref, wt_ref, bt_ref, hp_ref, skip_ref, gain_ref), refs = refs[:7], refs[7:]
    outs, (state_ref, memory, ext_x, ext_t) = refs[: 3 * seqs], refs[3 * seqs :]
    length, width = per_seq[0].shape[1], per_seq[0].shape[2] // 2

    @pl.when(pl.program_id(0) == 0)
    def _():
        memory[...] = jnp.zeros_like(memory)

    params = (wx_ref[...], bx_ref[...], wt_ref[...], bt_ref[...], hp_ref[...])
    for q in range(seqs):
        zx_ref, zxh_ref, tail_ref, tailh_ref, off_ref = per_seq[5 * q : 5 * q + 5]
        y_ref, gated_ref, square_ref = outs[3 * q : 3 * q + 3]
        offset = off_ref[0]
        conv_x, conv_t, _, _, _, _, cumul, _, step_x, entry_x, end_x = chunk_common(
            zx_ref[0, :, width:], zxh_ref[0, :, width:], tail_ref[0], tailh_ref[0], offset, params,
            ext_x.at[q], ext_t.at[q], width,
        )
        xs = conv_x * sigmoid(conv_x)
        act_t = conv_t * sigmoid(conv_t)
        bs = act_t[:, :STATE].astype(BF16)
        cs = act_t[:, STATE:].astype(BF16)
        scaled = xs * step_x
        scores = mm_tr(cs, bs)
        gap = iota((length, length), 0) - iota((length, length), 1)
        same = (gap >= 0) & (gap.astype(F32) <= offset)
        cumul_t = cumul.T
        old = memory[q]
        old_low = old.astype(BF16)
        state_ref[0, q] = old_low
        outside = mm(cs, old_low) * entry_x + skip_ref[...] * xs
        squares = jnp.zeros((length, 1), F32)
        for start, size, heads in head_tiles(width):
            mixing = []
            for head in heads:
                spans = cumul[:, head : head + 1] - cumul_t[head : head + 1, :]
                decays = jnp.exp(jnp.where(same, spans, -1e30))
                mixing.append((decays * scores).astype(BF16))
            tile = masked_heads(scaled[:, start : start + size].astype(BF16), heads)
            mix = mixing[0] if len(heads) == 1 else jnp.concatenate(mixing, axis=1)
            inside = jnp.dot(mix, tile, preferred_element_type=F32)
            y_low = (inside + outside[:, start : start + size]).astype(BF16)
            y_ref[0, :, start : start + size] = y_low
            z = zx_ref[0, :, start : start + size].astype(F32)
            gated = y_low.astype(F32) * (z * sigmoid(z))
            gated_ref[0, :, start : start + size] = (
                gated * gain_ref[:, start : start + size]
            ).astype(BF16)
            squares = squares + jnp.sum(gated * gated, axis=1, keepdims=True)
        square_ref[0] = jnp.broadcast_to(squares, (length, LANES)).T[0:1, :]
        fresh = tr_mm(bs, scaled * end_x)
        memory[q] = old * entry_x[length - 1 : length, :] + fresh


def backward_kernel(order_ref, *refs, seqs):
    del order_ref
    per_seq, refs = refs[: 10 * seqs], refs[10 * seqs :]
    (state_ref, wx_ref, bx_ref, wt_ref, bt_ref, hp_ref, skip_ref, gain_ref), refs = (
        refs[:8], refs[8:],
    )
    outs, refs = refs[:seqs], refs[seqs:]
    gx_ref, gt_ref, gh_ref, memory, ext_x, ext_t, next_x, next_t = refs
    length, width = per_seq[0].shape[1], per_seq[0].shape[2] // 2

    @pl.when(pl.program_id(0) == 0)
    def _():
        memory[...] = jnp.zeros_like(memory)
        gx_ref[...] = jnp.zeros_like(gx_ref)
        gt_ref[...] = jnp.zeros_like(gt_ref)
        gh_ref[...] = jnp.zeros_like(gh_ref)
        next_x[:, length:, :] = jnp.zeros_like(next_x[:, length:, :])
        next_t[:, length:, :] = jnp.zeros_like(next_t[:, length:, :])

    params = (wx_ref[...], bx_ref[...], wt_ref[...], bt_ref[...], hp_ref[...])
    for q in range(seqs):
        (zx_ref, zxh_ref, tail_ref, tailh_ref, off_ref, offr_ref, rem_ref, y_ref, grad_ref,
         stat_ref) = per_seq[10 * q : 10 * q + 10]
        out_ref = outs[q]
        offset = off_ref[0]
        conv_x, conv_t, raw, step, rate, decay_rate, cumul, spread, step_x, entry_x, end_x = (
            chunk_common(
                zx_ref[0, :, width:], zxh_ref[0, :, width:], tail_ref[0], tailh_ref[0], offset,
                params, ext_x.at[q], ext_t.at[q], width,
            )
        )
        stats = jnp.broadcast_to(stat_ref[0, 0:1, :], (LANES, length)).T
        slopes = jnp.broadcast_to(stat_ref[0, 1:2, :], (LANES, length)).T
        scale, slope = stats[:, 0:1], slopes[:, 0:1]
        z = zx_ref[0, :, :width].astype(F32)
        sig_z = sigmoid(z)
        silu_z = z * sig_z
        y = y_ref[0].astype(F32)
        gated = y * silu_z
        scaled_grad = grad_ref[0].astype(F32) * scale
        gx_ref[KERNEL + 2 : KERNEL + 3, :] += jnp.sum(scaled_grad * gated, axis=0, keepdims=True)
        grad_gated = gain_ref[...] * scaled_grad - gated * slope
        dy_low = (grad_gated * silu_z).astype(BF16)
        dz = (grad_gated * y * (sig_z + silu_z * (1.0 - sig_z))).astype(BF16)
        dy = dy_low.astype(F32)

        sig_x = sigmoid(conv_x)
        xs = conv_x * sig_x
        slope_x = sig_x + xs * (1.0 - sig_x)
        sig_t = sigmoid(conv_t)
        act_t = conv_t * sig_t
        slope_t = sig_t + act_t * (1.0 - sig_t)
        bs = act_t[:, :STATE].astype(BF16)
        cs = act_t[:, STATE:].astype(BF16)
        scaled = xs * step_x
        scaled_low = scaled.astype(BF16)
        scores = mm_tr(bs, cs)
        rows, cols = iota((length, length), 0), iota((length, length), 1)
        gap = cols - rows
        same = (gap >= 0) & (gap.astype(F32) <= offr_ref[0])
        strict = gap > 0
        upper = (rows >= cols).astype(BF16)
        cumul_t = cumul.T
        old = state_ref[0, q]
        grad_state = memory[q]
        state_low = grad_state.astype(BF16)
        grad_scores = jnp.zeros((length, length), F32)
        grad_scaled = []
        inside_rows = []
        for start, size, heads in head_tiles(width):
            dy_tile = masked_heads(dy_low[:, start : start + size], heads)
            grad_mix = mm_tr(scaled_low[:, start : start + size], dy_tile)
            mixing = []
            for place, head in enumerate(heads):
                spans = cumul_t[head : head + 1, :] - cumul[:, head : head + 1]
                decays = jnp.exp(jnp.where(same, spans, -1e30))
                weighted = grad_mix[:, place * length : (place + 1) * length] * decays
                grad_scores = grad_scores + weighted
                mixing.append((decays * scores).astype(BF16))
                terms = jnp.where(strict, weighted * scores, 0.0).astype(BF16)
                sums = jnp.dot(terms, upper, preferred_element_type=F32)
                inside_rows.append(
                    jnp.sum(jnp.where(strict, sums, 0.0), axis=0, keepdims=True)
                )
            mix = mixing[0] if len(heads) == 1 else jnp.concatenate(mixing, axis=1)
            grad_scaled.append(jnp.dot(mix, dy_tile, preferred_element_type=F32))
        inside_rows.append(jnp.zeros((LANES - len(inside_rows), length), F32))
        inside = jnp.concatenate(inside_rows, axis=0).T
        from_end = mm(bs, state_low) * end_x
        grad_scaled = jnp.concatenate(grad_scaled, axis=1) + from_end
        entry_dy = dy * entry_x
        entry_dy_low = entry_dy.astype(BF16)
        out_terms = mm(cs, old) * entry_dy
        end_terms = scaled * from_end
        grad_step = mm_ones_tr(xs * grad_scaled, spread, 2)
        out_terms = mm_ones_tr(out_terms, spread, 2)
        end_terms = mm_ones_tr(end_terms, spread, 2)
        keep_row = entry_x[length - 1 : length, :]
        carried = jnp.sum(grad_state * old.astype(F32), axis=0, keepdims=True) * keep_row
        carried = mm_ones_tr(jnp.broadcast_to(carried, (8, width)), spread, 2)[0:1, :]
        triu = (cols >= rows).astype(BF16)
        below = (rows > cols).astype(BF16)
        grad_rate = inside + ones_mm(triu, out_terms, 2) + ones_mm(below, end_terms, 2) + carried
        grad_step = grad_step - decay_rate * grad_rate
        grad_raw = grad_step * sigmoid(raw)
        grad_scores_low = grad_scores.astype(BF16)
        grad_b = mm(grad_scores_low, cs) + mm_tr(scaled * end_x, state_low)
        grad_c = tr_mm(grad_scores_low, bs) + mm_tr(entry_dy_low, old)
        memory[q] = grad_state * keep_row + tr_mm(cs, entry_dy_low)
        conv_grad_x = (skip_ref[...] * dy + step_x * grad_scaled) * slope_x
        conv_grad_t = jnp.concatenate([grad_b, grad_c], axis=1) * slope_t

        remain = rem_ref[0]
        results = [dz]
        for grad, ext, nxt, weight, sums in (
            (conv_grad_x, ext_x.at[q], next_x.at[q], params[0], gx_ref),
            (conv_grad_t, ext_t.at[q], next_t.at[q], params[2], gt_ref),
        ):
            current = ext[pl.ds(HALO, length), :]
            sums[KERNEL : KERNEL + 1, :] += jnp.sum(grad, axis=0, keepdims=True)
            sums[KERNEL - 1 : KERNEL, :] += jnp.sum(grad * current, axis=0, keepdims=True)
            nxt[0:length, :] = grad
            total = weight[KERNEL - 1 : KERNEL, :] * grad
            for back in range(1, KERNEL):
                tap = KERNEL - 1 - back
                shifted = jnp.where(offset >= back, ext[pl.ds(HALO - back, length), :], 0.0)
                sums[tap : tap + 1, :] += jnp.sum(grad * shifted, axis=0, keepdims=True)
                ahead = jnp.where(remain >= back, nxt[pl.ds(back, length), :], 0.0)
                total = total + weight[tap : tap + 1, :] * ahead
            nxt[length:, :] = grad[0:HALO, :]
            results.append(total.astype(BF16))
        results.append(grad_raw.astype(BF16))
        gx_ref[KERNEL + 1 : KERNEL + 2, :] += jnp.sum(dy * xs, axis=0, keepdims=True)
        gh_ref[0:1, :] += jnp.sum(grad_raw, axis=0, keepdims=True)
        gh_ref[1:2, :] += jnp.sum(grad_rate * rate, axis=0, keepdims=True)
        out_ref[0, :, : 2 * width] = jnp.concatenate(results[:2], axis=1)
        out_ref[0, :, 2 * width : 2 * width + 2 * STATE] = results[2]
        out_ref[0, :, 2 * width + 2 * STATE :] = results[3]


TAIL = 2 * STATE + LANES


def whole_spec(shape):
    return pl.BlockSpec(shape, lambda i, order: (0,) * len(shape))


def chunk_specs(steps, length, width, reverse):
    def place(i):
        return steps - 1 - i if reverse else i

    def ordered(q, cols, column=0):
        return pl.BlockSpec(
            (1, length, cols), lambda i, order: (order[q, place(i)], 0, column)
        )

    def before(q, cols, column=0):
        return pl.BlockSpec(
            (1, HALO, cols),
            lambda i, order: (
                order[q, jnp.maximum(place(i) - 1, 0)], length // HALO - 1, column
            ),
        )

    def plain(q, rows, cols):
        return pl.BlockSpec(
            (pl.Squeezed(), 1, rows, cols), lambda i, order: (q, place(i), 0, 0)
        )

    def row(q, rows, cols):
        return pl.BlockSpec((1, rows, cols), lambda i, order: (order[q, place(i)], 0, 0))

    return ordered, before, plain, row, place


def forward_mix(order, proj, off_col, consts):
    seqs = len(proj)
    steps, length, cols = proj[0].shape
    width = (cols - TAIL) // 2
    ordered, before, plain, row, _ = chunk_specs(steps, length, width, False)
    tail_at = 2 * width // TAIL
    in_specs, args, out_specs, out_shape = [], [], [], []
    for q in range(seqs):
        in_specs += [
            ordered(q, 2 * width), before(q, 2 * width),
            ordered(q, TAIL, tail_at), before(q, TAIL, tail_at), plain(q, length, 1),
        ]
        args += [proj[q]] * 4 + [off_col]
        out_specs += [ordered(q, width), ordered(q, width), row(q, 1, length)]
        out_shape += [jax.ShapeDtypeStruct((steps, length, width), BF16)] * 2
        out_shape += [jax.ShapeDtypeStruct((steps, 1, length), F32)]
    outs = pl.pallas_call(
        functools.partial(forward_kernel, seqs=seqs),
        grid_spec=pltpu.PrefetchScalarGridSpec(
            num_scalar_prefetch=1,
            grid=(steps,),
            in_specs=in_specs + [whole_spec(v.shape) for v in consts],
            out_specs=out_specs
            + [pl.BlockSpec((1, seqs, STATE, width), lambda i, order: (i, 0, 0, 0))],
            scratch_shapes=[
                pltpu.VMEM((seqs, STATE, width), F32),
                pltpu.VMEM((seqs, HALO + length, width), F32),
                pltpu.VMEM((seqs, HALO + length, 2 * STATE), F32),
            ],
        ),
        out_shape=out_shape + [jax.ShapeDtypeStruct((steps, seqs, STATE, width), BF16)],
        compiler_params=pltpu.CompilerParams(
            dimension_semantics=("arbitrary",), vmem_limit_bytes=32 << 20
        ),
        cost_estimate=pl.CostEstimate(
            flops=steps * seqs * 900_000_000, transcendentals=0, bytes_accessed=10_000_000
        ),
        name="mix_forward",
    )(order, *args, *consts)
    return outs[0:-1:3], outs[1:-1:3], outs[2:-1:3], outs[-1]


def backward_mix(order, proj, off_col, off_row, rem_col, y, grad_yn, stats, states, consts):
    seqs = len(proj)
    steps, length, cols = proj[0].shape
    width = (cols - TAIL) // 2
    ordered, before, plain, row, place = chunk_specs(steps, length, width, True)
    tail_at = 2 * width // TAIL
    in_specs, args = [], []
    for q in range(seqs):
        in_specs += [
            ordered(q, 2 * width), before(q, 2 * width),
            ordered(q, TAIL, tail_at), before(q, TAIL, tail_at),
            plain(q, length, 1), plain(q, 1, length), plain(q, length, 1),
            ordered(q, width), ordered(q, width), row(q, 2, length),
        ]
        args += [proj[q]] * 4 + [off_col, off_row, rem_col, y[q], grad_yn[q], stats[q]]
    in_specs += [
        pl.BlockSpec((1, seqs, STATE, width), lambda i, order: (place(i), 0, 0, 0))
    ] + [whole_spec(v.shape) for v in consts]
    sums = [(8, width), (8, 2 * STATE), (8, LANES)]
    outs = pl.pallas_call(
        functools.partial(backward_kernel, seqs=seqs),
        grid_spec=pltpu.PrefetchScalarGridSpec(
            num_scalar_prefetch=1,
            grid=(steps,),
            in_specs=in_specs,
            out_specs=[ordered(q, cols) for q in range(seqs)] + [whole_spec(v) for v in sums],
            scratch_shapes=[
                pltpu.VMEM((seqs, STATE, width), F32),
                pltpu.VMEM((seqs, HALO + length, width), F32),
                pltpu.VMEM((seqs, HALO + length, 2 * STATE), F32),
                pltpu.VMEM((seqs, length + HALO, width), F32),
                pltpu.VMEM((seqs, length + HALO, 2 * STATE), F32),
            ],
        ),
        out_shape=[jax.ShapeDtypeStruct(proj[0].shape, BF16)] * seqs
        + [jax.ShapeDtypeStruct(v, F32) for v in sums],
        compiler_params=pltpu.CompilerParams(
            dimension_semantics=("arbitrary",), vmem_limit_bytes=40 << 20
        ),
        cost_estimate=pl.CostEstimate(
            flops=steps * seqs * 2_000_000_000, transcendentals=0, bytes_accessed=16_000_000
        ),
        name="mix_backward",
    )(order, *args, states, *consts)
    return outs[:seqs], outs[seqs], outs[seqs + 1], outs[seqs + 2]


AXES = ("seq", "fsdp")


class Group:
    def __init__(self):
        self.seq = lax.axis_size("seq")
        self.fsdp = lax.axis_size("fsdp")
        self.half = self.seq // 2
        s, f = lax.axis_index("seq"), lax.axis_index("fsdp")
        self.s, self.f = s, f
        self.top, self.low = s // self.half, s % self.half
        self.core, self.pair = f % 2, f // 2
        self.home = self.core == self.top
        self.head_group = self.core * self.half + self.low
        self.low_bits = [1 << i for i in range(self.half.bit_length() - 1)]
        self.pair_bits = [2 << i for i in range((self.fsdp // 2).bit_length() - 1)]

    def swap(self, value, seq_bit=0, fsdp_bit=0, away=False, home=False):
        perm = []
        for s in range(self.seq):
            for f in range(self.fsdp):
                at_home = f % 2 == s // self.half
                if (away and at_home) or (home and not at_home):
                    continue
                perm.append((s * self.fsdp + f, (s ^ seq_bit) * self.fsdp + (f ^ fsdp_bit)))
        return lax.ppermute(value, AXES, perm)

    def bits_for(self, q):
        return self.low_bits if q % 2 == 0 else self.low_bits[::-1]

    def gather_tokens(self, block):
        moved = self.swap(block, self.half, 1, away=True)
        block = jnp.where(self.home, block, moved)
        out = []
        for q in range(block.shape[0]):
            held = block[q][None]
            for bit in self.bits_for(q):
                held = jnp.concatenate([held, self.swap(held, bit)], axis=0)
            out.append(jnp.concatenate([held, self.swap(held, 0, 1)], axis=0))
        return out

    def order(self, seqs):
        chunk = np.arange(self.seq)
        rows = []
        for q in range(seqs):
            table = np.zeros(self.half, np.int32)
            for value in range(self.half):
                table[value] = sum(
                    1 << i for i, bit in enumerate(self.bits_for(q)) if value & bit
                )
            low = (chunk % self.half) ^ self.low
            rows.append(
                jnp.asarray(table)[low] + self.half * ((chunk // self.half) ^ self.core)
            )
        return jnp.stack(rows).astype(jnp.int32)

    def scatter_tokens(self, parts):
        out = []
        for q, held in enumerate(parts):
            for seq_bit, fsdp_bit in [(0, 1)] + [(bit, 0) for bit in self.bits_for(q)[::-1]]:
                count = held.shape[0] // 2
                got = self.swap(held[count:], seq_bit, fsdp_bit)
                held = (held[:count].astype(F32) + got.astype(F32)).astype(BF16)
            out.append(held)
        held = jnp.concatenate(out, axis=0)
        moved = self.swap(held, self.half, 1, away=True)
        return jnp.where(self.home, held, moved).astype(F32)

    def bit_of(self, seq_bit, fsdp_bit):
        return (self.s // seq_bit) % 2 if seq_bit else (self.f // fsdp_bit) % 2

    def ordered(self, value, got, seq_bit, fsdp_bit, axis):
        first = self.bit_of(seq_bit, fsdp_bit) == 0
        return jnp.stack([jnp.where(first, value, got), jnp.where(first, got, value)], axis=axis)

    def merge(self, value, seq_bit, fsdp_bit, axis):
        got = self.swap(value, seq_bit, fsdp_bit)
        first = self.bit_of(seq_bit, fsdp_bit) == 0
        return jnp.concatenate(
            [jnp.where(first, value, got), jnp.where(first, got, value)], axis=axis
        )

    def split(self, value, seq_bit, fsdp_bit, axis):
        bit = self.bit_of(seq_bit, fsdp_bit)
        count = value.shape[axis] // 2
        keep = lax.dynamic_slice_in_dim(value, bit * count, count, axis)
        give = lax.dynamic_slice_in_dim(value, (1 - bit) * count, count, axis)
        return keep, self.swap(give, seq_bit, fsdp_bit)

    def all_bits(self):
        return [(self.half, 0)] + [(b, 0) for b in self.low_bits] + [
            (0, b) for b in self.pair_bits
        ] + [(0, 1)]

    def total(self, value, bits):
        for seq_bit, fsdp_bit in bits:
            value = value + self.swap(value, seq_bit, fsdp_bit)
        return value

    def group_total(self, parts):
        out = []
        for q, value in enumerate(parts):
            shape = value.shape
            steps = [(bit, 0) for bit in self.bits_for(q)] + [(0, 1)]
            for i, (seq_bit, fsdp_bit) in enumerate(steps):
                got = self.swap(value, seq_bit, fsdp_bit)
                pairs = got.reshape((-1, 2, 1 << i) + shape[1:])
                value = value + pairs[:, ::-1].reshape(shape)
            out.append(value)
        return out

    def gather_columns(self, value):
        rows, cols = value.shape[1:]
        keep, got = self.split(value, 0, 1, 0)
        value = self.ordered(keep, got, 0, 1, 1)[:, None]
        for bit in self.low_bits[::-1]:
            keep, got = self.split(value, bit, 0, 0)
            value = self.ordered(keep, got, bit, 0, 2)
            value = value.reshape((keep.shape[0], -1, 2, rows, cols))
        value = self.merge(value[0], self.half, 0, 0)[:, None]
        for bit in self.pair_bits[::-1]:
            got = self.swap(value, 0, bit)
            value = self.ordered(value, got, 0, bit, 2)
            value = value.reshape((self.seq, -1, 2, rows, cols))
        return value.reshape(-1, cols)

    def scatter_columns(self, value):
        cols = value.shape[1]
        pairs = self.fsdp // 2
        rows = value.shape[0] // (self.seq * self.fsdp)
        value = value.reshape(2, self.half, pairs, 2, rows, cols)
        for bit in self.pair_bits[::-1]:
            value = self.halve(value, 0, bit, 2)
        value = self.halve(value[:, :, 0], self.half, 0, 0)
        for bit in self.low_bits[::-1]:
            keep, got = self.split(value, bit, 0, 1)
            value = self.ordered(keep, got, bit, 0, 1)
            value = value.reshape((-1,) + keep.shape[1:])
        keep, got = self.split(value[:, 0], 0, 1, 1)
        return self.ordered(keep[:, 0], got[:, 0], 0, 1, 0).reshape(self.seq, rows, cols)

    def halve(self, value, seq_bit, fsdp_bit, axis):
        keep, got = self.split(value, seq_bit, fsdp_bit, axis)
        return (keep.astype(F32) + got.astype(F32)).astype(BF16)

    def gather_rows(self, value):
        rows, cols = value.shape
        value = self.merge(value[None], self.half, 0, 0)
        for bits in (
            [(b, 0) for b in self.low_bits[::-1]] + [(0, b) for b in self.pair_bits[::-1]] + [(0, 1)]
        ):
            value = self.merge(value[:, None], *bits, 1).reshape(-1, rows, cols)
        return value.reshape(-1, cols)

    def scatter_rows(self, value):
        cols = value.shape[1]
        rows = value.shape[0] // (self.seq * self.fsdp)
        value = value.reshape(2, self.half, self.fsdp // 2, 2, rows, cols)
        for bit in self.pair_bits[::-1]:
            value = self.halve(value, 0, bit, 2)
        value = self.halve(value, self.half, 0, 0)
        for bit in self.low_bits[::-1]:
            value = self.halve(value, bit, 0, 1)
        value = self.halve(value, 0, 1, 3)
        return value.reshape(rows, cols).astype(F32)

    def gather_own_rows(self, value):
        rows, cols = value.shape
        value = self.merge(value[None], 0, 1, 0)
        moved = self.swap(value, self.half, 0, home=True)
        value = jnp.where(self.home, value, moved)[None]
        for bit in self.pair_bits[::-1]:
            value = self.merge(value[:, None], 0, bit, 1).reshape(-1, 2, rows, cols)
        return value.reshape(-1, cols)

    def scatter_own_rows(self, value):
        cols = value.shape[1]
        rows = value.shape[0] // self.fsdp
        value = value.reshape(self.fsdp // 2, 2, rows, cols)
        for bit in self.pair_bits[::-1]:
            value = self.halve(value, 0, bit, 0)
        value = value[0].astype(F32) + self.swap(value[0], self.half, 0, away=True).astype(F32)
        value = value.astype(BF16)
        keep = lax.dynamic_index_in_dim(value, self.core, 0, False)
        give = lax.dynamic_index_in_dim(value, 1 - self.core, 0, False)
        moved = self.swap(give, 0, 1, home=True)
        return jnp.where(self.home, keep, moved).astype(F32)


def spread_last(piece, start, whole):
    zeros_full = jnp.zeros(piece.shape[:-1] + (whole,), F32)
    return lax.dynamic_update_slice_in_dim(zeros_full, piece, start, piece.ndim - 1)


def chunked(per_token, steps, length):
    return per_token.reshape(per_token.shape[0], steps, length)


def local(
    tokens, segments, gain_in, w_in, conv_w, conv_b, dt_bias, a_log, skip, gain_out, w_out,
    cotangent,
):
    group = Group()
    steps = group.seq
    seqs, length, _ = tokens.shape
    width = INNER // steps
    heads = HEADS // steps
    rows_in = w_in.shape[0]
    number = group.head_group

    def mine(array, size):
        return lax.dynamic_slice_in_dim(array, number * size, size, array.ndim - 1)

    wide = tokens.astype(F32)
    scale_in = lax.rsqrt(jnp.mean(wide * wide, axis=-1, keepdims=True) + EPSILON)
    normed = (wide * scale_in * gain_in).astype(BF16)
    h_all = group.gather_tokens(normed)
    order = group.order(seqs)

    zx = w_in[:, : 2 * INNER].reshape(rows_in, 2, steps, width).transpose(2, 0, 1, 3)
    zx = group.gather_columns(zx.reshape(steps, rows_in, 2 * width))
    tail_w = group.gather_rows(w_in[:, 2 * INNER :])
    w_mine = jnp.concatenate(
        [
            zx,
            tail_w[:, : 2 * STATE],
            mine(tail_w[:, 2 * STATE :], heads),
            jnp.zeros((D, LANES - heads), BF16),
        ],
        axis=1,
    )
    cot_all = group.gather_tokens(cotangent)
    out_w = group.gather_own_rows(w_out)

    segs = jnp.where(group.home, segments, group.swap(segments, 0, 1))
    total = steps * length
    index = lax.broadcasted_iota(jnp.int32, (seqs, total), 1)
    starts = jnp.concatenate([jnp.ones((seqs, 1), bool), segs[:, 1:] != segs[:, :-1]], axis=1)
    first = lax.cummax(jnp.where(starts, index, 0), axis=1)
    ends = jnp.concatenate([starts[:, 1:], jnp.ones((seqs, 1), bool)], axis=1)
    last = lax.cummin(jnp.where(ends, index, total), axis=1, reverse=True)
    off = chunked((index - first).astype(F32), steps, length)
    rem = chunked((last - index).astype(F32), steps, length)
    off_col, off_row, rem_col = off[..., None], off[:, :, None, :], rem[..., None]

    heads_p = jnp.stack([mine(dt_bias, heads), mine(a_log, heads)])
    consts = (
        mine(conv_w[:, :INNER], width),
        mine(conv_b[None, :INNER], width),
        conv_w[:, INNER:],
        conv_b[None, INNER:],
        jnp.pad(heads_p, ((0, 6), (0, LANES - heads))),
        jnp.repeat(mine(skip, heads), HEAD_DIM)[None],
        mine(gain_out[None], width),
    )

    def dot(a, b):
        return lax.dot_general(a, b, (((2,), (0,)), ((), ())), preferred_element_type=F32)

    def dot_tr(a, b):
        return lax.dot_general(a, b, (((2,), (1,)), ((), ())), preferred_element_type=F32)

    def dot_tokens(a, b):
        dims = (0, 1)
        return sum(
            lax.dot_general(l, r, ((dims, dims), ((), ())), preferred_element_type=F32)
            for l, r in zip(a, b)
        )

    proj = [dot(h, w_mine).astype(BF16) for h in h_all]
    y, gated, squares, states = forward_mix(order, proj, off_col, consts)

    grad_yn = [dot_tr(cot, out_w) for cot in cot_all]
    sums = group.group_total(
        [
            jnp.stack([sq[:, 0], jnp.sum(g * gt.astype(F32), axis=-1)], axis=1)
            for sq, g, gt in zip(squares, grad_yn, gated)
        ]
    )
    stats, scales = [], []
    for value in sums:
        scale = lax.rsqrt(value[:, 0] / INNER + EPSILON)
        stats.append(jnp.stack([scale, value[:, 1] * (scale * scale * scale / INNER)], axis=1))
        scales.append(scale[..., None])
    mixed = group.scatter_tokens(
        [(dot(gt, out_w) * scale).astype(BF16) for gt, scale in zip(gated, scales)]
    )
    mixed = (wide + mixed).astype(BF16)
    y_normed = [(gt.astype(F32) * scale).astype(BF16) for gt, scale in zip(gated, scales)]
    w_out_grad = group.scatter_own_rows(dot_tokens(y_normed, cot_all).astype(BF16))

    grad_proj, sums_x, sums_t, sums_h = backward_mix(
        order, proj, off_col, off_row, rem_col, y, grad_yn, stats, states, consts
    )

    grad_h = group.scatter_tokens([dot_tr(g, w_mine).astype(BF16) for g in grad_proj])
    part = dot_tokens(h_all, grad_proj)
    gain_part = jnp.sum(part * w_mine.astype(F32), axis=1)
    tail_part = jnp.concatenate(
        [
            part[:, 2 * width : 2 * width + 2 * STATE],
            spread_last(
                part[:, 2 * width + 2 * STATE : 2 * width + 2 * STATE + heads],
                number * heads,
                HEADS,
            ),
        ],
        axis=1,
    )
    zx_grad = group.scatter_columns(part[:, : 2 * width].astype(BF16)).astype(F32)
    tail_grad = group.scatter_rows(tail_part.astype(BF16))
    zx_grad = zx_grad.reshape(steps, rows_in, 2, width).transpose(1, 2, 0, 3)
    w_in_grad = jnp.concatenate([zx_grad.reshape(rows_in, 2 * INNER), tail_grad], axis=1)

    scaled = grad_h * gain_in
    unit = wide * scale_in
    tokens_grad = cotangent.astype(F32) + scale_in * (
        scaled - unit * jnp.mean(scaled * unit, axis=-1, keepdims=True)
    )

    everywhere = group.total(
        jnp.concatenate([gain_part, sums_t[: KERNEL + 1].reshape(-1)]), group.all_bits()
    )
    gain_in_grad = everywhere[:D] / gain_in
    grouped = jnp.concatenate(
        [
            sums_x[: KERNEL + 1].reshape(-1),
            sums_x[KERNEL + 2],
            jnp.sum(sums_x[KERNEL + 1].reshape(heads, HEAD_DIM), axis=-1),
            sums_h[:2, :heads].reshape(-1),
        ]
    )
    grouped = group.total(grouped, [(group.half, 0)] + [(0, b) for b in group.pair_bits])[None]
    for bits in [(b, 0) for b in group.low_bits] + [(0, 1)]:
        grouped = group.merge(grouped, *bits, 0)
    conv_x = grouped[:, : (KERNEL + 1) * width].reshape(steps, KERNEL + 1, width)
    conv_x = conv_x.transpose(1, 0, 2).reshape(KERNEL + 1, INNER)
    conv_grads = jnp.concatenate([conv_x, everywhere[D:].reshape(KERNEL + 1, -1)], axis=1)
    rest = grouped[:, (KERNEL + 1) * width :]
    gain_out_grad = rest[:, :width].reshape(-1)
    per_head = rest[:, width:].reshape(steps, 3, heads).transpose(1, 0, 2).reshape(3, HEADS)
    return (
        mixed, tokens_grad, gain_in_grad, w_in_grad, conv_grads[:KERNEL], conv_grads[KERNEL],
        per_head[1], per_head[2], per_head[0], gain_out_grad, w_out_grad,
    )


def solution(mesh):
    by_token = P("fsdp", "seq", None)
    by_row = P(("seq", "fsdp"), None)
    placed = (
        by_token, P("fsdp", None), P(), by_row, P(), P(), P(), P(), P(), P(), by_row, by_token,
    )
    return jax.shard_map(
        local,
        mesh=mesh,
        in_specs=placed,
        out_specs=(by_token, by_token, P(), by_row, P(), P(), P(), P(), P(), P(), by_row),
        check_vma=False,
    )
```

```python
import functools

import jax
import jax.numpy as jnp
import numpy as np
from jax import lax
from jax.experimental import pallas as pl
from jax.experimental.pallas import tpu as pltpu
from jax.sharding import PartitionSpec as P

D = 1536
HEADS = 48
HEAD_DIM = 64
STATE = 128
KERNEL = 4
INNER = 3072
LANES = 128
HALO = 16
EPSILON = 1e-05
F32 = jnp.float32
BF16 = jnp.bfloat16


def mm(a, b):
    return jnp.dot(a.astype(BF16), b.astype(BF16), preferred_element_type=F32)


def mm_tr(a, b):
    return lax.dot_general(
        a.astype(BF16), b.astype(BF16), (((1,), (1,)), ((), ())), preferred_element_type=F32
    )


def tr_mm(a, b):
    return lax.dot_general(
        a.astype(BF16), b.astype(BF16), (((0,), (0,)), ((), ())), preferred_element_type=F32
    )


def pieces(a, count):
    out = []
    for _ in range(count - 1):
        part = a.astype(BF16)
        out.append(part)
        a = a - part.astype(F32)
    out.append(a.astype(BF16))
    return out


def ones_mm(ones, a, count):
    return sum(jnp.dot(ones, part, preferred_element_type=F32) for part in pieces(a, count))


def mm_ones(a, ones, count):
    return sum(jnp.dot(part, ones, preferred_element_type=F32) for part in pieces(a, count))


def mm_ones_tr(a, ones, count):
    return sum(
        lax.dot_general(part, ones, (((1,), (1,)), ((), ())), preferred_element_type=F32)
        for part in pieces(a, count)
    )


def iota(shape, dim):
    return lax.broadcasted_iota(jnp.int32, shape, dim)


def softplus(v):
    return jnp.maximum(v, 0.0) + jnp.log1p(jnp.exp(-jnp.abs(v)))


def sigmoid(v):
    return 1.0 / (1.0 + jnp.exp(-v))


def causal_conv(ext, current, halo, weight, bias, offset):
    length = current.shape[0]
    ext[0:HALO, :] = halo
    ext[HALO : HALO + length, :] = current
    total = bias + weight[KERNEL - 1 : KERNEL, :] * current
    for back in range(1, KERNEL):
        shifted = jnp.where(offset >= back, ext[pl.ds(HALO - back, length), :], 0.0)
        total = total + weight[KERNEL - 1 - back : KERNEL - back, :] * shifted
    return total


def head_tiles(width):
    out = []
    for start in range(0, width, LANES):
        size = min(LANES, width - start)
        heads = [start // HEAD_DIM + i for i in range(size // HEAD_DIM)]
        out.append((start, size, heads))
    return out


def masked_heads(tile, heads):
    if len(heads) == 1:
        return tile
    lane = iota(tile.shape, 1) // HEAD_DIM
    return jnp.concatenate(
        [jnp.where(lane == i, tile, jnp.zeros_like(tile)) for i in range(len(heads))], axis=0
    )


def expander(width):
    return (iota((LANES, width), 1) // HEAD_DIM == iota((LANES, width), 0)).astype(BF16)


def chunk_common(x, xh, tail, tailh, offset, params, ext_x, ext_t, width):
    wx, bx, wt, bt, heads_p, pick = params
    length = x.shape[0]
    conv_x = causal_conv(ext_x, x.astype(F32), xh.astype(F32), wx, bx, offset)
    conv_t = causal_conv(
        ext_t,
        tail[:, : 2 * STATE].astype(F32),
        tailh[:, : 2 * STATE].astype(F32),
        wt,
        bt,
        offset,
    )
    raw = jnp.dot(tail[:, 2 * STATE :], pick, preferred_element_type=F32) + heads_p[0:1, :]
    step = softplus(raw)
    decay_rate = jnp.exp(heads_p[1:2, :])
    rate = -step * decay_rate
    tril = (iota((length, length), 0) >= iota((length, length), 1)).astype(BF16)
    cumul = ones_mm(tril, rate, 3)
    spread = expander(width)
    row = iota((length, 1), 0)
    entry = jnp.where(offset > row.astype(F32), jnp.exp(cumul), 0.0)
    last_off = offset[length - 1 : length, :]
    same_last = row.astype(F32) >= (length - 1) - last_off
    to_end = jnp.where(same_last, jnp.exp(cumul[length - 1 : length, :] - cumul), 0.0)
    step_x = mm_ones(step, spread, 2)
    entry_x = mm_ones(entry, spread, 2)
    end_x = mm_ones(to_end, spread, 2)
    return conv_x, conv_t, raw, step, rate, decay_rate, cumul, spread, step_x, entry_x, end_x


def forward_kernel(
    zx_ref, zxh_ref, tail_ref, tailh_ref, off_ref,
    wx_ref, bx_ref, wt_ref, bt_ref, hp_ref, pick_ref, skip_ref, gain_ref,
    y_ref, gated_ref, square_ref, state_ref, memory, ext_x, ext_t,
):
    seqs, _, length, width = y_ref.shape

    @pl.when(pl.program_id(0) == 0)
    def _():
        memory[...] = jnp.zeros_like(memory)

    params = tuple(r[...] for r in (wx_ref, bx_ref, wt_ref, bt_ref, hp_ref, pick_ref))
    for q in range(seqs):
        offset = off_ref[q, 0]
        conv_x, conv_t, _, _, _, _, cumul, _, step_x, entry_x, end_x = chunk_common(
            zx_ref[q, 0, :, width:], zxh_ref[q, 0, :, width:], tail_ref[q, 0], tailh_ref[q, 0], offset, params,
            ext_x.at[q], ext_t.at[q], width,
        )
        xs = conv_x * sigmoid(conv_x)
        act_t = conv_t * sigmoid(conv_t)
        bs = act_t[:, :STATE].astype(BF16)
        cs = act_t[:, STATE:].astype(BF16)
        scaled = xs * step_x
        scores = mm_tr(cs, bs)
        gap = iota((length, length), 0) - iota((length, length), 1)
        same = (gap >= 0) & (gap.astype(F32) <= offset)
        cumul_t = cumul.T
        old = memory[q]
        old_low = old.astype(BF16)
        state_ref[q, 0] = old_low
        outside = mm(cs, old_low) * entry_x + skip_ref[...] * xs
        squares = jnp.zeros((length, 1), F32)
        for start, size, heads in head_tiles(width):
            mixing = []
            for head in heads:
                spans = cumul[:, head : head + 1] - cumul_t[head : head + 1, :]
                decays = jnp.exp(jnp.where(same, spans, -1e30))
                mixing.append((decays * scores).astype(BF16))
            tile = masked_heads(scaled[:, start : start + size].astype(BF16), heads)
            mix = mixing[0] if len(heads) == 1 else jnp.concatenate(mixing, axis=1)
            inside = jnp.dot(mix, tile, preferred_element_type=F32)
            y_low = (inside + outside[:, start : start + size]).astype(BF16)
            y_ref[q, 0, :, start : start + size] = y_low
            z = zx_ref[q, 0, :, start : start + size].astype(F32)
            gated = y_low.astype(F32) * (z * sigmoid(z))
            gated_ref[q, 0, :, start : start + size] = (
                gated * gain_ref[:, start : start + size]
            ).astype(BF16)
            squares = squares + jnp.sum(gated * gated, axis=1, keepdims=True)
        square_ref[q, 0] = jnp.broadcast_to(squares, (length, LANES)).T[0:1, :]
        fresh = tr_mm(bs, scaled * end_x)
        memory[q] = old * entry_x[length - 1 : length, :] + fresh


def backward_kernel(
    zx_ref, zxh_ref, tail_ref, tailh_ref, off_ref, offr_ref, rem_ref, y_ref, grad_ref, stat_ref,
    state_ref, wx_ref, bx_ref, wt_ref, bt_ref, hp_ref, pick_ref, skip_ref, gain_ref,
    out_ref, gx_ref, gt_ref, gh_ref,
    memory, ext_x, ext_t, next_x, next_t,
):
    seqs, _, length, width = y_ref.shape

    @pl.when(pl.program_id(0) == 0)
    def _():
        memory[...] = jnp.zeros_like(memory)
        gx_ref[...] = jnp.zeros_like(gx_ref)
        gt_ref[...] = jnp.zeros_like(gt_ref)
        gh_ref[...] = jnp.zeros_like(gh_ref)
        next_x[:, length:, :] = jnp.zeros_like(next_x[:, length:, :])
        next_t[:, length:, :] = jnp.zeros_like(next_t[:, length:, :])

    params = tuple(r[...] for r in (wx_ref, bx_ref, wt_ref, bt_ref, hp_ref, pick_ref))
    for q in range(seqs):
        offset = off_ref[q, 0]
        conv_x, conv_t, raw, step, rate, decay_rate, cumul, spread, step_x, entry_x, end_x = (
            chunk_common(
                zx_ref[q, 0, :, width:], zxh_ref[q, 0, :, width:], tail_ref[q, 0], tailh_ref[q, 0], offset,
                params, ext_x.at[q], ext_t.at[q], width,
            )
        )
        stats = jnp.broadcast_to(stat_ref[q, 0, 0:1, :], (LANES, length)).T
        slopes = jnp.broadcast_to(stat_ref[q, 0, 1:2, :], (LANES, length)).T
        scale, slope = stats[:, 0:1], slopes[:, 0:1]
        z = zx_ref[q, 0, :, :width].astype(F32)
        sig_z = sigmoid(z)
        silu_z = z * sig_z
        y = y_ref[q, 0].astype(F32)
        gated = y * silu_z
        scaled_grad = grad_ref[q, 0].astype(F32) * scale
        gx_ref[KERNEL + 2 : KERNEL + 3, :] += jnp.sum(scaled_grad * gated, axis=0, keepdims=True)
        grad_gated = gain_ref[...] * scaled_grad - gated * slope
        dy_low = (grad_gated * silu_z).astype(BF16)
        dz = (grad_gated * y * (sig_z + silu_z * (1.0 - sig_z))).astype(BF16)
        dy = dy_low.astype(F32)

        sig_x = sigmoid(conv_x)
        xs = conv_x * sig_x
        slope_x = sig_x + xs * (1.0 - sig_x)
        sig_t = sigmoid(conv_t)
        act_t = conv_t * sig_t
        slope_t = sig_t + act_t * (1.0 - sig_t)
        bs = act_t[:, :STATE].astype(BF16)
        cs = act_t[:, STATE:].astype(BF16)
        scaled = xs * step_x
        scaled_low = scaled.astype(BF16)
        scores = mm_tr(bs, cs)
        rows, cols = iota((length, length), 0), iota((length, length), 1)
        gap = cols - rows
        same = (gap >= 0) & (gap.astype(F32) <= offr_ref[q, 0])
        strict = gap > 0
        upper = (rows >= cols).astype(BF16)
        cumul_t = cumul.T
        old = state_ref[q, 0]
        grad_state = memory[q]
        state_low = grad_state.astype(BF16)
        grad_scores = jnp.zeros((length, length), F32)
        grad_scaled = []
        inside_rows = []
        for start, size, heads in head_tiles(width):
            dy_tile = masked_heads(dy_low[:, start : start + size], heads)
            grad_mix = mm_tr(scaled_low[:, start : start + size], dy_tile)
            mixing = []
            for place, head in enumerate(heads):
                spans = cumul_t[head : head + 1, :] - cumul[:, head : head + 1]
                decays = jnp.exp(jnp.where(same, spans, -1e30))
                weighted = grad_mix[:, place * length : (place + 1) * length] * decays
                grad_scores = grad_scores + weighted
                mixing.append((decays * scores).astype(BF16))
                terms = jnp.where(strict, weighted * scores, 0.0).astype(BF16)
                sums = jnp.dot(terms, upper, preferred_element_type=F32)
                inside_rows.append(
                    jnp.sum(jnp.where(strict, sums, 0.0), axis=0, keepdims=True)
                )
            mix = mixing[0] if len(heads) == 1 else jnp.concatenate(mixing, axis=1)
            grad_scaled.append(jnp.dot(mix, dy_tile, preferred_element_type=F32))
        inside_rows.append(jnp.zeros((LANES - len(inside_rows), length), F32))
        inside = jnp.concatenate(inside_rows, axis=0).T
        from_end = mm(bs, state_low) * end_x
        grad_scaled = jnp.concatenate(grad_scaled, axis=1) + from_end
        entry_dy = dy * entry_x
        entry_dy_low = entry_dy.astype(BF16)
        out_terms = mm(cs, old) * entry_dy
        end_terms = scaled * from_end
        grad_step = mm_ones_tr(xs * grad_scaled, spread, 2)
        out_terms = mm_ones_tr(out_terms, spread, 2)
        end_terms = mm_ones_tr(end_terms, spread, 2)
        keep_row = entry_x[length - 1 : length, :]
        carried = jnp.sum(grad_state * old.astype(F32), axis=0, keepdims=True) * keep_row
        carried = mm_ones_tr(jnp.broadcast_to(carried, (8, width)), spread, 2)[0:1, :]
        triu = (cols >= rows).astype(BF16)
        below = (rows > cols).astype(BF16)
        grad_rate = inside + ones_mm(triu, out_terms, 2) + ones_mm(below, end_terms, 2) + carried
        grad_step = grad_step - decay_rate * grad_rate
        grad_raw = grad_step * sigmoid(raw)
        grad_scores_low = grad_scores.astype(BF16)
        grad_b = mm(grad_scores_low, cs) + mm_tr(scaled * end_x, state_low)
        grad_c = tr_mm(grad_scores_low, bs) + mm_tr(entry_dy_low, old)
        memory[q] = grad_state * keep_row + tr_mm(cs, entry_dy_low)
        conv_grad_x = (skip_ref[...] * dy + step_x * grad_scaled) * slope_x
        conv_grad_t = jnp.concatenate([grad_b, grad_c], axis=1) * slope_t

        remain = rem_ref[q, 0]
        results = [dz]
        for grad, ext, nxt, weight, sums in (
            (conv_grad_x, ext_x.at[q], next_x.at[q], params[0], gx_ref),
            (conv_grad_t, ext_t.at[q], next_t.at[q], params[2], gt_ref),
        ):
            current = ext[pl.ds(HALO, length), :]
            sums[KERNEL : KERNEL + 1, :] += jnp.sum(grad, axis=0, keepdims=True)
            sums[KERNEL - 1 : KERNEL, :] += jnp.sum(grad * current, axis=0, keepdims=True)
            nxt[0:length, :] = grad
            total = weight[KERNEL - 1 : KERNEL, :] * grad
            for back in range(1, KERNEL):
                tap = KERNEL - 1 - back
                shifted = jnp.where(offset >= back, ext[pl.ds(HALO - back, length), :], 0.0)
                sums[tap : tap + 1, :] += jnp.sum(grad * shifted, axis=0, keepdims=True)
                ahead = jnp.where(remain >= back, nxt[pl.ds(back, length), :], 0.0)
                total = total + weight[tap : tap + 1, :] * ahead
            nxt[length:, :] = grad[0:HALO, :]
            results.append(total.astype(BF16))
        results.append(mm_tr(grad_raw, params[5]).astype(BF16))
        gx_ref[KERNEL + 1 : KERNEL + 2, :] += jnp.sum(dy * xs, axis=0, keepdims=True)
        gh_ref[0:1, :] += jnp.sum(grad_raw, axis=0, keepdims=True)
        gh_ref[1:2, :] += jnp.sum(grad_rate * rate, axis=0, keepdims=True)
        out_ref[q, 0, :, : 2 * width] = jnp.concatenate(results[:2], axis=1)
        out_ref[q, 0, :, 2 * width : 2 * width + 2 * STATE] = results[2]
        out_ref[q, 0, :, 2 * width + 2 * STATE :] = results[3]


TAIL = 2 * STATE + LANES
AXES = ("seq", "fsdp")
MESH = pl.DeviceIdType.MESH


def whole_spec(shape):
    return pl.BlockSpec(shape, lambda i: (0,) * len(shape))


def chunk_specs(seqs, steps, length, reverse):
    def place(i):
        return steps - 1 - i if reverse else i

    def block(cols, column=0, rows=length):
        return pl.BlockSpec((seqs, 1, rows, cols), lambda i: (0, place(i), 0, column))

    def before(cols, column=0):
        return pl.BlockSpec(
            (seqs, 1, HALO, cols),
            lambda i: (0, jnp.maximum(place(i) - 1, 0), length // HALO - 1, column),
        )

    return block, before


def forward_mix(proj, off_col, consts):
    seqs, steps, length, cols = proj.shape
    width = (cols - TAIL) // 2
    block, before = chunk_specs(seqs, steps, length, False)
    tail_at = 2 * width // TAIL
    shape = (seqs, steps, length, width)
    return pl.pallas_call(
        forward_kernel,
        grid=(steps,),
        in_specs=[
            block(2 * width), before(2 * width), block(TAIL, tail_at), before(TAIL, tail_at),
            block(1),
        ]
        + [whole_spec(v.shape) for v in consts],
        out_specs=[
            block(width), block(width), block(length, 0, 1), block(width, 0, STATE),
        ],
        out_shape=[
            jax.ShapeDtypeStruct(shape, BF16),
            jax.ShapeDtypeStruct(shape, BF16),
            jax.ShapeDtypeStruct((seqs, steps, 1, length), F32),
            jax.ShapeDtypeStruct((seqs, steps, STATE, width), BF16),
        ],
        scratch_shapes=[
            pltpu.VMEM((seqs, STATE, width), F32),
            pltpu.VMEM((seqs, HALO + length, width), F32),
            pltpu.VMEM((seqs, HALO + length, 2 * STATE), F32),
        ],
        compiler_params=pltpu.CompilerParams(
            dimension_semantics=("arbitrary",), vmem_limit_bytes=32 << 20
        ),
        cost_estimate=pl.CostEstimate(
            flops=steps * seqs * 900_000_000, transcendentals=0, bytes_accessed=10_000_000
        ),
        name="mix_forward",
    )(proj, proj, proj, proj, off_col, *consts)


def backward_mix(proj, off_col, off_row, rem_col, y, grad_yn, stats, states, consts):
    seqs, steps, length, cols = proj.shape
    width = (cols - TAIL) // 2
    block, before = chunk_specs(seqs, steps, length, True)
    tail_at = 2 * width // TAIL
    sums = [(8, width), (8, 2 * STATE), (8, LANES)]
    return pl.pallas_call(
        backward_kernel,
        grid=(steps,),
        in_specs=[
            block(2 * width), before(2 * width), block(TAIL, tail_at), before(TAIL, tail_at),
            block(1), block(length, 0, 1), block(1), block(width), block(width),
            block(length, 0, 2), block(width, 0, STATE),
        ]
        + [whole_spec(v.shape) for v in consts],
        out_specs=[block(cols)] + [whole_spec(v) for v in sums],
        scratch_shapes=[
            pltpu.VMEM((seqs, STATE, width), F32),
            pltpu.VMEM((seqs, HALO + length, width), F32),
            pltpu.VMEM((seqs, HALO + length, 2 * STATE), F32),
            pltpu.VMEM((seqs, length + HALO, width), F32),
            pltpu.VMEM((seqs, length + HALO, 2 * STATE), F32),
        ],
        out_shape=[jax.ShapeDtypeStruct(proj.shape, BF16)]
        + [jax.ShapeDtypeStruct(v, F32) for v in sums],
        compiler_params=pltpu.CompilerParams(
            dimension_semantics=("arbitrary",), vmem_limit_bytes=40 << 20
        ),
        cost_estimate=pl.CostEstimate(
            flops=steps * seqs * 2_000_000_000, transcendentals=0, bytes_accessed=16_000_000
        ),
        name="mix_backward",
    )(
        proj, proj, proj, proj, off_col, off_row, rem_col, y, grad_yn, stats, states, *consts
    )


class Place:
    def __init__(self, seq, fsdp):
        self.seq, self.fsdp = seq, fsdp
        self.half, self.pairs = seq // 2, fsdp // 2
        s, f = lax.axis_index("seq"), lax.axis_index("fsdp")
        self.s, self.f = s, f
        self.top, self.low = s // self.half, lax.rem(s, self.half)
        self.core, self.pair = lax.rem(f, 2), f // 2
        self.home = self.core == self.top
        self.away = self.core != self.top
        self.chunk = self.low + self.half * self.core
        self.low_bits = [1 << i for i in range(self.half.bit_length() - 1)]

    def at(self, top=0, low=0, pair=0, core=0):
        return (
            flip(self.top, top) * self.half + flip(self.low, low),
            flip(self.pair, pair) * 2 + flip(self.core, core),
        )

    def bits_for(self, q):
        return self.low_bits if q % 2 == 0 else self.low_bits[::-1]


def flip(index, bits):
    for i in range(bits.bit_length()):
        if bits >> i & 1:
            bit = lax.rem(index // (1 << i), 2)
            index = index + (1 << i) * (1 - 2 * bit)
    return index


class Links:
    def __init__(self, send, recv, near):
        self.send, self.recv, self.near = send, recv, near
        self.far_count = self.near_count = 0

    def far(self, src, dst, device):
        i = self.far_count
        self.far_count += 1
        return pltpu.make_async_remote_copy(
            src_ref=src, dst_ref=dst, send_sem=self.send.at[i], recv_sem=self.recv.at[i],
            device_id=device, device_id_type=MESH,
        )

    def local(self, src, dst):
        i = self.near_count
        self.near_count += 1
        return pltpu.make_async_copy(src, dst, self.near.at[i])


def meet(devices):
    barrier = pltpu.get_barrier_semaphore()
    for device in devices:
        pl.semaphore_signal(barrier, inc=1, device_id=device, device_id_type=MESH)
    pl.semaphore_wait(barrier, len(devices))


def started(copy):
    copy.start()
    return copy


class TokenGather:
    def __init__(self, place, links, src, dst):
        self.place, self.src, self.dst = place, src, dst
        self.links = links
        chunk = place.s
        self.cross = links.far(src, dst.at[:, chunk], place.at(top=1, core=1))
        self.stay = links.local(src, dst.at[:, chunk])
        self.held = None
        self.sent = []
        self.stage = 0

    def begin(self):
        @pl.when(self.place.away)
        def _():
            self.cross.start()

        @pl.when(self.place.home)
        def _():
            self.stay.start()

    def arrive(self):
        @pl.when(self.place.away)
        def _():
            self.cross.wait_recv()

        @pl.when(self.place.home)
        def _():
            self.stay.wait()

        self.held = [[0] for _ in range(self.src.shape[0])]
        self.pending = [[] for _ in self.held]
        self.across = []
        for q in range(len(self.held)):
            self.share(q, [0])

    def block(self, q, low):
        return self.dst.at[q, flip(self.place.low, low) + self.place.half * self.place.core]

    def share(self, q, lows):
        for low in lows:
            ref = self.block(q, low)
            self.across.append(started(self.links.far(ref, ref, self.place.at(core=1))))

    def send_stage(self):
        for q, held in enumerate(self.held):
            bit = self.place.bits_for(q)[self.stage]
            for low in held:
                ref = self.block(q, low)
                self.pending[q].append(started(self.links.far(ref, ref, self.place.at(low=bit))))

    def finish_stage(self):
        for q, held in enumerate(self.held):
            bit = self.place.bits_for(q)[self.stage]
            for copy in self.pending[q]:
                copy.wait_recv()
            self.sent += self.pending[q]
            self.pending[q] = []
            fresh = [low ^ bit for low in held]
            held += fresh
            self.share(q, fresh)
        self.stage += 1

    def finish(self):
        for copy in self.across:
            copy.wait()
        for copy in self.sent:
            copy.wait_send()

        @pl.when(self.place.away)
        def _():
            self.cross.wait_send()


def peers_of(place):
    out = []
    for top in (1, 0):
        for low in range(place.half):
            for core in (0, 1):
                if (top, low, core) != (0, 0, 0):
                    out.append((top, low, core))
    return out


def entry_kernel(
    seq, fsdp,
    h_ref, zx_ref, tail_ref, ow_ref, cot_ref, seg_ref,
    h_out, w_out, ow_out, cot_out, seg_out,
    send, recv, near,
):
    place = Place(seq, fsdp)
    links = Links(send, recv, near)
    cols = zx_ref.shape[2]
    peers = peers_of(place)
    pair_steps = range(1, place.pairs)
    meet(
        [place.at(top=t, low=l, core=c) for t, l, c in peers]
        + [place.at(pair=p) for p in pair_steps]
    )
    tokens = TokenGather(place, links, h_ref, h_out)
    tokens.begin()

    def columns(ref):
        return ref.at[:, pl.ds(0, cols)]

    def tail_of(ref):
        return ref.at[:, pl.ds(cols, TAIL)]

    own = w_out.at[place.s, place.pair, place.core]
    other = w_out.at[flip(place.s, place.half), place.pair, place.core]

    tail_cross = started(links.far(tail_ref, tail_of(own), place.at(top=1)))
    zx_copies = []
    for t, l, c in peers:
        group = flip(place.core, c) * place.half + flip(place.low, l)
        zx_copies.append(
            started(links.far(zx_ref.at[group], columns(own), place.at(top=t, low=l, core=c)))
        )
    locals_ = [
        started(links.local(zx_ref.at[place.chunk], columns(own))),
        started(links.local(tail_ref, tail_of(own))),
    ]
    near_peers = [(l, c) for t, l, c in peers if t == 0]
    tail_copies = [
        started(links.far(tail_ref, tail_of(own), place.at(low=l, core=c))) for l, c in near_peers
    ]
    swap_segments = started(links.far(seg_ref, seg_out, place.at(core=1)))

    tokens.arrive()
    tokens.send_stage()
    tail_cross.wait_recv()
    tail_more = [
        started(links.far(tail_of(other), tail_of(other), place.at(low=l, core=c)))
        for l, c in near_peers
    ]
    for copy in locals_:
        copy.wait()
    cot = TokenGather(place, links, cot_ref, cot_out)
    cot.begin()
    tokens.finish_stage()

    index = lax.rem(place.core, 2)
    rows_own = ow_out.at[place.pair, index]
    to_home = links.far(ow_ref, rows_own, place.at(core=1))
    stay = links.local(ow_ref, rows_own)
    to_near = links.far(ow_ref, rows_own, place.at(top=1))
    to_far = links.far(ow_ref, rows_own, place.at(top=1, core=1))

    stages = len(place.low_bits)
    for _ in range(1, stages):
        tokens.send_stage()

    blocks = [(0, 0, 0)] + [p for p in peers if p[0] == 0] + [p for p in peers if p[0] == 1]
    arrival = {p: copy for p, copy in zip(peers, zx_copies)}
    tails = dict(zip(near_peers, tail_copies))
    tails_more = dict(zip(near_peers, tail_more))
    forwards = []
    for t, l, c in blocks:
        if (t, l, c) != (0, 0, 0):
            arrival[t, l, c].wait_recv()
            if t == 0:
                tails[l, c].wait_recv()
            elif (l, c) != (0, 0):
                tails_more[l, c].wait_recv()
        s, f = place.at(top=t, low=l, core=c)
        ref = w_out.at[s, place.pair, lax.rem(f, 2)]
        for p in pair_steps:
            forwards.append(started(links.far(ref, ref, place.at(pair=p))))
    for i in range(1, stages):
        tokens.finish_stage()

    cot.arrive()
    cot.send_stage()

    @pl.when(place.home)
    def _():
        stay.start()
        to_near.start()

    @pl.when(place.away)
    def _():
        to_home.start()
        to_far.start()

    for i in range(stages):
        cot.finish_stage()
        if i + 1 < stages:
            cot.send_stage()

    @pl.when(place.home)
    def _():
        stay.wait()
        to_home.wait_recv()

    @pl.when(place.away)
    def _():
        to_near.wait_recv()
        to_far.wait_recv()

    out_forwards = []
    for c in (0, 1):
        ref = ow_out.at[place.pair, c]
        for p in pair_steps:
            out_forwards.append(started(links.far(ref, ref, place.at(pair=p))))
    tokens.finish()
    cot.finish()
    for copy in forwards + out_forwards:
        copy.wait()
    for copy in [tail_cross] + zx_copies + tail_copies + tail_more:
        copy.wait_send()
    swap_segments.wait()

    @pl.when(place.home)
    def _():
        to_near.wait_send()

    @pl.when(place.away)
    def _():
        to_home.wait_send()
        to_far.wait_send()


ANYWHERE = pl.BlockSpec(memory_space=pl.ANY)


def entry_gather(seq, fsdp, normed, zx, tail, out_w, cotangent, segments):
    seqs, length, depth = normed.shape
    rows = tail.shape[0]
    tokens = jax.ShapeDtypeStruct((seqs, seq, length, depth), BF16)
    pairs = fsdp // 2
    return pl.pallas_call(
        functools.partial(entry_kernel, seq, fsdp),
        in_specs=[ANYWHERE] * 6,
        out_specs=[ANYWHERE] * 5,
        out_shape=[
            tokens,
            jax.ShapeDtypeStruct((seq, pairs, 2, rows, zx.shape[2] + TAIL), BF16),
            jax.ShapeDtypeStruct((pairs, 2) + out_w.shape, BF16),
            tokens,
            jax.ShapeDtypeStruct(segments.shape, segments.dtype),
        ],
        scratch_shapes=[
            pltpu.SemaphoreType.DMA((512,)),
            pltpu.SemaphoreType.DMA((512,)),
            pltpu.SemaphoreType.DMA((16,)),
        ],
        compiler_params=pltpu.CompilerParams(collective_id=0, has_side_effects=True),
        cost_estimate=pl.CostEstimate(
            flops=0, transcendentals=0, bytes_accessed=200_000_000
        ),
        name="entry_gather",
    )(normed, zx, tail, out_w, cotangent, segments)


def add_rows(out, left, right, rows=32):
    total = left.shape[0]
    step = next((size for size in (rows, 16) if total % size == 0), total)

    if step == total:
        out[...] = (left[...].astype(F32) + right[...].astype(F32)).astype(out.dtype)
        return

    @pl.loop(0, total // step)
    def _(i):
        at = pl.ds(pl.multiple_of(i * step, step), step)
        out[at] = (left[at].astype(F32) + right[at].astype(F32)).astype(out.dtype)


class TokenScatter:
    def __init__(self, place, links, src, out, own, first, later):
        self.place, self.links = place, links
        self.src, self.out, self.own, self.first, self.later = src, out, own, first, later
        self.seqs = src.shape[0]
        self.sent = []

    def begin(self):
        half, core = self.place.half, self.place.core
        self.loads, self.cores = [], []
        for q in range(self.seqs):
            give = self.src.at[q, pl.ds(half * (1 - core), half)]
            self.cores.append(
                started(self.links.far(give, self.first.at[q], self.place.at(core=1)))
            )
            keep = self.src.at[q, pl.ds(half * core, half)]
            self.loads.append(started(self.links.local(keep, self.own.at[q])))

    def add_cores(self):
        place = self.place
        self.live = [list(range(place.half)) for _ in range(self.seqs)]
        self.slot = [0] * self.seqs
        self.pending = [None] * self.seqs
        for q in range(self.seqs):
            self.loads[q].wait()
            self.cores[q].wait_recv()
            self.sent.append(self.cores[q])
            for low in self.away_first(q, 0):
                at = flip(place.low, low)
                add_rows(self.own.at[q, at], self.own.at[q, at], self.first.at[q, at])
            self.send(q, 0)

    def away_first(self, q, stage):
        return self.live[q]

    def send(self, q, stage):
        place = self.place
        bit = place.bits_for(q)[::-1][stage]
        give = [low for low in self.live[q] if low & bit]
        self.live[q] = [low for low in self.live[q] if not low & bit]
        self.pending[q] = []
        for low in give:
            slot = self.slot[q]
            self.slot[q] += 1
            copy = started(
                self.links.far(
                    self.own.at[q, flip(place.low, low)], self.later.at[q, slot],
                    place.at(low=bit),
                )
            )
            self.pending[q].append((copy, low ^ bit, slot))

    def add_stage(self, stage):
        for q in range(self.seqs):
            for copy, low, slot in self.pending[q]:
                copy.wait_recv()
                at = flip(self.place.low, low)
                add_rows(self.own.at[q, at], self.own.at[q, at], self.later.at[q, slot])
                self.sent.append(copy)
            if stage + 1 < len(self.place.low_bits):
                self.send(q, stage + 1)

    def deliver(self):
        place = self.place
        self.last = []
        for q in range(self.seqs):
            ref = self.own.at[q, place.low]
            cross = self.links.far(ref, self.out.at[q], place.at(top=1, core=1))
            stay = self.links.local(ref, self.out.at[q])
            self.last.append((cross, stay))

            @pl.when(place.away)
            def _():
                cross.start()

            @pl.when(place.home)
            def _():
                stay.start()

    def finish(self):
        for cross, stay in self.last:

            @pl.when(self.place.away)
            def _():
                cross.wait()

            @pl.when(self.place.home)
            def _():
                stay.wait()

        for copy in self.sent:
            copy.wait_send()


def exit_kernel(
    seq, fsdp,
    dh_ref, mixed_ref, part_ref, pout_ref, vec_ref,
    dh_out, mixed_out, slots_out, rows_out, vec_out,
    dh_own, dh_first, dh_later, mix_own, mix_first, mix_later,
    part_own, part_first, part_top, pout_own, pout_first, vec_val, vec_got,
    send, recv, near,
):
    place = Place(seq, fsdp)
    links = Links(send, recv, near)
    peers = peers_of(place)
    pair_steps = list(range(1, place.pairs))
    near_peers = [(l, c) for t, l, c in peers if t == 0]
    meet(
        [place.at(top=t, low=l, core=c) for t, l, c in peers]
        + [place.at(pair=p) for p in pair_steps]
    )
    half = place.half
    dh = TokenScatter(place, links, dh_ref, dh_out, dh_own, dh_first, dh_later)
    mixed = TokenScatter(place, links, mixed_ref, mixed_out, mix_own, mix_first, mix_later)
    dh.begin()

    far_rows = pl.ds(half * (1 - place.top), half)
    near_rows = pl.ds(half * place.top, half)
    by_pair = {}
    for name, rows in (("far", far_rows), ("near", near_rows)):
        by_pair[name] = [
            started(
                links.far(
                    part_ref.at[rows, flip(place.pair, p)], part_first.at[p - 1, rows],
                    place.at(pair=p),
                )
            )
            for p in pair_steps
        ]
    part_load = started(links.local(part_ref.at[:, place.pair], part_own))
    pout_pairs = [
        started(
            links.far(pout_ref.at[flip(place.pair, p)], pout_first.at[p - 1], place.at(pair=p))
        )
        for p in pair_steps
    ]
    pout_load = started(links.local(pout_ref.at[place.pair], pout_own))

    hops = [dict(pair=1 << i) for i in range(place.pairs.bit_length() - 1)]
    hops += [dict(top=1)] + [dict(low=b) for b in place.low_bits] + [dict(core=1)]
    vec_load = started(links.local(vec_ref, vec_val.at[0]))
    vec_copies = []

    def vec_send():
        i = len(vec_copies)
        vec_copies.append(
            started(links.far(vec_val.at[i], vec_got.at[i], place.at(**hops[i])))
        )

    def vec_add():
        i = len(vec_copies) - 1
        vec_copies[i].wait_recv()
        vec_val[i + 1] = vec_val[i] + vec_got[i]

    vec_load.wait()
    vec_send()
    mixed.begin()
    dh.add_cores()
    vec_add()
    vec_send()
    mixed.add_cores()

    def add_pairs(rows_at, copies):
        for copy in copies:
            copy.wait_recv()
        for p in pair_steps:
            for i in range(half):
                for c in (0, 1):
                    at = rows_at + i
                    add_rows(
                        part_own.at[at, c], part_own.at[at, c], part_first.at[p - 1, at, c], 16
                    )

    part_load.wait()
    add_pairs(half * (1 - place.top), by_pair["far"])
    cross = started(links.far(part_own.at[far_rows], part_top, place.at(top=1)))
    dh.add_stage(0)
    vec_add()
    vec_send()
    mixed.add_stage(0)
    add_pairs(half * place.top, by_pair["near"])

    pout_load.wait()
    for copy in pout_pairs:
        copy.wait_recv()
    for p in pair_steps:
        for c in (0, 1):
            add_rows(pout_own.at[c], pout_own.at[c], pout_first.at[p - 1, c])
    row_copies = []
    for c in (0, 1):
        to_far = links.far(
            pout_own.at[flip(place.core, c)], rows_out.at[1], place.at(top=1, core=c)
        )
        row_copies.append(to_far)

        @pl.when(place.away)
        def _():
            to_far.start()

    row_home = links.far(pout_own.at[1 - place.core], rows_out.at[0], place.at(core=1))
    row_stay = links.local(pout_own.at[place.core], rows_out.at[0])

    @pl.when(place.home)
    def _():
        row_home.start()
        row_stay.start()

    for stage in range(1, len(place.low_bits)):
        dh.add_stage(stage)
    dh.deliver()
    vec_add()
    vec_send()
    for stage in range(1, len(place.low_bits)):
        mixed.add_stage(stage)
    mixed.deliver()

    cross.wait_recv()
    slots = []
    for l, c in near_peers + [(0, 0)]:
        low, core = flip(place.low, l), flip(place.core, c)
        ref = part_own.at[half * place.top + low, core]
        add_rows(ref, ref, part_top.at[low, core], 16)
        slot = slots_out.at[place.core, place.low]
        if (l, c) == (0, 0):
            slots.append(started(links.local(ref, slot)))
        else:
            slots.append(started(links.far(ref, slot, place.at(low=l, core=c))))
    while len(vec_copies) < len(hops):
        vec_add()
        vec_send()
    vec_add()
    vec_store = started(links.local(vec_val.at[len(hops)], vec_out))

    for copy in slots:
        copy.wait()
    vec_store.wait()
    dh.finish()
    mixed.finish()
    cross.wait_send()
    for copy in by_pair["far"] + by_pair["near"] + pout_pairs + vec_copies:
        copy.wait_send()

    @pl.when(place.home)
    def _():
        row_stay.wait()
        row_home.wait_send()
        row_copies[0].wait_recv()

    @pl.when(place.away)
    def _():
        row_home.wait_recv()
        row_copies[1].wait_recv()
        row_copies[0].wait_send()
        row_copies[1].wait_send()


def exit_scatter(seq, fsdp, grad_h, mixed, part, part_out, vector):
    seqs, _, length, depth = grad_h.shape
    half, pairs = seq // 2, fsdp // 2
    rows, cols = part.shape[3:]
    rows_out = part_out.shape[2]
    bits = (half.bit_length() - 1) + (pairs.bit_length() - 1) + 2
    token_own = pltpu.VMEM((seqs, half, length, depth), BF16)
    token_later = pltpu.VMEM((seqs, max(half - 1, 1), length, depth), BF16)
    tokens = jax.ShapeDtypeStruct((seqs, length, depth), BF16)
    return pl.pallas_call(
        functools.partial(exit_kernel, seq, fsdp),
        in_specs=[ANYWHERE] * 5,
        out_specs=[ANYWHERE] * 5,
        out_shape=[
            tokens,
            tokens,
            jax.ShapeDtypeStruct((2, half, rows, cols), BF16),
            jax.ShapeDtypeStruct((2, rows_out, depth), BF16),
            jax.ShapeDtypeStruct(vector.shape, F32),
        ],
        scratch_shapes=[
            token_own, token_own, token_later, token_own, token_own, token_later,
            pltpu.VMEM((seq, 2, rows, cols), BF16),
            pltpu.VMEM((max(pairs - 1, 1), seq, 2, rows, cols), BF16),
            pltpu.VMEM((half, 2, rows, cols), BF16),
            pltpu.VMEM((2, rows_out, depth), BF16),
            pltpu.VMEM((max(pairs - 1, 1), 2, rows_out, depth), BF16),
            pltpu.VMEM((bits + 1,) + vector.shape, F32),
            pltpu.VMEM((bits,) + vector.shape, F32),
            pltpu.SemaphoreType.DMA((128,)),
            pltpu.SemaphoreType.DMA((128,)),
            pltpu.SemaphoreType.DMA((32,)),
        ],
        compiler_params=pltpu.CompilerParams(
            collective_id=1, has_side_effects=True, vmem_limit_bytes=56 << 20
        ),
        cost_estimate=pl.CostEstimate(
            flops=0, transcendentals=0, bytes_accessed=200_000_000
        ),
        name="exit_scatter",
    )(grad_h, mixed, part, part_out, vector)


def local(
    tokens, segments, gain_in, w_in, conv_w, conv_b, dt_bias, a_log, skip, gain_out, w_out,
    cotangent,
):
    steps, shards = lax.axis_size("seq"), lax.axis_size("fsdp")
    place = Place(steps, shards)
    seqs, length, _ = tokens.shape
    width = INNER // steps
    heads = HEADS // steps
    rows_in = w_in.shape[0]
    number = place.chunk

    def mine(array, size):
        return lax.dynamic_slice_in_dim(array, number * size, size, array.ndim - 1)

    wide = tokens.astype(F32)
    scale_in = lax.rsqrt(jnp.mean(wide * wide, axis=-1, keepdims=True) + EPSILON)
    normed = (wide * scale_in * gain_in).astype(BF16)
    zx = w_in[:, : 2 * INNER].reshape(rows_in, 2, steps, width).transpose(2, 0, 1, 3)
    zx = zx.reshape(steps, rows_in, 2 * width)
    tail = jnp.pad(w_in[:, 2 * INNER :], ((0, 0), (0, LANES - HEADS)))
    h_all, w_mine, out_w, cot_all, segs = entry_gather(
        steps, shards, normed, zx, tail, w_out, cotangent, segments
    )
    w_mine = w_mine.reshape(D, 2 * width + TAIL)
    out_w = out_w.reshape(width, D)
    segs = jnp.where(place.home, segments, segs)

    total = steps * length
    index = lax.broadcasted_iota(jnp.int32, (seqs, total), 1)
    starts = jnp.concatenate([jnp.ones((seqs, 1), bool), segs[:, 1:] != segs[:, :-1]], axis=1)
    first = lax.cummax(jnp.where(starts, index, 0), axis=1)
    ends = jnp.concatenate([starts[:, 1:], jnp.ones((seqs, 1), bool)], axis=1)
    last = lax.cummin(jnp.where(ends, index, total), axis=1, reverse=True)
    off = (index - first).astype(F32).reshape(seqs, steps, length)
    rem = (last - index).astype(F32).reshape(seqs, steps, length)
    off_col, off_row, rem_col = off[..., None], off[:, :, None, :], rem[..., None]

    heads_p = jnp.stack([mine(dt_bias, heads), mine(a_log, heads)])
    lane = lax.broadcasted_iota(jnp.int32, (LANES, LANES), 1)
    source = lax.broadcasted_iota(jnp.int32, (LANES, LANES), 0)
    pick = ((lane < heads) & (source == lane + number * heads)).astype(BF16)
    consts = (
        mine(conv_w[:, :INNER], width),
        mine(conv_b[None, :INNER], width),
        conv_w[:, INNER:],
        conv_b[None, INNER:],
        jnp.pad(heads_p, ((0, 6), (0, LANES - heads))),
        pick,
        jnp.repeat(mine(skip, heads), HEAD_DIM)[None],
        mine(gain_out[None], width),
    )

    def dot(a, b):
        return lax.dot_general(a, b, (((3,), (0,)), ((), ())), preferred_element_type=F32)

    def dot_tr(a, b):
        return lax.dot_general(a, b, (((3,), (1,)), ((), ())), preferred_element_type=F32)

    def dot_tokens(a, b):
        dims = (0, 1, 2)
        return lax.dot_general(a, b, ((dims, dims), ((), ())), preferred_element_type=F32)

    proj = dot(h_all, w_mine).astype(BF16)
    y, gated, squares, states = forward_mix(proj, off_col, consts)

    grad_yn = dot_tr(cot_all, out_w)
    sums = jnp.stack(
        [squares[:, :, 0], jnp.sum(grad_yn * gated.astype(F32), axis=-1)], axis=2
    )
    for offsets in [dict(core=1)] + [dict(low=b) for b in place.low_bits]:
        sums = sums + exchange(sums, steps, shards, **offsets)
    scale = lax.rsqrt(sums[:, :, 0] / INNER + EPSILON)
    stats = jnp.stack([scale, sums[:, :, 1] * (scale * scale * scale / INNER)], axis=2)
    scale = scale[..., None]
    mixed = (dot(gated, out_w) * scale).astype(BF16)
    y_normed = (gated.astype(F32) * scale).astype(BF16)
    part_out = dot_tokens(y_normed, cot_all).astype(BF16)

    grad_proj, sums_x, sums_t, sums_h = backward_mix(
        proj, off_col, off_row, rem_col, y, grad_yn, stats, states, consts
    )

    grad_h = dot_tr(grad_proj, w_mine).astype(BF16)
    part = dot_tokens(h_all, grad_proj)
    gain_part = jnp.sum(part * w_mine.astype(F32), axis=1)
    part = part.astype(BF16).reshape(steps, shards // 2, 2, rows_in, 2 * width + TAIL)
    grouped = jnp.concatenate(
        [
            sums_x[: KERNEL + 1].reshape(-1),
            sums_x[KERNEL + 2],
            jnp.sum(sums_x[KERNEL + 1].reshape(heads, HEAD_DIM), axis=-1),
            sums_h[:2, :heads].reshape(-1),
        ]
    )
    size = -(-grouped.shape[0] // LANES) * LANES
    grouped = jnp.pad(grouped, (0, size - grouped.shape[0])).reshape(1, -1, LANES)
    grouped = lax.dynamic_update_slice_in_dim(
        jnp.zeros((steps,) + grouped.shape[1:], F32), grouped, number, 0
    )
    everywhere = jnp.concatenate([gain_part, sums_t[: KERNEL + 1].reshape(-1)])
    vector = jnp.concatenate([grouped.reshape(-1, LANES), everywhere.reshape(-1, LANES)])
    grad_h, mixed, slots, rows, vector = exit_scatter(
        steps, shards, grad_h, mixed, part,
        part_out.reshape((shards // 2, 2) + w_out.shape), vector,
    )

    mixed = (wide + mixed.astype(F32)).astype(BF16)
    w_out_grad = rows[0].astype(F32) + rows[1].astype(F32)
    slots = slots.reshape(steps, rows_in, 2 * width + TAIL).astype(F32)
    zx_grad = slots[:, :, : 2 * width].reshape(steps, rows_in, 2, width).transpose(1, 2, 0, 3)
    tail_grad = jnp.sum(slots[:, :, 2 * width : 2 * width + 2 * STATE + HEADS], axis=0)
    w_in_grad = jnp.concatenate([zx_grad.reshape(rows_in, 2 * INNER), tail_grad], axis=1)

    grad_h = grad_h.astype(F32)
    scaled = grad_h * gain_in
    unit = wide * scale_in
    tokens_grad = cotangent.astype(F32) + scale_in * (
        scaled - unit * jnp.mean(scaled * unit, axis=-1, keepdims=True)
    )

    edge = steps * size // LANES
    everywhere = vector[edge:].reshape(-1)
    grouped = vector[:edge].reshape(steps, size)
    gain_in_grad = everywhere[:D] / gain_in
    conv_x = grouped[:, : (KERNEL + 1) * width].reshape(steps, KERNEL + 1, width)
    conv_x = conv_x.transpose(1, 0, 2).reshape(KERNEL + 1, INNER)
    conv_grads = jnp.concatenate([conv_x, everywhere[D:].reshape(KERNEL + 1, -1)], axis=1)
    rest = grouped[:, (KERNEL + 1) * width :]
    gain_out_grad = rest[:, :width].reshape(-1)
    per_head = rest[:, width : width + 3 * heads].reshape(steps, 3, heads)
    per_head = per_head.transpose(1, 0, 2).reshape(3, HEADS)
    return (
        mixed, tokens_grad, gain_in_grad, w_in_grad, conv_grads[:KERNEL], conv_grads[KERNEL],
        per_head[1], per_head[2], per_head[0], gain_out_grad, w_out_grad,
    )


def exchange(value, seq, fsdp, low=0, core=0):
    perm = [
        (s * fsdp + f, (s ^ low) * fsdp + (f ^ core)) for s in range(seq) for f in range(fsdp)
    ]
    return lax.ppermute(value, AXES, perm)


def solution(mesh):
    by_token = P("fsdp", "seq", None)
    by_row = P(("seq", "fsdp"), None)
    placed = (
        by_token, P("fsdp", None), P(), by_row, P(), P(), P(), P(), P(), P(), by_row, by_token,
    )
    return jax.shard_map(
        local,
        mesh=mesh,
        in_specs=placed,
        out_specs=(by_token, by_token, P(), by_row, P(), P(), P(), P(), P(), P(), by_row),
        check_vma=False,
    )
```

```python
import functools

import jax
import jax.numpy as jnp
import numpy as np
from jax import lax
from jax.experimental import pallas as pl
from jax.experimental.pallas import tpu as pltpu
from jax.sharding import PartitionSpec as P

D = 1536
HEADS = 48
HEAD_DIM = 64
STATE = 128
KERNEL = 4
INNER = 3072
LANES = 128
HALO = 16
EPSILON = 1e-05
F32 = jnp.float32
BF16 = jnp.bfloat16


def mm(a, b):
    return jnp.dot(a.astype(BF16), b.astype(BF16), preferred_element_type=F32)


def mm_tr(a, b):
    return lax.dot_general(
        a.astype(BF16), b.astype(BF16), (((1,), (1,)), ((), ())), preferred_element_type=F32
    )


def tr_mm(a, b):
    return lax.dot_general(
        a.astype(BF16), b.astype(BF16), (((0,), (0,)), ((), ())), preferred_element_type=F32
    )


def pieces(a, count):
    out = []
    for _ in range(count - 1):
        part = a.astype(BF16)
        out.append(part)
        a = a - part.astype(F32)
    out.append(a.astype(BF16))
    return out


def ones_mm(ones, a, count):
    return sum(jnp.dot(ones, part, preferred_element_type=F32) for part in pieces(a, count))


def mm_ones(a, ones, count):
    return sum(jnp.dot(part, ones, preferred_element_type=F32) for part in pieces(a, count))


def mm_ones_tr(a, ones, count):
    return sum(
        lax.dot_general(part, ones, (((1,), (1,)), ((), ())), preferred_element_type=F32)
        for part in pieces(a, count)
    )


def iota(shape, dim):
    return lax.broadcasted_iota(jnp.int32, shape, dim)


def softplus(v):
    return jnp.maximum(v, 0.0) + jnp.log1p(jnp.exp(-jnp.abs(v)))


def sigmoid(v):
    return 1.0 / (1.0 + jnp.exp(-v))


def causal_conv(ext, current, halo, weight, bias, offset):
    length = current.shape[0]
    ext[0:HALO, :] = halo
    ext[HALO : HALO + length, :] = current
    total = bias + weight[KERNEL - 1 : KERNEL, :] * current
    for back in range(1, KERNEL):
        shifted = jnp.where(offset >= back, ext[pl.ds(HALO - back, length), :], 0.0)
        total = total + weight[KERNEL - 1 - back : KERNEL - back, :] * shifted
    return total


def head_tiles(width):
    out = []
    for start in range(0, width, LANES):
        size = min(LANES, width - start)
        heads = [start // HEAD_DIM + i for i in range(size // HEAD_DIM)]
        out.append((start, size, heads))
    return out


def masked_heads(tile, heads):
    if len(heads) == 1:
        return tile
    lane = iota(tile.shape, 1) // HEAD_DIM
    return jnp.concatenate(
        [jnp.where(lane == i, tile, jnp.zeros_like(tile)) for i in range(len(heads))], axis=0
    )


def expander(width):
    return (iota((LANES, width), 1) // HEAD_DIM == iota((LANES, width), 0)).astype(BF16)


def chunk_common(x, xh, tail, tailh, offset, params, ext_x, ext_t, width):
    wx, bx, wt, bt, heads_p, pick = params
    length = x.shape[0]
    conv_x = causal_conv(ext_x, x.astype(F32), xh.astype(F32), wx, bx, offset)
    conv_t = causal_conv(
        ext_t,
        tail[:, : 2 * STATE].astype(F32),
        tailh[:, : 2 * STATE].astype(F32),
        wt,
        bt,
        offset,
    )
    raw = jnp.dot(tail[:, 2 * STATE :], pick, preferred_element_type=F32) + heads_p[0:1, :]
    step = softplus(raw)
    decay_rate = jnp.exp(heads_p[1:2, :])
    rate = -step * decay_rate
    tril = (iota((length, length), 0) >= iota((length, length), 1)).astype(BF16)
    cumul = ones_mm(tril, rate, 3)
    spread = expander(width)
    row = iota((length, 1), 0)
    entry = jnp.where(offset > row.astype(F32), jnp.exp(cumul), 0.0)
    last_off = offset[length - 1 : length, :]
    same_last = row.astype(F32) >= (length - 1) - last_off
    to_end = jnp.where(same_last, jnp.exp(cumul[length - 1 : length, :] - cumul), 0.0)
    step_x = mm_ones(step, spread, 2)
    entry_x = mm_ones(entry, spread, 2)
    end_x = mm_ones(to_end, spread, 2)
    return conv_x, conv_t, raw, step, rate, decay_rate, cumul, spread, step_x, entry_x, end_x


def forward_kernel(
    seq, fsdp,
    h_ref, w_ref, cot_ref, ow_ref, off_ref,
    wx_ref, bx_ref, wt_ref, bt_ref, hp_ref, pick_ref, skip_ref, gain_ref,
    proj_ref, y_ref, gated_ref, square_ref, state_ref, cot_out, ow_out,
    memory, ext_x, ext_t, last_rows, send, recv, near,
):
    seqs, _, length, width = y_ref.shape
    depth = h_ref.shape[3]
    step_at = pl.program_id(0)

    place = Place(seq, fsdp)
    links = Links(send, recv, near)
    cot = TokenGather(place, links, cot_ref, cot_out)
    w_rows = RowGather(place, links, ow_ref, ow_out)
    stages = len(place.low_bits)
    arrive_at = max(seq // 2 - 1, 1)

    @pl.when(step_at == 0)
    def _():
        memory[...] = jnp.zeros_like(memory)
        last_rows[...] = jnp.zeros_like(last_rows)
        meet_pair(place)
        cot.begin()

    @pl.when(step_at == 1)
    def _():
        w_rows.begin()

    @pl.when(step_at == arrive_at)
    def _():
        cot.arrive()
        cot.send_stage(0)

    proj = jnp.dot(
        h_ref[...].reshape(seqs * length, depth), w_ref[...], preferred_element_type=F32
    ).astype(BF16)
    proj_ref[...] = proj.reshape(proj_ref.shape)
    params = tuple(r[...] for r in (wx_ref, bx_ref, wt_ref, bt_ref, hp_ref, pick_ref))
    for q in range(seqs):
        offset = off_ref[q, 0]
        chunk_rows = proj[q * length : (q + 1) * length]
        zx, tail = chunk_rows[:, : 2 * width], chunk_rows[:, 2 * width :]
        earlier = last_rows[q]
        conv_x, conv_t, _, _, _, _, cumul, _, step_x, entry_x, end_x = chunk_common(
            zx[:, width:], earlier[:, width : 2 * width], tail, earlier[:, 2 * width :], offset, params,
            ext_x.at[q], ext_t.at[q], width,
        )
        xs = conv_x * sigmoid(conv_x)
        act_t = conv_t * sigmoid(conv_t)
        bs = act_t[:, :STATE].astype(BF16)
        cs = act_t[:, STATE:].astype(BF16)
        scaled = xs * step_x
        scores = mm_tr(cs, bs)
        gap = iota((length, length), 0) - iota((length, length), 1)
        same = (gap >= 0) & (gap.astype(F32) <= offset)
        cumul_t = cumul.T
        old = memory[q]
        old_low = old.astype(BF16)
        state_ref[q, 0] = old_low
        outside = mm(cs, old_low) * entry_x + skip_ref[...] * xs
        squares = jnp.zeros((length, 1), F32)
        for start, size, heads in head_tiles(width):
            mixing = []
            for head in heads:
                spans = cumul[:, head : head + 1] - cumul_t[head : head + 1, :]
                decays = jnp.exp(jnp.where(same, spans, -1e30))
                mixing.append((decays * scores).astype(BF16))
            tile = masked_heads(scaled[:, start : start + size].astype(BF16), heads)
            mix = mixing[0] if len(heads) == 1 else jnp.concatenate(mixing, axis=1)
            inside = jnp.dot(mix, tile, preferred_element_type=F32)
            y_low = (inside + outside[:, start : start + size]).astype(BF16)
            y_ref[q, 0, :, start : start + size] = y_low
            z = zx[:, start : start + size].astype(F32)
            gated = y_low.astype(F32) * (z * sigmoid(z))
            gated_ref[q, 0, :, start : start + size] = (
                gated * gain_ref[:, start : start + size]
            ).astype(BF16)
            squares = squares + jnp.sum(gated * gated, axis=1, keepdims=True)
        square_ref[q, 0] = jnp.broadcast_to(squares, (length, LANES)).T[0:1, :]
        fresh = tr_mm(bs, scaled * end_x)
        memory[q] = old * entry_x[length - 1 : length, :] + fresh
        last_rows[q] = chunk_rows[length - HALO :]

    @pl.when(step_at == pl.num_programs(0) - 2)
    def _():
        w_rows.forward()

    @pl.when(step_at == pl.num_programs(0) - 1)
    def _():
        for stage in range(stages):
            cot.finish_stage(stage)
            if stage + 1 < stages:
                cot.send_stage(stage + 1)
        w_rows.finish()
        cot.finish()


def backward_kernel(
    seq, fsdp,
    zx_ref, zxh_ref, tail_ref, tailh_ref, off_ref, offr_ref, rem_ref, y_ref, grad_ref, stat_ref,
    state_ref, mixed_ref, pout_ref,
    wx_ref, bx_ref, wt_ref, bt_ref, hp_ref, pick_ref, skip_ref, gain_ref,
    out_ref, gx_ref, gt_ref, gh_ref, mixed_out, rows_out,
    memory, ext_x, ext_t, next_x, next_t,
    mix_own, mix_first, mix_later, pout_own, pout_first, send, recv, near,
):
    seqs, _, length, width = y_ref.shape
    step_at = pl.program_id(0)

    place = Place(seq, fsdp)
    links = Links(send, recv, near)
    mixed = TokenScatter(place, links, mixed_ref, mixed_out, mix_own, mix_first, mix_later)
    w_rows = RowScatter(place, links, pout_ref, rows_out, pout_own, pout_first)
    stages = len(place.low_bits)

    @pl.when(step_at == 0)
    def _():
        meet_pair(place)
        mixed.begin()
        w_rows.begin()

    @pl.when(step_at == 2)
    def _():
        mixed.add_cores()
        mixed.send_stage(0)

    @pl.when(step_at == 4)
    def _():
        w_rows.add_pairs()

    @pl.when(step_at == pl.num_programs(0) - 2)
    def _():
        mixed.add_stage(0)
        if stages > 1:
            mixed.send_stage(1)

    @pl.when(pl.program_id(0) == 0)
    def _():
        memory[...] = jnp.zeros_like(memory)
        gx_ref[...] = jnp.zeros_like(gx_ref)
        gt_ref[...] = jnp.zeros_like(gt_ref)
        gh_ref[...] = jnp.zeros_like(gh_ref)
        next_x[:, length:, :] = jnp.zeros_like(next_x[:, length:, :])
        next_t[:, length:, :] = jnp.zeros_like(next_t[:, length:, :])

    params = tuple(r[...] for r in (wx_ref, bx_ref, wt_ref, bt_ref, hp_ref, pick_ref))
    for q in range(seqs):
        offset = off_ref[q, 0]
        conv_x, conv_t, raw, step, rate, decay_rate, cumul, spread, step_x, entry_x, end_x = (
            chunk_common(
                zx_ref[q, 0, :, width:], zxh_ref[q, 0, :, width:], tail_ref[q, 0], tailh_ref[q, 0], offset,
                params, ext_x.at[q], ext_t.at[q], width,
            )
        )
        stats = jnp.broadcast_to(stat_ref[q, 0, 0:1, :], (LANES, length)).T
        slopes = jnp.broadcast_to(stat_ref[q, 0, 1:2, :], (LANES, length)).T
        scale, slope = stats[:, 0:1], slopes[:, 0:1]
        z = zx_ref[q, 0, :, :width].astype(F32)
        sig_z = sigmoid(z)
        silu_z = z * sig_z
        y = y_ref[q, 0].astype(F32)
        gated = y * silu_z
        scaled_grad = grad_ref[q, 0].astype(F32) * scale
        gx_ref[KERNEL + 2 : KERNEL + 3, :] += jnp.sum(scaled_grad * gated, axis=0, keepdims=True)
        grad_gated = gain_ref[...] * scaled_grad - gated * slope
        dy_low = (grad_gated * silu_z).astype(BF16)
        dz = (grad_gated * y * (sig_z + silu_z * (1.0 - sig_z))).astype(BF16)
        dy = dy_low.astype(F32)

        sig_x = sigmoid(conv_x)
        xs = conv_x * sig_x
        slope_x = sig_x + xs * (1.0 - sig_x)
        sig_t = sigmoid(conv_t)
        act_t = conv_t * sig_t
        slope_t = sig_t + act_t * (1.0 - sig_t)
        bs = act_t[:, :STATE].astype(BF16)
        cs = act_t[:, STATE:].astype(BF16)
        scaled = xs * step_x
        scaled_low = scaled.astype(BF16)
        scores = mm_tr(bs, cs)
        rows, cols = iota((length, length), 0), iota((length, length), 1)
        gap = cols - rows
        same = (gap >= 0) & (gap.astype(F32) <= offr_ref[q, 0])
        strict = gap > 0
        upper = (rows >= cols).astype(BF16)
        cumul_t = cumul.T
        old = state_ref[q, 0]
        grad_state = memory[q]
        state_low = grad_state.astype(BF16)
        grad_scores = jnp.zeros((length, length), F32)
        grad_scaled = []
        inside_rows = []
        for start, size, heads in head_tiles(width):
            dy_tile = masked_heads(dy_low[:, start : start + size], heads)
            grad_mix = mm_tr(scaled_low[:, start : start + size], dy_tile)
            mixing = []
            for place, head in enumerate(heads):
                spans = cumul_t[head : head + 1, :] - cumul[:, head : head + 1]
                decays = jnp.exp(jnp.where(same, spans, -1e30))
                weighted = grad_mix[:, place * length : (place + 1) * length] * decays
                grad_scores = grad_scores + weighted
                mixing.append((decays * scores).astype(BF16))
                terms = jnp.where(strict, weighted * scores, 0.0).astype(BF16)
                sums = jnp.dot(terms, upper, preferred_element_type=F32)
                inside_rows.append(
                    jnp.sum(jnp.where(strict, sums, 0.0), axis=0, keepdims=True)
                )
            mix = mixing[0] if len(heads) == 1 else jnp.concatenate(mixing, axis=1)
            grad_scaled.append(jnp.dot(mix, dy_tile, preferred_element_type=F32))
        inside_rows.append(jnp.zeros((LANES - len(inside_rows), length), F32))
        inside = jnp.concatenate(inside_rows, axis=0).T
        from_end = mm(bs, state_low) * end_x
        grad_scaled = jnp.concatenate(grad_scaled, axis=1) + from_end
        entry_dy = dy * entry_x
        entry_dy_low = entry_dy.astype(BF16)
        out_terms = mm(cs, old) * entry_dy
        end_terms = scaled * from_end
        grad_step = mm_ones_tr(xs * grad_scaled, spread, 2)
        out_terms = mm_ones_tr(out_terms, spread, 2)
        end_terms = mm_ones_tr(end_terms, spread, 2)
        keep_row = entry_x[length - 1 : length, :]
        carried = jnp.sum(grad_state * old.astype(F32), axis=0, keepdims=True) * keep_row
        carried = mm_ones_tr(jnp.broadcast_to(carried, (8, width)), spread, 2)[0:1, :]
        triu = (cols >= rows).astype(BF16)
        below = (rows > cols).astype(BF16)
        grad_rate = inside + ones_mm(triu, out_terms, 2) + ones_mm(below, end_terms, 2) + carried
        grad_step = grad_step - decay_rate * grad_rate
        grad_raw = grad_step * sigmoid(raw)
        grad_scores_low = grad_scores.astype(BF16)
        grad_b = mm(grad_scores_low, cs) + mm_tr(scaled * end_x, state_low)
        grad_c = tr_mm(grad_scores_low, bs) + mm_tr(entry_dy_low, old)
        memory[q] = grad_state * keep_row + tr_mm(cs, entry_dy_low)
        conv_grad_x = (skip_ref[...] * dy + step_x * grad_scaled) * slope_x
        conv_grad_t = jnp.concatenate([grad_b, grad_c], axis=1) * slope_t

        remain = rem_ref[q, 0]
        results = [dz]
        for grad, ext, nxt, weight, sums in (
            (conv_grad_x, ext_x.at[q], next_x.at[q], params[0], gx_ref),
            (conv_grad_t, ext_t.at[q], next_t.at[q], params[2], gt_ref),
        ):
            current = ext[pl.ds(HALO, length), :]
            sums[KERNEL : KERNEL + 1, :] += jnp.sum(grad, axis=0, keepdims=True)
            sums[KERNEL - 1 : KERNEL, :] += jnp.sum(grad * current, axis=0, keepdims=True)
            nxt[0:length, :] = grad
            total = weight[KERNEL - 1 : KERNEL, :] * grad
            for back in range(1, KERNEL):
                tap = KERNEL - 1 - back
                shifted = jnp.where(offset >= back, ext[pl.ds(HALO - back, length), :], 0.0)
                sums[tap : tap + 1, :] += jnp.sum(grad * shifted, axis=0, keepdims=True)
                ahead = jnp.where(remain >= back, nxt[pl.ds(back, length), :], 0.0)
                total = total + weight[tap : tap + 1, :] * ahead
            nxt[length:, :] = grad[0:HALO, :]
            results.append(total.astype(BF16))
        results.append(mm_tr(grad_raw, params[5]).astype(BF16))
        gx_ref[KERNEL + 1 : KERNEL + 2, :] += jnp.sum(dy * xs, axis=0, keepdims=True)
        gh_ref[0:1, :] += jnp.sum(grad_raw, axis=0, keepdims=True)
        gh_ref[1:2, :] += jnp.sum(grad_rate * rate, axis=0, keepdims=True)
        out_ref[q, 0, :, : 2 * width] = jnp.concatenate(results[:2], axis=1)
        out_ref[q, 0, :, 2 * width : 2 * width + 2 * STATE] = results[2]
        out_ref[q, 0, :, 2 * width + 2 * STATE :] = results[3]

    @pl.when(step_at == pl.num_programs(0) - 1)
    def _():
        for stage in range(1, stages):
            mixed.add_stage(stage)
            if stage + 1 < stages:
                mixed.send_stage(stage + 1)
        mixed.store()
        w_rows.finish()
        mixed.finish()


TAIL = 2 * STATE + LANES
AXES = ("seq", "fsdp")
MESH = pl.DeviceIdType.MESH


def whole_spec(shape):
    return pl.BlockSpec(shape, lambda i: (0,) * len(shape))


def chunk_specs(seqs, steps, length, reverse):
    def place(i):
        return steps - 1 - i if reverse else i

    def block(cols, column=0, rows=length):
        return pl.BlockSpec((seqs, 1, rows, cols), lambda i: (0, place(i), 0, column))

    def before(cols, column=0):
        return pl.BlockSpec(
            (seqs, 1, HALO, cols),
            lambda i: (0, jnp.maximum(place(i) - 1, 0), length // HALO - 1, column),
        )

    return block, before


def forward_mix(h_all, w_mine, cotangent, out_w, off_col, consts, seq, fsdp):
    seqs, steps, length, depth = h_all.shape
    cols = w_mine.shape[1]
    width = (cols - TAIL) // 2
    block, _ = chunk_specs(seqs, steps, length, False)
    shape = (seqs, steps, length, width)
    return pl.pallas_call(
        functools.partial(forward_kernel, seq, fsdp),
        grid=(steps,),
        in_specs=[
            block(depth),
            pl.BlockSpec(w_mine.shape, lambda i: (0, 0), pipeline_mode=pl.Buffered(1)),
            ANYWHERE, ANYWHERE, block(1),
        ]
        + [whole_spec(v.shape) for v in consts],
        out_specs=[
            block(cols), block(width), block(width), block(length, 0, 1), block(width, 0, STATE),
            ANYWHERE, ANYWHERE,
        ],
        out_shape=[
            jax.ShapeDtypeStruct((seqs, steps, length, cols), BF16),
            jax.ShapeDtypeStruct(shape, BF16),
            jax.ShapeDtypeStruct(shape, BF16),
            jax.ShapeDtypeStruct((seqs, steps, 1, length), F32),
            jax.ShapeDtypeStruct((seqs, steps, STATE, width), BF16),
            jax.ShapeDtypeStruct(h_all.shape, BF16),
            jax.ShapeDtypeStruct((fsdp // 2, 2) + out_w.shape, BF16),
        ],
        scratch_shapes=[
            pltpu.VMEM((seqs, STATE, width), F32),
            pltpu.VMEM((seqs, HALO + length, width), F32),
            pltpu.VMEM((seqs, HALO + length, 2 * STATE), F32),
            pltpu.VMEM((seqs, HALO, cols), BF16),
            pltpu.SemaphoreType.DMA((64,)),
            pltpu.SemaphoreType.DMA((64,)),
            pltpu.SemaphoreType.DMA((8,)),
        ],
        compiler_params=pltpu.CompilerParams(
            dimension_semantics=("arbitrary",), vmem_limit_bytes=48 << 20, collective_id=2,
            has_side_effects=True,
        ),
        cost_estimate=pl.CostEstimate(
            flops=steps * seqs * 900_000_000, transcendentals=0, bytes_accessed=10_000_000
        ),
        name="mix_forward",
    )(h_all, w_mine, cotangent, out_w, off_col, *consts)


def backward_mix(
    proj, off_col, off_row, rem_col, y, grad_yn, stats, states, mixed, part_out, consts, seq, fsdp
):
    seqs, steps, length, cols = proj.shape
    depth = mixed.shape[3]
    width = (cols - TAIL) // 2
    block, before = chunk_specs(seqs, steps, length, True)
    tail_at = 2 * width // TAIL
    half, pairs = seq // 2, fsdp // 2
    rows_out = part_out.shape[2]
    sums = [(8, width), (8, 2 * STATE), (8, LANES)]
    token_own = pltpu.VMEM((seqs, half, length, depth), BF16)
    return pl.pallas_call(
        functools.partial(backward_kernel, seq, fsdp),
        grid=(steps,),
        in_specs=[
            block(2 * width), before(2 * width), block(TAIL, tail_at), before(TAIL, tail_at),
            block(1), block(length, 0, 1), block(1), block(width), block(width),
            block(length, 0, 2), block(width, 0, STATE), ANYWHERE, ANYWHERE,
        ]
        + [whole_spec(v.shape) for v in consts],
        out_specs=[block(cols)] + [whole_spec(v) for v in sums] + [ANYWHERE, ANYWHERE],
        scratch_shapes=[
            pltpu.VMEM((seqs, STATE, width), F32),
            pltpu.VMEM((seqs, HALO + length, width), F32),
            pltpu.VMEM((seqs, HALO + length, 2 * STATE), F32),
            pltpu.VMEM((seqs, length + HALO, width), F32),
            pltpu.VMEM((seqs, length + HALO, 2 * STATE), F32),
            token_own, token_own, pltpu.VMEM((seqs, max(half - 1, 1), length, depth), BF16),
            pltpu.VMEM((2, rows_out, depth), BF16),
            pltpu.VMEM((max(pairs - 1, 1), 2, rows_out, depth), BF16),
            pltpu.SemaphoreType.DMA((64,)),
            pltpu.SemaphoreType.DMA((64,)),
            pltpu.SemaphoreType.DMA((16,)),
        ],
        out_shape=[jax.ShapeDtypeStruct(proj.shape, BF16)]
        + [jax.ShapeDtypeStruct(v, F32) for v in sums]
        + [
            jax.ShapeDtypeStruct((seqs, length, depth), BF16),
            jax.ShapeDtypeStruct((2, rows_out, depth), BF16),
        ],
        compiler_params=pltpu.CompilerParams(
            dimension_semantics=("arbitrary",), vmem_limit_bytes=56 << 20, collective_id=3,
            has_side_effects=True,
        ),
        cost_estimate=pl.CostEstimate(
            flops=steps * seqs * 2_000_000_000, transcendentals=0, bytes_accessed=16_000_000
        ),
        name="mix_backward",
    )(
        proj, proj, proj, proj, off_col, off_row, rem_col, y, grad_yn, stats, states, mixed,
        part_out, *consts,
    )


class Place:
    def __init__(self, seq, fsdp):
        self.seq, self.fsdp = seq, fsdp
        self.half, self.pairs = seq // 2, fsdp // 2
        s, f = lax.axis_index("seq"), lax.axis_index("fsdp")
        self.s, self.f = s, f
        self.top, self.low = s // self.half, lax.rem(s, self.half)
        self.core, self.pair = lax.rem(f, 2), f // 2
        self.home = self.core == self.top
        self.away = self.core != self.top
        self.chunk = self.low + self.half * self.core
        self.low_bits = [1 << i for i in range(self.half.bit_length() - 1)]

    def at(self, top=0, low=0, pair=0, core=0):
        return (
            flip(self.top, top) * self.half + flip(self.low, low),
            flip(self.pair, pair) * 2 + flip(self.core, core),
        )

    def bits_for(self, q):
        return self.low_bits if q % 2 == 0 else self.low_bits[::-1]


def flip(index, bits):
    for i in range(bits.bit_length()):
        if bits >> i & 1:
            bit = lax.rem(index // (1 << i), 2)
            index = index + (1 << i) * (1 - 2 * bit)
    return index


class Copy:
    def __init__(self, make):
        self.make = make

    def start(self):
        self.make().start()
        return self

    def wait(self):
        self.make().wait()

    def wait_send(self):
        self.make().wait_send()

    def wait_recv(self):
        self.make().wait_recv()


class Links:
    def __init__(self, send, recv, near):
        self.send, self.recv, self.near = send, recv, near
        self.far_count = self.near_count = 0

    def far(self, make):
        i = self.far_count
        self.far_count += 1

        def build():
            src, dst, device = make()
            return pltpu.make_async_remote_copy(
                src_ref=src, dst_ref=dst, send_sem=self.send.at[i], recv_sem=self.recv.at[i],
                device_id=device, device_id_type=MESH,
            )

        return Copy(build)

    def local(self, make):
        i = self.near_count
        self.near_count += 1
        return Copy(lambda: pltpu.make_async_copy(*make(), self.near.at[i]))


def meet(devices):
    barrier = pltpu.get_barrier_semaphore()
    for device in devices:
        pl.semaphore_signal(barrier, inc=1, device_id=device, device_id_type=MESH)
    pl.semaphore_wait(barrier, len(devices))


def meet_pair(place):
    meet(
        [place.at(top=t, low=l, core=c) for t, l, c in peers_of(place)]
        + [place.at(pair=p) for p in range(1, place.pairs)]
    )


def peers_of(place):
    out = []
    for top in (0, 1):
        for low in range(place.half):
            for core in (0, 1):
                if (top, low, core) != (0, 0, 0):
                    out.append((top, low, core))
    return out


class TokenGather:
    def __init__(self, place, links, src, dst):
        self.place, self.src, self.dst = place, src, dst
        seqs = src.shape[0]
        self.cross = links.far(
            lambda: (src, dst.at[:, place.s], place.at(top=1, core=1))
        )
        self.stay = links.local(lambda: (src, dst.at[:, place.s]))
        self.share = [[] for _ in range(seqs)]
        self.stages = []
        held = [[0] for _ in range(seqs)]
        for q in range(seqs):
            self.share[q].append([self.copy(links, q, low, core=1) for low in held[q]])
        for i in range(len(place.low_bits)):
            stage = []
            for q in range(seqs):
                bit = place.bits_for(q)[i]
                stage.append([self.copy(links, q, low, low_bit=bit) for low in held[q]])
                fresh = [low ^ bit for low in held[q]]
                held[q] = held[q] + fresh
                self.share[q].append([self.copy(links, q, low, core=1) for low in fresh])
            self.stages.append(stage)

    def copy(self, links, q, low, low_bit=0, core=0):
        def make():
            place = self.place
            ref = self.dst.at[q, flip(place.low, low) + place.half * place.core]
            return ref, ref, place.at(low=low_bit, core=core)

        return links.far(make)

    def begin(self):
        @pl.when(self.place.away)
        def _():
            self.cross.start()

        @pl.when(self.place.home)
        def _():
            self.stay.start()

    def arrive(self):
        @pl.when(self.place.away)
        def _():
            self.cross.wait_recv()

        @pl.when(self.place.home)
        def _():
            self.stay.wait()

    def send_stage(self, i):
        for copies in self.stages[i]:
            for copy in copies:
                copy.start()
        for share in self.share:
            for copy in share[i]:
                copy.start()

    def finish_stage(self, i):
        for copies in self.stages[i]:
            for copy in copies:
                copy.wait_recv()
        if i + 1 == len(self.stages):
            for share in self.share:
                for copy in share[i + 1]:
                    copy.start()

    def finish(self):
        for share in self.share:
            for copies in share:
                for copy in copies:
                    copy.wait()
        for stage in self.stages:
            for copies in stage:
                for copy in copies:
                    copy.wait_send()

        @pl.when(self.place.away)
        def _():
            self.cross.wait_send()


class RowGather:
    def __init__(self, place, links, src, dst):
        self.place = place
        pairs = range(1, place.pairs)

        def slot():
            return dst.at[place.pair, place.core]

        self.stay = links.local(lambda: (src, slot()))
        self.to_home = links.far(lambda: (src, slot(), place.at(core=1)))
        self.to_near = links.far(lambda: (src, slot(), place.at(top=1)))
        self.to_far = links.far(lambda: (src, slot(), place.at(top=1, core=1)))

        def forward(c, p):
            return links.far(
                lambda: (dst.at[place.pair, c], dst.at[place.pair, c], place.at(pair=p))
            )

        self.forwards = [forward(c, p) for c in (0, 1) for p in pairs]

    def begin(self):
        @pl.when(self.place.home)
        def _():
            self.stay.start()
            self.to_near.start()

        @pl.when(self.place.away)
        def _():
            self.to_home.start()
            self.to_far.start()

    def forward(self):
        @pl.when(self.place.home)
        def _():
            self.stay.wait()
            self.to_home.wait_recv()

        @pl.when(self.place.away)
        def _():
            self.to_near.wait_recv()
            self.to_far.wait_recv()

        for copy in self.forwards:
            copy.start()

    def finish(self):
        for copy in self.forwards:
            copy.wait()

        @pl.when(self.place.home)
        def _():
            self.to_near.wait_send()

        @pl.when(self.place.away)
        def _():
            self.to_home.wait_send()
            self.to_far.wait_send()


def entry_kernel(
    seq, fsdp, h_ref, zx_ref, tail_ref, seg_ref, h_out, w_out, seg_out, send, recv, near
):
    place = Place(seq, fsdp)
    links = Links(send, recv, near)
    cols = zx_ref.shape[2]
    peers = peers_of(place)
    others = range(1, place.pairs)
    tokens = TokenGather(place, links, h_ref, h_out)

    def block(t=0, l=0, c=0):
        s, f = place.at(top=t, low=l, core=c)
        return w_out.at[s, place.pair, lax.rem(f, 2)]

    def columns(ref):
        return ref.at[:, pl.ds(0, cols)]

    def tail_of(ref):
        return ref.at[:, pl.ds(cols, TAIL)]

    def send_zx(t, l, c):
        group = flip(place.core, c) * place.half + flip(place.low, l)
        return zx_ref.at[group], columns(block()), place.at(top=t, low=l, core=c)

    zx = {p: links.far(functools.partial(send_zx, *p)) for p in peers}
    own = [
        links.local(lambda: (zx_ref.at[place.chunk], columns(block()))),
        links.local(lambda: (tail_ref, tail_of(block()))),
    ]
    tail_cross = links.far(lambda: (tail_ref, tail_of(block()), place.at(top=1)))
    near_peers = [(l, c) for t, l, c in peers if t == 0]

    def send_tail(l, c):
        return tail_ref, tail_of(block()), place.at(low=l, core=c)

    def send_other(l, c):
        return tail_of(block(1)), tail_of(block(1)), place.at(low=l, core=c)

    tails = {p: links.far(functools.partial(send_tail, *p)) for p in near_peers}
    tails_more = {p: links.far(functools.partial(send_other, *p)) for p in near_peers}
    swap_segments = links.far(lambda: (seg_ref, seg_out, place.at(core=1)))

    def send_on(t, l, c, p):
        return block(t, l, c), block(t, l, c), place.at(pair=p)

    forwards = {
        p: [links.far(functools.partial(send_on, *p, other)) for other in others]
        for p in [(0, 0, 0)] + peers
    }

    meet_pair(place)
    tokens.begin()
    tail_cross.start()
    for copy in own:
        copy.start()
    for p in near_peers:
        zx[0, *p].start()
        tails[p].start()
    swap_segments.start()
    for copy in own:
        copy.wait()
    for copy in forwards[0, 0, 0]:
        copy.start()
    tail_cross.wait_recv()
    for p in near_peers:
        tails_more[p].start()
    for p in near_peers:
        zx[0, *p].wait_recv()
        tails[p].wait_recv()
        for copy in forwards[0, *p]:
            copy.start()
    for p in peers:
        if p[0] == 1:
            zx[p].start()

    tokens.arrive()
    tokens.send_stage(0)
    for p in near_peers:
        tails_more[p].wait_recv()
    stages = len(place.low_bits)
    far_peers = [p for p in peers if p[0] == 1]
    for i in range(stages):
        tokens.finish_stage(i)
        if i + 1 < stages:
            tokens.send_stage(i + 1)
        at, to = (len(far_peers) * k // stages for k in (i, i + 1))
        for p in far_peers[at:to]:
            zx[p].wait_recv()
            for copy in forwards[p]:
                copy.start()

    tokens.finish()
    for p in forwards:
        for copy in forwards[p]:
            copy.wait()
    tail_cross.wait_send()
    for group in (zx, tails, tails_more):
        for copy in group.values():
            copy.wait_send()
    swap_segments.wait()


ANYWHERE = pl.BlockSpec(memory_space=pl.ANY)


def entry_gather(seq, fsdp, normed, zx, tail, segments):
    seqs, length, depth = normed.shape
    rows = tail.shape[0]
    return pl.pallas_call(
        functools.partial(entry_kernel, seq, fsdp),
        in_specs=[ANYWHERE] * 4,
        out_specs=[ANYWHERE] * 3,
        out_shape=[
            jax.ShapeDtypeStruct((seqs, seq, length, depth), BF16),
            jax.ShapeDtypeStruct((seq, fsdp // 2, 2, rows, zx.shape[2] + TAIL), BF16),
            jax.ShapeDtypeStruct(segments.shape, segments.dtype),
        ],
        scratch_shapes=[
            pltpu.SemaphoreType.DMA((256,)),
            pltpu.SemaphoreType.DMA((256,)),
            pltpu.SemaphoreType.DMA((8,)),
        ],
        compiler_params=pltpu.CompilerParams(collective_id=0, has_side_effects=True),
        cost_estimate=pl.CostEstimate(
            flops=0, transcendentals=0, bytes_accessed=200_000_000
        ),
        name="entry_gather",
    )(normed, zx, tail, segments)


def add_rows(out, left, right, rows=32):
    total = left.shape[0]
    step = next((size for size in (rows, 16) if total % size == 0), total)

    if step == total:
        out[...] = (left[...].astype(F32) + right[...].astype(F32)).astype(out.dtype)
        return

    @pl.loop(0, total // step)
    def _(i):
        at = pl.ds(pl.multiple_of(i * step, step), step)
        out[at] = (left[at].astype(F32) + right[at].astype(F32)).astype(out.dtype)


class TokenScatter:
    def __init__(self, place, links, src, out, own, first, later):
        self.place = place
        self.out, self.own, self.first, self.later = out, own, first, later
        self.seqs = src.shape[0]
        half = place.half

        def give(q):
            return links.far(
                lambda: (
                    src.at[q, pl.ds(half * (1 - place.core), half)], first.at[q],
                    place.at(core=1),
                )
            )

        def keep(q):
            return links.local(
                lambda: (src.at[q, pl.ds(half * place.core, half)], own.at[q])
            )

        self.cores = [give(q) for q in range(self.seqs)]
        self.loads = [keep(q) for q in range(self.seqs)]
        self.stages = [[] for _ in place.low_bits]
        for q in range(self.seqs):
            live, slot = list(range(half)), 0
            for i, bit in enumerate(place.bits_for(q)[::-1]):
                for low in [low for low in live if low & bit]:
                    self.stages[i].append((self.copy(links, q, low, slot, bit), q, low ^ bit, slot))
                    slot += 1
                live = [low for low in live if not low & bit]
        self.stay = links.local(lambda: (own.at[:, place.low], out))

    def copy(self, links, q, low, slot, bit):
        return links.far(
            lambda: (
                self.own.at[q, flip(self.place.low, low)], self.later.at[q, slot],
                self.place.at(low=bit),
            )
        )

    def begin(self):
        for q in range(self.seqs):
            self.cores[q].start()
            self.loads[q].start()

    def add_cores(self):
        for q in range(self.seqs):
            self.loads[q].wait()
            self.cores[q].wait_recv()
            for low in range(self.place.half):
                add_rows(self.own.at[q, low], self.own.at[q, low], self.first.at[q, low])

    def send_stage(self, i):
        for copy, _, _, _ in self.stages[i]:
            copy.start()

    def add_stage(self, i):
        for copy, q, low, slot in self.stages[i]:
            copy.wait_recv()
            ref = self.own.at[q, flip(self.place.low, low)]
            add_rows(ref, ref, self.later.at[q, slot])

    def store(self):
        self.stay.start()
        self.stay.wait()

    def finish(self):
        for copy in self.cores:
            copy.wait_send()
        for stage in self.stages:
            for copy, _, _, _ in stage:
                copy.wait_send()


class RowScatter:
    def __init__(self, place, links, src, out, own, first):
        self.place, self.own, self.first = place, own, first

        def over(p):
            return links.far(
                lambda: (src.at[flip(place.pair, p)], first.at[p - 1], place.at(pair=p))
            )

        def far(c):
            return links.far(
                lambda: (own.at[flip(place.core, c)], out.at[1], place.at(top=1, core=c))
            )

        self.over = [over(p) for p in range(1, place.pairs)]
        self.load = links.local(lambda: (src.at[place.pair], own))
        self.far = [far(0), far(1)]
        self.near = links.far(lambda: (own.at[1 - place.core], out.at[0], place.at(core=1)))
        self.stay = links.local(lambda: (own.at[place.core], out.at[0]))

    def begin(self):
        self.load.start()
        for copy in self.over:
            copy.start()

    def add_pairs(self):
        self.load.wait()
        for i, copy in enumerate(self.over):
            copy.wait_recv()
            for c in (0, 1):
                add_rows(self.own.at[c], self.own.at[c], self.first.at[i, c])

        @pl.when(self.place.away)
        def _():
            for copy in self.far:
                copy.start()

        @pl.when(self.place.home)
        def _():
            self.near.start()
            self.stay.start()

    def finish(self):
        for copy in self.over:
            copy.wait_send()

        @pl.when(self.place.home)
        def _():
            self.stay.wait()
            self.near.wait_send()
            self.far[0].wait_recv()

        @pl.when(self.place.away)
        def _():
            self.near.wait_recv()
            self.far[1].wait_recv()
            for copy in self.far:
                copy.wait_send()


class Deliver:
    def __init__(self, place, links, src, out):
        self.place = place
        self.cross = links.far(lambda: (src(), out, place.at(top=1, core=1)))
        self.stay = links.local(lambda: (src(), out))

    def begin(self):
        @pl.when(self.place.away)
        def _():
            self.cross.start()

        @pl.when(self.place.home)
        def _():
            self.stay.start()

    def finish(self):
        @pl.when(self.place.away)
        def _():
            self.cross.wait()

        @pl.when(self.place.home)
        def _():
            self.stay.wait()


def exit_kernel(
    seq, fsdp,
    dh_ref, mixed_ref, part_ref, vec_ref,
    dh_out, mixed_out, slots_out, vec_out,
    dh_own, dh_first, dh_later, part_own, part_first, part_top, vec_val, vec_got,
    send, recv, near,
):
    place = Place(seq, fsdp)
    links = Links(send, recv, near)
    half = place.half
    others = list(range(1, place.pairs))
    dh = TokenScatter(place, links, dh_ref, dh_out, dh_own, dh_first, dh_later)
    dh_last = Deliver(place, links, lambda: dh_own.at[:, place.low], dh_out)
    mixed = Deliver(place, links, lambda: mixed_ref, mixed_out)

    def rows_of(top):
        return pl.ds(half * flip(place.top, top), half)

    def over(top, p):
        return links.far(
            lambda: (
                part_ref.at[rows_of(top), flip(place.pair, p)],
                part_first.at[p - 1, rows_of(top)],
                place.at(pair=p),
            )
        )

    over_pairs = [[over(top, p) for p in others] for top in (0, 1)]
    part_load = links.local(lambda: (part_ref.at[:, place.pair], part_own))
    cross = links.far(lambda: (part_own.at[rows_of(1)], part_top, place.at(top=1)))

    def row_block(l, c):
        return part_own.at[half * place.top + flip(place.low, l), flip(place.core, c)]

    def spread(l, c):
        return links.far(
            lambda: (
                row_block(l, c), slots_out.at[place.core, place.low], place.at(low=l, core=c)
            )
        )

    near_peers = [(l, c) for t, l, c in peers_of(place) if t == 0]
    slots = {p: spread(*p) for p in near_peers}
    slots[0, 0] = links.local(lambda: (row_block(0, 0), slots_out.at[place.core, place.low]))

    hops = [dict(pair=1 << i) for i in range(place.pairs.bit_length() - 1)]
    hops += [dict(top=1)] + [dict(low=b) for b in place.low_bits] + [dict(core=1)]

    def hop(i):
        return links.far(lambda: (vec_val.at[i], vec_got.at[i], place.at(**hops[i])))

    vec = [hop(i) for i in range(len(hops))]
    vec_load = links.local(lambda: (vec_ref, vec_val.at[0]))
    vec_store = links.local(lambda: (vec_val.at[len(hops)], vec_out))
    state = {"at": 0}

    def vec_next():
        i = state["at"]
        state["at"] += 1
        if i < len(hops):
            vec[i].wait_recv()
            vec_val[i + 1] = vec_val[i] + vec_got[i]
            if i + 1 < len(hops):
                vec[i + 1].start()
            else:
                vec_store.start()

    def add_pairs(top):
        for i, copy in enumerate(over_pairs[top]):
            copy.wait_recv()
            for low in range(half):
                for c in (0, 1):
                    ref = part_own.at[half * flip(place.top, top) + low, c]
                    got = part_first.at[i, half * flip(place.top, top) + low, c]
                    add_rows(ref, ref, got, 16)

    meet_pair(place)
    for copy in over_pairs[1]:
        copy.start()
    mixed.begin()
    dh.begin()
    part_load.start()
    vec_load.start()
    for copy in over_pairs[0]:
        copy.start()
    vec_load.wait()
    vec[0].start()
    dh.add_cores()
    dh.send_stage(0)
    vec_next()
    part_load.wait()
    add_pairs(1)
    cross.start()
    stages = len(place.low_bits)
    for i in range(stages):
        dh.add_stage(i)
        if i + 1 < stages:
            dh.send_stage(i + 1)
        else:
            dh_last.begin()
        vec_next()
    add_pairs(0)
    vec_next()
    cross.wait_recv()
    for l, c in near_peers + [(0, 0)]:
        ref = row_block(l, c)
        add_rows(ref, ref, part_top.at[flip(place.low, l), flip(place.core, c)], 16)
        slots[l, c].start()
    while state["at"] < len(hops):
        vec_next()
    for copy in slots.values():
        copy.wait()
    vec_store.wait()
    mixed.finish()
    dh_last.finish()
    dh.finish()
    cross.wait_send()
    for copy in over_pairs[0] + over_pairs[1] + vec:
        copy.wait_send()


def exit_scatter(seq, fsdp, grad_h, mixed, part, vector):
    seqs, _, length, depth = grad_h.shape
    half, pairs = seq // 2, fsdp // 2
    rows, cols = part.shape[3:]
    bits = (half.bit_length() - 1) + (pairs.bit_length() - 1) + 2
    token_own = pltpu.VMEM((seqs, half, length, depth), BF16)
    tokens = jax.ShapeDtypeStruct((seqs, length, depth), BF16)
    return pl.pallas_call(
        functools.partial(exit_kernel, seq, fsdp),
        in_specs=[ANYWHERE] * 4,
        out_specs=[ANYWHERE] * 4,
        out_shape=[
            tokens,
            tokens,
            jax.ShapeDtypeStruct((2, half, rows, cols), BF16),
            jax.ShapeDtypeStruct(vector.shape, F32),
        ],
        scratch_shapes=[
            token_own, token_own, pltpu.VMEM((seqs, max(half - 1, 1), length, depth), BF16),
            pltpu.VMEM((seq, 2, rows, cols), BF16),
            pltpu.VMEM((max(pairs - 1, 1), seq, 2, rows, cols), BF16),
            pltpu.VMEM((half, 2, rows, cols), BF16),
            pltpu.VMEM((bits + 1,) + vector.shape, F32),
            pltpu.VMEM((bits,) + vector.shape, F32),
            pltpu.SemaphoreType.DMA((96,)),
            pltpu.SemaphoreType.DMA((96,)),
            pltpu.SemaphoreType.DMA((16,)),
        ],
        compiler_params=pltpu.CompilerParams(
            collective_id=1, has_side_effects=True, vmem_limit_bytes=56 << 20
        ),
        cost_estimate=pl.CostEstimate(
            flops=0, transcendentals=0, bytes_accessed=200_000_000
        ),
        name="exit_scatter",
    )(grad_h, mixed, part, vector)


def local(
    tokens, segments, gain_in, w_in, conv_w, conv_b, dt_bias, a_log, skip, gain_out, w_out,
    cotangent,
):
    steps, shards = lax.axis_size("seq"), lax.axis_size("fsdp")
    place = Place(steps, shards)
    seqs, length, _ = tokens.shape
    width = INNER // steps
    heads = HEADS // steps
    rows_in = w_in.shape[0]
    number = place.chunk

    def mine(array, size):
        return lax.dynamic_slice_in_dim(array, number * size, size, array.ndim - 1)

    wide = tokens.astype(F32)
    scale_in = lax.rsqrt(jnp.mean(wide * wide, axis=-1, keepdims=True) + EPSILON)
    normed = (wide * scale_in * gain_in).astype(BF16)
    zx = w_in[:, : 2 * INNER].reshape(rows_in, 2, steps, width).transpose(2, 0, 1, 3)
    zx = zx.reshape(steps, rows_in, 2 * width)
    tail = jnp.pad(w_in[:, 2 * INNER :], ((0, 0), (0, LANES - HEADS)))
    h_all, w_mine, segs = entry_gather(steps, shards, normed, zx, tail, segments)
    w_mine = w_mine.reshape(D, 2 * width + TAIL)
    segs = jnp.where(place.home, segments, segs)

    total = steps * length
    index = lax.broadcasted_iota(jnp.int32, (seqs, total), 1)
    starts = jnp.concatenate([jnp.ones((seqs, 1), bool), segs[:, 1:] != segs[:, :-1]], axis=1)
    first = lax.cummax(jnp.where(starts, index, 0), axis=1)
    ends = jnp.concatenate([starts[:, 1:], jnp.ones((seqs, 1), bool)], axis=1)
    last = lax.cummin(jnp.where(ends, index, total), axis=1, reverse=True)
    off = (index - first).astype(F32).reshape(seqs, steps, length)
    rem = (last - index).astype(F32).reshape(seqs, steps, length)
    off_col, off_row, rem_col = off[..., None], off[:, :, None, :], rem[..., None]

    heads_p = jnp.stack([mine(dt_bias, heads), mine(a_log, heads)])
    lane = lax.broadcasted_iota(jnp.int32, (LANES, LANES), 1)
    source = lax.broadcasted_iota(jnp.int32, (LANES, LANES), 0)
    pick = ((lane < heads) & (source == lane + number * heads)).astype(BF16)
    consts = (
        mine(conv_w[:, :INNER], width),
        mine(conv_b[None, :INNER], width),
        conv_w[:, INNER:],
        conv_b[None, INNER:],
        jnp.pad(heads_p, ((0, 6), (0, LANES - heads))),
        pick,
        jnp.repeat(mine(skip, heads), HEAD_DIM)[None],
        mine(gain_out[None], width),
    )

    def dot(a, b):
        return lax.dot_general(a, b, (((3,), (0,)), ((), ())), preferred_element_type=F32)

    def dot_tr(a, b):
        return lax.dot_general(a, b, (((3,), (1,)), ((), ())), preferred_element_type=F32)

    def dot_tokens(a, b):
        dims = (0, 1, 2)
        return lax.dot_general(a, b, ((dims, dims), ((), ())), preferred_element_type=F32)

    proj, y, gated, squares, states, cot_all, out_w = forward_mix(
        h_all, w_mine, cotangent, w_out, off_col, consts, steps, shards
    )
    out_w = out_w.reshape(width, D)

    grad_yn = dot_tr(cot_all, out_w)
    sums = jnp.stack(
        [squares[:, :, 0], jnp.sum(grad_yn * gated.astype(F32), axis=-1)], axis=2
    )
    for offsets in [dict(core=1)] + [dict(low=b) for b in place.low_bits]:
        sums = sums + exchange(sums, steps, shards, **offsets)
    scale = lax.rsqrt(sums[:, :, 0] / INNER + EPSILON)
    stats = jnp.stack([scale, sums[:, :, 1] * (scale * scale * scale / INNER)], axis=2)
    scale = scale[..., None]
    mixed = (dot(gated, out_w) * scale).astype(BF16)
    y_normed = (gated.astype(F32) * scale).astype(BF16)
    part_out = dot_tokens(y_normed, cot_all).astype(BF16)

    part_out = part_out.reshape((shards // 2, 2) + w_out.shape)
    grad_proj, sums_x, sums_t, sums_h, mixed, rows = backward_mix(
        proj, off_col, off_row, rem_col, y, grad_yn, stats, states, mixed, part_out, consts,
        steps, shards,
    )

    grad_h = dot_tr(grad_proj, w_mine).astype(BF16)
    part = dot_tokens(h_all, grad_proj)
    gain_part = jnp.sum(part * w_mine.astype(F32), axis=1)
    part = part.astype(BF16).reshape(steps, shards // 2, 2, rows_in, 2 * width + TAIL)
    grouped = jnp.concatenate(
        [
            sums_x[: KERNEL + 1].reshape(-1),
            sums_x[KERNEL + 2],
            jnp.sum(sums_x[KERNEL + 1].reshape(heads, HEAD_DIM), axis=-1),
            sums_h[:2, :heads].reshape(-1),
        ]
    )
    size = -(-grouped.shape[0] // LANES) * LANES
    grouped = jnp.pad(grouped, (0, size - grouped.shape[0])).reshape(1, -1, LANES)
    grouped = lax.dynamic_update_slice_in_dim(
        jnp.zeros((steps,) + grouped.shape[1:], F32), grouped, number, 0
    )
    everywhere = jnp.concatenate([gain_part, sums_t[: KERNEL + 1].reshape(-1)])
    vector = jnp.concatenate([grouped.reshape(-1, LANES), everywhere.reshape(-1, LANES)])
    grad_h, mixed, slots, vector = exit_scatter(steps, shards, grad_h, mixed, part, vector)

    mixed = (wide + mixed.astype(F32)).astype(BF16)
    w_out_grad = rows[0].astype(F32) + rows[1].astype(F32)
    slots = slots.reshape(steps, rows_in, 2 * width + TAIL).astype(F32)
    zx_grad = slots[:, :, : 2 * width].reshape(steps, rows_in, 2, width).transpose(1, 2, 0, 3)
    tail_grad = jnp.sum(slots[:, :, 2 * width : 2 * width + 2 * STATE + HEADS], axis=0)
    w_in_grad = jnp.concatenate([zx_grad.reshape(rows_in, 2 * INNER), tail_grad], axis=1)

    grad_h = grad_h.astype(F32)
    scaled = grad_h * gain_in
    unit = wide * scale_in
    tokens_grad = cotangent.astype(F32) + scale_in * (
        scaled - unit * jnp.mean(scaled * unit, axis=-1, keepdims=True)
    )

    edge = steps * size // LANES
    everywhere = vector[edge:].reshape(-1)
    grouped = vector[:edge].reshape(steps, size)
    gain_in_grad = everywhere[:D] / gain_in
    conv_x = grouped[:, : (KERNEL + 1) * width].reshape(steps, KERNEL + 1, width)
    conv_x = conv_x.transpose(1, 0, 2).reshape(KERNEL + 1, INNER)
    conv_grads = jnp.concatenate([conv_x, everywhere[D:].reshape(KERNEL + 1, -1)], axis=1)
    rest = grouped[:, (KERNEL + 1) * width :]
    gain_out_grad = rest[:, :width].reshape(-1)
    per_head = rest[:, width : width + 3 * heads].reshape(steps, 3, heads)
    per_head = per_head.transpose(1, 0, 2).reshape(3, HEADS)
    return (
        mixed, tokens_grad, gain_in_grad, w_in_grad, conv_grads[:KERNEL], conv_grads[KERNEL],
        per_head[1], per_head[2], per_head[0], gain_out_grad, w_out_grad,
    )


def exchange(value, seq, fsdp, low=0, core=0):
    perm = [
        (s * fsdp + f, (s ^ low) * fsdp + (f ^ core)) for s in range(seq) for f in range(fsdp)
    ]
    return lax.ppermute(value, AXES, perm)


def solution(mesh):
    by_token = P("fsdp", "seq", None)
    by_row = P(("seq", "fsdp"), None)
    placed = (
        by_token, P("fsdp", None), P(), by_row, P(), P(), P(), P(), P(), P(), by_row, by_token,
    )
    return jax.shard_map(
        local,
        mesh=mesh,
        in_specs=placed,
        out_specs=(by_token, by_token, P(), by_row, P(), P(), P(), P(), P(), P(), by_row),
        check_vma=False,
    )
```

```python
import functools

import jax
import jax.numpy as jnp
import numpy as np
from jax import lax
from jax.experimental import pallas as pl
from jax.experimental.pallas import tpu as pltpu
from jax.sharding import PartitionSpec as P

D = 1536
HEADS = 48
HEAD_DIM = 64
STATE = 128
KERNEL = 4
INNER = 3072
LANES = 128
HALO = 16
EPSILON = 1e-05
F32 = jnp.float32
BF16 = jnp.bfloat16


def mm(a, b):
    return jnp.dot(a.astype(BF16), b.astype(BF16), preferred_element_type=F32)


def mm_tr(a, b):
    return lax.dot_general(
        a.astype(BF16), b.astype(BF16), (((1,), (1,)), ((), ())), preferred_element_type=F32
    )


def tr_mm(a, b):
    return lax.dot_general(
        a.astype(BF16), b.astype(BF16), (((0,), (0,)), ((), ())), preferred_element_type=F32
    )


def pieces(a, count):
    out = []
    for _ in range(count - 1):
        part = a.astype(BF16)
        out.append(part)
        a = a - part.astype(F32)
    out.append(a.astype(BF16))
    return out


def ones_mm(ones, a, count):
    return sum(jnp.dot(ones, part, preferred_element_type=F32) for part in pieces(a, count))


def mm_ones(a, ones, count):
    return sum(jnp.dot(part, ones, preferred_element_type=F32) for part in pieces(a, count))


def mm_ones_tr(a, ones, count):
    return sum(
        lax.dot_general(part, ones, (((1,), (1,)), ((), ())), preferred_element_type=F32)
        for part in pieces(a, count)
    )


def iota(shape, dim):
    return lax.broadcasted_iota(jnp.int32, shape, dim)


def softplus(v):
    return jnp.maximum(v, 0.0) + jnp.log1p(jnp.exp(-jnp.abs(v)))


def sigmoid(v):
    return 1.0 / (1.0 + jnp.exp(-v))


def causal_conv(ext, current, halo, weight, bias, offset):
    length = current.shape[0]
    ext[0:HALO, :] = halo
    ext[HALO : HALO + length, :] = current
    total = bias + weight[KERNEL - 1 : KERNEL, :] * current
    for back in range(1, KERNEL):
        shifted = jnp.where(offset >= back, ext[pl.ds(HALO - back, length), :], 0.0)
        total = total + weight[KERNEL - 1 - back : KERNEL - back, :] * shifted
    return total


def head_tiles(width):
    out = []
    for start in range(0, width, LANES):
        size = min(LANES, width - start)
        heads = [start // HEAD_DIM + i for i in range(size // HEAD_DIM)]
        out.append((start, size, heads))
    return out


def masked_heads(tile, heads):
    if len(heads) == 1:
        return tile
    lane = iota(tile.shape, 1) // HEAD_DIM
    return jnp.concatenate(
        [jnp.where(lane == i, tile, jnp.zeros_like(tile)) for i in range(len(heads))], axis=0
    )


def expander(width):
    return (iota((LANES, width), 1) // HEAD_DIM == iota((LANES, width), 0)).astype(BF16)


def chunk_common(x, xh, tail, tailh, offset, params, ext_x, ext_t, width):
    wx, bx, wt, bt, heads_p, pick = params
    length = x.shape[0]
    conv_x = causal_conv(ext_x, x.astype(F32), xh.astype(F32), wx, bx, offset)
    conv_t = causal_conv(
        ext_t,
        tail[:, : 2 * STATE].astype(F32),
        tailh[:, : 2 * STATE].astype(F32),
        wt,
        bt,
        offset,
    )
    raw = jnp.dot(tail[:, 2 * STATE :], pick, preferred_element_type=F32) + heads_p[0:1, :]
    step = softplus(raw)
    decay_rate = jnp.exp(heads_p[1:2, :])
    rate = -step * decay_rate
    tril = (iota((length, length), 0) >= iota((length, length), 1)).astype(BF16)
    cumul = ones_mm(tril, rate, 3)
    spread = expander(width)
    row = iota((length, 1), 0)
    entry = jnp.where(offset > row.astype(F32), jnp.exp(cumul), 0.0)
    last_off = offset[length - 1 : length, :]
    same_last = row.astype(F32) >= (length - 1) - last_off
    to_end = jnp.where(same_last, jnp.exp(cumul[length - 1 : length, :] - cumul), 0.0)
    step_x = mm_ones(step, spread, 2)
    entry_x = mm_ones(entry, spread, 2)
    end_x = mm_ones(to_end, spread, 2)
    return conv_x, conv_t, raw, step, rate, decay_rate, cumul, spread, step_x, entry_x, end_x


def forward_kernel(
    seq, fsdp,
    h_ref, w_ref, cot_ref, ow_ref, off_ref,
    wx_ref, bx_ref, wt_ref, bt_ref, hp_ref, pick_ref, skip_ref, gain_ref,
    proj_ref, y_ref, gated_ref, square_ref, state_ref, cot_out, ow_out,
    memory, ext_x, ext_t, last_rows, send, recv, near,
):
    seqs, _, length, width = y_ref.shape
    depth = h_ref.shape[3]
    step_at = pl.program_id(0)

    place = Place(seq, fsdp)
    links = Links(send, recv, near)
    cot = TokenGather(place, links, cot_ref, cot_out)
    w_rows = RowGather(place, links, ow_ref, ow_out)
    stages = len(place.low_bits)

    @pl.when(step_at == 0)
    def _():
        memory[...] = jnp.zeros_like(memory)
        last_rows[...] = jnp.zeros_like(last_rows)
        meet_pair(place)
        cot.begin()

    @pl.when(step_at == 1)
    def _():
        w_rows.begin()

    last = pl.num_programs(0) - 1
    for i in range(stages):

        @pl.when(step_at == min(2 + 2 * i, seq - 2))
        def _():
            cot.pass_on(i, "home")

    @pl.when(step_at == last - 3)
    def _():
        cot.arrive()

    @pl.when(step_at == last - 1)
    def _():
        cot.pass_on(0, "away")

    proj = jnp.dot(
        h_ref[...].reshape(seqs * length, depth), w_ref[...], preferred_element_type=F32
    ).astype(BF16)
    proj_ref[...] = proj.reshape(proj_ref.shape)
    params = tuple(r[...] for r in (wx_ref, bx_ref, wt_ref, bt_ref, hp_ref, pick_ref))
    for q in range(seqs):
        offset = off_ref[q, 0]
        chunk_rows = proj[q * length : (q + 1) * length]
        zx, tail = chunk_rows[:, : 2 * width], chunk_rows[:, 2 * width :]
        earlier = last_rows[q]
        conv_x, conv_t, _, _, _, _, cumul, _, step_x, entry_x, end_x = chunk_common(
            zx[:, width:], earlier[:, width : 2 * width], tail, earlier[:, 2 * width :], offset, params,
            ext_x.at[q], ext_t.at[q], width,
        )
        xs = conv_x * sigmoid(conv_x)
        act_t = conv_t * sigmoid(conv_t)
        bs = act_t[:, :STATE].astype(BF16)
        cs = act_t[:, STATE:].astype(BF16)
        scaled = xs * step_x
        scores = mm_tr(cs, bs)
        gap = iota((length, length), 0) - iota((length, length), 1)
        same = (gap >= 0) & (gap.astype(F32) <= offset)
        cumul_t = cumul.T
        old = memory[q]
        old_low = old.astype(BF16)
        state_ref[q, 0] = old_low
        outside = mm(cs, old_low) * entry_x + skip_ref[...] * xs
        squares = jnp.zeros((length, 1), F32)
        for start, size, heads in head_tiles(width):
            mixing = []
            for head in heads:
                spans = cumul[:, head : head + 1] - cumul_t[head : head + 1, :]
                decays = jnp.exp(jnp.where(same, spans, -1e30))
                mixing.append((decays * scores).astype(BF16))
            tile = masked_heads(scaled[:, start : start + size].astype(BF16), heads)
            mix = mixing[0] if len(heads) == 1 else jnp.concatenate(mixing, axis=1)
            inside = jnp.dot(mix, tile, preferred_element_type=F32)
            y_low = (inside + outside[:, start : start + size]).astype(BF16)
            y_ref[q, 0, :, start : start + size] = y_low
            z = zx[:, start : start + size].astype(F32)
            gated = y_low.astype(F32) * (z * sigmoid(z))
            gated_ref[q, 0, :, start : start + size] = (
                gated * gain_ref[:, start : start + size]
            ).astype(BF16)
            squares = squares + jnp.sum(gated * gated, axis=1, keepdims=True)
        square_ref[q, 0] = jnp.broadcast_to(squares, (length, LANES)).T[0:1, :]
        fresh = tr_mm(bs, scaled * end_x)
        memory[q] = old * entry_x[length - 1 : length, :] + fresh
        last_rows[q] = chunk_rows[length - HALO :]

    @pl.when(step_at == last - 1)
    def _():
        w_rows.forward()

    @pl.when(step_at == last)
    def _():
        for i in range(1, stages):
            cot.pass_on(i, "away")
        w_rows.finish()
        cot.finish()


def backward_kernel(
    seq, fsdp,
    zx_ref, zxh_ref, tail_ref, tailh_ref, off_ref, offr_ref, rem_ref, y_ref, grad_ref, stat_ref,
    state_ref, mixed_ref, pout_ref,
    wx_ref, bx_ref, wt_ref, bt_ref, hp_ref, pick_ref, skip_ref, gain_ref,
    out_ref, gx_ref, gt_ref, gh_ref, mixed_out, rows_out,
    memory, ext_x, ext_t, next_x, next_t,
    mix_own, mix_first, mix_later, pout_own, pout_first, send, recv, near,
):
    seqs, _, length, width = y_ref.shape
    step_at = pl.program_id(0)

    place = Place(seq, fsdp)
    links = Links(send, recv, near)
    mixed = TokenScatter(place, links, mixed_ref, mixed_out, mix_own, mix_first, mix_later)
    w_rows = RowScatter(place, links, pout_ref, rows_out, pout_own, pout_first)
    stages = len(place.low_bits)

    @pl.when(step_at == 0)
    def _():
        meet_pair(place)
        mixed.begin()
        w_rows.begin()

    @pl.when(step_at == 2)
    def _():
        mixed.add_cores()
        mixed.send_stage(0)

    @pl.when(step_at == 4)
    def _():
        w_rows.add_pairs()

    @pl.when(step_at == pl.num_programs(0) - 2)
    def _():
        mixed.add_stage(0)
        if stages > 1:
            mixed.send_stage(1)

    @pl.when(pl.program_id(0) == 0)
    def _():
        memory[...] = jnp.zeros_like(memory)
        gx_ref[...] = jnp.zeros_like(gx_ref)
        gt_ref[...] = jnp.zeros_like(gt_ref)
        gh_ref[...] = jnp.zeros_like(gh_ref)
        next_x[:, length:, :] = jnp.zeros_like(next_x[:, length:, :])
        next_t[:, length:, :] = jnp.zeros_like(next_t[:, length:, :])

    params = tuple(r[...] for r in (wx_ref, bx_ref, wt_ref, bt_ref, hp_ref, pick_ref))
    for q in range(seqs):
        offset = off_ref[q, 0]
        conv_x, conv_t, raw, step, rate, decay_rate, cumul, spread, step_x, entry_x, end_x = (
            chunk_common(
                zx_ref[q, 0, :, width:], zxh_ref[q, 0, :, width:], tail_ref[q, 0], tailh_ref[q, 0], offset,
                params, ext_x.at[q], ext_t.at[q], width,
            )
        )
        stats = jnp.broadcast_to(stat_ref[q, 0, 0:1, :], (LANES, length)).T
        slopes = jnp.broadcast_to(stat_ref[q, 0, 1:2, :], (LANES, length)).T
        scale, slope = stats[:, 0:1], slopes[:, 0:1]
        z = zx_ref[q, 0, :, :width].astype(F32)
        sig_z = sigmoid(z)
        silu_z = z * sig_z
        y = y_ref[q, 0].astype(F32)
        gated = y * silu_z
        scaled_grad = grad_ref[q, 0].astype(F32) * scale
        gx_ref[KERNEL + 2 : KERNEL + 3, :] += jnp.sum(scaled_grad * gated, axis=0, keepdims=True)
        grad_gated = gain_ref[...] * scaled_grad - gated * slope
        dy_low = (grad_gated * silu_z).astype(BF16)
        dz = (grad_gated * y * (sig_z + silu_z * (1.0 - sig_z))).astype(BF16)
        dy = dy_low.astype(F32)

        sig_x = sigmoid(conv_x)
        xs = conv_x * sig_x
        slope_x = sig_x + xs * (1.0 - sig_x)
        sig_t = sigmoid(conv_t)
        act_t = conv_t * sig_t
        slope_t = sig_t + act_t * (1.0 - sig_t)
        bs = act_t[:, :STATE].astype(BF16)
        cs = act_t[:, STATE:].astype(BF16)
        scaled = xs * step_x
        scaled_low = scaled.astype(BF16)
        scores = mm_tr(bs, cs)
        rows, cols = iota((length, length), 0), iota((length, length), 1)
        gap = cols - rows
        same = (gap >= 0) & (gap.astype(F32) <= offr_ref[q, 0])
        strict = gap > 0
        upper = (rows >= cols).astype(BF16)
        cumul_t = cumul.T
        old = state_ref[q, 0]
        grad_state = memory[q]
        state_low = grad_state.astype(BF16)
        grad_scores = jnp.zeros((length, length), F32)
        grad_scaled = []
        inside_rows = []
        for start, size, heads in head_tiles(width):
            dy_tile = masked_heads(dy_low[:, start : start + size], heads)
            grad_mix = mm_tr(scaled_low[:, start : start + size], dy_tile)
            mixing = []
            for place, head in enumerate(heads):
                spans = cumul_t[head : head + 1, :] - cumul[:, head : head + 1]
                decays = jnp.exp(jnp.where(same, spans, -1e30))
                weighted = grad_mix[:, place * length : (place + 1) * length] * decays
                grad_scores = grad_scores + weighted
                mixing.append((decays * scores).astype(BF16))
                terms = jnp.where(strict, weighted * scores, 0.0).astype(BF16)
                sums = jnp.dot(terms, upper, preferred_element_type=F32)
                inside_rows.append(
                    jnp.sum(jnp.where(strict, sums, 0.0), axis=0, keepdims=True)
                )
            mix = mixing[0] if len(heads) == 1 else jnp.concatenate(mixing, axis=1)
            grad_scaled.append(jnp.dot(mix, dy_tile, preferred_element_type=F32))
        inside_rows.append(jnp.zeros((LANES - len(inside_rows), length), F32))
        inside = jnp.concatenate(inside_rows, axis=0).T
        from_end = mm(bs, state_low) * end_x
        grad_scaled = jnp.concatenate(grad_scaled, axis=1) + from_end
        entry_dy = dy * entry_x
        entry_dy_low = entry_dy.astype(BF16)
        out_terms = mm(cs, old) * entry_dy
        end_terms = scaled * from_end
        grad_step = mm_ones_tr(xs * grad_scaled, spread, 2)
        out_terms = mm_ones_tr(out_terms, spread, 2)
        end_terms = mm_ones_tr(end_terms, spread, 2)
        keep_row = entry_x[length - 1 : length, :]
        carried = jnp.sum(grad_state * old.astype(F32), axis=0, keepdims=True) * keep_row
        carried = mm_ones_tr(jnp.broadcast_to(carried, (8, width)), spread, 2)[0:1, :]
        triu = (cols >= rows).astype(BF16)
        below = (rows > cols).astype(BF16)
        grad_rate = inside + ones_mm(triu, out_terms, 2) + ones_mm(below, end_terms, 2) + carried
        grad_step = grad_step - decay_rate * grad_rate
        grad_raw = grad_step * sigmoid(raw)
        grad_scores_low = grad_scores.astype(BF16)
        grad_b = mm(grad_scores_low, cs) + mm_tr(scaled * end_x, state_low)
        grad_c = tr_mm(grad_scores_low, bs) + mm_tr(entry_dy_low, old)
        memory[q] = grad_state * keep_row + tr_mm(cs, entry_dy_low)
        conv_grad_x = (skip_ref[...] * dy + step_x * grad_scaled) * slope_x
        conv_grad_t = jnp.concatenate([grad_b, grad_c], axis=1) * slope_t

        remain = rem_ref[q, 0]
        results = [dz]
        for grad, ext, nxt, weight, sums in (
            (conv_grad_x, ext_x.at[q], next_x.at[q], params[0], gx_ref),
            (conv_grad_t, ext_t.at[q], next_t.at[q], params[2], gt_ref),
        ):
            current = ext[pl.ds(HALO, length), :]
            sums[KERNEL : KERNEL + 1, :] += jnp.sum(grad, axis=0, keepdims=True)
            sums[KERNEL - 1 : KERNEL, :] += jnp.sum(grad * current, axis=0, keepdims=True)
            nxt[0:length, :] = grad
            total = weight[KERNEL - 1 : KERNEL, :] * grad
            for back in range(1, KERNEL):
                tap = KERNEL - 1 - back
                shifted = jnp.where(offset >= back, ext[pl.ds(HALO - back, length), :], 0.0)
                sums[tap : tap + 1, :] += jnp.sum(grad * shifted, axis=0, keepdims=True)
                ahead = jnp.where(remain >= back, nxt[pl.ds(back, length), :], 0.0)
                total = total + weight[tap : tap + 1, :] * ahead
            nxt[length:, :] = grad[0:HALO, :]
            results.append(total.astype(BF16))
        results.append(mm_tr(grad_raw, params[5]).astype(BF16))
        gx_ref[KERNEL + 1 : KERNEL + 2, :] += jnp.sum(dy * xs, axis=0, keepdims=True)
        gh_ref[0:1, :] += jnp.sum(grad_raw, axis=0, keepdims=True)
        gh_ref[1:2, :] += jnp.sum(grad_rate * rate, axis=0, keepdims=True)
        out_ref[q, 0, :, : 2 * width] = jnp.concatenate(results[:2], axis=1)
        out_ref[q, 0, :, 2 * width : 2 * width + 2 * STATE] = results[2]
        out_ref[q, 0, :, 2 * width + 2 * STATE :] = results[3]

    @pl.when(step_at == pl.num_programs(0) - 1)
    def _():
        for stage in range(1, stages):
            mixed.add_stage(stage)
            if stage + 1 < stages:
                mixed.send_stage(stage + 1)
        mixed.store()
        w_rows.finish()
        mixed.finish()


TAIL = 2 * STATE + LANES
AXES = ("seq", "fsdp")
MESH = pl.DeviceIdType.MESH


def whole_spec(shape):
    return pl.BlockSpec(shape, lambda i: (0,) * len(shape))


def chunk_specs(seqs, steps, length, reverse):
    def place(i):
        return steps - 1 - i if reverse else i

    def block(cols, column=0, rows=length):
        return pl.BlockSpec((seqs, 1, rows, cols), lambda i: (0, place(i), 0, column))

    def before(cols, column=0):
        return pl.BlockSpec(
            (seqs, 1, HALO, cols),
            lambda i: (0, jnp.maximum(place(i) - 1, 0), length // HALO - 1, column),
        )

    return block, before


def forward_mix(h_all, w_mine, cotangent, out_w, off_col, consts, seq, fsdp):
    seqs, steps, length, depth = h_all.shape
    cols = w_mine.shape[1]
    width = (cols - TAIL) // 2
    block, _ = chunk_specs(seqs, steps, length, False)
    shape = (seqs, steps, length, width)
    return pl.pallas_call(
        functools.partial(forward_kernel, seq, fsdp),
        grid=(steps,),
        in_specs=[
            block(depth),
            pl.BlockSpec(w_mine.shape, lambda i: (0, 0), pipeline_mode=pl.Buffered(1)),
            ANYWHERE, ANYWHERE, block(1),
        ]
        + [whole_spec(v.shape) for v in consts],
        out_specs=[
            block(cols), block(width), block(width), block(length, 0, 1), block(width, 0, STATE),
            ANYWHERE, ANYWHERE,
        ],
        out_shape=[
            jax.ShapeDtypeStruct((seqs, steps, length, cols), BF16),
            jax.ShapeDtypeStruct(shape, BF16),
            jax.ShapeDtypeStruct(shape, BF16),
            jax.ShapeDtypeStruct((seqs, steps, 1, length), F32),
            jax.ShapeDtypeStruct((seqs, steps, STATE, width), BF16),
            jax.ShapeDtypeStruct(h_all.shape, BF16),
            jax.ShapeDtypeStruct((fsdp // 2, 2) + out_w.shape, BF16),
        ],
        scratch_shapes=[
            pltpu.VMEM((seqs, STATE, width), F32),
            pltpu.VMEM((seqs, HALO + length, width), F32),
            pltpu.VMEM((seqs, HALO + length, 2 * STATE), F32),
            pltpu.VMEM((seqs, HALO, cols), BF16),
            pltpu.SemaphoreType.DMA((64,)),
            pltpu.SemaphoreType.DMA((64,)),
            pltpu.SemaphoreType.DMA((8,)),
        ],
        compiler_params=pltpu.CompilerParams(
            dimension_semantics=("arbitrary",), vmem_limit_bytes=48 << 20, collective_id=2,
            has_side_effects=True,
        ),
        cost_estimate=pl.CostEstimate(
            flops=steps * seqs * 900_000_000, transcendentals=0, bytes_accessed=10_000_000
        ),
        name="mix_forward",
    )(h_all, w_mine, cotangent, out_w, off_col, *consts)


def backward_mix(
    proj, off_col, off_row, rem_col, y, grad_yn, stats, states, mixed, part_out, consts, seq, fsdp
):
    seqs, steps, length, cols = proj.shape
    depth = mixed.shape[3]
    width = (cols - TAIL) // 2
    block, before = chunk_specs(seqs, steps, length, True)
    tail_at = 2 * width // TAIL
    half, pairs = seq // 2, fsdp // 2
    rows_out = part_out.shape[2]
    sums = [(8, width), (8, 2 * STATE), (8, LANES)]
    token_own = pltpu.VMEM((seqs, half, length, depth), BF16)
    return pl.pallas_call(
        functools.partial(backward_kernel, seq, fsdp),
        grid=(steps,),
        in_specs=[
            block(2 * width), before(2 * width), block(TAIL, tail_at), before(TAIL, tail_at),
            block(1), block(length, 0, 1), block(1), block(width), block(width),
            block(length, 0, 2), block(width, 0, STATE), ANYWHERE, ANYWHERE,
        ]
        + [whole_spec(v.shape) for v in consts],
        out_specs=[block(cols)] + [whole_spec(v) for v in sums] + [ANYWHERE, ANYWHERE],
        scratch_shapes=[
            pltpu.VMEM((seqs, STATE, width), F32),
            pltpu.VMEM((seqs, HALO + length, width), F32),
            pltpu.VMEM((seqs, HALO + length, 2 * STATE), F32),
            pltpu.VMEM((seqs, length + HALO, width), F32),
            pltpu.VMEM((seqs, length + HALO, 2 * STATE), F32),
            token_own, token_own, pltpu.VMEM((seqs, max(half - 1, 1), length, depth), BF16),
            pltpu.VMEM((2, rows_out, depth), BF16),
            pltpu.VMEM((max(pairs - 1, 1), 2, rows_out, depth), BF16),
            pltpu.SemaphoreType.DMA((64,)),
            pltpu.SemaphoreType.DMA((64,)),
            pltpu.SemaphoreType.DMA((16,)),
        ],
        out_shape=[jax.ShapeDtypeStruct(proj.shape, BF16)]
        + [jax.ShapeDtypeStruct(v, F32) for v in sums]
        + [
            jax.ShapeDtypeStruct((seqs, length, depth), BF16),
            jax.ShapeDtypeStruct((2, rows_out, depth), BF16),
        ],
        compiler_params=pltpu.CompilerParams(
            dimension_semantics=("arbitrary",), vmem_limit_bytes=56 << 20, collective_id=3,
            has_side_effects=True,
        ),
        cost_estimate=pl.CostEstimate(
            flops=steps * seqs * 2_000_000_000, transcendentals=0, bytes_accessed=16_000_000
        ),
        name="mix_backward",
    )(
        proj, proj, proj, proj, off_col, off_row, rem_col, y, grad_yn, stats, states, mixed,
        part_out, *consts,
    )


class Place:
    def __init__(self, seq, fsdp):
        self.seq, self.fsdp = seq, fsdp
        self.half, self.pairs = seq // 2, fsdp // 2
        s, f = lax.axis_index("seq"), lax.axis_index("fsdp")
        self.s, self.f = s, f
        self.top, self.low = s // self.half, lax.rem(s, self.half)
        self.core, self.pair = lax.rem(f, 2), f // 2
        self.home = self.core == self.top
        self.away = self.core != self.top
        self.chunk = self.low + self.half * self.core
        self.low_bits = [1 << i for i in range(self.half.bit_length() - 1)]

    def at(self, top=0, low=0, pair=0, core=0):
        return (
            flip(self.top, top) * self.half + flip(self.low, low),
            flip(self.pair, pair) * 2 + flip(self.core, core),
        )

    def bits_for(self, q):
        return self.low_bits if q % 2 == 0 else self.low_bits[::-1]


def flip(index, bits):
    for i in range(bits.bit_length()):
        if bits >> i & 1:
            bit = lax.rem(index // (1 << i), 2)
            index = index + (1 << i) * (1 - 2 * bit)
    return index


class Copy:
    def __init__(self, make):
        self.make = make

    def start(self):
        self.make().start()
        return self

    def wait(self):
        self.make().wait()

    def wait_send(self):
        self.make().wait_send()

    def wait_recv(self):
        self.make().wait_recv()


class Links:
    def __init__(self, send, recv, near):
        self.send, self.recv, self.near = send, recv, near
        self.far_count = self.near_count = 0

    def far(self, make):
        i = self.far_count
        self.far_count += 1

        def build():
            src, dst, device = make()
            return pltpu.make_async_remote_copy(
                src_ref=src, dst_ref=dst, send_sem=self.send.at[i], recv_sem=self.recv.at[i],
                device_id=device, device_id_type=MESH,
            )

        return Copy(build)

    def local(self, make):
        i = self.near_count
        self.near_count += 1
        return Copy(lambda: pltpu.make_async_copy(*make(), self.near.at[i]))


def meet(devices):
    barrier = pltpu.get_barrier_semaphore()
    for device in devices:
        pl.semaphore_signal(barrier, inc=1, device_id=device, device_id_type=MESH)
    pl.semaphore_wait(barrier, len(devices))


def meet_pair(place):
    meet(
        [place.at(top=t, low=l, core=c) for t, l, c in peers_of(place)]
        + [place.at(pair=p) for p in range(1, place.pairs)]
    )


def peers_of(place):
    out = []
    for top in (0, 1):
        for low in range(place.half):
            for core in (0, 1):
                if (top, low, core) != (0, 0, 0):
                    out.append((top, low, core))
    return out


class TokenGather:
    def __init__(self, place, links, src, dst):
        self.place, self.src, self.dst = place, src, dst
        seqs = src.shape[0]

        def over(q):
            return links.far(
                lambda: (src.at[q], dst.at[q, place.s], place.at(top=1, core=1))
            )

        self.cross = [over(q) for q in range(seqs)]
        self.stay = links.local(lambda: (src, dst.at[:, place.s]))
        self.share = [[] for _ in range(seqs)]
        self.stages = []
        held = [[0] for _ in range(seqs)]
        for q in range(seqs):
            self.share[q].append([self.copy(links, q, low, core=1) for low in held[q]])
        for i in range(len(place.low_bits)):
            stage = []
            for q in range(seqs):
                bit = place.bits_for(q)[i]
                stage.append([self.copy(links, q, low, low_bit=bit) for low in held[q]])
                fresh = [low ^ bit for low in held[q]]
                held[q] = held[q] + fresh
                self.share[q].append([self.copy(links, q, low, core=1) for low in fresh])
            self.stages.append(stage)

    def copy(self, links, q, low, low_bit=0, core=0):
        def make():
            place = self.place
            ref = self.dst.at[q, flip(place.low, low) + place.half * place.core]
            return ref, ref, place.at(low=low_bit, core=core)

        return links.far(make)

    def begin(self):
        @pl.when(self.place.away)
        def _():
            for copy in self.cross:
                copy.start()

        @pl.when(self.place.home)
        def _():
            self.stay.start()
            self.stay.wait()
            self.send_stage(0)

    def arrive(self):
        @pl.when(self.place.away)
        def _():
            for copy in self.cross:
                copy.wait_recv()
            self.send_stage(0)

    def send_stage(self, i):
        for q in range(len(self.share)):
            for copy in self.stages[i][q] + self.share[q][i]:
                copy.start()

    def pass_on(self, i, role):
        @pl.when(self.place.home if role == "home" else self.place.away)
        def _():
            for q in range(len(self.share)):
                for copy in self.stages[i][q]:
                    copy.wait_recv()
                for copy in (self.stages[i + 1][q] if i + 1 < len(self.stages) else []):
                    copy.start()
                for copy in self.share[q][i + 1]:
                    copy.start()

    def finish(self):
        for share in self.share:
            for copies in share:
                for copy in copies:
                    copy.wait()
        for stage in self.stages:
            for copies in stage:
                for copy in copies:
                    copy.wait_send()

        @pl.when(self.place.away)
        def _():
            for copy in self.cross:
                copy.wait_send()


class RowGather:
    def __init__(self, place, links, src, dst):
        self.place = place
        pairs = range(1, place.pairs)

        def slot():
            return dst.at[place.pair, place.core]

        self.stay = links.local(lambda: (src, slot()))
        self.to_home = links.far(lambda: (src, slot(), place.at(core=1)))
        self.to_near = links.far(lambda: (src, slot(), place.at(top=1)))
        self.to_far = links.far(lambda: (src, slot(), place.at(top=1, core=1)))

        def forward(c, p):
            return links.far(
                lambda: (dst.at[place.pair, c], dst.at[place.pair, c], place.at(pair=p))
            )

        self.forwards = [forward(c, p) for c in (0, 1) for p in pairs]

    def begin(self):
        @pl.when(self.place.home)
        def _():
            self.stay.start()
            self.to_near.start()

        @pl.when(self.place.away)
        def _():
            self.to_home.start()
            self.to_far.start()

    def forward(self):
        @pl.when(self.place.home)
        def _():
            self.stay.wait()
            self.to_home.wait_recv()

        @pl.when(self.place.away)
        def _():
            self.to_near.wait_recv()
            self.to_far.wait_recv()

        for copy in self.forwards:
            copy.start()

    def finish(self):
        for copy in self.forwards:
            copy.wait()

        @pl.when(self.place.home)
        def _():
            self.to_near.wait_send()

        @pl.when(self.place.away)
        def _():
            self.to_home.wait_send()
            self.to_far.wait_send()


def entry_kernel(
    seq, fsdp, h_ref, zx_ref, tail_ref, seg_ref, h_out, w_out, seg_out, send, recv, near
):
    place = Place(seq, fsdp)
    links = Links(send, recv, near)
    cols = zx_ref.shape[2]
    peers = peers_of(place)
    others = range(1, place.pairs)
    tokens = TokenGather(place, links, h_ref, h_out)

    def block(t=0, l=0, c=0):
        s, f = place.at(top=t, low=l, core=c)
        return w_out.at[s, place.pair, lax.rem(f, 2)]

    def columns(ref):
        return ref.at[:, pl.ds(0, cols)]

    def tail_of(ref):
        return ref.at[:, pl.ds(cols, TAIL)]

    def send_zx(t, l, c):
        group = flip(place.core, c) * place.half + flip(place.low, l)
        return zx_ref.at[group], columns(block()), place.at(top=t, low=l, core=c)

    zx = {p: links.far(functools.partial(send_zx, *p)) for p in peers}
    own = [
        links.local(lambda: (zx_ref.at[place.chunk], columns(block()))),
        links.local(lambda: (tail_ref, tail_of(block()))),
    ]
    tail_cross = links.far(lambda: (tail_ref, tail_of(block()), place.at(top=1)))
    near_peers = [(l, c) for t, l, c in peers if t == 0]

    def send_tail(l, c):
        return tail_ref, tail_of(block()), place.at(low=l, core=c)

    def send_other(l, c):
        return tail_of(block(1)), tail_of(block(1)), place.at(low=l, core=c)

    tails = {p: links.far(functools.partial(send_tail, *p)) for p in near_peers}
    tails_more = {p: links.far(functools.partial(send_other, *p)) for p in near_peers}
    swap_segments = links.far(lambda: (seg_ref, seg_out, place.at(core=1)))

    def send_on(t, l, c, p):
        return block(t, l, c), block(t, l, c), place.at(pair=p)

    forwards = {
        p: [links.far(functools.partial(send_on, *p, other)) for other in others]
        for p in [(0, 0, 0)] + peers
    }

    meet_pair(place)
    stages = len(place.low_bits)
    far_peers = [p for p in peers if p[0] == 1]
    tokens.begin()
    tail_cross.start()
    for copy in own:
        copy.start()
    for p in near_peers:
        zx[0, *p].start()
        tails[p].start()
    swap_segments.start()
    for copy in own:
        copy.wait()
    for copy in forwards[0, 0, 0]:
        copy.start()
    tail_cross.wait_recv()
    for p in near_peers:
        tails_more[p].start()
    tokens.pass_on(0, "home")
    for p in near_peers:
        zx[0, *p].wait_recv()
        tails[p].wait_recv()
        for copy in forwards[0, *p]:
            copy.start()
    for p in far_peers:
        zx[p].start()
    for i in range(1, stages):
        tokens.pass_on(i, "home")

    tokens.arrive()
    for p in near_peers:
        tails_more[p].wait_recv()
    for i in range(stages):
        tokens.pass_on(i, "away")
        at, to = (len(far_peers) * k // stages for k in (i, i + 1))
        for p in far_peers[at:to]:
            zx[p].wait_recv()
            for copy in forwards[p]:
                copy.start()

    tokens.finish()
    for p in forwards:
        for copy in forwards[p]:
            copy.wait()
    tail_cross.wait_send()
    for group in (zx, tails, tails_more):
        for copy in group.values():
            copy.wait_send()
    swap_segments.wait()


ANYWHERE = pl.BlockSpec(memory_space=pl.ANY)


def entry_gather(seq, fsdp, normed, zx, tail, segments):
    seqs, length, depth = normed.shape
    rows = tail.shape[0]
    return pl.pallas_call(
        functools.partial(entry_kernel, seq, fsdp),
        in_specs=[ANYWHERE] * 4,
        out_specs=[ANYWHERE] * 3,
        out_shape=[
            jax.ShapeDtypeStruct((seqs, seq, length, depth), BF16),
            jax.ShapeDtypeStruct((seq, fsdp // 2, 2, rows, zx.shape[2] + TAIL), BF16),
            jax.ShapeDtypeStruct(segments.shape, segments.dtype),
        ],
        scratch_shapes=[
            pltpu.SemaphoreType.DMA((256,)),
            pltpu.SemaphoreType.DMA((256,)),
            pltpu.SemaphoreType.DMA((8,)),
        ],
        compiler_params=pltpu.CompilerParams(collective_id=0, has_side_effects=True),
        cost_estimate=pl.CostEstimate(
            flops=0, transcendentals=0, bytes_accessed=200_000_000
        ),
        name="entry_gather",
    )(normed, zx, tail, segments)


def add_rows(out, left, right, rows=32):
    total = left.shape[0]
    step = next((size for size in (rows, 16) if total % size == 0), total)

    if step == total:
        out[...] = (left[...].astype(F32) + right[...].astype(F32)).astype(out.dtype)
        return

    @pl.loop(0, total // step)
    def _(i):
        at = pl.ds(pl.multiple_of(i * step, step), step)
        out[at] = (left[at].astype(F32) + right[at].astype(F32)).astype(out.dtype)


class TokenScatter:
    def __init__(self, place, links, src, out, own, first, later, loads=True):
        self.place = place
        self.out, self.own, self.first, self.later = out, own, first, later
        self.seqs = src.shape[0]
        half = place.half

        def give(q):
            def make():
                part = src.at[q, pl.ds(half * (1 - place.core), half)] if loads else src.at[q]
                return part, first.at[q], place.at(core=1)

            return links.far(make)

        def keep(q):
            return links.local(
                lambda: (src.at[q, pl.ds(half * place.core, half)], own.at[q])
            )

        self.cores = [give(q) for q in range(self.seqs)]
        self.loads = [keep(q) for q in range(self.seqs)] if loads else []
        self.stages = [[] for _ in place.low_bits]
        for q in range(self.seqs):
            live, slot = list(range(half)), 0
            for i, bit in enumerate(place.bits_for(q)[::-1]):
                for low in [low for low in live if low & bit]:
                    self.stages[i].append((self.copy(links, q, low, slot, bit), q, low ^ bit, slot))
                    slot += 1
                live = [low for low in live if not low & bit]
        self.stay = links.local(lambda: (own.at[:, place.low], out))

    def copy(self, links, q, low, slot, bit):
        return links.far(
            lambda: (
                self.own.at[q, flip(self.place.low, low)], self.later.at[q, slot],
                self.place.at(low=bit),
            )
        )

    def begin(self):
        for copy in self.cores + self.loads:
            copy.start()

    def add_cores(self):
        for q in range(self.seqs):
            if self.loads:
                self.loads[q].wait()
            self.cores[q].wait_recv()
            for low in range(self.place.half):
                add_rows(self.own.at[q, low], self.own.at[q, low], self.first.at[q, low])

    def send_stage(self, i):
        for copy, _, _, _ in self.stages[i]:
            copy.start()

    def add_stage(self, i):
        for copy, q, low, slot in self.stages[i]:
            copy.wait_recv()
            ref = self.own.at[q, flip(self.place.low, low)]
            add_rows(ref, ref, self.later.at[q, slot])

    def store(self):
        self.stay.start()
        self.stay.wait()

    def finish(self):
        for copy in self.cores:
            copy.wait_send()
        for stage in self.stages:
            for copy, _, _, _ in stage:
                copy.wait_send()


class RowScatter:
    def __init__(self, place, links, src, out, own, first):
        self.place, self.own, self.first = place, own, first

        def over(p):
            return links.far(
                lambda: (src.at[flip(place.pair, p)], first.at[p - 1], place.at(pair=p))
            )

        def far(c):
            return links.far(
                lambda: (own.at[flip(place.core, c)], out.at[1], place.at(top=1, core=c))
            )

        self.over = [over(p) for p in range(1, place.pairs)]
        self.load = links.local(lambda: (src.at[place.pair], own))
        self.far = [far(0), far(1)]
        self.near = links.far(lambda: (own.at[1 - place.core], out.at[0], place.at(core=1)))
        self.stay = links.local(lambda: (own.at[place.core], out.at[0]))

    def begin(self):
        self.load.start()
        for copy in self.over:
            copy.start()

    def add_pairs(self):
        self.load.wait()
        for i, copy in enumerate(self.over):
            copy.wait_recv()
            for c in (0, 1):
                add_rows(self.own.at[c], self.own.at[c], self.first.at[i, c])

        @pl.when(self.place.away)
        def _():
            for copy in self.far:
                copy.start()

        @pl.when(self.place.home)
        def _():
            self.near.start()
            self.stay.start()

    def finish(self):
        for copy in self.over:
            copy.wait_send()

        @pl.when(self.place.home)
        def _():
            self.stay.wait()
            self.near.wait_send()
            self.far[0].wait_recv()

        @pl.when(self.place.away)
        def _():
            self.near.wait_recv()
            self.far[1].wait_recv()
            for copy in self.far:
                copy.wait_send()


class Deliver:
    def __init__(self, place, links, src, out):
        self.place = place
        self.cross = links.far(lambda: (src(), out, place.at(top=1, core=1)))
        self.stay = links.local(lambda: (src(), out))

    def begin(self):
        @pl.when(self.place.away)
        def _():
            self.cross.start()

        @pl.when(self.place.home)
        def _():
            self.stay.start()

    def finish(self):
        @pl.when(self.place.away)
        def _():
            self.cross.wait()

        @pl.when(self.place.home)
        def _():
            self.stay.wait()


TILE = 384
ROWS = 256


def exit_kernel(
    seq, fsdp,
    h_ref, grad_ref, w_ref, mixed_ref, vec_ref,
    dh_out, mixed_out, slots_out, vec_out,
    h_all, grads, weights, part,
    dh_give, dh_own, dh_first, dh_later, part_first, part_top, vec_val, vec_got,
    send, recv, near,
):
    place = Place(seq, fsdp)
    links = Links(send, recv, near)
    half = place.half
    others = list(range(1, place.pairs))
    seqs, _, length, depth = dh_own.shape
    rows = part.shape[3]
    dh = TokenScatter(
        place, links, dh_give, dh_out, dh_own, dh_first, dh_later, loads=False
    )
    dh_last = Deliver(place, links, lambda: dh_own.at[:, place.low], dh_out)
    mixed = Deliver(place, links, lambda: mixed_ref, mixed_out)
    loads = [
        links.local(lambda: (h_ref, h_all)),
        links.local(lambda: (grad_ref, grads)),
        links.local(lambda: (w_ref, weights)),
    ]

    def rows_of(top):
        return pl.ds(half * flip(place.top, top), half)

    def over(top, p):
        return links.far(
            lambda: (
                part.at[rows_of(top), flip(place.pair, p)],
                part_first.at[p - 1, rows_of(top)],
                place.at(pair=p),
            )
        )

    over_pairs = [[over(top, p) for p in others] for top in (0, 1)]
    cross = links.far(lambda: (part.at[rows_of(1), place.pair], part_top, place.at(top=1)))

    def row_block(l, c):
        return part.at[
            half * place.top + flip(place.low, l), place.pair, flip(place.core, c)
        ]

    def spread(l, c):
        return links.far(
            lambda: (
                row_block(l, c), slots_out.at[place.core, place.low], place.at(low=l, core=c)
            )
        )

    near_peers = [(l, c) for t, l, c in peers_of(place) if t == 0]
    slots = {p: spread(*p) for p in near_peers}
    slots[0, 0] = links.local(lambda: (row_block(0, 0), slots_out.at[place.core, place.low]))

    hops = [dict(pair=1 << i) for i in range(place.pairs.bit_length() - 1)]
    hops += [dict(top=1)] + [dict(low=b) for b in place.low_bits] + [dict(core=1)]

    def hop(i):
        return links.far(lambda: (vec_val.at[i], vec_got.at[i], place.at(**hops[i])))

    vec = [hop(i) for i in range(len(hops))]
    vec_load = links.local(lambda: (vec_ref, vec_val.at[0]))
    vec_store = links.local(lambda: (vec_val.at[len(hops)], vec_out))
    state = {"at": 0}

    def vec_next():
        i = state["at"]
        state["at"] += 1
        if i < len(hops):
            vec[i].wait_recv()
            vec_val[i + 1] = vec_val[i] + vec_got[i]
            if i + 1 < len(hops):
                vec[i + 1].start()
            else:
                vec_store.start()

    def add_pairs(top):
        for i, copy in enumerate(over_pairs[top]):
            copy.wait_recv()
            for low in range(half):
                for c in (0, 1):
                    at = half * flip(place.top, top) + low
                    ref = part.at[at, place.pair, c]
                    add_rows(ref, ref, part_first.at[i, at, c], 16)

    tiles = depth // 2 // TILE
    blocks = TILE // rows
    per_seq = fsdp

    def weight_rows(top):
        @pl.loop(0, tiles)
        def _(k):
            t = tiles * flip(place.top, top) + k
            lanes = pl.ds(pl.multiple_of(t * TILE, LANES), TILE)
            term = tr_mm(h_all[:, lanes], grads[...])
            for b in range(blocks):
                at = t * (blocks // per_seq) + b // per_seq if blocks >= per_seq else None
                part[at, b % per_seq // 2, b % 2] = term[b * rows : (b + 1) * rows].astype(BF16)
            sums = jnp.sum(term * weights[lanes, :].astype(F32), axis=1, keepdims=True)
            wide = jnp.broadcast_to(sums, (TILE, LANES))
            for i in range(TILE // LANES):
                vec_val[0, pl.ds(t * (TILE // LANES) + i, 1), :] = (
                    wide[i * LANES : (i + 1) * LANES].T[0:1, :]
                )

    def token_rows(out, side):
        per_chunk = ROWS // length
        count = half // per_chunk
        for q in range(seqs):

            @pl.loop(0, count)
            def _(k):
                at = (q * seq + half * side + k * per_chunk) * length
                term = mm_tr(grads[pl.ds(pl.multiple_of(at, LANES), ROWS), :], weights[...])
                out[q, pl.ds(k * per_chunk, per_chunk)] = term.astype(BF16).reshape(
                    per_chunk, length, depth
                )

    for copy in loads:
        copy.start()
    vec_load.start()
    meet_pair(place)
    mixed.begin()
    for copy in loads:
        copy.wait()
    vec_load.wait()
    weight_rows(1)
    for copy in over_pairs[1]:
        copy.start()
    token_rows(dh_give, 1 - place.core)
    dh.begin()
    weight_rows(0)
    for copy in over_pairs[0]:
        copy.start()
    vec[0].start()
    token_rows(dh_own, place.core)
    dh.add_cores()
    dh.send_stage(0)
    add_pairs(1)
    cross.start()
    vec_next()
    stages = len(place.low_bits)
    for i in range(stages):
        dh.add_stage(i)
        if i + 1 < stages:
            dh.send_stage(i + 1)
        else:
            dh_last.begin()
        vec_next()
    add_pairs(0)
    vec_next()
    cross.wait_recv()
    for l, c in near_peers + [(0, 0)]:
        ref = row_block(l, c)
        add_rows(ref, ref, part_top.at[flip(place.low, l), flip(place.core, c)], 16)
        slots[l, c].start()
    while state["at"] < len(hops):
        vec_next()
    for copy in slots.values():
        copy.wait()
    vec_store.wait()
    mixed.finish()
    dh_last.finish()
    dh.finish()
    cross.wait_send()
    for copy in over_pairs[0] + over_pairs[1] + vec:
        copy.wait_send()


def exit_scatter(seq, fsdp, h_all, grad_proj, w_mine, mixed, vector):
    seqs, _, length, depth = h_all.shape
    half, pairs = seq // 2, fsdp // 2
    cols = w_mine.shape[1]
    rows = depth // (seq * fsdp)
    count = seqs * seq * length
    bits = (half.bit_length() - 1) + (pairs.bit_length() - 1) + 2
    token_own = pltpu.VMEM((seqs, half, length, depth), BF16)
    tokens = jax.ShapeDtypeStruct((seqs, length, depth), BF16)
    return pl.pallas_call(
        functools.partial(exit_kernel, seq, fsdp),
        in_specs=[ANYWHERE] * 5,
        out_specs=[ANYWHERE] * 4,
        out_shape=[
            tokens,
            tokens,
            jax.ShapeDtypeStruct((2, half, rows, cols), BF16),
            jax.ShapeDtypeStruct(vector.shape, F32),
        ],
        scratch_shapes=[
            pltpu.VMEM((count, depth), BF16),
            pltpu.VMEM((count, cols), BF16),
            pltpu.VMEM((depth, cols), BF16),
            pltpu.VMEM((seq, pairs, 2, rows, cols), BF16),
            token_own, token_own, token_own,
            pltpu.VMEM((seqs, max(half - 1, 1), length, depth), BF16),
            pltpu.VMEM((max(pairs - 1, 1), seq, 2, rows, cols), BF16),
            pltpu.VMEM((half, 2, rows, cols), BF16),
            pltpu.VMEM((bits + 1,) + vector.shape, F32),
            pltpu.VMEM((bits,) + vector.shape, F32),
            pltpu.SemaphoreType.DMA((96,)),
            pltpu.SemaphoreType.DMA((96,)),
            pltpu.SemaphoreType.DMA((16,)),
        ],
        compiler_params=pltpu.CompilerParams(
            collective_id=1, has_side_effects=True, vmem_limit_bytes=60 << 20
        ),
        cost_estimate=pl.CostEstimate(
            flops=0, transcendentals=0, bytes_accessed=200_000_000
        ),
        name="exit_scatter",
    )(h_all.reshape(count, depth), grad_proj.reshape(count, cols), w_mine, mixed, vector)


def finish_kernel(
    tok_ref, cot_ref, gain_ref, dh_ref, mixed_ref, slots_ref, rows_ref,
    mixed_out, tokens_out, w_in_out, w_out_out,
):
    gain = gain_ref[...]
    for q in range(tok_ref.shape[0]):
        wide = tok_ref[q].astype(F32)
        mixed_out[q] = (wide + mixed_ref[q].astype(F32)).astype(BF16)
        scale = lax.rsqrt(jnp.mean(wide * wide, axis=-1, keepdims=True) + EPSILON)
        unit = wide * scale
        scaled = dh_ref[q].astype(F32) * gain
        tokens_out[q] = cot_ref[q].astype(F32) + scale * (
            scaled - unit * jnp.mean(scaled * unit, axis=-1, keepdims=True)
        )
    groups, _, cols = slots_ref.shape
    width = (cols - TAIL) // 2
    tail = jnp.zeros((slots_ref.shape[1], TAIL), F32)
    for g in range(groups):
        w_in_out[:, g * width : (g + 1) * width] = slots_ref[g, :, :width].astype(F32)
        w_in_out[:, INNER + g * width : INNER + (g + 1) * width] = (
            slots_ref[g, :, width : 2 * width].astype(F32)
        )
        tail = tail + slots_ref[g, :, 2 * width :].astype(F32)
    w_in_out[:, 2 * INNER :] = tail[:, : 2 * STATE + HEADS]
    w_out_out[...] = rows_ref[0].astype(F32) + rows_ref[1].astype(F32)


def finish(tokens, cotangent, gain_in, grad_h, mixed, slots, rows, shapes):
    return pl.pallas_call(
        finish_kernel,
        out_shape=[
            jax.ShapeDtypeStruct(tokens.shape, BF16),
            jax.ShapeDtypeStruct(tokens.shape, F32),
            jax.ShapeDtypeStruct(shapes[0], F32),
            jax.ShapeDtypeStruct(shapes[1], F32),
        ],
        compiler_params=pltpu.CompilerParams(vmem_limit_bytes=32 << 20),
        name="finish",
    )(tokens, cotangent, gain_in[None], grad_h, mixed, slots, rows)


def local(
    tokens, segments, gain_in, w_in, conv_w, conv_b, dt_bias, a_log, skip, gain_out, w_out,
    cotangent,
):
    steps, shards = lax.axis_size("seq"), lax.axis_size("fsdp")
    place = Place(steps, shards)
    seqs, length, _ = tokens.shape
    width = INNER // steps
    heads = HEADS // steps
    rows_in = w_in.shape[0]
    number = place.chunk

    def mine(array, size):
        return lax.dynamic_slice_in_dim(array, number * size, size, array.ndim - 1)

    wide = tokens.astype(F32)
    scale_in = lax.rsqrt(jnp.mean(wide * wide, axis=-1, keepdims=True) + EPSILON)
    normed = (wide * scale_in * gain_in).astype(BF16)
    zx = w_in[:, : 2 * INNER].reshape(rows_in, 2, steps, width).transpose(2, 0, 1, 3)
    zx = zx.reshape(steps, rows_in, 2 * width)
    tail = jnp.pad(w_in[:, 2 * INNER :], ((0, 0), (0, LANES - HEADS)))
    h_all, w_mine, segs = entry_gather(steps, shards, normed, zx, tail, segments)
    w_mine = w_mine.reshape(D, 2 * width + TAIL)
    segs = jnp.where(place.home, segments, segs)

    total = steps * length
    index = lax.broadcasted_iota(jnp.int32, (seqs, total), 1)
    starts = jnp.concatenate([jnp.ones((seqs, 1), bool), segs[:, 1:] != segs[:, :-1]], axis=1)
    first = lax.cummax(jnp.where(starts, index, 0), axis=1)
    ends = jnp.concatenate([starts[:, 1:], jnp.ones((seqs, 1), bool)], axis=1)
    last = lax.cummin(jnp.where(ends, index, total), axis=1, reverse=True)
    off = (index - first).astype(F32).reshape(seqs, steps, length)
    rem = (last - index).astype(F32).reshape(seqs, steps, length)
    off_col, off_row, rem_col = off[..., None], off[:, :, None, :], rem[..., None]

    heads_p = jnp.stack([mine(dt_bias, heads), mine(a_log, heads)])
    lane = lax.broadcasted_iota(jnp.int32, (LANES, LANES), 1)
    source = lax.broadcasted_iota(jnp.int32, (LANES, LANES), 0)
    pick = ((lane < heads) & (source == lane + number * heads)).astype(BF16)
    consts = (
        mine(conv_w[:, :INNER], width),
        mine(conv_b[None, :INNER], width),
        conv_w[:, INNER:],
        conv_b[None, INNER:],
        jnp.pad(heads_p, ((0, 6), (0, LANES - heads))),
        pick,
        jnp.repeat(mine(skip, heads), HEAD_DIM)[None],
        mine(gain_out[None], width),
    )

    def dot(a, b):
        return lax.dot_general(a, b, (((3,), (0,)), ((), ())), preferred_element_type=F32)

    def dot_tr(a, b):
        return lax.dot_general(a, b, (((3,), (1,)), ((), ())), preferred_element_type=F32)

    def dot_tokens(a, b):
        dims = (0, 1, 2)
        return lax.dot_general(a, b, ((dims, dims), ((), ())), preferred_element_type=F32)

    proj, y, gated, squares, states, cot_all, out_w = forward_mix(
        h_all, w_mine, cotangent, w_out, off_col, consts, steps, shards
    )
    out_w = out_w.reshape(width, D)

    grad_yn = dot_tr(cot_all, out_w)
    sums = jnp.stack(
        [squares[:, :, 0], jnp.sum(grad_yn * gated.astype(F32), axis=-1)], axis=2
    )
    for offsets in [dict(core=1)] + [dict(low=b) for b in place.low_bits]:
        sums = sums + exchange(sums, steps, shards, **offsets)
    scale = lax.rsqrt(sums[:, :, 0] / INNER + EPSILON)
    stats = jnp.stack([scale, sums[:, :, 1] * (scale * scale * scale / INNER)], axis=2)
    scale = scale[..., None]
    mixed = (dot(gated, out_w) * scale).astype(BF16)
    y_normed = (gated.astype(F32) * scale).astype(BF16)
    part_out = dot_tokens(y_normed, cot_all).astype(BF16)

    part_out = part_out.reshape((shards // 2, 2) + w_out.shape)
    grad_proj, sums_x, sums_t, sums_h, mixed, rows = backward_mix(
        proj, off_col, off_row, rem_col, y, grad_yn, stats, states, mixed, part_out, consts,
        steps, shards,
    )

    grouped = jnp.concatenate(
        [
            sums_x[: KERNEL + 1].reshape(-1),
            sums_x[KERNEL + 2],
            jnp.sum(sums_x[KERNEL + 1].reshape(heads, HEAD_DIM), axis=-1),
            sums_h[:2, :heads].reshape(-1),
        ]
    )
    size = -(-grouped.shape[0] // LANES) * LANES
    grouped = jnp.pad(grouped, (0, size - grouped.shape[0])).reshape(1, -1, LANES)
    grouped = lax.dynamic_update_slice_in_dim(
        jnp.zeros((steps,) + grouped.shape[1:], F32), grouped, number, 0
    )
    vector = jnp.concatenate(
        [
            jnp.zeros((D // LANES, LANES), F32),
            sums_t[: KERNEL + 1].reshape(-1, LANES),
            grouped.reshape(-1, LANES),
        ]
    )
    grad_h, mixed, slots, vector = exit_scatter(
        steps, shards, h_all, grad_proj, w_mine, mixed, vector
    )
    mixed, tokens_grad, w_in_grad, w_out_grad = finish(
        tokens, cotangent, gain_in, grad_h, mixed,
        slots.reshape(steps, rows_in, 2 * width + TAIL), rows, (w_in.shape, w_out.shape),
    )

    edge = vector.shape[0] - steps * size // LANES
    everywhere = vector[:edge].reshape(-1)
    grouped = vector[edge:].reshape(steps, size)
    gain_in_grad = everywhere[:D] / gain_in
    conv_x = grouped[:, : (KERNEL + 1) * width].reshape(steps, KERNEL + 1, width)
    conv_x = conv_x.transpose(1, 0, 2).reshape(KERNEL + 1, INNER)
    conv_grads = jnp.concatenate([conv_x, everywhere[D:].reshape(KERNEL + 1, -1)], axis=1)
    rest = grouped[:, (KERNEL + 1) * width :]
    gain_out_grad = rest[:, :width].reshape(-1)
    per_head = rest[:, width : width + 3 * heads].reshape(steps, 3, heads)
    per_head = per_head.transpose(1, 0, 2).reshape(3, HEADS)
    return (
        mixed, tokens_grad, gain_in_grad, w_in_grad, conv_grads[:KERNEL], conv_grads[KERNEL],
        per_head[1], per_head[2], per_head[0], gain_out_grad, w_out_grad,
    )


def exchange(value, seq, fsdp, low=0, core=0):
    perm = [
        (s * fsdp + f, (s ^ low) * fsdp + (f ^ core)) for s in range(seq) for f in range(fsdp)
    ]
    return lax.ppermute(value, AXES, perm)


def solution(mesh):
    by_token = P("fsdp", "seq", None)
    by_row = P(("seq", "fsdp"), None)
    placed = (
        by_token, P("fsdp", None), P(), by_row, P(), P(), P(), P(), P(), P(), by_row, by_token,
    )
    return jax.shard_map(
        local,
        mesh=mesh,
        in_specs=placed,
        out_specs=(by_token, by_token, P(), by_row, P(), P(), P(), P(), P(), P(), by_row),
        check_vma=False,
    )
```

```python
import functools

import jax
import jax.numpy as jnp
import numpy as np
from jax import lax
from jax.experimental import pallas as pl
from jax.experimental.pallas import tpu as pltpu
from jax.sharding import PartitionSpec as P

D = 1536
HEADS = 48
HEAD_DIM = 64
STATE = 128
KERNEL = 4
INNER = 3072
LANES = 128
HALO = 16
EPSILON = 1e-05
F32 = jnp.float32
BF16 = jnp.bfloat16


def mm(a, b):
    return jnp.dot(a.astype(BF16), b.astype(BF16), preferred_element_type=F32)


def mm_tr(a, b):
    return lax.dot_general(
        a.astype(BF16), b.astype(BF16), (((1,), (1,)), ((), ())), preferred_element_type=F32
    )


def tr_mm(a, b):
    return lax.dot_general(
        a.astype(BF16), b.astype(BF16), (((0,), (0,)), ((), ())), preferred_element_type=F32
    )


def pieces(a, count):
    out = []
    for _ in range(count - 1):
        part = a.astype(BF16)
        out.append(part)
        a = a - part.astype(F32)
    out.append(a.astype(BF16))
    return out


def ones_mm(ones, a, count):
    return sum(jnp.dot(ones, part, preferred_element_type=F32) for part in pieces(a, count))


def mm_ones(a, ones, count):
    return sum(jnp.dot(part, ones, preferred_element_type=F32) for part in pieces(a, count))


def mm_ones_tr(a, ones, count):
    return sum(
        lax.dot_general(part, ones, (((1,), (1,)), ((), ())), preferred_element_type=F32)
        for part in pieces(a, count)
    )


def iota(shape, dim):
    return lax.broadcasted_iota(jnp.int32, shape, dim)


def softplus(v):
    return jnp.maximum(v, 0.0) + jnp.log1p(jnp.exp(-jnp.abs(v)))


def sigmoid(v):
    return 1.0 / (1.0 + jnp.exp(-v))


def causal_conv(ext, current, halo, weight, bias, offset):
    length = current.shape[0]
    ext[0:HALO, :] = halo
    ext[HALO : HALO + length, :] = current
    total = bias + weight[KERNEL - 1 : KERNEL, :] * current
    for back in range(1, KERNEL):
        shifted = jnp.where(offset >= back, ext[pl.ds(HALO - back, length), :], 0.0)
        total = total + weight[KERNEL - 1 - back : KERNEL - back, :] * shifted
    return total


def head_tiles(width):
    out = []
    for start in range(0, width, LANES):
        size = min(LANES, width - start)
        heads = [start // HEAD_DIM + i for i in range(size // HEAD_DIM)]
        out.append((start, size, heads))
    return out


def masked_heads(tile, heads):
    if len(heads) == 1:
        return tile
    lane = iota(tile.shape, 1) // HEAD_DIM
    return jnp.concatenate(
        [jnp.where(lane == i, tile, jnp.zeros_like(tile)) for i in range(len(heads))], axis=0
    )


def expander(width):
    return (iota((LANES, width), 1) // HEAD_DIM == iota((LANES, width), 0)).astype(BF16)


def chunk_common(x, xh, tail, tailh, offset, params, ext_x, ext_t, width):
    wx, bx, wt, bt, heads_p, pick = params
    length = x.shape[0]
    conv_x = causal_conv(ext_x, x.astype(F32), xh.astype(F32), wx, bx, offset)
    conv_t = causal_conv(
        ext_t,
        tail[:, : 2 * STATE].astype(F32),
        tailh[:, : 2 * STATE].astype(F32),
        wt,
        bt,
        offset,
    )
    raw = jnp.dot(tail[:, 2 * STATE :], pick, preferred_element_type=F32) + heads_p[0:1, :]
    step = softplus(raw)
    decay_rate = jnp.exp(heads_p[1:2, :])
    rate = -step * decay_rate
    tril = (iota((length, length), 0) >= iota((length, length), 1)).astype(BF16)
    cumul = ones_mm(tril, rate, 3)
    spread = expander(width)
    row = iota((length, 1), 0)
    entry = jnp.where(offset > row.astype(F32), jnp.exp(cumul), 0.0)
    last_off = offset[length - 1 : length, :]
    same_last = row.astype(F32) >= (length - 1) - last_off
    to_end = jnp.where(same_last, jnp.exp(cumul[length - 1 : length, :] - cumul), 0.0)
    step_x = mm_ones(step, spread, 2)
    entry_x = mm_ones(entry, spread, 2)
    end_x = mm_ones(to_end, spread, 2)
    return conv_x, conv_t, raw, step, rate, decay_rate, cumul, spread, step_x, entry_x, end_x


def positions(segments, chunk, length):
    here = jnp.zeros((1, length), F32)
    total = segments.shape[1] // length
    rows = [segments[:, i * length : (i + 1) * length].astype(F32) for i in range(total)]
    for i in range(total):
        here = here + jnp.where(chunk == i, rows[i], 0.0)
    own = jnp.broadcast_to(here, (length, length)).T
    less = jnp.zeros((length, length), F32)
    upto = jnp.zeros((length, length), F32)
    for row in rows:
        less = less + jnp.where(row < own, 1.0, 0.0)
        upto = upto + jnp.where(row <= own, 1.0, 0.0)
    index = (chunk * length + iota((length, 1), 0)).astype(F32)
    offset = index - jnp.sum(less, axis=1, keepdims=True)
    return offset, jnp.sum(upto, axis=1, keepdims=True) - 1.0 - index


def flat_rows(ref, flat):
    rows, cols = ref.shape[-2:]
    if rows % HALO == 0:
        return ref[...].reshape(-1, cols)
    shape = ref.shape[:-2]
    for i, at in enumerate(np.ndindex(*shape)):
        flat[i * rows : (i + 1) * rows, :] = ref[at]
    return flat[...]


def forward_kernel(
    seq, fsdp,
    h_ref, zx_ref, tail_ref, seg_ref, cot_ref, ow_ref,
    wx_ref, bx_ref, wt_ref, bt_ref, hp_ref, pick_ref, skip_ref, gain_ref,
    proj_ref, y_ref, state_ref, off_ref, rem_ref, offr_ref,
    h_out, w_out, grad_out, stat_out, mixed_out, pout_out,
    h_v, w_v, w_flat, seg_v, cot_v, ow_v, ow_flat, gated_v, sums_v, sums_got, grad_v, mixed_v,
    pout_v, memory, ext_x, ext_t, last_rows, send, recv, near,
):
    seqs, _, length, width = y_ref.shape
    depth = h_v.shape[3]
    cols = proj_ref.shape[3]
    step_at = pl.program_id(0)
    place = Place(seq, fsdp)
    links = Links(send, recv, near)
    peers = peers_of(place)
    near_peers = [(l, c) for t, l, c in peers if t == 0]
    entry = Entry(place, links, h_ref, zx_ref, tail_ref, seg_ref, h_v, w_v, seg_v)
    cot = TokenGather(place, links, cot_ref, cot_v)
    w_rows = RowGather(place, links, ow_ref, ow_v)
    keep = [links.local(lambda: (h_v, h_out)), links.local(lambda: (w_v, w_out))]
    stages = len(place.low_bits)

    def send_sums(i):
        l, c = near_peers[i]
        return links.far(lambda: (sums_v, sums_got.at[i], place.at(low=l, core=c)))

    sums = [send_sums(i) for i in range(len(near_peers))]

    @pl.when(step_at == 0)
    def _():
        memory[...] = jnp.zeros_like(memory)
        last_rows[...] = jnp.zeros_like(last_rows)
        meet_pair(place)
        entry.run(cot.cross_over)
        if w_v.shape[-2] % HALO:
            flat_rows(w_v, w_flat)

    @pl.when(step_at == 1)
    def _():
        for copy in keep:
            copy.start()
        cot.begin_home()
        w_rows.begin()

    for i in range(stages):

        @pl.when(step_at == min(3 + 2 * i, seq - 1))
        def _():
            cot.pass_on(i, "home")

    @pl.when(step_at == 2)
    def _():
        cot.arrive()

    for i in range(stages):

        @pl.when(step_at == min(4 + 2 * i, seq - 1))
        def _():
            cot.pass_on(i, "away")

    @pl.when(step_at == seq - 2)
    def _():
        w_rows.forward()

    @pl.when(step_at < seq)
    def _():
        weights = flat_rows(w_v, w_flat) if w_v.shape[-2] % HALO == 0 else w_flat[...]
        proj = jnp.dot(
            h_v[:, step_at].reshape(seqs * length, depth), weights, preferred_element_type=F32
        ).astype(BF16)
        proj_ref[...] = proj.reshape(proj_ref.shape)
        params = tuple(r[...] for r in (wx_ref, bx_ref, wt_ref, bt_ref, hp_ref, pick_ref))
        for q in range(seqs):
            offset, remain = positions(seg_v[q : q + 1, :], step_at, length)
            off_ref[q, 0] = offset
            rem_ref[q, 0] = remain
            offr_ref[q, 0] = jnp.broadcast_to(offset, (length, LANES)).T[0:1, :]
            chunk_rows = proj[q * length : (q + 1) * length]
            zx, tail = chunk_rows[:, : 2 * width], chunk_rows[:, 2 * width :]
            earlier = last_rows[q]
            here = pl.ds(pl.multiple_of((q * seq + step_at) * length, length), length)
            conv_x, conv_t, _, _, _, _, cumul, _, step_x, entry_x, end_x = chunk_common(
                zx[:, width:], earlier[:, width : 2 * width], tail, earlier[:, 2 * width :], offset, params,
                ext_x.at[q], ext_t.at[q], width,
            )
            xs = conv_x * sigmoid(conv_x)
            act_t = conv_t * sigmoid(conv_t)
            bs = act_t[:, :STATE].astype(BF16)
            cs = act_t[:, STATE:].astype(BF16)
            scaled = xs * step_x
            scores = mm_tr(cs, bs)
            gap = iota((length, length), 0) - iota((length, length), 1)
            same = (gap >= 0) & (gap.astype(F32) <= offset)
            cumul_t = cumul.T
            old = memory[q]
            old_low = old.astype(BF16)
            state_ref[q, 0] = old_low
            outside = mm(cs, old_low) * entry_x + skip_ref[...] * xs
            squares = jnp.zeros((length, 1), F32)
            for start, size, heads in head_tiles(width):
                mixing = []
                for head in heads:
                    spans = cumul[:, head : head + 1] - cumul_t[head : head + 1, :]
                    decays = jnp.exp(jnp.where(same, spans, -1e30))
                    mixing.append((decays * scores).astype(BF16))
                tile = masked_heads(scaled[:, start : start + size].astype(BF16), heads)
                mix = mixing[0] if len(heads) == 1 else jnp.concatenate(mixing, axis=1)
                inside = jnp.dot(mix, tile, preferred_element_type=F32)
                y_low = (inside + outside[:, start : start + size]).astype(BF16)
                y_ref[q, 0, :, start : start + size] = y_low
                z = zx[:, start : start + size].astype(F32)
                gated = y_low.astype(F32) * (z * sigmoid(z))
                gated_v[here, start : start + size] = (
                    gated * gain_ref[:, start : start + size]
                ).astype(BF16)
                squares = squares + jnp.sum(gated * gated, axis=1, keepdims=True)
            sums_v[pl.ds(2 * (q * seq + step_at), 1), :] = jnp.broadcast_to(
                squares, (length, LANES)
            ).T[0:1, :]
            fresh = tr_mm(bs, scaled * end_x)
            memory[q] = old * entry_x[length - 1 : length, :] + fresh
            last_rows[q] = chunk_rows[length - HALO :]

    @pl.when(step_at == seq)
    def _():
        w_rows.finish()
        cot.finish()
        rows_out = flat_rows(ow_v, ow_flat)
        tile = 2 * length
        tiles = seqs * seq // 2

        @pl.loop(0, tiles)
        def _(k):
            at = pl.ds(pl.multiple_of(k * tile, tile), tile)
            cots = cot_v[k // (seq // 2), pl.ds(lax.rem(k, seq // 2) * 2, 2)].reshape(tile, depth)
            grad = mm_tr(cots, rows_out)
            grad_v[at, :] = grad
            part = jnp.sum(grad * gated_v[at, :].astype(F32), axis=1, keepdims=True)
            part = jnp.broadcast_to(part, (tile, LANES))
            for i in (0, 1):
                sums_v[pl.ds(4 * k + 2 * i + 1, 1), :] = (
                    part[i * length : (i + 1) * length].T[0:1, :]
                )

        grad_store = links.local(lambda: (grad_v, grad_out))
        grad_store.start()
        for copy in sums:
            copy.start()
        for copy in sums:
            copy.wait_recv()
        total = sums_v[...]
        for i in range(len(near_peers)):
            total = total + sums_got[i]
        is_square = lax.rem(iota(total.shape, 0), 2) == 0
        scale = lax.rsqrt(total / INNER + EPSILON)
        other = pltpu.roll(scale, 1, 0)
        stat_out[...] = jnp.where(is_square, scale, total * (other * other * other / INNER))

        @pl.loop(0, tiles)
        def _(k):
            at = pl.ds(pl.multiple_of(k * tile, tile), tile)
            scales = [
                jnp.broadcast_to(stat_out[pl.ds(4 * k + 2 * i, 1), :], (LANES, length)).T[:, 0:1]
                for i in (0, 1)
            ]
            scale_col = jnp.concatenate(scales, axis=0)
            gated = gated_v[at, :]
            mixed = jnp.dot(gated, rows_out, preferred_element_type=F32)
            mixed_v[at, :] = (mixed * scale_col).astype(BF16)
            gated_v[at, :] = (gated.astype(F32) * scale_col).astype(BF16)

        mixed_store = links.local(lambda: (mixed_v, mixed_out))
        mixed_store.start()
        pout_v[...] = tr_mm(gated_v[...], cot_v[...].reshape(-1, depth)).astype(BF16)
        pout_store = links.local(lambda: (pout_v, pout_out))
        pout_store.start()
        for copy in [grad_store, mixed_store, pout_store] + keep:
            copy.wait()
        for copy in sums:
            copy.wait_send()
        entry.finish()


def backward_kernel(
    seq, fsdp,
    zx_ref, zxh_ref, tail_ref, tailh_ref, off_ref, offr_ref, rem_ref, y_ref, grad_ref, stat_ref,
    state_ref, mixed_ref, pout_ref,
    wx_ref, bx_ref, wt_ref, bt_ref, hp_ref, pick_ref, skip_ref, gain_ref,
    out_ref, gx_ref, gt_ref, gh_ref, mixed_out, rows_out,
    memory, ext_x, ext_t, next_x, next_t,
    mix_own, mix_first, mix_later, pout_own, pout_first, send, recv, near,
):
    seqs, _, length, width = y_ref.shape
    step_at = pl.program_id(0)

    place = Place(seq, fsdp)
    links = Links(send, recv, near)
    mixed = TokenScatter(place, links, mixed_ref, mixed_out, mix_own, mix_first, mix_later)
    w_rows = RowScatter(place, links, pout_ref, rows_out, pout_own, pout_first)
    stages = len(place.low_bits)

    @pl.when(step_at == 0)
    def _():
        meet_pair(place)
        mixed.begin()
        w_rows.begin()

    @pl.when(step_at == 2)
    def _():
        mixed.add_cores()
        mixed.send_stage(0)

    @pl.when(step_at == 4)
    def _():
        w_rows.add_pairs()

    @pl.when(step_at == pl.num_programs(0) - 2)
    def _():
        mixed.add_stage(0)
        if stages > 1:
            mixed.send_stage(1)

    @pl.when(pl.program_id(0) == 0)
    def _():
        memory[...] = jnp.zeros_like(memory)
        gx_ref[...] = jnp.zeros_like(gx_ref)
        gt_ref[...] = jnp.zeros_like(gt_ref)
        gh_ref[...] = jnp.zeros_like(gh_ref)
        next_x[:, length:, :] = jnp.zeros_like(next_x[:, length:, :])
        next_t[:, length:, :] = jnp.zeros_like(next_t[:, length:, :])

    params = tuple(r[...] for r in (wx_ref, bx_ref, wt_ref, bt_ref, hp_ref, pick_ref))
    for q in range(seqs):
        offset = off_ref[q, 0]
        conv_x, conv_t, raw, step, rate, decay_rate, cumul, spread, step_x, entry_x, end_x = (
            chunk_common(
                zx_ref[q, 0, :, width:], zxh_ref[q, 0, :, width:], tail_ref[q, 0], tailh_ref[q, 0], offset,
                params, ext_x.at[q], ext_t.at[q], width,
            )
        )
        stats = jnp.broadcast_to(stat_ref[q, 0, 0:1, :], (LANES, length)).T
        slopes = jnp.broadcast_to(stat_ref[q, 0, 1:2, :], (LANES, length)).T
        scale, slope = stats[:, 0:1], slopes[:, 0:1]
        z = zx_ref[q, 0, :, :width].astype(F32)
        sig_z = sigmoid(z)
        silu_z = z * sig_z
        y = y_ref[q, 0].astype(F32)
        gated = y * silu_z
        scaled_grad = grad_ref[q, 0].astype(F32) * scale
        gx_ref[KERNEL + 2 : KERNEL + 3, :] += jnp.sum(scaled_grad * gated, axis=0, keepdims=True)
        grad_gated = gain_ref[...] * scaled_grad - gated * slope
        dy_low = (grad_gated * silu_z).astype(BF16)
        dz = (grad_gated * y * (sig_z + silu_z * (1.0 - sig_z))).astype(BF16)
        dy = dy_low.astype(F32)

        sig_x = sigmoid(conv_x)
        xs = conv_x * sig_x
        slope_x = sig_x + xs * (1.0 - sig_x)
        sig_t = sigmoid(conv_t)
        act_t = conv_t * sig_t
        slope_t = sig_t + act_t * (1.0 - sig_t)
        bs = act_t[:, :STATE].astype(BF16)
        cs = act_t[:, STATE:].astype(BF16)
        scaled = xs * step_x
        scaled_low = scaled.astype(BF16)
        scores = mm_tr(bs, cs)
        rows, cols = iota((length, length), 0), iota((length, length), 1)
        gap = cols - rows
        same = (gap >= 0) & (gap.astype(F32) <= offr_ref[q, 0])
        strict = gap > 0
        upper = (rows >= cols).astype(BF16)
        cumul_t = cumul.T
        old = state_ref[q, 0]
        grad_state = memory[q]
        state_low = grad_state.astype(BF16)
        grad_scores = jnp.zeros((length, length), F32)
        grad_scaled = []
        inside_rows = []
        for start, size, heads in head_tiles(width):
            dy_tile = masked_heads(dy_low[:, start : start + size], heads)
            grad_mix = mm_tr(scaled_low[:, start : start + size], dy_tile)
            mixing = []
            for place, head in enumerate(heads):
                spans = cumul_t[head : head + 1, :] - cumul[:, head : head + 1]
                decays = jnp.exp(jnp.where(same, spans, -1e30))
                weighted = grad_mix[:, place * length : (place + 1) * length] * decays
                grad_scores = grad_scores + weighted
                mixing.append((decays * scores).astype(BF16))
                terms = jnp.where(strict, weighted * scores, 0.0).astype(BF16)
                sums = jnp.dot(terms, upper, preferred_element_type=F32)
                inside_rows.append(
                    jnp.sum(jnp.where(strict, sums, 0.0), axis=0, keepdims=True)
                )
            mix = mixing[0] if len(heads) == 1 else jnp.concatenate(mixing, axis=1)
            grad_scaled.append(jnp.dot(mix, dy_tile, preferred_element_type=F32))
        inside_rows.append(jnp.zeros((LANES - len(inside_rows), length), F32))
        inside = jnp.concatenate(inside_rows, axis=0).T
        from_end = mm(bs, state_low) * end_x
        grad_scaled = jnp.concatenate(grad_scaled, axis=1) + from_end
        entry_dy = dy * entry_x
        entry_dy_low = entry_dy.astype(BF16)
        out_terms = mm(cs, old) * entry_dy
        end_terms = scaled * from_end
        grad_step = mm_ones_tr(xs * grad_scaled, spread, 2)
        out_terms = mm_ones_tr(out_terms, spread, 2)
        end_terms = mm_ones_tr(end_terms, spread, 2)
        keep_row = entry_x[length - 1 : length, :]
        carried = jnp.sum(grad_state * old.astype(F32), axis=0, keepdims=True) * keep_row
        carried = mm_ones_tr(jnp.broadcast_to(carried, (8, width)), spread, 2)[0:1, :]
        triu = (cols >= rows).astype(BF16)
        below = (rows > cols).astype(BF16)
        grad_rate = inside + ones_mm(triu, out_terms, 2) + ones_mm(below, end_terms, 2) + carried
        grad_step = grad_step - decay_rate * grad_rate
        grad_raw = grad_step * sigmoid(raw)
        grad_scores_low = grad_scores.astype(BF16)
        grad_b = mm(grad_scores_low, cs) + mm_tr(scaled * end_x, state_low)
        grad_c = tr_mm(grad_scores_low, bs) + mm_tr(entry_dy_low, old)
        memory[q] = grad_state * keep_row + tr_mm(cs, entry_dy_low)
        conv_grad_x = (skip_ref[...] * dy + step_x * grad_scaled) * slope_x
        conv_grad_t = jnp.concatenate([grad_b, grad_c], axis=1) * slope_t

        remain = rem_ref[q, 0]
        results = [dz]
        for grad, ext, nxt, weight, sums in (
            (conv_grad_x, ext_x.at[q], next_x.at[q], params[0], gx_ref),
            (conv_grad_t, ext_t.at[q], next_t.at[q], params[2], gt_ref),
        ):
            current = ext[pl.ds(HALO, length), :]
            sums[KERNEL : KERNEL + 1, :] += jnp.sum(grad, axis=0, keepdims=True)
            sums[KERNEL - 1 : KERNEL, :] += jnp.sum(grad * current, axis=0, keepdims=True)
            nxt[0:length, :] = grad
            total = weight[KERNEL - 1 : KERNEL, :] * grad
            for back in range(1, KERNEL):
                tap = KERNEL - 1 - back
                shifted = jnp.where(offset >= back, ext[pl.ds(HALO - back, length), :], 0.0)
                sums[tap : tap + 1, :] += jnp.sum(grad * shifted, axis=0, keepdims=True)
                ahead = jnp.where(remain >= back, nxt[pl.ds(back, length), :], 0.0)
                total = total + weight[tap : tap + 1, :] * ahead
            nxt[length:, :] = grad[0:HALO, :]
            results.append(total.astype(BF16))
        results.append(mm_tr(grad_raw, params[5]).astype(BF16))
        gx_ref[KERNEL + 1 : KERNEL + 2, :] += jnp.sum(dy * xs, axis=0, keepdims=True)
        gh_ref[0:1, :] += jnp.sum(grad_raw, axis=0, keepdims=True)
        gh_ref[1:2, :] += jnp.sum(grad_rate * rate, axis=0, keepdims=True)
        out_ref[q, 0, :, : 2 * width] = jnp.concatenate(results[:2], axis=1)
        out_ref[q, 0, :, 2 * width : 2 * width + 2 * STATE] = results[2]
        out_ref[q, 0, :, 2 * width + 2 * STATE :] = results[3]

    @pl.when(step_at == pl.num_programs(0) - 1)
    def _():
        for stage in range(1, stages):
            mixed.add_stage(stage)
            if stage + 1 < stages:
                mixed.send_stage(stage + 1)
        mixed.store()
        w_rows.finish()
        mixed.finish()


TAIL = 2 * STATE + LANES
AXES = ("seq", "fsdp")
MESH = pl.DeviceIdType.MESH
ANYWHERE = pl.BlockSpec(memory_space=pl.ANY)


def whole_spec(shape):
    return pl.BlockSpec(shape, lambda i: (0,) * len(shape))


def chunk_specs(seqs, steps, length, reverse):
    def place(i):
        return steps - 1 - i if reverse else i

    def block(cols, column=0, rows=length):
        return pl.BlockSpec((seqs, 1, rows, cols), lambda i: (0, place(i), 0, column))

    def before(cols, column=0):
        return pl.BlockSpec(
            (seqs, 1, HALO, cols),
            lambda i: (0, jnp.maximum(place(i) - 1, 0), length // HALO - 1, column),
        )

    return block, before


def forward_mix(normed, zx, tail, segments, cotangent, out_w, consts, seq, fsdp):
    seqs, length, depth = normed.shape
    rows = tail.shape[0]
    cols = zx.shape[2] + TAIL
    width = zx.shape[2] // 2
    pairs = fsdp // 2
    count = seqs * seq * length

    def block(columns, height=length):
        return pl.BlockSpec(
            (seqs, 1, height, columns), lambda i: (0, jnp.minimum(i, seq - 1), 0, 0)
        )

    def blocks(columns, kind, height=length):
        return jax.ShapeDtypeStruct((seqs, seq, height, columns), kind)

    w_shape = (seq, pairs, 2, rows, cols)
    out_shape = (pairs, 2) + out_w.shape
    sums = (seqs * seq * 2, length)
    flat = 8 if rows % HALO == 0 else depth
    flat_out = 8 if out_w.shape[0] % HALO == 0 else width
    outs = pl.pallas_call(
        functools.partial(forward_kernel, seq, fsdp),
        grid=(seq + 1,),
        in_specs=[ANYWHERE] * 6 + [whole_spec(v.shape) for v in consts],
        out_specs=[
            block(cols), block(width), block(width, STATE), block(1), block(1), block(length, 1),
            ANYWHERE, ANYWHERE, ANYWHERE, whole_spec(sums), ANYWHERE, ANYWHERE,
        ],
        out_shape=[
            blocks(cols, BF16), blocks(width, BF16), blocks(width, BF16, STATE),
            blocks(1, F32), blocks(1, F32), blocks(length, F32, 1),
            blocks(depth, BF16),
            jax.ShapeDtypeStruct(w_shape, BF16),
            jax.ShapeDtypeStruct((count, width), F32),
            jax.ShapeDtypeStruct(sums, F32),
            jax.ShapeDtypeStruct((count, depth), BF16),
            jax.ShapeDtypeStruct((width, depth), BF16),
        ],
        scratch_shapes=[
            pltpu.VMEM((seqs, seq, length, depth), BF16),
            pltpu.VMEM(w_shape, BF16),
            pltpu.VMEM((flat, cols), BF16),
            pltpu.VMEM(segments.shape, segments.dtype),
            pltpu.VMEM((seqs, seq, length, depth), BF16),
            pltpu.VMEM(out_shape, BF16),
            pltpu.VMEM((flat_out, depth), BF16),
            pltpu.VMEM((count, width), BF16),
            pltpu.VMEM(sums, F32),
            pltpu.VMEM((seq - 1,) + sums, F32),
            pltpu.VMEM((count, width), F32),
            pltpu.VMEM((count, depth), BF16),
            pltpu.VMEM((width, depth), BF16),
            pltpu.VMEM((seqs, STATE, width), F32),
            pltpu.VMEM((seqs, HALO + length, width), F32),
            pltpu.VMEM((seqs, HALO + length, 2 * STATE), F32),
            pltpu.VMEM((seqs, HALO, cols), BF16),
            pltpu.SemaphoreType.DMA((320,)),
            pltpu.SemaphoreType.DMA((320,)),
            pltpu.SemaphoreType.DMA((24,)),
        ],
        compiler_params=pltpu.CompilerParams(
            dimension_semantics=("arbitrary",), vmem_limit_bytes=60 << 20, collective_id=0,
            has_side_effects=True,
        ),
        cost_estimate=pl.CostEstimate(
            flops=30_000_000_000, transcendentals=0, bytes_accessed=60_000_000
        ),
        name="mix_forward",
    )(normed, zx, tail, segments, cotangent, out_w, *consts)
    proj, y, states, off_col, rem_col, off_row, h_all, w_mine, grad_yn, stats, mixed, part = outs
    shape = (seqs, seq, length)
    return (
        proj, y, states, off_col, rem_col, off_row, h_all, w_mine.reshape(depth, cols),
        grad_yn.reshape(shape + (width,)), stats.reshape(seqs, seq, 2, length),
        mixed.reshape(shape + (depth,)), part.reshape(out_shape),
    )


def backward_mix(
    proj, off_col, off_row, rem_col, y, grad_yn, stats, states, mixed, part_out, consts, seq, fsdp
):
    seqs, steps, length, cols = proj.shape
    depth = mixed.shape[3]
    width = (cols - TAIL) // 2
    block, before = chunk_specs(seqs, steps, length, True)
    tail_at = 2 * width // TAIL
    half, pairs = seq // 2, fsdp // 2
    rows_out = part_out.shape[2]
    sums = [(8, width), (8, 2 * STATE), (8, LANES)]
    token_own = pltpu.VMEM((seqs, half, length, depth), BF16)
    return pl.pallas_call(
        functools.partial(backward_kernel, seq, fsdp),
        grid=(steps,),
        in_specs=[
            block(2 * width), before(2 * width), block(TAIL, tail_at), before(TAIL, tail_at),
            block(1), block(length, 0, 1), block(1), block(width), block(width),
            block(length, 0, 2), block(width, 0, STATE), ANYWHERE, ANYWHERE,
        ]
        + [whole_spec(v.shape) for v in consts],
        out_specs=[block(cols)] + [whole_spec(v) for v in sums] + [ANYWHERE, ANYWHERE],
        scratch_shapes=[
            pltpu.VMEM((seqs, STATE, width), F32),
            pltpu.VMEM((seqs, HALO + length, width), F32),
            pltpu.VMEM((seqs, HALO + length, 2 * STATE), F32),
            pltpu.VMEM((seqs, length + HALO, width), F32),
            pltpu.VMEM((seqs, length + HALO, 2 * STATE), F32),
            token_own, token_own, pltpu.VMEM((seqs, max(half - 1, 1), length, depth), BF16),
            pltpu.VMEM((2, rows_out, depth), BF16),
            pltpu.VMEM((max(pairs - 1, 1), 2, rows_out, depth), BF16),
            pltpu.SemaphoreType.DMA((64,)),
            pltpu.SemaphoreType.DMA((64,)),
            pltpu.SemaphoreType.DMA((16,)),
        ],
        out_shape=[jax.ShapeDtypeStruct(proj.shape, BF16)]
        + [jax.ShapeDtypeStruct(v, F32) for v in sums]
        + [
            jax.ShapeDtypeStruct((seqs, length, depth), BF16),
            jax.ShapeDtypeStruct((2, rows_out, depth), BF16),
        ],
        compiler_params=pltpu.CompilerParams(
            dimension_semantics=("arbitrary",), vmem_limit_bytes=56 << 20, collective_id=3,
            has_side_effects=True,
        ),
        cost_estimate=pl.CostEstimate(
            flops=steps * seqs * 2_000_000_000, transcendentals=0, bytes_accessed=16_000_000
        ),
        name="mix_backward",
    )(
        proj, proj, proj, proj, off_col, off_row, rem_col, y, grad_yn, stats, states, mixed,
        part_out, *consts,
    )


class Place:
    def __init__(self, seq, fsdp):
        self.seq, self.fsdp = seq, fsdp
        self.half, self.pairs = seq // 2, fsdp // 2
        s, f = lax.axis_index("seq"), lax.axis_index("fsdp")
        self.s, self.f = s, f
        self.top, self.low = s // self.half, lax.rem(s, self.half)
        self.core, self.pair = lax.rem(f, 2), f // 2
        self.home = self.core == self.top
        self.away = self.core != self.top
        self.chunk = self.low + self.half * self.core
        self.low_bits = [1 << i for i in range(self.half.bit_length() - 1)]

    def at(self, top=0, low=0, pair=0, core=0):
        return (
            flip(self.top, top) * self.half + flip(self.low, low),
            flip(self.pair, pair) * 2 + flip(self.core, core),
        )

    def bits_for(self, q):
        return self.low_bits if q % 2 == 0 else self.low_bits[::-1]


def flip(index, bits):
    for i in range(bits.bit_length()):
        if bits >> i & 1:
            bit = lax.rem(index // (1 << i), 2)
            index = index + (1 << i) * (1 - 2 * bit)
    return index


class Copy:
    def __init__(self, make):
        self.make = make

    def start(self):
        self.make().start()
        return self

    def wait(self):
        self.make().wait()

    def wait_send(self):
        self.make().wait_send()

    def wait_recv(self):
        self.make().wait_recv()


class Links:
    def __init__(self, send, recv, near):
        self.send, self.recv, self.near = send, recv, near
        self.far_count = self.near_count = 0

    def far(self, make):
        i = self.far_count
        self.far_count += 1

        def build():
            src, dst, device = make()
            return pltpu.make_async_remote_copy(
                src_ref=src, dst_ref=dst, send_sem=self.send.at[i], recv_sem=self.recv.at[i],
                device_id=device, device_id_type=MESH,
            )

        return Copy(build)

    def local(self, make):
        i = self.near_count
        self.near_count += 1
        return Copy(lambda: pltpu.make_async_copy(*make(), self.near.at[i]))


def meet(devices):
    barrier = pltpu.get_barrier_semaphore()
    for device in devices:
        pl.semaphore_signal(barrier, inc=1, device_id=device, device_id_type=MESH)
    pl.semaphore_wait(barrier, len(devices))


def meet_pair(place):
    meet(
        [place.at(top=t, low=l, core=c) for t, l, c in peers_of(place)]
        + [place.at(pair=p) for p in range(1, place.pairs)]
    )


def peers_of(place):
    out = []
    for top in (0, 1):
        for low in range(place.half):
            for core in (0, 1):
                if (top, low, core) != (0, 0, 0):
                    out.append((top, low, core))
    return out


class TokenGather:
    def __init__(self, place, links, src, dst):
        self.place, self.src, self.dst = place, src, dst
        seqs = src.shape[0]

        def over(q):
            return links.far(
                lambda: (src.at[q], dst.at[q, place.s], place.at(top=1, core=1))
            )

        self.cross = [over(q) for q in range(seqs)]
        self.stay = links.local(lambda: (src, dst.at[:, place.s]))
        self.share = [[] for _ in range(seqs)]
        self.stages = []
        held = [[0] for _ in range(seqs)]
        for q in range(seqs):
            self.share[q].append([self.copy(links, q, low, core=1) for low in held[q]])
        for i in range(len(place.low_bits)):
            stage = []
            for q in range(seqs):
                bit = place.bits_for(q)[i]
                stage.append([self.copy(links, q, low, low_bit=bit) for low in held[q]])
                fresh = [low ^ bit for low in held[q]]
                held[q] = held[q] + fresh
                self.share[q].append([self.copy(links, q, low, core=1) for low in fresh])
            self.stages.append(stage)

    def copy(self, links, q, low, low_bit=0, core=0):
        def make():
            place = self.place
            ref = self.dst.at[q, flip(place.low, low) + place.half * place.core]
            return ref, ref, place.at(low=low_bit, core=core)

        return links.far(make)

    def begin(self):
        self.cross_over()
        self.begin_home()

    def cross_over(self):
        @pl.when(self.place.away)
        def _():
            for copy in self.cross:
                copy.start()

    def begin_home(self):
        @pl.when(self.place.home)
        def _():
            self.stay.start()
            self.stay.wait()
            self.send_stage(0)

    def arrive(self):
        @pl.when(self.place.away)
        def _():
            for copy in self.cross:
                copy.wait_recv()
            self.send_stage(0)

    def send_stage(self, i):
        for q in range(len(self.share)):
            for copy in self.stages[i][q] + self.share[q][i]:
                copy.start()

    def pass_on(self, i, role):
        @pl.when(self.place.home if role == "home" else self.place.away)
        def _():
            for q in range(len(self.share)):
                for copy in self.stages[i][q]:
                    copy.wait_recv()
                for copy in (self.stages[i + 1][q] if i + 1 < len(self.stages) else []):
                    copy.start()
                for copy in self.share[q][i + 1]:
                    copy.start()

    def finish(self):
        for share in self.share:
            for copies in share:
                for copy in copies:
                    copy.wait()
        for stage in self.stages:
            for copies in stage:
                for copy in copies:
                    copy.wait_send()

        @pl.when(self.place.away)
        def _():
            for copy in self.cross:
                copy.wait_send()


class RowGather:
    def __init__(self, place, links, src, dst):
        self.place = place
        pairs = range(1, place.pairs)

        def slot():
            return dst.at[place.pair, place.core]

        self.stay = links.local(lambda: (src, slot()))
        self.to_home = links.far(lambda: (src, slot(), place.at(core=1)))
        self.to_near = links.far(lambda: (src, slot(), place.at(top=1)))
        self.to_far = links.far(lambda: (src, slot(), place.at(top=1, core=1)))

        def forward(c, p):
            return links.far(
                lambda: (dst.at[place.pair, c], dst.at[place.pair, c], place.at(pair=p))
            )

        self.forwards = [forward(c, p) for c in (0, 1) for p in pairs]

    def begin(self):
        @pl.when(self.place.home)
        def _():
            self.stay.start()
            self.to_near.start()

        @pl.when(self.place.away)
        def _():
            self.to_home.start()
            self.to_far.start()

    def forward(self):
        @pl.when(self.place.home)
        def _():
            self.stay.wait()
            self.to_home.wait_recv()

        @pl.when(self.place.away)
        def _():
            self.to_near.wait_recv()
            self.to_far.wait_recv()

        for copy in self.forwards:
            copy.start()

    def finish(self):
        for copy in self.forwards:
            copy.wait()

        @pl.when(self.place.home)
        def _():
            self.to_near.wait_send()

        @pl.when(self.place.away)
        def _():
            self.to_home.wait_send()
            self.to_far.wait_send()


class Entry:
    def __init__(self, place, links, h_ref, zx_ref, tail_ref, seg_ref, h_v, w_v, seg_v):
        self.place = place
        cols = zx_ref.shape[2]
        self.peers = peers = peers_of(place)
        others = range(1, place.pairs)
        self.tokens = TokenGather(place, links, h_ref, h_v)

        def block(t=0, l=0, c=0):
            s, f = place.at(top=t, low=l, core=c)
            return w_v.at[s, place.pair, lax.rem(f, 2)]

        def columns(ref):
            return ref.at[:, pl.ds(0, cols)]

        def tail_of(ref):
            return ref.at[:, pl.ds(cols, TAIL)]

        def send_zx(t, l, c):
            group = flip(place.core, c) * place.half + flip(place.low, l)
            return zx_ref.at[group], columns(block()), place.at(top=t, low=l, core=c)

        self.zx = {p: links.far(functools.partial(send_zx, *p)) for p in peers}
        self.own = [
            links.local(lambda: (zx_ref.at[place.chunk], columns(block()))),
            links.local(lambda: (tail_ref, tail_of(block()))),
        ]
        self.tail_cross = links.far(lambda: (tail_ref, tail_of(block()), place.at(top=1)))
        self.near_peers = [(l, c) for t, l, c in peers if t == 0]

        def send_tail(l, c):
            return tail_ref, tail_of(block()), place.at(low=l, core=c)

        def send_other(l, c):
            return tail_of(block(1)), tail_of(block(1)), place.at(low=l, core=c)

        self.tails = {p: links.far(functools.partial(send_tail, *p)) for p in self.near_peers}
        self.tails_more = {
            p: links.far(functools.partial(send_other, *p)) for p in self.near_peers
        }
        self.seg_send = links.far(lambda: (seg_ref, seg_v, place.at(core=1)))
        self.seg_keep = links.local(lambda: (seg_ref, seg_v))

        def send_on(t, l, c, p):
            return block(t, l, c), block(t, l, c), place.at(pair=p)

        self.forwards = {
            p: [links.far(functools.partial(send_on, *p, other)) for other in others]
            for p in [(0, 0, 0)] + peers
        }

    def run(self, then):
        tokens, zx, forwards = self.tokens, self.zx, self.forwards
        stages = len(self.place.low_bits)
        far_peers = [p for p in self.peers if p[0] == 1]
        tokens.begin()
        self.tail_cross.start()
        for copy in self.own:
            copy.start()
        for p in self.near_peers:
            zx[0, *p].start()
            self.tails[p].start()

        @pl.when(self.place.home)
        def _():
            self.seg_send.start()
            self.seg_keep.start()

        for copy in self.own:
            copy.wait()
        for copy in forwards[0, 0, 0]:
            copy.start()
        self.tail_cross.wait_recv()
        for p in self.near_peers:
            self.tails_more[p].start()
        tokens.pass_on(0, "home")
        for p in self.near_peers:
            zx[0, *p].wait_recv()
            self.tails[p].wait_recv()
            for copy in forwards[0, *p]:
                copy.start()
        for p in far_peers:
            zx[p].start()
        for i in range(1, stages):
            tokens.pass_on(i, "home")
        tokens.arrive()
        for p in self.near_peers:
            self.tails_more[p].wait_recv()
        for i in range(stages):
            tokens.pass_on(i, "away")
            at, to = (len(far_peers) * k // stages for k in (i, i + 1))
            for p in far_peers[at:to]:
                zx[p].wait_recv()
                for copy in forwards[p]:
                    copy.start()
        then()

        @pl.when(self.place.home)
        def _():
            self.seg_keep.wait()
            self.seg_send.wait_send()

        @pl.when(self.place.away)
        def _():
            self.seg_send.wait_recv()

        tokens.finish()
        for p in forwards:
            for copy in forwards[p]:
                copy.wait()

    def finish(self):
        self.tail_cross.wait_send()
        for group in (self.zx, self.tails, self.tails_more):
            for copy in group.values():
                copy.wait_send()


def add_rows(out, left, right, rows=32):
    total = left.shape[0]
    step = next((size for size in (rows, 16) if total % size == 0), total)

    if step == total:
        out[...] = (left[...].astype(F32) + right[...].astype(F32)).astype(out.dtype)
        return

    @pl.loop(0, total // step)
    def _(i):
        at = pl.ds(pl.multiple_of(i * step, step), step)
        out[at] = (left[at].astype(F32) + right[at].astype(F32)).astype(out.dtype)


class TokenScatter:
    def __init__(self, place, links, src, out, own, first, later, loads=True):
        self.place = place
        self.out, self.own, self.first, self.later = out, own, first, later
        self.seqs = src.shape[0]
        half = place.half

        def give(q):
            def make():
                part = src.at[q, pl.ds(half * (1 - place.core), half)] if loads else src.at[q]
                return part, first.at[q], place.at(core=1)

            return links.far(make)

        def keep(q):
            return links.local(
                lambda: (src.at[q, pl.ds(half * place.core, half)], own.at[q])
            )

        self.cores = [give(q) for q in range(self.seqs)]
        self.loads = [keep(q) for q in range(self.seqs)] if loads else []
        self.stages = [[] for _ in place.low_bits]
        for q in range(self.seqs):
            live, slot = list(range(half)), 0
            for i, bit in enumerate(place.bits_for(q)[::-1]):
                for low in [low for low in live if low & bit]:
                    self.stages[i].append((self.copy(links, q, low, slot, bit), q, low ^ bit, slot))
                    slot += 1
                live = [low for low in live if not low & bit]
        self.stay = links.local(lambda: (own.at[:, place.low], out))

    def copy(self, links, q, low, slot, bit):
        return links.far(
            lambda: (
                self.own.at[q, flip(self.place.low, low)], self.later.at[q, slot],
                self.place.at(low=bit),
            )
        )

    def begin(self):
        for copy in self.cores + self.loads:
            copy.start()

    def add_cores(self):
        for q in range(self.seqs):
            if self.loads:
                self.loads[q].wait()
            self.cores[q].wait_recv()
            for low in range(self.place.half):
                add_rows(self.own.at[q, low], self.own.at[q, low], self.first.at[q, low])

    def send_stage(self, i):
        for copy, _, _, _ in self.stages[i]:
            copy.start()

    def add_stage(self, i):
        for copy, q, low, slot in self.stages[i]:
            copy.wait_recv()
            ref = self.own.at[q, flip(self.place.low, low)]
            add_rows(ref, ref, self.later.at[q, slot])

    def store(self):
        self.stay.start()
        self.stay.wait()

    def finish(self):
        for copy in self.cores:
            copy.wait_send()
        for stage in self.stages:
            for copy, _, _, _ in stage:
                copy.wait_send()


class RowScatter:
    def __init__(self, place, links, src, out, own, first):
        self.place, self.own, self.first = place, own, first

        def over(p):
            return links.far(
                lambda: (src.at[flip(place.pair, p)], first.at[p - 1], place.at(pair=p))
            )

        def far(c):
            return links.far(
                lambda: (own.at[flip(place.core, c)], out.at[1], place.at(top=1, core=c))
            )

        self.over = [over(p) for p in range(1, place.pairs)]
        self.load = links.local(lambda: (src.at[place.pair], own))
        self.far = [far(0), far(1)]
        self.near = links.far(lambda: (own.at[1 - place.core], out.at[0], place.at(core=1)))
        self.stay = links.local(lambda: (own.at[place.core], out.at[0]))

    def begin(self):
        self.load.start()
        for copy in self.over:
            copy.start()

    def add_pairs(self):
        self.load.wait()
        for i, copy in enumerate(self.over):
            copy.wait_recv()
            for c in (0, 1):
                add_rows(self.own.at[c], self.own.at[c], self.first.at[i, c])

        @pl.when(self.place.away)
        def _():
            for copy in self.far:
                copy.start()

        @pl.when(self.place.home)
        def _():
            self.near.start()
            self.stay.start()

    def finish(self):
        for copy in self.over:
            copy.wait_send()

        @pl.when(self.place.home)
        def _():
            self.stay.wait()
            self.near.wait_send()
            self.far[0].wait_recv()

        @pl.when(self.place.away)
        def _():
            self.near.wait_recv()
            self.far[1].wait_recv()
            for copy in self.far:
                copy.wait_send()


class Deliver:
    def __init__(self, place, links, src, out):
        self.place = place
        self.cross = links.far(lambda: (src(), out, place.at(top=1, core=1)))
        self.stay = links.local(lambda: (src(), out))

    def begin(self):
        @pl.when(self.place.away)
        def _():
            self.cross.start()

        @pl.when(self.place.home)
        def _():
            self.stay.start()

    def finish(self):
        @pl.when(self.place.away)
        def _():
            self.cross.wait()

        @pl.when(self.place.home)
        def _():
            self.stay.wait()


TILE = 384
ROWS = 256


def exit_kernel(
    seq, fsdp,
    h_ref, grad_ref, w_ref, mixed_ref, vec_ref,
    dh_out, mixed_out, slots_out, vec_out,
    h_all, grads, weights, part,
    dh_give, dh_own, dh_first, dh_later, part_first, part_top, vec_val, vec_got,
    send, recv, near,
):
    place = Place(seq, fsdp)
    links = Links(send, recv, near)
    half = place.half
    others = list(range(1, place.pairs))
    seqs, _, length, depth = dh_own.shape
    rows = part.shape[3]
    dh = TokenScatter(
        place, links, dh_give, dh_out, dh_own, dh_first, dh_later, loads=False
    )
    dh_last = Deliver(place, links, lambda: dh_own.at[:, place.low], dh_out)
    mixed = Deliver(place, links, lambda: mixed_ref, mixed_out)
    loads = [
        links.local(lambda: (h_ref, h_all)),
        links.local(lambda: (grad_ref, grads)),
        links.local(lambda: (w_ref, weights)),
    ]

    def rows_of(top):
        return pl.ds(half * flip(place.top, top), half)

    def over(top, p):
        return links.far(
            lambda: (
                part.at[rows_of(top), flip(place.pair, p)],
                part_first.at[p - 1, rows_of(top)],
                place.at(pair=p),
            )
        )

    over_pairs = [[over(top, p) for p in others] for top in (0, 1)]
    cross = links.far(lambda: (part.at[rows_of(1), place.pair], part_top, place.at(top=1)))

    def row_block(l, c):
        return part.at[
            half * place.top + flip(place.low, l), place.pair, flip(place.core, c)
        ]

    def spread(l, c):
        return links.far(
            lambda: (
                row_block(l, c), slots_out.at[place.core, place.low], place.at(low=l, core=c)
            )
        )

    near_peers = [(l, c) for t, l, c in peers_of(place) if t == 0]
    slots = {p: spread(*p) for p in near_peers}
    slots[0, 0] = links.local(lambda: (row_block(0, 0), slots_out.at[place.core, place.low]))

    hops = [dict(pair=1 << i) for i in range(place.pairs.bit_length() - 1)]
    hops += [dict(top=1)] + [dict(low=b) for b in place.low_bits] + [dict(core=1)]

    def hop(i):
        return links.far(lambda: (vec_val.at[i], vec_got.at[i], place.at(**hops[i])))

    vec = [hop(i) for i in range(len(hops))]
    vec_load = links.local(lambda: (vec_ref, vec_val.at[0]))
    vec_store = links.local(lambda: (vec_val.at[len(hops)], vec_out))
    state = {"at": 0}

    def vec_next():
        i = state["at"]
        state["at"] += 1
        if i < len(hops):
            vec[i].wait_recv()
            vec_val[i + 1] = vec_val[i] + vec_got[i]
            if i + 1 < len(hops):
                vec[i + 1].start()
            else:
                vec_store.start()

    def add_pairs(top):
        for i, copy in enumerate(over_pairs[top]):
            copy.wait_recv()
            for low in range(half):
                for c in (0, 1):
                    at = half * flip(place.top, top) + low
                    ref = part.at[at, place.pair, c]
                    add_rows(ref, ref, part_first.at[i, at, c], 16)

    tiles = depth // 2 // TILE
    blocks = TILE // rows
    per_seq = fsdp

    def weight_rows(top):
        @pl.loop(0, tiles)
        def _(k):
            t = tiles * flip(place.top, top) + k
            lanes = pl.ds(pl.multiple_of(t * TILE, LANES), TILE)
            term = tr_mm(h_all[:, lanes], grads[...])
            for b in range(blocks):
                at = t * (blocks // per_seq) + b // per_seq if blocks >= per_seq else None
                part[at, b % per_seq // 2, b % 2] = term[b * rows : (b + 1) * rows].astype(BF16)
            sums = jnp.sum(term * weights[lanes, :].astype(F32), axis=1, keepdims=True)
            wide = jnp.broadcast_to(sums, (TILE, LANES))
            for i in range(TILE // LANES):
                vec_val[0, pl.ds(t * (TILE // LANES) + i, 1), :] = (
                    wide[i * LANES : (i + 1) * LANES].T[0:1, :]
                )

    def token_rows(out, side):
        per_chunk = ROWS // length
        count = half // per_chunk
        for q in range(seqs):

            @pl.loop(0, count)
            def _(k):
                at = (q * seq + half * side + k * per_chunk) * length
                term = mm_tr(grads[pl.ds(pl.multiple_of(at, LANES), ROWS), :], weights[...])
                out[q, pl.ds(k * per_chunk, per_chunk)] = term.astype(BF16).reshape(
                    per_chunk, length, depth
                )

    for copy in loads:
        copy.start()
    vec_load.start()
    meet_pair(place)
    mixed.begin()
    for copy in loads:
        copy.wait()
    vec_load.wait()
    weight_rows(1)
    for copy in over_pairs[1]:
        copy.start()
    token_rows(dh_give, 1 - place.core)
    dh.begin()
    weight_rows(0)
    for copy in over_pairs[0]:
        copy.start()
    vec[0].start()
    token_rows(dh_own, place.core)
    dh.add_cores()
    dh.send_stage(0)
    add_pairs(1)
    cross.start()
    vec_next()
    stages = len(place.low_bits)
    for i in range(stages):
        dh.add_stage(i)
        if i + 1 < stages:
            dh.send_stage(i + 1)
        else:
            dh_last.begin()
        vec_next()
    add_pairs(0)
    vec_next()
    cross.wait_recv()
    for l, c in near_peers + [(0, 0)]:
        ref = row_block(l, c)
        add_rows(ref, ref, part_top.at[flip(place.low, l), flip(place.core, c)], 16)
        slots[l, c].start()
    while state["at"] < len(hops):
        vec_next()
    for copy in slots.values():
        copy.wait()
    vec_store.wait()
    mixed.finish()
    dh_last.finish()
    dh.finish()
    cross.wait_send()
    for copy in over_pairs[0] + over_pairs[1] + vec:
        copy.wait_send()


def exit_scatter(seq, fsdp, h_all, grad_proj, w_mine, mixed, vector):
    seqs, _, length, depth = h_all.shape
    half, pairs = seq // 2, fsdp // 2
    cols = w_mine.shape[1]
    rows = depth // (seq * fsdp)
    count = seqs * seq * length
    bits = (half.bit_length() - 1) + (pairs.bit_length() - 1) + 2
    token_own = pltpu.VMEM((seqs, half, length, depth), BF16)
    tokens = jax.ShapeDtypeStruct((seqs, length, depth), BF16)
    return pl.pallas_call(
        functools.partial(exit_kernel, seq, fsdp),
        in_specs=[ANYWHERE] * 5,
        out_specs=[ANYWHERE] * 4,
        out_shape=[
            tokens,
            tokens,
            jax.ShapeDtypeStruct((2, half, rows, cols), BF16),
            jax.ShapeDtypeStruct(vector.shape, F32),
        ],
        scratch_shapes=[
            pltpu.VMEM((count, depth), BF16),
            pltpu.VMEM((count, cols), BF16),
            pltpu.VMEM((depth, cols), BF16),
            pltpu.VMEM((seq, pairs, 2, rows, cols), BF16),
            token_own, token_own, token_own,
            pltpu.VMEM((seqs, max(half - 1, 1), length, depth), BF16),
            pltpu.VMEM((max(pairs - 1, 1), seq, 2, rows, cols), BF16),
            pltpu.VMEM((half, 2, rows, cols), BF16),
            pltpu.VMEM((bits + 1,) + vector.shape, F32),
            pltpu.VMEM((bits,) + vector.shape, F32),
            pltpu.SemaphoreType.DMA((96,)),
            pltpu.SemaphoreType.DMA((96,)),
            pltpu.SemaphoreType.DMA((16,)),
        ],
        compiler_params=pltpu.CompilerParams(
            collective_id=1, has_side_effects=True, vmem_limit_bytes=60 << 20
        ),
        cost_estimate=pl.CostEstimate(
            flops=0, transcendentals=0, bytes_accessed=200_000_000
        ),
        name="exit_scatter",
    )(h_all.reshape(count, depth), grad_proj.reshape(count, cols), w_mine, mixed, vector)


def finish_kernel(
    tok_ref, cot_ref, gain_ref, dh_ref, mixed_ref, slots_ref, rows_ref,
    mixed_out, tokens_out, w_in_out, w_out_out,
):
    gain = gain_ref[...]
    for q in range(tok_ref.shape[0]):
        wide = tok_ref[q].astype(F32)
        mixed_out[q] = (wide + mixed_ref[q].astype(F32)).astype(BF16)
        scale = lax.rsqrt(jnp.mean(wide * wide, axis=-1, keepdims=True) + EPSILON)
        unit = wide * scale
        scaled = dh_ref[q].astype(F32) * gain
        tokens_out[q] = cot_ref[q].astype(F32) + scale * (
            scaled - unit * jnp.mean(scaled * unit, axis=-1, keepdims=True)
        )
    groups, _, cols = slots_ref.shape
    width = (cols - TAIL) // 2
    tail = jnp.zeros((slots_ref.shape[1], TAIL), F32)
    for g in range(groups):
        w_in_out[:, g * width : (g + 1) * width] = slots_ref[g, :, :width].astype(F32)
        w_in_out[:, INNER + g * width : INNER + (g + 1) * width] = (
            slots_ref[g, :, width : 2 * width].astype(F32)
        )
        tail = tail + slots_ref[g, :, 2 * width :].astype(F32)
    w_in_out[:, 2 * INNER :] = tail[:, : 2 * STATE + HEADS]
    w_out_out[...] = rows_ref[0].astype(F32) + rows_ref[1].astype(F32)


def finish(tokens, cotangent, gain_in, grad_h, mixed, slots, rows, shapes):
    return pl.pallas_call(
        finish_kernel,
        out_shape=[
            jax.ShapeDtypeStruct(tokens.shape, BF16),
            jax.ShapeDtypeStruct(tokens.shape, F32),
            jax.ShapeDtypeStruct(shapes[0], F32),
            jax.ShapeDtypeStruct(shapes[1], F32),
        ],
        compiler_params=pltpu.CompilerParams(vmem_limit_bytes=32 << 20),
        name="finish",
    )(tokens, cotangent, gain_in[None], grad_h, mixed, slots, rows)


def local(
    tokens, segments, gain_in, w_in, conv_w, conv_b, dt_bias, a_log, skip, gain_out, w_out,
    cotangent,
):
    steps, shards = lax.axis_size("seq"), lax.axis_size("fsdp")
    place = Place(steps, shards)
    seqs, length, _ = tokens.shape
    width = INNER // steps
    heads = HEADS // steps
    rows_in = w_in.shape[0]
    number = place.chunk

    def mine(array, size):
        return lax.dynamic_slice_in_dim(array, number * size, size, array.ndim - 1)

    wide = tokens.astype(F32)
    scale_in = lax.rsqrt(jnp.mean(wide * wide, axis=-1, keepdims=True) + EPSILON)
    normed = (wide * scale_in * gain_in).astype(BF16)
    zx = w_in[:, : 2 * INNER].reshape(rows_in, 2, steps, width).transpose(2, 0, 1, 3)
    zx = zx.reshape(steps, rows_in, 2 * width)
    tail = jnp.pad(w_in[:, 2 * INNER :], ((0, 0), (0, LANES - HEADS)))
    heads_p = jnp.stack([mine(dt_bias, heads), mine(a_log, heads)])
    lane = lax.broadcasted_iota(jnp.int32, (LANES, LANES), 1)
    source = lax.broadcasted_iota(jnp.int32, (LANES, LANES), 0)
    pick = ((lane < heads) & (source == lane + number * heads)).astype(BF16)
    consts = (
        mine(conv_w[:, :INNER], width),
        mine(conv_b[None, :INNER], width),
        conv_w[:, INNER:],
        conv_b[None, INNER:],
        jnp.pad(heads_p, ((0, 6), (0, LANES - heads))),
        pick,
        jnp.repeat(mine(skip, heads), HEAD_DIM)[None],
        mine(gain_out[None], width),
    )

    (
        proj, y, states, off_col, rem_col, off_row, h_all, w_mine, grad_yn, stats, mixed, part_out,
    ) = forward_mix(normed, zx, tail, segments, cotangent, w_out, consts, steps, shards)
    grad_proj, sums_x, sums_t, sums_h, mixed, rows = backward_mix(
        proj, off_col, off_row, rem_col, y, grad_yn, stats, states, mixed, part_out, consts,
        steps, shards,
    )

    grouped = jnp.concatenate(
        [
            sums_x[: KERNEL + 1].reshape(-1),
            sums_x[KERNEL + 2],
            jnp.sum(sums_x[KERNEL + 1].reshape(heads, HEAD_DIM), axis=-1),
            sums_h[:2, :heads].reshape(-1),
        ]
    )
    size = -(-grouped.shape[0] // LANES) * LANES
    grouped = jnp.pad(grouped, (0, size - grouped.shape[0])).reshape(1, -1, LANES)
    grouped = lax.dynamic_update_slice_in_dim(
        jnp.zeros((steps,) + grouped.shape[1:], F32), grouped, number, 0
    )
    vector = jnp.concatenate(
        [
            jnp.zeros((D // LANES, LANES), F32),
            sums_t[: KERNEL + 1].reshape(-1, LANES),
            grouped.reshape(-1, LANES),
        ]
    )
    grad_h, mixed, slots, vector = exit_scatter(
        steps, shards, h_all, grad_proj, w_mine, mixed, vector
    )
    mixed, tokens_grad, w_in_grad, w_out_grad = finish(
        tokens, cotangent, gain_in, grad_h, mixed,
        slots.reshape(steps, rows_in, 2 * width + TAIL), rows, (w_in.shape, w_out.shape),
    )

    edge = vector.shape[0] - steps * size // LANES
    everywhere = vector[:edge].reshape(-1)
    grouped = vector[edge:].reshape(steps, size)
    gain_in_grad = everywhere[:D] / gain_in
    conv_x = grouped[:, : (KERNEL + 1) * width].reshape(steps, KERNEL + 1, width)
    conv_x = conv_x.transpose(1, 0, 2).reshape(KERNEL + 1, INNER)
    conv_grads = jnp.concatenate([conv_x, everywhere[D:].reshape(KERNEL + 1, -1)], axis=1)
    rest = grouped[:, (KERNEL + 1) * width :]
    gain_out_grad = rest[:, :width].reshape(-1)
    per_head = rest[:, width : width + 3 * heads].reshape(steps, 3, heads)
    per_head = per_head.transpose(1, 0, 2).reshape(3, HEADS)
    return (
        mixed, tokens_grad, gain_in_grad, w_in_grad, conv_grads[:KERNEL], conv_grads[KERNEL],
        per_head[1], per_head[2], per_head[0], gain_out_grad, w_out_grad,
    )


def solution(mesh):
    by_token = P("fsdp", "seq", None)
    by_row = P(("seq", "fsdp"), None)
    placed = (
        by_token, P("fsdp", None), P(), by_row, P(), P(), P(), P(), P(), P(), by_row, by_token,
    )
    return jax.shard_map(
        local,
        mesh=mesh,
        in_specs=placed,
        out_specs=(by_token, by_token, P(), by_row, P(), P(), P(), P(), P(), P(), by_row),
        check_vma=False,
    )
```

```python
import functools

import jax
import jax.numpy as jnp
import numpy as np
from jax import lax
from jax.experimental import pallas as pl
from jax.experimental.pallas import tpu as pltpu
from jax.sharding import PartitionSpec as P

D = 1536
HEADS = 48
HEAD_DIM = 64
STATE = 128
KERNEL = 4
INNER = 3072
LANES = 128
HALO = 16
EPSILON = 1e-05
F32 = jnp.float32
BF16 = jnp.bfloat16


def mm(a, b):
    return jnp.dot(a.astype(BF16), b.astype(BF16), preferred_element_type=F32)


def mm_tr(a, b):
    return lax.dot_general(
        a.astype(BF16), b.astype(BF16), (((1,), (1,)), ((), ())), preferred_element_type=F32
    )


def tr_mm(a, b):
    return lax.dot_general(
        a.astype(BF16), b.astype(BF16), (((0,), (0,)), ((), ())), preferred_element_type=F32
    )


def pieces(a, count):
    out = []
    for _ in range(count - 1):
        part = a.astype(BF16)
        out.append(part)
        a = a - part.astype(F32)
    out.append(a.astype(BF16))
    return out


def ones_mm(ones, a, count):
    return sum(jnp.dot(ones, part, preferred_element_type=F32) for part in pieces(a, count))


def mm_ones(a, ones, count):
    return sum(jnp.dot(part, ones, preferred_element_type=F32) for part in pieces(a, count))


def mm_ones_tr(a, ones, count):
    return sum(
        lax.dot_general(part, ones, (((1,), (1,)), ((), ())), preferred_element_type=F32)
        for part in pieces(a, count)
    )


def iota(shape, dim):
    return lax.broadcasted_iota(jnp.int32, shape, dim)


def softplus(v):
    return jnp.maximum(v, 0.0) + jnp.log1p(jnp.exp(-jnp.abs(v)))


def sigmoid(v):
    return 1.0 / (1.0 + jnp.exp(-v))


def causal_conv(ext, current, halo, weight, bias, offset):
    length = current.shape[0]
    ext[0:HALO, :] = halo
    ext[HALO : HALO + length, :] = current
    total = bias + weight[KERNEL - 1 : KERNEL, :] * current
    for back in range(1, KERNEL):
        shifted = jnp.where(offset >= back, ext[pl.ds(HALO - back, length), :], 0.0)
        total = total + weight[KERNEL - 1 - back : KERNEL - back, :] * shifted
    return total


def head_tiles(width):
    out = []
    for start in range(0, width, LANES):
        size = min(LANES, width - start)
        heads = [start // HEAD_DIM + i for i in range(size // HEAD_DIM)]
        out.append((start, size, heads))
    return out


def masked_heads(tile, heads):
    if len(heads) == 1:
        return tile
    lane = iota(tile.shape, 1) // HEAD_DIM
    return jnp.concatenate(
        [jnp.where(lane == i, tile, jnp.zeros_like(tile)) for i in range(len(heads))], axis=0
    )


def expander(width):
    return (iota((LANES, width), 1) // HEAD_DIM == iota((LANES, width), 0)).astype(BF16)


def chunk_common(x, xh, tail, tailh, offset, params, ext_x, ext_t, width):
    wx, bx, wt, bt, heads_p, pick = params
    length = x.shape[0]
    conv_x = causal_conv(ext_x, x.astype(F32), xh.astype(F32), wx, bx, offset)
    conv_t = causal_conv(
        ext_t,
        tail[:, : 2 * STATE].astype(F32),
        tailh[:, : 2 * STATE].astype(F32),
        wt,
        bt,
        offset,
    )
    raw = jnp.dot(tail[:, 2 * STATE :], pick, preferred_element_type=F32) + heads_p[0:1, :]
    step = softplus(raw)
    decay_rate = jnp.exp(heads_p[1:2, :])
    rate = -step * decay_rate
    tril = (iota((length, length), 0) >= iota((length, length), 1)).astype(BF16)
    cumul = ones_mm(tril, rate, 3)
    spread = expander(width)
    row = iota((length, 1), 0)
    entry = jnp.where(offset > row.astype(F32), jnp.exp(cumul), 0.0)
    last_off = offset[length - 1 : length, :]
    same_last = row.astype(F32) >= (length - 1) - last_off
    to_end = jnp.where(same_last, jnp.exp(cumul[length - 1 : length, :] - cumul), 0.0)
    step_x = mm_ones(step, spread, 2)
    entry_x = mm_ones(entry, spread, 2)
    end_x = mm_ones(to_end, spread, 2)
    return conv_x, conv_t, raw, step, rate, decay_rate, cumul, spread, step_x, entry_x, end_x


def positions(segments, chunk, length):
    here = jnp.zeros((1, length), F32)
    total = segments.shape[1] // length
    rows = [segments[:, i * length : (i + 1) * length].astype(F32) for i in range(total)]
    for i in range(total):
        here = here + jnp.where(chunk == i, rows[i], 0.0)
    own = jnp.broadcast_to(here, (length, length)).T
    less = jnp.zeros((length, length), F32)
    upto = jnp.zeros((length, length), F32)
    for row in rows:
        less = less + jnp.where(row < own, 1.0, 0.0)
        upto = upto + jnp.where(row <= own, 1.0, 0.0)
    index = (chunk * length + iota((length, 1), 0)).astype(F32)
    offset = index - jnp.sum(less, axis=1, keepdims=True)
    return offset, jnp.sum(upto, axis=1, keepdims=True) - 1.0 - index


def flat_rows(ref, flat):
    rows, cols = ref.shape[-2:]
    if rows % HALO == 0:
        return ref[...].reshape(-1, cols)
    shape = ref.shape[:-2]
    for i, at in enumerate(np.ndindex(*shape)):
        flat[i * rows : (i + 1) * rows, :] = ref[at]
    return flat[...]


def forward_kernel(
    seq, fsdp,
    h_ref, zx_ref, tail_ref, seg_ref, cot_ref, ow_ref,
    wx_ref, bx_ref, wt_ref, bt_ref, hp_ref, pick_ref, skip_ref, gain_ref,
    proj_ref, y_ref, state_ref, off_ref, rem_ref, offr_ref,
    h_out, w_out, grad_out, stat_out, mixed_out, pout_out,
    h_v, w_v, w_flat, seg_v, cot_v, ow_v, ow_flat, gated_v, sums_v, sums_got, grad_v, mixed_v,
    pout_v, memory, ext_x, ext_t, last_rows, send, recv, near,
):
    seqs, _, length, width = y_ref.shape
    depth = h_v.shape[3]
    cols = proj_ref.shape[3]
    step_at = pl.program_id(0)
    place = Place(seq, fsdp)
    links = Links(send, recv, near)
    peers = peers_of(place)
    near_peers = [(l, c) for t, l, c in peers if t == 0]
    entry = Entry(place, links, h_ref, zx_ref, tail_ref, seg_ref, h_v, w_v, seg_v)
    cot = TokenGather(place, links, cot_ref, cot_v)
    w_rows = RowGather(place, links, ow_ref, ow_v)
    keep = [links.local(lambda: (h_v, h_out)), links.local(lambda: (w_v, w_out))]
    stages = len(place.low_bits)

    def send_sums(i):
        l, c = near_peers[i]
        return links.far(lambda: (sums_v, sums_got.at[i], place.at(low=l, core=c)))

    sums = [send_sums(i) for i in range(len(near_peers))]

    @pl.when(step_at == 0)
    def _():
        memory[...] = jnp.zeros_like(memory)
        last_rows[...] = jnp.zeros_like(last_rows)
        meet_pair(place)
        entry.run(cot.cross_over)
        if w_v.shape[-2] % HALO:
            flat_rows(w_v, w_flat)

    @pl.when(step_at == 1)
    def _():
        for copy in keep:
            copy.start()
        cot.begin_home()
        w_rows.begin()

    for i in range(stages):

        @pl.when(step_at == min(3 + 2 * i, seq - 1))
        def _():
            cot.pass_on(i, "home")

    @pl.when(step_at == 2)
    def _():
        cot.arrive()

    for i in range(stages):

        @pl.when(step_at == min(4 + 2 * i, seq - 1))
        def _():
            cot.pass_on(i, "away")

    @pl.when(step_at == seq - 2)
    def _():
        w_rows.forward()

    @pl.when(step_at < seq)
    def _():
        weights = flat_rows(w_v, w_flat) if w_v.shape[-2] % HALO == 0 else w_flat[...]
        proj = jnp.dot(
            h_v[:, step_at].reshape(seqs * length, depth), weights, preferred_element_type=F32
        ).astype(BF16)
        proj_ref[...] = proj.reshape(proj_ref.shape)
        params = tuple(r[...] for r in (wx_ref, bx_ref, wt_ref, bt_ref, hp_ref, pick_ref))
        for q in range(seqs):
            offset, remain = positions(seg_v[q : q + 1, :], step_at, length)
            off_ref[q, 0] = offset
            rem_ref[q, 0] = remain
            offr_ref[q, 0] = jnp.broadcast_to(offset, (length, LANES)).T[0:1, :]
            chunk_rows = proj[q * length : (q + 1) * length]
            zx, tail = chunk_rows[:, : 2 * width], chunk_rows[:, 2 * width :]
            earlier = last_rows[q]
            here = pl.ds(pl.multiple_of((q * seq + step_at) * length, length), length)
            conv_x, conv_t, _, _, _, _, cumul, _, step_x, entry_x, end_x = chunk_common(
                zx[:, width:], earlier[:, width : 2 * width], tail, earlier[:, 2 * width :], offset, params,
                ext_x.at[q], ext_t.at[q], width,
            )
            xs = conv_x * sigmoid(conv_x)
            act_t = conv_t * sigmoid(conv_t)
            bs = act_t[:, :STATE].astype(BF16)
            cs = act_t[:, STATE:].astype(BF16)
            scaled = xs * step_x
            scores = mm_tr(cs, bs)
            gap = iota((length, length), 0) - iota((length, length), 1)
            same = (gap >= 0) & (gap.astype(F32) <= offset)
            cumul_t = cumul.T
            old = memory[q]
            old_low = old.astype(BF16)
            state_ref[q, 0] = old_low
            outside = mm(cs, old_low) * entry_x + skip_ref[...] * xs
            squares = jnp.zeros((length, 1), F32)
            for start, size, heads in head_tiles(width):
                mixing = []
                for head in heads:
                    spans = cumul[:, head : head + 1] - cumul_t[head : head + 1, :]
                    decays = jnp.exp(jnp.where(same, spans, -1e30))
                    mixing.append((decays * scores).astype(BF16))
                tile = masked_heads(scaled[:, start : start + size].astype(BF16), heads)
                mix = mixing[0] if len(heads) == 1 else jnp.concatenate(mixing, axis=1)
                inside = jnp.dot(mix, tile, preferred_element_type=F32)
                y_low = (inside + outside[:, start : start + size]).astype(BF16)
                y_ref[q, 0, :, start : start + size] = y_low
                z = zx[:, start : start + size].astype(F32)
                gated = y_low.astype(F32) * (z * sigmoid(z))
                gated_v[here, start : start + size] = (
                    gated * gain_ref[:, start : start + size]
                ).astype(BF16)
                squares = squares + jnp.sum(gated * gated, axis=1, keepdims=True)
            sums_v[pl.ds(2 * (q * seq + step_at), 1), :] = jnp.broadcast_to(
                squares, (length, LANES)
            ).T[0:1, :]
            fresh = tr_mm(bs, scaled * end_x)
            memory[q] = old * entry_x[length - 1 : length, :] + fresh
            last_rows[q] = chunk_rows[length - HALO :]

    @pl.when(step_at == seq)
    def _():
        w_rows.finish()
        cot.finish()
        rows_out = flat_rows(ow_v, ow_flat)
        tile = 2 * length
        tiles = seqs * seq // 2

        @pl.loop(0, tiles)
        def _(k):
            at = pl.ds(pl.multiple_of(k * tile, tile), tile)
            cots = cot_v[k // (seq // 2), pl.ds(lax.rem(k, seq // 2) * 2, 2)].reshape(tile, depth)
            grad = mm_tr(cots, rows_out)
            grad_v[at, :] = grad
            part = jnp.sum(grad * gated_v[at, :].astype(F32), axis=1, keepdims=True)
            part = jnp.broadcast_to(part, (tile, LANES))
            for i in (0, 1):
                sums_v[pl.ds(4 * k + 2 * i + 1, 1), :] = (
                    part[i * length : (i + 1) * length].T[0:1, :]
                )

        grad_store = links.local(lambda: (grad_v, grad_out))
        grad_store.start()
        for copy in sums:
            copy.start()
        for copy in sums:
            copy.wait_recv()
        total = sums_v[...]
        for i in range(len(near_peers)):
            total = total + sums_got[i]
        is_square = lax.rem(iota(total.shape, 0), 2) == 0
        scale = lax.rsqrt(total / INNER + EPSILON)
        other = pltpu.roll(scale, 1, 0)
        stat_out[...] = jnp.where(is_square, scale, total * (other * other * other / INNER))

        @pl.loop(0, tiles)
        def _(k):
            at = pl.ds(pl.multiple_of(k * tile, tile), tile)
            scales = [
                jnp.broadcast_to(stat_out[pl.ds(4 * k + 2 * i, 1), :], (LANES, length)).T[:, 0:1]
                for i in (0, 1)
            ]
            scale_col = jnp.concatenate(scales, axis=0)
            gated = gated_v[at, :]
            mixed = jnp.dot(gated, rows_out, preferred_element_type=F32)
            mixed_v[at, :] = (mixed * scale_col).astype(BF16)
            gated_v[at, :] = (gated.astype(F32) * scale_col).astype(BF16)

        mixed_store = links.local(lambda: (mixed_v, mixed_out))
        mixed_store.start()
        pout_v[...] = tr_mm(gated_v[...], cot_v[...].reshape(-1, depth)).astype(BF16)
        pout_store = links.local(lambda: (pout_v, pout_out))
        pout_store.start()
        for copy in [grad_store, mixed_store, pout_store] + keep:
            copy.wait()
        for copy in sums:
            copy.wait_send()
        entry.finish()


def backward_kernel(
    seq, fsdp,
    zx_ref, zxh_ref, tail_ref, tailh_ref, off_ref, offr_ref, rem_ref, y_ref, grad_ref, stat_ref,
    state_ref, mixed_ref, pout_ref,
    wx_ref, bx_ref, wt_ref, bt_ref, hp_ref, pick_ref, skip_ref, gain_ref,
    out_ref, gx_ref, gt_ref, gh_ref, mixed_out, rows_out,
    memory, ext_x, ext_t, next_x, next_t,
    mix_own, mix_first, mix_later, pout_own, pout_first, send, recv, near,
):
    seqs, _, length, width = y_ref.shape
    step_at = pl.program_id(0)

    place = Place(seq, fsdp)
    links = Links(send, recv, near)
    mixed = TokenScatter(place, links, mixed_ref, mixed_out, mix_own, mix_first, mix_later)
    w_rows = RowScatter(place, links, pout_ref, rows_out, pout_own, pout_first)
    stages = len(place.low_bits)

    @pl.when(step_at == 0)
    def _():
        meet_pair(place)
        mixed.begin()
        w_rows.begin()

    @pl.when(step_at == 2)
    def _():
        mixed.add_cores()
        mixed.send_stage(0)

    @pl.when(step_at == 4)
    def _():
        w_rows.add_pairs()

    @pl.when(step_at == pl.num_programs(0) - 2)
    def _():
        mixed.add_stage(0)
        if stages > 1:
            mixed.send_stage(1)

    @pl.when(pl.program_id(0) == 0)
    def _():
        memory[...] = jnp.zeros_like(memory)
        gx_ref[...] = jnp.zeros_like(gx_ref)
        gt_ref[...] = jnp.zeros_like(gt_ref)
        gh_ref[...] = jnp.zeros_like(gh_ref)
        next_x[:, length:, :] = jnp.zeros_like(next_x[:, length:, :])
        next_t[:, length:, :] = jnp.zeros_like(next_t[:, length:, :])

    params = tuple(r[...] for r in (wx_ref, bx_ref, wt_ref, bt_ref, hp_ref, pick_ref))
    for q in range(seqs):
        offset = off_ref[q, 0]
        conv_x, conv_t, raw, step, rate, decay_rate, cumul, spread, step_x, entry_x, end_x = (
            chunk_common(
                zx_ref[q, 0, :, width:], zxh_ref[q, 0, :, width:], tail_ref[q, 0], tailh_ref[q, 0], offset,
                params, ext_x.at[q], ext_t.at[q], width,
            )
        )
        stats = jnp.broadcast_to(stat_ref[q, 0, 0:1, :], (LANES, length)).T
        slopes = jnp.broadcast_to(stat_ref[q, 0, 1:2, :], (LANES, length)).T
        scale, slope = stats[:, 0:1], slopes[:, 0:1]
        z = zx_ref[q, 0, :, :width].astype(F32)
        sig_z = sigmoid(z)
        silu_z = z * sig_z
        y = y_ref[q, 0].astype(F32)
        gated = y * silu_z
        scaled_grad = grad_ref[q, 0].astype(F32) * scale
        gx_ref[KERNEL + 2 : KERNEL + 3, :width] += jnp.sum(scaled_grad * gated, axis=0, keepdims=True)
        grad_gated = gain_ref[...] * scaled_grad - gated * slope
        dy_low = (grad_gated * silu_z).astype(BF16)
        dz = (grad_gated * y * (sig_z + silu_z * (1.0 - sig_z))).astype(BF16)
        dy = dy_low.astype(F32)

        sig_x = sigmoid(conv_x)
        xs = conv_x * sig_x
        slope_x = sig_x + xs * (1.0 - sig_x)
        sig_t = sigmoid(conv_t)
        act_t = conv_t * sig_t
        slope_t = sig_t + act_t * (1.0 - sig_t)
        bs = act_t[:, :STATE].astype(BF16)
        cs = act_t[:, STATE:].astype(BF16)
        scaled = xs * step_x
        scaled_low = scaled.astype(BF16)
        scores = mm_tr(bs, cs)
        rows, cols = iota((length, length), 0), iota((length, length), 1)
        gap = cols - rows
        same = (gap >= 0) & (gap.astype(F32) <= offr_ref[q, 0])
        strict = gap > 0
        upper = (rows >= cols).astype(BF16)
        cumul_t = cumul.T
        old = state_ref[q, 0]
        grad_state = memory[q]
        state_low = grad_state.astype(BF16)
        grad_scores = jnp.zeros((length, length), F32)
        grad_scaled = []
        inside_rows = []
        for start, size, heads in head_tiles(width):
            dy_tile = masked_heads(dy_low[:, start : start + size], heads)
            grad_mix = mm_tr(scaled_low[:, start : start + size], dy_tile)
            mixing = []
            for place, head in enumerate(heads):
                spans = cumul_t[head : head + 1, :] - cumul[:, head : head + 1]
                decays = jnp.exp(jnp.where(same, spans, -1e30))
                weighted = grad_mix[:, place * length : (place + 1) * length] * decays
                grad_scores = grad_scores + weighted
                mixing.append((decays * scores).astype(BF16))
                terms = jnp.where(strict, weighted * scores, 0.0).astype(BF16)
                sums = jnp.dot(terms, upper, preferred_element_type=F32)
                inside_rows.append(
                    jnp.sum(jnp.where(strict, sums, 0.0), axis=0, keepdims=True)
                )
            mix = mixing[0] if len(heads) == 1 else jnp.concatenate(mixing, axis=1)
            grad_scaled.append(jnp.dot(mix, dy_tile, preferred_element_type=F32))
        inside_rows.append(jnp.zeros((LANES - len(inside_rows), length), F32))
        inside = jnp.concatenate(inside_rows, axis=0).T
        from_end = mm(bs, state_low) * end_x
        grad_scaled = jnp.concatenate(grad_scaled, axis=1) + from_end
        entry_dy = dy * entry_x
        entry_dy_low = entry_dy.astype(BF16)
        out_terms = mm(cs, old) * entry_dy
        end_terms = scaled * from_end
        grad_step = mm_ones_tr(xs * grad_scaled, spread, 2)
        out_terms = mm_ones_tr(out_terms, spread, 2)
        end_terms = mm_ones_tr(end_terms, spread, 2)
        keep_row = entry_x[length - 1 : length, :]
        carried = jnp.sum(grad_state * old.astype(F32), axis=0, keepdims=True) * keep_row
        carried = mm_ones_tr(jnp.broadcast_to(carried, (8, width)), spread, 2)[0:1, :]
        triu = (cols >= rows).astype(BF16)
        below = (rows > cols).astype(BF16)
        grad_rate = inside + ones_mm(triu, out_terms, 2) + ones_mm(below, end_terms, 2) + carried
        grad_step = grad_step - decay_rate * grad_rate
        grad_raw = grad_step * sigmoid(raw)
        grad_scores_low = grad_scores.astype(BF16)
        grad_b = mm(grad_scores_low, cs) + mm_tr(scaled * end_x, state_low)
        grad_c = tr_mm(grad_scores_low, bs) + mm_tr(entry_dy_low, old)
        memory[q] = grad_state * keep_row + tr_mm(cs, entry_dy_low)
        conv_grad_x = (skip_ref[...] * dy + step_x * grad_scaled) * slope_x
        conv_grad_t = jnp.concatenate([grad_b, grad_c], axis=1) * slope_t

        remain = rem_ref[q, 0]
        results = [dz]
        for grad, ext, nxt, weight, sums in (
            (conv_grad_x, ext_x.at[q], next_x.at[q], params[0], gx_ref),
            (conv_grad_t, ext_t.at[q], next_t.at[q], params[2], gt_ref),
        ):
            columns = grad.shape[1]
            current = ext[pl.ds(HALO, length), :]
            sums[KERNEL : KERNEL + 1, :columns] += jnp.sum(grad, axis=0, keepdims=True)
            sums[KERNEL - 1 : KERNEL, :columns] += jnp.sum(grad * current, axis=0, keepdims=True)
            nxt[0:length, :] = grad
            total = weight[KERNEL - 1 : KERNEL, :] * grad
            for back in range(1, KERNEL):
                tap = KERNEL - 1 - back
                shifted = jnp.where(offset >= back, ext[pl.ds(HALO - back, length), :], 0.0)
                sums[tap : tap + 1, :columns] += jnp.sum(grad * shifted, axis=0, keepdims=True)
                ahead = jnp.where(remain >= back, nxt[pl.ds(back, length), :], 0.0)
                total = total + weight[tap : tap + 1, :] * ahead
            nxt[length:, :] = grad[0:HALO, :]
            results.append(total.astype(BF16))
        results.append(mm_tr(grad_raw, params[5]).astype(BF16))
        gx_ref[KERNEL + 1 : KERNEL + 2, :width] += jnp.sum(dy * xs, axis=0, keepdims=True)
        gh_ref[0:1, :] += jnp.sum(grad_raw, axis=0, keepdims=True)
        gh_ref[1:2, :] += jnp.sum(grad_rate * rate, axis=0, keepdims=True)
        out_ref[q, 0, :, : 2 * width] = jnp.concatenate(results[:2], axis=1)
        out_ref[q, 0, :, 2 * width : 2 * width + 2 * STATE] = results[2]
        out_ref[q, 0, :, 2 * width + 2 * STATE :] = results[3]

    @pl.when(step_at == pl.num_programs(0) - 1)
    def _():
        for stage in range(1, stages):
            mixed.add_stage(stage)
            if stage + 1 < stages:
                mixed.send_stage(stage + 1)
        mixed.store()
        w_rows.finish()
        mixed.finish()


TAIL = 2 * STATE + LANES
AXES = ("seq", "fsdp")
MESH = pl.DeviceIdType.MESH
ANYWHERE = pl.BlockSpec(memory_space=pl.ANY)


def lane_rows(width):
    return -(-width // LANES)


def sum_rows(width, seq):
    shared = D // LANES + (KERNEL + 1) * 2 * STATE // LANES
    group = (KERNEL + 3) * lane_rows(width) + 2
    return shared, group, -(-(shared + seq * group) // 8) * 8


def whole_spec(shape):
    return pl.BlockSpec(shape, lambda i: (0,) * len(shape))


def chunk_specs(seqs, steps, length, reverse):
    def place(i):
        return steps - 1 - i if reverse else i

    def block(cols, column=0, rows=length):
        return pl.BlockSpec((seqs, 1, rows, cols), lambda i: (0, place(i), 0, column))

    def before(cols, column=0):
        return pl.BlockSpec(
            (seqs, 1, HALO, cols),
            lambda i: (0, jnp.maximum(place(i) - 1, 0), length // HALO - 1, column),
        )

    return block, before


def forward_mix(normed, zx, tail, segments, cotangent, out_w, consts, seq, fsdp):
    seqs, length, depth = normed.shape
    rows = tail.shape[0]
    cols = zx.shape[2] + TAIL
    width = zx.shape[2] // 2
    pairs = fsdp // 2
    count = seqs * seq * length

    def block(columns, height=length):
        return pl.BlockSpec(
            (seqs, 1, height, columns), lambda i: (0, jnp.minimum(i, seq - 1), 0, 0)
        )

    def blocks(columns, kind, height=length):
        return jax.ShapeDtypeStruct((seqs, seq, height, columns), kind)

    w_shape = (seq, pairs, 2, rows, cols)
    out_shape = (pairs, 2) + out_w.shape
    sums = (seqs * seq * 2, length)
    flat = 8 if rows % HALO == 0 else depth
    flat_out = 8 if out_w.shape[0] % HALO == 0 else width
    outs = pl.pallas_call(
        functools.partial(forward_kernel, seq, fsdp),
        grid=(seq + 1,),
        in_specs=[ANYWHERE] * 6 + [whole_spec(v.shape) for v in consts],
        out_specs=[
            block(cols), block(width), block(width, STATE), block(1), block(1), block(length, 1),
            ANYWHERE, ANYWHERE, ANYWHERE, whole_spec(sums), ANYWHERE, ANYWHERE,
        ],
        out_shape=[
            blocks(cols, BF16), blocks(width, BF16), blocks(width, BF16, STATE),
            blocks(1, F32), blocks(1, F32), blocks(length, F32, 1),
            blocks(depth, BF16),
            jax.ShapeDtypeStruct(w_shape, BF16),
            jax.ShapeDtypeStruct((count, width), F32),
            jax.ShapeDtypeStruct(sums, F32),
            jax.ShapeDtypeStruct((count, depth), BF16),
            jax.ShapeDtypeStruct((width, depth), BF16),
        ],
        scratch_shapes=[
            pltpu.VMEM((seqs, seq, length, depth), BF16),
            pltpu.VMEM(w_shape, BF16),
            pltpu.VMEM((flat, cols), BF16),
            pltpu.VMEM(segments.shape, segments.dtype),
            pltpu.VMEM((seqs, seq, length, depth), BF16),
            pltpu.VMEM(out_shape, BF16),
            pltpu.VMEM((flat_out, depth), BF16),
            pltpu.VMEM((count, width), BF16),
            pltpu.VMEM(sums, F32),
            pltpu.VMEM((seq - 1,) + sums, F32),
            pltpu.VMEM((count, width), F32),
            pltpu.VMEM((count, depth), BF16),
            pltpu.VMEM((width, depth), BF16),
            pltpu.VMEM((seqs, STATE, width), F32),
            pltpu.VMEM((seqs, HALO + length, width), F32),
            pltpu.VMEM((seqs, HALO + length, 2 * STATE), F32),
            pltpu.VMEM((seqs, HALO, cols), BF16),
            pltpu.SemaphoreType.DMA((320,)),
            pltpu.SemaphoreType.DMA((320,)),
            pltpu.SemaphoreType.DMA((24,)),
        ],
        compiler_params=pltpu.CompilerParams(
            dimension_semantics=("arbitrary",), vmem_limit_bytes=60 << 20, collective_id=0,
            has_side_effects=True,
        ),
        cost_estimate=pl.CostEstimate(
            flops=30_000_000_000, transcendentals=0, bytes_accessed=60_000_000
        ),
        name="mix_forward",
    )(normed, zx, tail, segments, cotangent, out_w, *consts)
    proj, y, states, off_col, rem_col, off_row, h_all, w_mine, grad_yn, stats, mixed, part = outs
    shape = (seqs, seq, length)
    return (
        proj, y, states, off_col, rem_col, off_row, h_all, w_mine.reshape(depth, cols),
        grad_yn.reshape(shape + (width,)), stats.reshape(seqs, seq, 2, length),
        mixed.reshape(shape + (depth,)), part.reshape(out_shape),
    )


def backward_mix(
    proj, off_col, off_row, rem_col, y, grad_yn, stats, states, mixed, part_out, consts, seq, fsdp
):
    seqs, steps, length, cols = proj.shape
    depth = mixed.shape[3]
    width = (cols - TAIL) // 2
    block, before = chunk_specs(seqs, steps, length, True)
    tail_at = 2 * width // TAIL
    half, pairs = seq // 2, fsdp // 2
    rows_out = part_out.shape[2]
    sums = [(8, lane_rows(width) * LANES), (8, 2 * STATE), (8, LANES)]
    token_own = pltpu.VMEM((seqs, half, length, depth), BF16)
    return pl.pallas_call(
        functools.partial(backward_kernel, seq, fsdp),
        grid=(steps,),
        in_specs=[
            block(2 * width), before(2 * width), block(TAIL, tail_at), before(TAIL, tail_at),
            block(1), block(length, 0, 1), block(1), block(width), block(width),
            block(length, 0, 2), block(width, 0, STATE), ANYWHERE, ANYWHERE,
        ]
        + [whole_spec(v.shape) for v in consts],
        out_specs=[block(cols)] + [whole_spec(v) for v in sums] + [ANYWHERE, ANYWHERE],
        scratch_shapes=[
            pltpu.VMEM((seqs, STATE, width), F32),
            pltpu.VMEM((seqs, HALO + length, width), F32),
            pltpu.VMEM((seqs, HALO + length, 2 * STATE), F32),
            pltpu.VMEM((seqs, length + HALO, width), F32),
            pltpu.VMEM((seqs, length + HALO, 2 * STATE), F32),
            token_own, token_own, pltpu.VMEM((seqs, max(half - 1, 1), length, depth), BF16),
            pltpu.VMEM((2, rows_out, depth), BF16),
            pltpu.VMEM((max(pairs - 1, 1), 2, rows_out, depth), BF16),
            pltpu.SemaphoreType.DMA((64,)),
            pltpu.SemaphoreType.DMA((64,)),
            pltpu.SemaphoreType.DMA((16,)),
        ],
        out_shape=[jax.ShapeDtypeStruct(proj.shape, BF16)]
        + [jax.ShapeDtypeStruct(v, F32) for v in sums]
        + [
            jax.ShapeDtypeStruct((seqs, length, depth), BF16),
            jax.ShapeDtypeStruct((2, rows_out, depth), BF16),
        ],
        compiler_params=pltpu.CompilerParams(
            dimension_semantics=("arbitrary",), vmem_limit_bytes=56 << 20, collective_id=3,
            has_side_effects=True,
        ),
        cost_estimate=pl.CostEstimate(
            flops=steps * seqs * 2_000_000_000, transcendentals=0, bytes_accessed=16_000_000
        ),
        name="mix_backward",
    )(
        proj, proj, proj, proj, off_col, off_row, rem_col, y, grad_yn, stats, states, mixed,
        part_out, *consts,
    )


class Place:
    def __init__(self, seq, fsdp):
        self.seq, self.fsdp = seq, fsdp
        self.half, self.pairs = seq // 2, fsdp // 2
        s, f = lax.axis_index("seq"), lax.axis_index("fsdp")
        self.s, self.f = s, f
        self.top, self.low = s // self.half, lax.rem(s, self.half)
        self.core, self.pair = lax.rem(f, 2), f // 2
        self.home = self.core == self.top
        self.away = self.core != self.top
        self.chunk = self.low + self.half * self.core
        self.low_bits = [1 << i for i in range(self.half.bit_length() - 1)]

    def at(self, top=0, low=0, pair=0, core=0):
        return (
            flip(self.top, top) * self.half + flip(self.low, low),
            flip(self.pair, pair) * 2 + flip(self.core, core),
        )

    def bits_for(self, q):
        return self.low_bits if q % 2 == 0 else self.low_bits[::-1]


def flip(index, bits):
    for i in range(bits.bit_length()):
        if bits >> i & 1:
            bit = lax.rem(index // (1 << i), 2)
            index = index + (1 << i) * (1 - 2 * bit)
    return index


class Copy:
    def __init__(self, make):
        self.make = make

    def start(self):
        self.make().start()
        return self

    def wait(self):
        self.make().wait()

    def wait_send(self):
        self.make().wait_send()

    def wait_recv(self):
        self.make().wait_recv()


class Links:
    def __init__(self, send, recv, near):
        self.send, self.recv, self.near = send, recv, near
        self.far_count = self.near_count = 0

    def far(self, make):
        i = self.far_count
        self.far_count += 1

        def build():
            src, dst, device = make()
            return pltpu.make_async_remote_copy(
                src_ref=src, dst_ref=dst, send_sem=self.send.at[i], recv_sem=self.recv.at[i],
                device_id=device, device_id_type=MESH,
            )

        return Copy(build)

    def local(self, make):
        i = self.near_count
        self.near_count += 1
        return Copy(lambda: pltpu.make_async_copy(*make(), self.near.at[i]))


def meet(devices):
    barrier = pltpu.get_barrier_semaphore()
    for device in devices:
        pl.semaphore_signal(barrier, inc=1, device_id=device, device_id_type=MESH)
    pl.semaphore_wait(barrier, len(devices))


def meet_pair(place):
    meet(
        [place.at(top=t, low=l, core=c) for t, l, c in peers_of(place)]
        + [place.at(pair=p) for p in range(1, place.pairs)]
    )


def peers_of(place):
    out = []
    for top in (0, 1):
        for low in range(place.half):
            for core in (0, 1):
                if (top, low, core) != (0, 0, 0):
                    out.append((top, low, core))
    return out


class TokenGather:
    def __init__(self, place, links, src, dst):
        self.place, self.src, self.dst = place, src, dst
        seqs = src.shape[0]

        def over(q):
            return links.far(
                lambda: (src.at[q], dst.at[q, place.s], place.at(top=1, core=1))
            )

        self.cross = [over(q) for q in range(seqs)]
        self.stay = links.local(lambda: (src, dst.at[:, place.s]))
        self.share = [[] for _ in range(seqs)]
        self.stages = []
        held = [[0] for _ in range(seqs)]
        for q in range(seqs):
            self.share[q].append([self.copy(links, q, low, core=1) for low in held[q]])
        for i in range(len(place.low_bits)):
            stage = []
            for q in range(seqs):
                bit = place.bits_for(q)[i]
                stage.append([self.copy(links, q, low, low_bit=bit) for low in held[q]])
                fresh = [low ^ bit for low in held[q]]
                held[q] = held[q] + fresh
                self.share[q].append([self.copy(links, q, low, core=1) for low in fresh])
            self.stages.append(stage)

    def copy(self, links, q, low, low_bit=0, core=0):
        def make():
            place = self.place
            ref = self.dst.at[q, flip(place.low, low) + place.half * place.core]
            return ref, ref, place.at(low=low_bit, core=core)

        return links.far(make)

    def begin(self):
        self.cross_over()
        self.begin_home()

    def cross_over(self):
        @pl.when(self.place.away)
        def _():
            for copy in self.cross:
                copy.start()

    def begin_home(self):
        @pl.when(self.place.home)
        def _():
            self.stay.start()
            self.stay.wait()
            self.send_stage(0)

    def arrive(self):
        @pl.when(self.place.away)
        def _():
            for copy in self.cross:
                copy.wait_recv()
            self.send_stage(0)

    def send_stage(self, i):
        for q in range(len(self.share)):
            for copy in self.stages[i][q] + self.share[q][i]:
                copy.start()

    def pass_on(self, i, role):
        @pl.when(self.place.home if role == "home" else self.place.away)
        def _():
            for q in range(len(self.share)):
                for copy in self.stages[i][q]:
                    copy.wait_recv()
                for copy in (self.stages[i + 1][q] if i + 1 < len(self.stages) else []):
                    copy.start()
                for copy in self.share[q][i + 1]:
                    copy.start()

    def finish(self):
        for share in self.share:
            for copies in share:
                for copy in copies:
                    copy.wait()
        for stage in self.stages:
            for copies in stage:
                for copy in copies:
                    copy.wait_send()

        @pl.when(self.place.away)
        def _():
            for copy in self.cross:
                copy.wait_send()


class RowGather:
    def __init__(self, place, links, src, dst):
        self.place = place
        pairs = range(1, place.pairs)

        def slot():
            return dst.at[place.pair, place.core]

        self.stay = links.local(lambda: (src, slot()))
        self.to_home = links.far(lambda: (src, slot(), place.at(core=1)))
        self.to_near = links.far(lambda: (src, slot(), place.at(top=1)))
        self.to_far = links.far(lambda: (src, slot(), place.at(top=1, core=1)))

        def forward(c, p):
            return links.far(
                lambda: (dst.at[place.pair, c], dst.at[place.pair, c], place.at(pair=p))
            )

        self.forwards = [forward(c, p) for c in (0, 1) for p in pairs]

    def begin(self):
        @pl.when(self.place.home)
        def _():
            self.stay.start()
            self.to_near.start()

        @pl.when(self.place.away)
        def _():
            self.to_home.start()
            self.to_far.start()

    def forward(self):
        @pl.when(self.place.home)
        def _():
            self.stay.wait()
            self.to_home.wait_recv()

        @pl.when(self.place.away)
        def _():
            self.to_near.wait_recv()
            self.to_far.wait_recv()

        for copy in self.forwards:
            copy.start()

    def finish(self):
        for copy in self.forwards:
            copy.wait()

        @pl.when(self.place.home)
        def _():
            self.to_near.wait_send()

        @pl.when(self.place.away)
        def _():
            self.to_home.wait_send()
            self.to_far.wait_send()


class Entry:
    def __init__(self, place, links, h_ref, zx_ref, tail_ref, seg_ref, h_v, w_v, seg_v):
        self.place = place
        cols = zx_ref.shape[2]
        self.peers = peers = peers_of(place)
        others = range(1, place.pairs)
        self.tokens = TokenGather(place, links, h_ref, h_v)

        def block(t=0, l=0, c=0):
            s, f = place.at(top=t, low=l, core=c)
            return w_v.at[s, place.pair, lax.rem(f, 2)]

        def columns(ref):
            return ref.at[:, pl.ds(0, cols)]

        def tail_of(ref):
            return ref.at[:, pl.ds(cols, TAIL)]

        def send_zx(t, l, c):
            group = flip(place.core, c) * place.half + flip(place.low, l)
            return zx_ref.at[group], columns(block()), place.at(top=t, low=l, core=c)

        self.zx = {p: links.far(functools.partial(send_zx, *p)) for p in peers}
        self.own = [
            links.local(lambda: (zx_ref.at[place.chunk], columns(block()))),
            links.local(lambda: (tail_ref, tail_of(block()))),
        ]
        self.tail_cross = links.far(lambda: (tail_ref, tail_of(block()), place.at(top=1)))
        self.near_peers = [(l, c) for t, l, c in peers if t == 0]

        def send_tail(l, c):
            return tail_ref, tail_of(block()), place.at(low=l, core=c)

        def send_other(l, c):
            return tail_of(block(1)), tail_of(block(1)), place.at(low=l, core=c)

        self.tails = {p: links.far(functools.partial(send_tail, *p)) for p in self.near_peers}
        self.tails_more = {
            p: links.far(functools.partial(send_other, *p)) for p in self.near_peers
        }
        self.seg_send = links.far(lambda: (seg_ref, seg_v, place.at(core=1)))
        self.seg_keep = links.local(lambda: (seg_ref, seg_v))

        def send_on(t, l, c, p):
            return block(t, l, c), block(t, l, c), place.at(pair=p)

        self.forwards = {
            p: [links.far(functools.partial(send_on, *p, other)) for other in others]
            for p in [(0, 0, 0)] + peers
        }

    def run(self, then):
        tokens, zx, forwards = self.tokens, self.zx, self.forwards
        stages = len(self.place.low_bits)
        far_peers = [p for p in self.peers if p[0] == 1]
        tokens.begin()
        self.tail_cross.start()
        for copy in self.own:
            copy.start()
        for p in self.near_peers:
            zx[0, *p].start()
            self.tails[p].start()

        @pl.when(self.place.home)
        def _():
            self.seg_send.start()
            self.seg_keep.start()

        for copy in self.own:
            copy.wait()
        for copy in forwards[0, 0, 0]:
            copy.start()
        self.tail_cross.wait_recv()
        for p in self.near_peers:
            self.tails_more[p].start()
        tokens.pass_on(0, "home")
        for p in self.near_peers:
            zx[0, *p].wait_recv()
            self.tails[p].wait_recv()
            for copy in forwards[0, *p]:
                copy.start()
        for p in far_peers:
            zx[p].start()
        for i in range(1, stages):
            tokens.pass_on(i, "home")
        tokens.arrive()
        for p in self.near_peers:
            self.tails_more[p].wait_recv()
        for i in range(stages):
            tokens.pass_on(i, "away")
            at, to = (len(far_peers) * k // stages for k in (i, i + 1))
            for p in far_peers[at:to]:
                zx[p].wait_recv()
                for copy in forwards[p]:
                    copy.start()
        then()

        @pl.when(self.place.home)
        def _():
            self.seg_keep.wait()
            self.seg_send.wait_send()

        @pl.when(self.place.away)
        def _():
            self.seg_send.wait_recv()

        tokens.finish()
        for p in forwards:
            for copy in forwards[p]:
                copy.wait()

    def finish(self):
        self.tail_cross.wait_send()
        for group in (self.zx, self.tails, self.tails_more):
            for copy in group.values():
                copy.wait_send()


def add_rows(out, left, right, rows=32):
    total = left.shape[0]
    step = next((size for size in (rows, 16) if total % size == 0), total)

    if step == total:
        out[...] = (left[...].astype(F32) + right[...].astype(F32)).astype(out.dtype)
        return

    @pl.loop(0, total // step)
    def _(i):
        at = pl.ds(pl.multiple_of(i * step, step), step)
        out[at] = (left[at].astype(F32) + right[at].astype(F32)).astype(out.dtype)


class TokenScatter:
    def __init__(self, place, links, src, out, own, first, later, loads=True):
        self.place = place
        self.out, self.own, self.first, self.later = out, own, first, later
        self.seqs = src.shape[0]
        half = place.half

        def give(q):
            def make():
                part = src.at[q, pl.ds(half * (1 - place.core), half)] if loads else src.at[q]
                return part, first.at[q], place.at(core=1)

            return links.far(make)

        def keep(q):
            return links.local(
                lambda: (src.at[q, pl.ds(half * place.core, half)], own.at[q])
            )

        self.cores = [give(q) for q in range(self.seqs)]
        self.loads = [keep(q) for q in range(self.seqs)] if loads else []
        self.stages = [[] for _ in place.low_bits]
        for q in range(self.seqs):
            live, slot = list(range(half)), 0
            for i, bit in enumerate(place.bits_for(q)[::-1]):
                for low in [low for low in live if low & bit]:
                    self.stages[i].append((self.copy(links, q, low, slot, bit), q, low ^ bit, slot))
                    slot += 1
                live = [low for low in live if not low & bit]
        self.stay = links.local(lambda: (own.at[:, place.low], out))

    def copy(self, links, q, low, slot, bit):
        return links.far(
            lambda: (
                self.own.at[q, flip(self.place.low, low)], self.later.at[q, slot],
                self.place.at(low=bit),
            )
        )

    def begin(self):
        for copy in self.cores + self.loads:
            copy.start()

    def add_cores(self):
        for q in range(self.seqs):
            if self.loads:
                self.loads[q].wait()
            self.cores[q].wait_recv()
            for low in range(self.place.half):
                add_rows(self.own.at[q, low], self.own.at[q, low], self.first.at[q, low])

    def send_stage(self, i):
        for copy, _, _, _ in self.stages[i]:
            copy.start()

    def add_stage(self, i):
        for copy, q, low, slot in self.stages[i]:
            copy.wait_recv()
            ref = self.own.at[q, flip(self.place.low, low)]
            add_rows(ref, ref, self.later.at[q, slot])

    def store(self):
        self.stay.start()
        self.stay.wait()

    def finish(self):
        for copy in self.cores:
            copy.wait_send()
        for stage in self.stages:
            for copy, _, _, _ in stage:
                copy.wait_send()


class RowScatter:
    def __init__(self, place, links, src, out, own, first):
        self.place, self.own, self.first = place, own, first

        def over(p):
            return links.far(
                lambda: (src.at[flip(place.pair, p)], first.at[p - 1], place.at(pair=p))
            )

        def far(c):
            return links.far(
                lambda: (own.at[flip(place.core, c)], out.at[1], place.at(top=1, core=c))
            )

        self.over = [over(p) for p in range(1, place.pairs)]
        self.load = links.local(lambda: (src.at[place.pair], own))
        self.far = [far(0), far(1)]
        self.near = links.far(lambda: (own.at[1 - place.core], out.at[0], place.at(core=1)))
        self.stay = links.local(lambda: (own.at[place.core], out.at[0]))

    def begin(self):
        self.load.start()
        for copy in self.over:
            copy.start()

    def add_pairs(self):
        self.load.wait()
        for i, copy in enumerate(self.over):
            copy.wait_recv()
            for c in (0, 1):
                add_rows(self.own.at[c], self.own.at[c], self.first.at[i, c])

        @pl.when(self.place.away)
        def _():
            for copy in self.far:
                copy.start()

        @pl.when(self.place.home)
        def _():
            self.near.start()
            self.stay.start()

    def finish(self):
        for copy in self.over:
            copy.wait_send()

        @pl.when(self.place.home)
        def _():
            self.stay.wait()
            self.near.wait_send()
            self.far[0].wait_recv()

        @pl.when(self.place.away)
        def _():
            self.near.wait_recv()
            self.far[1].wait_recv()
            for copy in self.far:
                copy.wait_send()


class Deliver:
    def __init__(self, place, links, src, out):
        self.place = place
        self.cross = links.far(lambda: (src(), out, place.at(top=1, core=1)))
        self.stay = links.local(lambda: (src(), out))

    def begin(self):
        @pl.when(self.place.away)
        def _():
            self.cross.start()

        @pl.when(self.place.home)
        def _():
            self.stay.start()

    def finish(self):
        @pl.when(self.place.away)
        def _():
            self.cross.wait()

        @pl.when(self.place.home)
        def _():
            self.stay.wait()


TILE = 384
ROWS = 256


def exit_kernel(
    seq, fsdp,
    h_ref, grad_ref, w_ref, mixed_ref, gx_ref, gt_ref, gh_ref,
    dh_out, mixed_out, slots_out, vec_out,
    h_all, grads, weights, part,
    dh_give, dh_own, dh_first, dh_later, part_first, part_top, vec_val, vec_got,
    send, recv, near,
):
    place = Place(seq, fsdp)
    links = Links(send, recv, near)
    half = place.half
    others = list(range(1, place.pairs))
    seqs, _, length, depth = dh_own.shape
    rows = part.shape[3]
    width = (weights.shape[1] - TAIL) // 2
    dh = TokenScatter(
        place, links, dh_give, dh_out, dh_own, dh_first, dh_later, loads=False
    )
    dh_last = Deliver(place, links, lambda: dh_own.at[:, place.low], dh_out)
    mixed = Deliver(place, links, lambda: mixed_ref, mixed_out)
    loads = [
        links.local(lambda: (h_ref, h_all)),
        links.local(lambda: (grad_ref, grads)),
        links.local(lambda: (w_ref, weights)),
    ]

    tiles = depth // 2 // TILE
    high = half // tiles

    def rows_of(top, k):
        return pl.ds(half * flip(place.top, top) + k * high, high)

    def over(top, k, p):
        return links.far(
            lambda: (
                part.at[rows_of(top, k), flip(place.pair, p)],
                part_first.at[p - 1, rows_of(top, k)],
                place.at(pair=p),
            )
        )

    def crossing(k):
        return links.far(
            lambda: (
                part.at[rows_of(1, k), place.pair], part_top.at[pl.ds(k * high, high)],
                place.at(top=1),
            )
        )

    over_pairs = [[[over(top, k, p) for p in others] for k in range(tiles)] for top in (0, 1)]
    cross = [crossing(k) for k in range(tiles)]

    def row_block(l, c):
        return part.at[
            half * place.top + flip(place.low, l), place.pair, flip(place.core, c)
        ]

    def spread(l, c):
        return links.far(
            lambda: (
                row_block(l, c), slots_out.at[place.core, place.low], place.at(low=l, core=c)
            )
        )

    near_peers = [(l, c) for t, l, c in peers_of(place) if t == 0]
    slots = {p: spread(*p) for p in near_peers}
    slots[0, 0] = links.local(lambda: (row_block(0, 0), slots_out.at[place.core, place.low]))

    hops = [dict(pair=1 << i) for i in range(place.pairs.bit_length() - 1)]
    hops += [dict(top=1)] + [dict(low=b) for b in place.low_bits] + [dict(core=1)]

    def hop(i):
        return links.far(lambda: (vec_val.at[i], vec_got.at[i], place.at(**hops[i])))

    vec = [hop(i) for i in range(len(hops))]
    vec_store = links.local(lambda: (vec_val.at[len(hops)], vec_out))
    state = {"at": 0}

    def vec_next():
        i = state["at"]
        state["at"] += 1
        if i < len(hops):
            vec[i].wait_recv()
            vec_val[i + 1] = vec_val[i] + vec_got[i]
            if i + 1 < len(hops):
                vec[i + 1].start()
            else:
                vec_store.start()

    def add_pairs(top, k):
        for i, copy in enumerate(over_pairs[top][k]):
            copy.wait_recv()
            for low in range(high):
                for c in (0, 1):
                    at = half * flip(place.top, top) + k * high + low
                    ref = part.at[at, place.pair, c]
                    add_rows(ref, ref, part_first.at[i, at, c], 16)

    blocks = TILE // rows

    def weight_rows(top, k):
        t = tiles * flip(place.top, top) + k
        lanes = pl.ds(pl.multiple_of(t * TILE, LANES), TILE)
        term = tr_mm(h_all[:, lanes], grads[...])
        for b in range(blocks):
            at = t * (blocks // fsdp) + b // fsdp
            part[at, b % fsdp // 2, b % 2] = term[b * rows : (b + 1) * rows].astype(BF16)
        sums = jnp.sum(term * weights[lanes, :].astype(F32), axis=1, keepdims=True)
        wide = jnp.broadcast_to(sums, (TILE, LANES))
        for i in range(TILE // LANES):
            vec_val[0, pl.ds(t * (TILE // LANES) + i, 1), :] = (
                wide[i * LANES : (i + 1) * LANES].T[0:1, :]
            )
        for copy in over_pairs[top][k]:
            copy.start()

    def place_sums():
        shared, group, _ = sum_rows(width, seq)
        vec_val[0] = jnp.zeros_like(vec_val[0])
        at = D // LANES
        for tap in range(KERNEL + 1):
            for j in range(2 * STATE // LANES):
                vec_val[0, at : at + 1, :] = gt_ref[
                    tap : tap + 1, j * LANES : (j + 1) * LANES
                ]
                at += 1
        at = shared + place.chunk * group
        pieces_of = [
            gx_ref[line : line + 1, j * LANES : (j + 1) * LANES]
            for line in range(KERNEL + 3)
            for j in range(lane_rows(width))
        ] + [gh_ref[0:1, :], gh_ref[1:2, :]]
        for i, piece in enumerate(pieces_of):
            vec_val[0, pl.ds(at + i, 1), :] = piece

    def token_rows(out, side):
        per_chunk = ROWS // length
        count = half // per_chunk
        for q in range(seqs):

            @pl.loop(0, count)
            def _(k):
                at = (q * seq + half * side + k * per_chunk) * length
                term = mm_tr(grads[pl.ds(pl.multiple_of(at, LANES), ROWS), :], weights[...])
                out[q, pl.ds(k * per_chunk, per_chunk)] = term.astype(BF16).reshape(
                    per_chunk, length, depth
                )

    for copy in loads:
        copy.start()
    place_sums()
    meet_pair(place)
    mixed.begin()
    for copy in loads:
        copy.wait()
    token_rows(dh_give, 1 - place.core)
    dh.begin()
    for k in range(tiles):
        weight_rows(1, k)
    token_rows(dh_own, place.core)
    dh.add_cores()
    dh.send_stage(0)
    add_pairs(1, 0)
    cross[0].start()
    for k in range(tiles):
        weight_rows(0, k)
    vec[0].start()
    for k in range(1, tiles):
        add_pairs(1, k)
        cross[k].start()
    stages = len(place.low_bits)
    for i in range(stages):
        dh.add_stage(i)
        if i + 1 < stages:
            dh.send_stage(i + 1)
        else:
            dh_last.begin()
        vec_next()
    for k in range(tiles):
        add_pairs(0, k)
    vec_next()
    for copy in cross:
        copy.wait_recv()
    for l, c in near_peers + [(0, 0)]:
        ref = row_block(l, c)
        add_rows(ref, ref, part_top.at[flip(place.low, l), flip(place.core, c)], 16)
        slots[l, c].start()
    while state["at"] < len(hops):
        vec_next()
    for copy in slots.values():
        copy.wait()
    vec_store.wait()
    mixed.finish()
    dh_last.finish()
    dh.finish()
    for copy in cross + vec + [c for top in over_pairs for tile in top for c in tile]:
        copy.wait_send()


def exit_scatter(seq, fsdp, h_all, grad_proj, w_mine, mixed, sums):
    seqs, _, length, depth = h_all.shape
    half, pairs = seq // 2, fsdp // 2
    cols = w_mine.shape[1]
    rows = depth // (seq * fsdp)
    count = seqs * seq * length
    vector = (sum_rows((cols - TAIL) // 2, seq)[2], LANES)
    bits = (half.bit_length() - 1) + (pairs.bit_length() - 1) + 2
    token_own = pltpu.VMEM((seqs, half, length, depth), BF16)
    tokens = jax.ShapeDtypeStruct((seqs, length, depth), BF16)
    return pl.pallas_call(
        functools.partial(exit_kernel, seq, fsdp),
        in_specs=[ANYWHERE] * 4 + [pl.BlockSpec(memory_space=pltpu.VMEM)] * 3,
        out_specs=[ANYWHERE] * 4,
        out_shape=[
            tokens,
            tokens,
            jax.ShapeDtypeStruct((2, half, rows, cols), BF16),
            jax.ShapeDtypeStruct(vector, F32),
        ],
        scratch_shapes=[
            pltpu.VMEM((count, depth), BF16),
            pltpu.VMEM((count, cols), BF16),
            pltpu.VMEM((depth, cols), BF16),
            pltpu.VMEM((seq, pairs, 2, rows, cols), BF16),
            token_own, token_own, token_own,
            pltpu.VMEM((seqs, max(half - 1, 1), length, depth), BF16),
            pltpu.VMEM((max(pairs - 1, 1), seq, 2, rows, cols), BF16),
            pltpu.VMEM((half, 2, rows, cols), BF16),
            pltpu.VMEM((bits + 1,) + vector, F32),
            pltpu.VMEM((bits,) + vector, F32),
            pltpu.SemaphoreType.DMA((96,)),
            pltpu.SemaphoreType.DMA((96,)),
            pltpu.SemaphoreType.DMA((16,)),
        ],
        compiler_params=pltpu.CompilerParams(
            collective_id=1, has_side_effects=True, vmem_limit_bytes=60 << 20
        ),
        cost_estimate=pl.CostEstimate(
            flops=0, transcendentals=0, bytes_accessed=200_000_000
        ),
        name="exit_scatter",
    )(h_all.reshape(count, depth), grad_proj.reshape(count, cols), w_mine, mixed, *sums)


def finish_kernel(
    seq,
    tok_ref, cot_ref, gain_ref, dh_ref, mixed_ref, slots_ref, rows_ref, vec_ref,
    mixed_out, tokens_out, gain_in_out, w_in_out, conv_w_out, conv_b_out, heads_out, gain_out_out,
    w_out_out,
):
    gain = gain_ref[...]
    for q in range(tok_ref.shape[0]):
        wide = tok_ref[q].astype(F32)
        mixed_out[q] = (wide + mixed_ref[q].astype(F32)).astype(BF16)
        scale = lax.rsqrt(jnp.mean(wide * wide, axis=-1, keepdims=True) + EPSILON)
        unit = wide * scale
        scaled = dh_ref[q].astype(F32) * gain
        tokens_out[q] = cot_ref[q].astype(F32) + scale * (
            scaled - unit * jnp.mean(scaled * unit, axis=-1, keepdims=True)
        )
    groups, _, cols = slots_ref.shape
    width = (cols - TAIL) // 2
    tail = jnp.zeros((slots_ref.shape[1], TAIL), F32)
    for g in range(groups):
        w_in_out[:, g * width : (g + 1) * width] = slots_ref[g, :, :width].astype(F32)
        w_in_out[:, INNER + g * width : INNER + (g + 1) * width] = (
            slots_ref[g, :, width : 2 * width].astype(F32)
        )
        tail = tail + slots_ref[g, :, 2 * width :].astype(F32)
    w_in_out[:, 2 * INNER :] = tail[:, : 2 * STATE + HEADS]
    w_out_out[...] = rows_ref[0].astype(F32) + rows_ref[1].astype(F32)

    shared, size, _ = sum_rows(width, seq)
    heads = HEADS // seq
    for j in range(D // LANES):
        at = slice(j * LANES, (j + 1) * LANES)
        gain_in_out[:, at] = vec_ref[j : j + 1, :] / gain_ref[:, at]
    row = D // LANES
    targets = [conv_w_out.at[k : k + 1] for k in range(KERNEL)] + [conv_b_out]
    for out in targets:
        for j in range(2 * STATE // LANES):
            out[:, INNER + j * LANES : INNER + (j + 1) * LANES] = vec_ref[row : row + 1, :]
            row += 1
    across = lane_rows(width)
    lane = iota((8, LANES), 1)
    per_head = jnp.zeros((8, LANES), F32)
    fold = expander(across * LANES)
    for g in range(groups):
        row = shared + g * size

        def lanes_of(line):
            first = row + line * across
            return jnp.concatenate(
                [vec_ref[first + j : first + j + 1, :] for j in range(across)], axis=1
            )

        at = slice(g * width, (g + 1) * width)
        for line, out in enumerate(targets):
            out[:, at] = lanes_of(line)[:, :width]
        gain_out_out[:, at] = lanes_of(KERNEL + 2)[:, :width]
        skip = mm_ones_tr(jnp.broadcast_to(lanes_of(KERNEL + 1), (8, across * LANES)), fold, 3)
        last = row + (KERNEL + 3) * across
        lines = jnp.concatenate(
            [skip[0:1, :], vec_ref[last : last + 2, :], jnp.zeros((5, LANES), F32)], axis=0
        )
        lines = jnp.where(lane < heads, lines, 0.0)
        per_head = per_head + (pltpu.roll(lines, g * heads, 1) if g else lines)
    heads_out[...] = per_head


def finish(seq, tokens, cotangent, gain_in, grad_h, mixed, slots, rows, vector, shapes):
    columns = INNER + 2 * STATE
    kinds = [
        (tokens.shape, BF16), (tokens.shape, F32), ((1, D), F32), (shapes[0], F32),
        ((KERNEL, columns), F32), ((1, columns), F32), ((8, LANES), F32), ((1, INNER), F32),
        (shapes[1], F32),
    ]
    return pl.pallas_call(
        functools.partial(finish_kernel, seq),
        out_shape=[jax.ShapeDtypeStruct(*kind) for kind in kinds],
        compiler_params=pltpu.CompilerParams(vmem_limit_bytes=32 << 20),
        name="finish",
    )(tokens, cotangent, gain_in[None], grad_h, mixed, slots, rows, vector)


def local(
    tokens, segments, gain_in, w_in, conv_w, conv_b, dt_bias, a_log, skip, gain_out, w_out,
    cotangent,
):
    steps, shards = lax.axis_size("seq"), lax.axis_size("fsdp")
    place = Place(steps, shards)
    seqs, length, _ = tokens.shape
    width = INNER // steps
    heads = HEADS // steps
    rows_in = w_in.shape[0]
    number = place.chunk

    def mine(array, size):
        return lax.dynamic_slice_in_dim(array, number * size, size, array.ndim - 1)

    wide = tokens.astype(F32)
    scale_in = lax.rsqrt(jnp.mean(wide * wide, axis=-1, keepdims=True) + EPSILON)
    normed = (wide * scale_in * gain_in).astype(BF16)
    zx = w_in[:, : 2 * INNER].reshape(rows_in, 2, steps, width).transpose(2, 0, 1, 3)
    zx = zx.reshape(steps, rows_in, 2 * width)
    tail = jnp.pad(w_in[:, 2 * INNER :], ((0, 0), (0, LANES - HEADS)))
    heads_p = jnp.stack([mine(dt_bias, heads), mine(a_log, heads)])
    lane = lax.broadcasted_iota(jnp.int32, (LANES, LANES), 1)
    source = lax.broadcasted_iota(jnp.int32, (LANES, LANES), 0)
    pick = ((lane < heads) & (source == lane + number * heads)).astype(BF16)
    consts = (
        mine(conv_w[:, :INNER], width),
        mine(conv_b[None, :INNER], width),
        conv_w[:, INNER:],
        conv_b[None, INNER:],
        jnp.pad(heads_p, ((0, 6), (0, LANES - heads))),
        pick,
        jnp.repeat(mine(skip, heads), HEAD_DIM)[None],
        mine(gain_out[None], width),
    )

    (
        proj, y, states, off_col, rem_col, off_row, h_all, w_mine, grad_yn, stats, mixed, part_out,
    ) = forward_mix(normed, zx, tail, segments, cotangent, w_out, consts, steps, shards)
    grad_proj, sums_x, sums_t, sums_h, mixed, rows = backward_mix(
        proj, off_col, off_row, rem_col, y, grad_yn, stats, states, mixed, part_out, consts,
        steps, shards,
    )

    grad_h, mixed, slots, vector = exit_scatter(
        steps, shards, h_all, grad_proj, w_mine, mixed, (sums_x, sums_t, sums_h)
    )
    (
        mixed, tokens_grad, gain_in_grad, w_in_grad, conv_w_grad, conv_b_grad, per_head,
        gain_out_grad, w_out_grad,
    ) = finish(
        steps, tokens, cotangent, gain_in, grad_h, mixed,
        slots.reshape(steps, rows_in, 2 * width + TAIL), rows, vector, (w_in.shape, w_out.shape),
    )
    return (
        mixed, tokens_grad, gain_in_grad[0], w_in_grad, conv_w_grad, conv_b_grad[0],
        per_head[1, :HEADS], per_head[2, :HEADS], per_head[0, :HEADS], gain_out_grad[0],
        w_out_grad,
    )


def solution(mesh):
    by_token = P("fsdp", "seq", None)
    by_row = P(("seq", "fsdp"), None)
    placed = (
        by_token, P("fsdp", None), P(), by_row, P(), P(), P(), P(), P(), P(), by_row, by_token,
    )
    return jax.shard_map(
        local,
        mesh=mesh,
        in_specs=placed,
        out_specs=(by_token, by_token, P(), by_row, P(), P(), P(), P(), P(), P(), by_row),
        check_vma=False,
    )
```

```python
import functools

import jax
import jax.numpy as jnp
import numpy as np
from jax import lax
from jax.experimental import pallas as pl
from jax.experimental.pallas import tpu as pltpu
from jax.sharding import PartitionSpec as P

D = 1536
HEADS = 48
HEAD_DIM = 64
STATE = 128
KERNEL = 4
INNER = 3072
LANES = 128
HALO = 16
EPSILON = 1e-05
F32 = jnp.float32
BF16 = jnp.bfloat16


def mm(a, b):
    return jnp.dot(a.astype(BF16), b.astype(BF16), preferred_element_type=F32)


def mm_tr(a, b):
    return lax.dot_general(
        a.astype(BF16), b.astype(BF16), (((1,), (1,)), ((), ())), preferred_element_type=F32
    )


def tr_mm(a, b):
    return lax.dot_general(
        a.astype(BF16), b.astype(BF16), (((0,), (0,)), ((), ())), preferred_element_type=F32
    )


def pieces(a, count):
    out = []
    for _ in range(count - 1):
        part = a.astype(BF16)
        out.append(part)
        a = a - part.astype(F32)
    out.append(a.astype(BF16))
    return out


def ones_mm(ones, a, count):
    return sum(jnp.dot(ones, part, preferred_element_type=F32) for part in pieces(a, count))


def mm_ones(a, ones, count):
    return sum(jnp.dot(part, ones, preferred_element_type=F32) for part in pieces(a, count))


def mm_ones_tr(a, ones, count):
    return sum(
        lax.dot_general(part, ones, (((1,), (1,)), ((), ())), preferred_element_type=F32)
        for part in pieces(a, count)
    )


def iota(shape, dim):
    return lax.broadcasted_iota(jnp.int32, shape, dim)


def softplus(v):
    return jnp.maximum(v, 0.0) + jnp.log1p(jnp.exp(-jnp.abs(v)))


def sigmoid(v):
    return 1.0 / (1.0 + jnp.exp(-v))


def causal_conv(ext, current, halo, weight, bias, offset):
    length = current.shape[0]
    ext[0:HALO, :] = halo
    ext[HALO : HALO + length, :] = current
    total = bias + weight[KERNEL - 1 : KERNEL, :] * current
    for back in range(1, KERNEL):
        shifted = jnp.where(offset >= back, ext[pl.ds(HALO - back, length), :], 0.0)
        total = total + weight[KERNEL - 1 - back : KERNEL - back, :] * shifted
    return total


def head_tiles(width):
    out = []
    for start in range(0, width, LANES):
        size = min(LANES, width - start)
        heads = [start // HEAD_DIM + i for i in range(size // HEAD_DIM)]
        out.append((start, size, heads))
    return out


def masked_heads(tile, heads):
    if len(heads) == 1:
        return tile
    lane = iota(tile.shape, 1) // HEAD_DIM
    return jnp.concatenate(
        [jnp.where(lane == i, tile, jnp.zeros_like(tile)) for i in range(len(heads))], axis=0
    )


def expander(width):
    return (iota((LANES, width), 1) // HEAD_DIM == iota((LANES, width), 0)).astype(BF16)


def chunk_common(x, xh, tail, tailh, offset, params, ext_x, ext_t, width):
    wx, bx, wt, bt, heads_p, pick = params
    length = x.shape[0]
    conv_x = causal_conv(ext_x, x.astype(F32), xh.astype(F32), wx, bx, offset)
    conv_t = causal_conv(
        ext_t,
        tail[:, : 2 * STATE].astype(F32),
        tailh[:, : 2 * STATE].astype(F32),
        wt,
        bt,
        offset,
    )
    raw = jnp.dot(tail[:, 2 * STATE :], pick, preferred_element_type=F32) + heads_p[0:1, :]
    step = softplus(raw)
    decay_rate = jnp.exp(heads_p[1:2, :])
    rate = -step * decay_rate
    tril = (iota((length, length), 0) >= iota((length, length), 1)).astype(BF16)
    cumul = ones_mm(tril, rate, 3)
    spread = expander(width)
    row = iota((length, 1), 0)
    entry = jnp.where(offset > row.astype(F32), jnp.exp(cumul), 0.0)
    last_off = offset[length - 1 : length, :]
    same_last = row.astype(F32) >= (length - 1) - last_off
    to_end = jnp.where(same_last, jnp.exp(cumul[length - 1 : length, :] - cumul), 0.0)
    step_x = mm_ones(step, spread, 2)
    entry_x = mm_ones(entry, spread, 2)
    end_x = mm_ones(to_end, spread, 2)
    return conv_x, conv_t, raw, step, rate, decay_rate, cumul, spread, step_x, entry_x, end_x


def positions(segments, chunk, length):
    here = jnp.zeros((1, length), F32)
    total = segments.shape[1] // length
    rows = [segments[:, i * length : (i + 1) * length].astype(F32) for i in range(total)]
    for i in range(total):
        here = here + jnp.where(chunk == i, rows[i], 0.0)
    own = jnp.broadcast_to(here, (length, length)).T
    less = jnp.zeros((length, length), F32)
    upto = jnp.zeros((length, length), F32)
    for row in rows:
        less = less + jnp.where(row < own, 1.0, 0.0)
        upto = upto + jnp.where(row <= own, 1.0, 0.0)
    index = (chunk * length + iota((length, 1), 0)).astype(F32)
    offset = index - jnp.sum(less, axis=1, keepdims=True)
    return offset, jnp.sum(upto, axis=1, keepdims=True) - 1.0 - index


def flat_rows(ref, flat):
    rows, cols = ref.shape[-2:]
    if rows % HALO == 0:
        return ref[...].reshape(-1, cols)
    shape = ref.shape[:-2]
    for i, at in enumerate(np.ndindex(*shape)):
        flat[i * rows : (i + 1) * rows, :] = ref[at]
    return flat[...]


def pick_params(place, pack_ref, cx_ref, hp_ref, pick_ref):
    width = cx_ref.shape[1]
    heads = width // HEAD_DIM
    mine = jnp.zeros((8, width), F32)
    for g in range(INNER // width):
        mine = mine + jnp.where(place.chunk == g, pack_ref[:, g * width : (g + 1) * width], 0.0)
    lane, source = iota((LANES, LANES), 1), iota((LANES, LANES), 0)
    pick = ((lane < heads) & (source == lane + place.chunk * heads)).astype(BF16)
    pick_ref[...] = pick
    lines = [pack_ref[6:7, i * LANES : (i + 1) * LANES] for i in range(3)]
    lines = jnp.concatenate(lines + [jnp.zeros((5, LANES), F32)], axis=0)
    lines = mm_ones(lines, pick, 3)
    hp_ref[...] = lines
    cx_ref[...] = mine
    cx_ref[6:7, :] = mm_ones(lines, expander(width), 3)[2:3, :]


def forward_kernel(
    seq, fsdp,
    h_ref, zx_ref, tail_ref, seg_ref, cot_ref, ow_ref,
    pack_ref,
    proj_ref, y_ref, state_ref, off_ref, rem_ref, offr_ref,
    h_out, w_out, grad_out, stat_out, mixed_out, pout_out, cx_ref, hp_ref, pick_ref,
    h_v, w_v, w_flat, seg_v, cot_v, ow_v, ow_flat, gated_v, sums_v, sums_got, grad_v, mix_give,
    mix_own, mix_first, pout_v, memory, ext_x, ext_t, last_rows, send, recv, near,
):
    seqs, _, length, width = y_ref.shape
    depth = h_v.shape[3]
    cols = proj_ref.shape[3]
    step_at = pl.program_id(0)
    place = Place(seq, fsdp)
    links = Links(send, recv, near)
    peers = peers_of(place)
    near_peers = [(l, c) for t, l, c in peers if t == 0]
    entry = Entry(place, links, h_ref, zx_ref, tail_ref, seg_ref, h_v, w_v, seg_v)
    cot = TokenGather(place, links, cot_ref, cot_v)
    w_rows = RowGather(place, links, ow_ref, ow_v)
    keep = [links.local(lambda: (h_v, h_out)), links.local(lambda: (w_v, w_out))]
    stages = len(place.low_bits)

    def send_sums(i):
        l, c = near_peers[i]
        return links.far(lambda: (sums_v, sums_got.at[i], place.at(low=l, core=c)))

    sums = [send_sums(i) for i in range(len(near_peers))]

    def send_core(q):
        return links.far(lambda: (mix_give.at[q], mix_first.at[q], place.at(core=1)))

    cores = [send_core(q) for q in range(seqs)]

    @pl.when(step_at == 0)
    def _():
        memory[...] = jnp.zeros_like(memory)
        last_rows[...] = jnp.zeros_like(last_rows)
        pick_params(place, pack_ref, cx_ref, hp_ref, pick_ref)
        meet_pair(place)
        entry.run(cot.cross_over)
        if w_v.shape[-2] % HALO:
            flat_rows(w_v, w_flat)

    @pl.when(step_at == 1)
    def _():
        for copy in keep:
            copy.start()
        cot.begin_home()
        w_rows.begin()

    for i in range(stages):

        @pl.when(step_at == min(3 + 2 * i, seq - 1))
        def _():
            cot.pass_on(i, "home")

    @pl.when(step_at == 2)
    def _():
        cot.arrive()

    for i in range(stages):

        @pl.when(step_at == min(4 + 2 * i, seq - 1))
        def _():
            cot.pass_on(i, "away")

    @pl.when(step_at == seq - 2)
    def _():
        w_rows.forward()

    @pl.when(step_at < seq)
    def _():
        weights = flat_rows(w_v, w_flat) if w_v.shape[-2] % HALO == 0 else w_flat[...]
        proj = jnp.dot(
            h_v[:, step_at].reshape(seqs * length, depth), weights, preferred_element_type=F32
        ).astype(BF16)
        proj_ref[...] = proj.reshape(proj_ref.shape)
        params = (
            cx_ref[:KERNEL, :], cx_ref[KERNEL : KERNEL + 1, :],
            pack_ref[:KERNEL, INNER:], pack_ref[KERNEL : KERNEL + 1, INNER:],
            hp_ref[...], pick_ref[...],
        )
        gain_row, skip_row = cx_ref[KERNEL + 1 : KERNEL + 2, :], cx_ref[KERNEL + 2 : KERNEL + 3, :]
        for q in range(seqs):
            offset, remain = positions(seg_v[q : q + 1, :], step_at, length)
            off_ref[q, 0] = offset
            rem_ref[q, 0] = remain
            offr_ref[q, 0] = jnp.broadcast_to(offset, (length, LANES)).T[0:1, :]
            chunk_rows = proj[q * length : (q + 1) * length]
            zx, tail = chunk_rows[:, : 2 * width], chunk_rows[:, 2 * width :]
            earlier = last_rows[q]
            here = pl.ds(pl.multiple_of((q * seq + step_at) * length, length), length)
            conv_x, conv_t, _, _, _, _, cumul, _, step_x, entry_x, end_x = chunk_common(
                zx[:, width:], earlier[:, width : 2 * width], tail, earlier[:, 2 * width :], offset, params,
                ext_x.at[q], ext_t.at[q], width,
            )
            xs = conv_x * sigmoid(conv_x)
            act_t = conv_t * sigmoid(conv_t)
            bs = act_t[:, :STATE].astype(BF16)
            cs = act_t[:, STATE:].astype(BF16)
            scaled = xs * step_x
            scores = mm_tr(cs, bs)
            gap = iota((length, length), 0) - iota((length, length), 1)
            same = (gap >= 0) & (gap.astype(F32) <= offset)
            cumul_t = cumul.T
            old = memory[q]
            old_low = old.astype(BF16)
            state_ref[q, 0] = old_low
            outside = mm(cs, old_low) * entry_x + skip_row * xs
            squares = jnp.zeros((length, 1), F32)
            for start, size, heads in head_tiles(width):
                mixing = []
                for head in heads:
                    spans = cumul[:, head : head + 1] - cumul_t[head : head + 1, :]
                    decays = jnp.exp(jnp.where(same, spans, -1e30))
                    mixing.append((decays * scores).astype(BF16))
                tile = masked_heads(scaled[:, start : start + size].astype(BF16), heads)
                mix = mixing[0] if len(heads) == 1 else jnp.concatenate(mixing, axis=1)
                inside = jnp.dot(mix, tile, preferred_element_type=F32)
                y_low = (inside + outside[:, start : start + size]).astype(BF16)
                y_ref[q, 0, :, start : start + size] = y_low
                z = zx[:, start : start + size].astype(F32)
                gated = y_low.astype(F32) * (z * sigmoid(z))
                gated_v[here, start : start + size] = (
                    gated * gain_row[:, start : start + size]
                ).astype(BF16)
                squares = squares + jnp.sum(gated * gated, axis=1, keepdims=True)
            sums_v[pl.ds(2 * (q * seq + step_at), 1), :] = jnp.broadcast_to(
                squares, (length, LANES)
            ).T[0:1, :]
            fresh = tr_mm(bs, scaled * end_x)
            memory[q] = old * entry_x[length - 1 : length, :] + fresh
            last_rows[q] = chunk_rows[length - HALO :]

    @pl.when(step_at == seq)
    def _():
        w_rows.finish()
        cot.finish()
        rows_out = flat_rows(ow_v, ow_flat)
        tile = 2 * length
        tiles = seqs * seq // 2

        @pl.loop(0, tiles)
        def _(k):
            at = pl.ds(pl.multiple_of(k * tile, tile), tile)
            cots = cot_v[k // (seq // 2), pl.ds(lax.rem(k, seq // 2) * 2, 2)].reshape(tile, depth)
            grad = mm_tr(cots, rows_out)
            grad_v[at, :] = grad
            part = jnp.sum(grad * gated_v[at, :].astype(F32), axis=1, keepdims=True)
            part = jnp.broadcast_to(part, (tile, LANES))
            for i in (0, 1):
                sums_v[pl.ds(4 * k + 2 * i + 1, 1), :] = (
                    part[i * length : (i + 1) * length].T[0:1, :]
                )

        grad_store = links.local(lambda: (grad_v, grad_out))
        grad_store.start()
        for copy in sums:
            copy.start()

        def mixed_rows(out, side):
            per_side = seq // 2 // 2
            for q in range(seqs):

                @pl.loop(0, per_side)
                def _(k):
                    at = (q * seq + seq // 2 * side + 2 * k) * length
                    rows = gated_v[pl.ds(pl.multiple_of(at, tile), tile), :]
                    mixed = jnp.dot(rows, rows_out, preferred_element_type=F32)
                    out[q, pl.ds(2 * k, 2)] = mixed.astype(BF16).reshape(2, length, depth)

        mixed_rows(mix_give, 1 - place.core)
        for copy in cores:
            copy.start()
        mixed_rows(mix_own, place.core)
        for copy in sums:
            copy.wait_recv()
        total = sums_v[...]
        for i in range(len(near_peers)):
            total = total + sums_got[i]
        is_square = lax.rem(iota(total.shape, 0), 2) == 0
        scale = lax.rsqrt(total / INNER + EPSILON)
        other = pltpu.roll(scale, 1, 0)
        stat_out[...] = jnp.where(is_square, scale, total * (other * other * other / INNER))

        @pl.loop(0, tiles)
        def _(k):
            at = pl.ds(pl.multiple_of(k * tile, tile), tile)
            scales = [
                jnp.broadcast_to(stat_out[pl.ds(4 * k + 2 * i, 1), :], (LANES, length)).T[:, 0:1]
                for i in (0, 1)
            ]
            scale_col = jnp.concatenate(scales, axis=0)
            gated_v[at, :] = (gated_v[at, :].astype(F32) * scale_col).astype(BF16)

        pout_v[...] = tr_mm(gated_v[...], cot_v[...].reshape(-1, depth)).astype(BF16)
        pout_store = links.local(lambda: (pout_v, pout_out))
        pout_store.start()
        for q in range(seqs):
            cores[q].wait_recv()
            for low in range(seq // 2):
                add_rows(mix_own.at[q, low], mix_own.at[q, low], mix_first.at[q, low])
        mixed_store = links.local(lambda: (mix_own, mixed_out))
        mixed_store.start()
        for copy in [grad_store, mixed_store, pout_store] + keep:
            copy.wait()
        for copy in cores:
            copy.wait_send()
        for copy in sums:
            copy.wait_send()
        entry.finish()


def backward_kernel(
    seq, fsdp,
    zx_ref, zxh_ref, tail_ref, tailh_ref, off_ref, offr_ref, rem_ref, y_ref, grad_ref, stat_ref,
    state_ref, all_stat_ref, mixed_ref, pout_ref,
    cx_ref, ct_ref, hp_ref, pick_ref,
    out_ref, gx_ref, gt_ref, gh_ref, mixed_out, rows_out,
    memory, ext_x, ext_t, next_x, next_t,
    mix_own, mix_later, pout_own, pout_first, send, recv, near,
):
    seqs, _, length, width = y_ref.shape
    step_at = pl.program_id(0)

    place = Place(seq, fsdp)
    links = Links(send, recv, near)
    mixed = TokenScatter(place, links, mixed_ref, mixed_out, mix_own, None, mix_later, "halves")
    w_rows = RowScatter(place, links, pout_ref, rows_out, pout_own, pout_first)
    stages = len(place.low_bits)

    @pl.when(step_at == 0)
    def _():
        meet_pair(place)
        mixed.begin()
        w_rows.begin()

    @pl.when(step_at == 1)
    def _():
        mixed.add_cores()
        mixed.send_stage(0)

    @pl.when(step_at == 3)
    def _():
        w_rows.add_pairs()

    @pl.when(step_at == pl.num_programs(0) - 3)
    def _():
        mixed.add_stage(0)
        if stages > 1:
            mixed.send_stage(1)

    @pl.when(pl.program_id(0) == 0)
    def _():
        memory[...] = jnp.zeros_like(memory)
        gx_ref[...] = jnp.zeros_like(gx_ref)
        gt_ref[...] = jnp.zeros_like(gt_ref)
        gh_ref[...] = jnp.zeros_like(gh_ref)
        next_x[:, length:, :] = jnp.zeros_like(next_x[:, length:, :])
        next_t[:, length:, :] = jnp.zeros_like(next_t[:, length:, :])

    params = (
        cx_ref[:KERNEL, :], cx_ref[KERNEL : KERNEL + 1, :],
        ct_ref[:KERNEL, :], ct_ref[KERNEL : KERNEL + 1, :],
        hp_ref[...], pick_ref[...],
    )
    gain_row, skip_row = cx_ref[KERNEL + 1 : KERNEL + 2, :], cx_ref[KERNEL + 2 : KERNEL + 3, :]
    for q in range(seqs):
        offset = off_ref[q, 0]
        conv_x, conv_t, raw, step, rate, decay_rate, cumul, spread, step_x, entry_x, end_x = (
            chunk_common(
                zx_ref[q, 0, :, width:], zxh_ref[q, 0, :, width:], tail_ref[q, 0], tailh_ref[q, 0], offset,
                params, ext_x.at[q], ext_t.at[q], width,
            )
        )
        stats = jnp.broadcast_to(stat_ref[q, 0, 0:1, :], (LANES, length)).T
        slopes = jnp.broadcast_to(stat_ref[q, 0, 1:2, :], (LANES, length)).T
        scale, slope = stats[:, 0:1], slopes[:, 0:1]
        z = zx_ref[q, 0, :, :width].astype(F32)
        sig_z = sigmoid(z)
        silu_z = z * sig_z
        y = y_ref[q, 0].astype(F32)
        gated = y * silu_z
        scaled_grad = grad_ref[q, 0].astype(F32) * scale
        gx_ref[KERNEL + 2 : KERNEL + 3, :width] += jnp.sum(scaled_grad * gated, axis=0, keepdims=True)
        grad_gated = gain_row * scaled_grad - gated * slope
        dy_low = (grad_gated * silu_z).astype(BF16)
        dz = (grad_gated * y * (sig_z + silu_z * (1.0 - sig_z))).astype(BF16)
        dy = dy_low.astype(F32)

        sig_x = sigmoid(conv_x)
        xs = conv_x * sig_x
        slope_x = sig_x + xs * (1.0 - sig_x)
        sig_t = sigmoid(conv_t)
        act_t = conv_t * sig_t
        slope_t = sig_t + act_t * (1.0 - sig_t)
        bs = act_t[:, :STATE].astype(BF16)
        cs = act_t[:, STATE:].astype(BF16)
        scaled = xs * step_x
        scaled_low = scaled.astype(BF16)
        scores = mm_tr(bs, cs)
        rows, cols = iota((length, length), 0), iota((length, length), 1)
        gap = cols - rows
        same = (gap >= 0) & (gap.astype(F32) <= offr_ref[q, 0])
        strict = gap > 0
        upper = (rows >= cols).astype(BF16)
        cumul_t = cumul.T
        old = state_ref[q, 0]
        grad_state = memory[q]
        state_low = grad_state.astype(BF16)
        grad_scores = jnp.zeros((length, length), F32)
        grad_scaled = []
        inside_rows = []
        for start, size, heads in head_tiles(width):
            dy_tile = masked_heads(dy_low[:, start : start + size], heads)
            grad_mix = mm_tr(scaled_low[:, start : start + size], dy_tile)
            mixing = []
            for i, head in enumerate(heads):
                spans = cumul_t[head : head + 1, :] - cumul[:, head : head + 1]
                decays = jnp.exp(jnp.where(same, spans, -1e30))
                weighted = grad_mix[:, i * length : (i + 1) * length] * decays
                grad_scores = grad_scores + weighted
                mixing.append((decays * scores).astype(BF16))
                terms = jnp.where(strict, weighted * scores, 0.0).astype(BF16)
                sums = jnp.dot(terms, upper, preferred_element_type=F32)
                inside_rows.append(
                    jnp.sum(jnp.where(strict, sums, 0.0), axis=0, keepdims=True)
                )
            mix = mixing[0] if len(heads) == 1 else jnp.concatenate(mixing, axis=1)
            grad_scaled.append(jnp.dot(mix, dy_tile, preferred_element_type=F32))
        inside_rows.append(jnp.zeros((LANES - len(inside_rows), length), F32))
        inside = jnp.concatenate(inside_rows, axis=0).T
        from_end = mm(bs, state_low) * end_x
        grad_scaled = jnp.concatenate(grad_scaled, axis=1) + from_end
        entry_dy = dy * entry_x
        entry_dy_low = entry_dy.astype(BF16)
        out_terms = mm(cs, old) * entry_dy
        end_terms = scaled * from_end
        grad_step = mm_ones_tr(xs * grad_scaled, spread, 2)
        out_terms = mm_ones_tr(out_terms, spread, 2)
        end_terms = mm_ones_tr(end_terms, spread, 2)
        keep_row = entry_x[length - 1 : length, :]
        carried = jnp.sum(grad_state * old.astype(F32), axis=0, keepdims=True) * keep_row
        carried = mm_ones_tr(jnp.broadcast_to(carried, (8, width)), spread, 2)[0:1, :]
        triu = (cols >= rows).astype(BF16)
        below = (rows > cols).astype(BF16)
        grad_rate = inside + ones_mm(triu, out_terms, 2) + ones_mm(below, end_terms, 2) + carried
        grad_step = grad_step - decay_rate * grad_rate
        grad_raw = grad_step * sigmoid(raw)
        grad_scores_low = grad_scores.astype(BF16)
        grad_b = mm(grad_scores_low, cs) + mm_tr(scaled * end_x, state_low)
        grad_c = tr_mm(grad_scores_low, bs) + mm_tr(entry_dy_low, old)
        memory[q] = grad_state * keep_row + tr_mm(cs, entry_dy_low)
        conv_grad_x = (skip_row * dy + step_x * grad_scaled) * slope_x
        conv_grad_t = jnp.concatenate([grad_b, grad_c], axis=1) * slope_t

        remain = rem_ref[q, 0]
        results = [dz]
        for grad, ext, nxt, weight, sums in (
            (conv_grad_x, ext_x.at[q], next_x.at[q], params[0], gx_ref),
            (conv_grad_t, ext_t.at[q], next_t.at[q], params[2], gt_ref),
        ):
            columns = grad.shape[1]
            current = ext[pl.ds(HALO, length), :]
            sums[KERNEL : KERNEL + 1, :columns] += jnp.sum(grad, axis=0, keepdims=True)
            sums[KERNEL - 1 : KERNEL, :columns] += jnp.sum(grad * current, axis=0, keepdims=True)
            nxt[0:length, :] = grad
            total = weight[KERNEL - 1 : KERNEL, :] * grad
            for back in range(1, KERNEL):
                tap = KERNEL - 1 - back
                shifted = jnp.where(offset >= back, ext[pl.ds(HALO - back, length), :], 0.0)
                sums[tap : tap + 1, :columns] += jnp.sum(grad * shifted, axis=0, keepdims=True)
                ahead = jnp.where(remain >= back, nxt[pl.ds(back, length), :], 0.0)
                total = total + weight[tap : tap + 1, :] * ahead
            nxt[length:, :] = grad[0:HALO, :]
            results.append(total.astype(BF16))
        results.append(mm_tr(grad_raw, params[5]).astype(BF16))
        gx_ref[KERNEL + 1 : KERNEL + 2, :width] += jnp.sum(dy * xs, axis=0, keepdims=True)
        gh_ref[0:1, :] += jnp.sum(grad_raw, axis=0, keepdims=True)
        gh_ref[1:2, :] += jnp.sum(grad_rate * rate, axis=0, keepdims=True)
        out_ref[q, 0, :, : 2 * width] = jnp.concatenate(results[:2], axis=1)
        out_ref[q, 0, :, 2 * width : 2 * width + 2 * STATE] = results[2]
        out_ref[q, 0, :, 2 * width + 2 * STATE :] = results[3]

    @pl.when(step_at == pl.num_programs(0) - 1)
    def _():
        for stage in range(1, stages):
            mixed.add_stage(stage)
            if stage + 1 < stages:
                mixed.send_stage(stage + 1)
        for q in range(seqs):
            row = all_stat_ref[pl.ds(2 * (q * seq + place.chunk), 1), :]
            column = jnp.broadcast_to(row, (LANES, length)).T[:, 0:1]
            done = mix_own.at[q, place.low]
            done[...] = (done[...].astype(F32) * column).astype(BF16)
        mixed.store()
        w_rows.finish()
        mixed.finish()


TAIL = 2 * STATE + LANES
AXES = ("seq", "fsdp")
MESH = pl.DeviceIdType.MESH
ANYWHERE = pl.BlockSpec(memory_space=pl.ANY)


def lane_rows(width):
    return -(-width // LANES)


def sum_rows(width, seq):
    shared = D // LANES + (KERNEL + 1) * 2 * STATE // LANES
    group = (KERNEL + 3) * lane_rows(width) + 2
    return shared, group, -(-(shared + seq * group) // 8) * 8


def whole_spec(shape):
    return pl.BlockSpec(shape, lambda i: (0,) * len(shape))


def chunk_specs(seqs, steps, length, reverse):
    def place(i):
        return steps - 1 - i if reverse else i

    def block(cols, column=0, rows=length):
        return pl.BlockSpec((seqs, 1, rows, cols), lambda i: (0, place(i), 0, column))

    def before(cols, column=0):
        return pl.BlockSpec(
            (seqs, 1, HALO, cols),
            lambda i: (0, jnp.maximum(place(i) - 1, 0), length // HALO - 1, column),
        )

    return block, before


def forward_mix(normed, zx, tail, segments, cotangent, out_w, packed, seq, fsdp):
    seqs, length, depth = normed.shape
    rows = tail.shape[0]
    cols = zx.shape[2] + TAIL
    width = zx.shape[2] // 2
    pairs = fsdp // 2
    count = seqs * seq * length

    def block(columns, height=length):
        return pl.BlockSpec(
            (seqs, 1, height, columns), lambda i: (0, jnp.minimum(i, seq - 1), 0, 0)
        )

    def blocks(columns, kind, height=length):
        return jax.ShapeDtypeStruct((seqs, seq, height, columns), kind)

    w_shape = (seq, pairs, 2, rows, cols)
    out_shape = (pairs, 2) + out_w.shape
    sums = (seqs * seq * 2, length)
    flat = 8 if rows % HALO == 0 else depth
    flat_out = 8 if out_w.shape[0] % HALO == 0 else width
    outs = pl.pallas_call(
        functools.partial(forward_kernel, seq, fsdp),
        grid=(seq + 1,),
        in_specs=[ANYWHERE] * 6 + [whole_spec(packed.shape)],
        out_specs=[
            block(cols), block(width), block(width, STATE), block(1), block(1), block(length, 1),
            ANYWHERE, ANYWHERE, ANYWHERE, whole_spec(sums), ANYWHERE, ANYWHERE,
            whole_spec((8, width)), whole_spec((8, LANES)), whole_spec((LANES, LANES)),
        ],
        out_shape=[
            blocks(cols, BF16), blocks(width, BF16), blocks(width, BF16, STATE),
            blocks(1, F32), blocks(1, F32), blocks(length, F32, 1),
            blocks(depth, BF16),
            jax.ShapeDtypeStruct(w_shape, BF16),
            jax.ShapeDtypeStruct((count, width), F32),
            jax.ShapeDtypeStruct(sums, F32),
            jax.ShapeDtypeStruct((seqs, seq // 2, length, depth), BF16),
            jax.ShapeDtypeStruct((width, depth), BF16),
            jax.ShapeDtypeStruct((8, width), F32),
            jax.ShapeDtypeStruct((8, LANES), F32),
            jax.ShapeDtypeStruct((LANES, LANES), BF16),
        ],
        scratch_shapes=[
            pltpu.VMEM((seqs, seq, length, depth), BF16),
            pltpu.VMEM(w_shape, BF16),
            pltpu.VMEM((flat, cols), BF16),
            pltpu.VMEM(segments.shape, segments.dtype),
            pltpu.VMEM((seqs, seq, length, depth), BF16),
            pltpu.VMEM(out_shape, BF16),
            pltpu.VMEM((flat_out, depth), BF16),
            pltpu.VMEM((count, width), BF16),
            pltpu.VMEM(sums, F32),
            pltpu.VMEM((seq - 1,) + sums, F32),
            pltpu.VMEM((count, width), F32),
            pltpu.VMEM((seqs, seq // 2, length, depth), BF16),
            pltpu.VMEM((seqs, seq // 2, length, depth), BF16),
            pltpu.VMEM((seqs, seq // 2, length, depth), BF16),
            pltpu.VMEM((width, depth), BF16),
            pltpu.VMEM((seqs, STATE, width), F32),
            pltpu.VMEM((seqs, HALO + length, width), F32),
            pltpu.VMEM((seqs, HALO + length, 2 * STATE), F32),
            pltpu.VMEM((seqs, HALO, cols), BF16),
            pltpu.SemaphoreType.DMA((320,)),
            pltpu.SemaphoreType.DMA((320,)),
            pltpu.SemaphoreType.DMA((24,)),
        ],
        compiler_params=pltpu.CompilerParams(
            dimension_semantics=("arbitrary",), vmem_limit_bytes=60 << 20, collective_id=0,
            has_side_effects=True,
        ),
        cost_estimate=pl.CostEstimate(
            flops=30_000_000_000, transcendentals=0, bytes_accessed=60_000_000
        ),
        name="mix_forward",
    )(normed, zx, tail, segments, cotangent, out_w, packed)
    proj, y, states, off_col, rem_col, off_row, h_all, w_mine, grad_yn, stats, mixed, part = outs[:12]
    shape = (seqs, seq, length)
    return (
        proj, y, states, off_col, rem_col, off_row, h_all, w_mine.reshape(depth, cols),
        grad_yn.reshape(shape + (width,)), stats, mixed, part.reshape(out_shape), outs[12:],
    )


def backward_mix(
    proj, off_col, off_row, rem_col, y, grad_yn, stats, states, mixed, part_out, packed, consts, seq, fsdp
):
    seqs, steps, length, cols = proj.shape
    depth = mixed.shape[3]
    width = (cols - TAIL) // 2
    block, before = chunk_specs(seqs, steps, length, True)
    tail_at = 2 * width // TAIL
    half, pairs = seq // 2, fsdp // 2
    rows_out = part_out.shape[2]
    sums = [(8, lane_rows(width) * LANES), (8, 2 * STATE), (8, LANES)]
    token_own = pltpu.VMEM((seqs, half, length, depth), BF16)
    return pl.pallas_call(
        functools.partial(backward_kernel, seq, fsdp),
        grid=(steps,),
        in_specs=[
            block(2 * width), before(2 * width), block(TAIL, tail_at), before(TAIL, tail_at),
            block(1), block(length, 0, 1), block(1), block(width), block(width),
            block(length, 0, 2), block(width, 0, STATE), whole_spec(stats.shape),
            ANYWHERE, ANYWHERE, whole_spec(consts[0].shape),
            pl.BlockSpec((8, 2 * STATE), lambda i: (0, INNER // (2 * STATE))),
            whole_spec(consts[1].shape), whole_spec(consts[2].shape),
        ],
        out_specs=[block(cols)] + [whole_spec(v) for v in sums] + [ANYWHERE, ANYWHERE],
        scratch_shapes=[
            pltpu.VMEM((seqs, STATE, width), F32),
            pltpu.VMEM((seqs, HALO + length, width), F32),
            pltpu.VMEM((seqs, HALO + length, 2 * STATE), F32),
            pltpu.VMEM((seqs, length + HALO, width), F32),
            pltpu.VMEM((seqs, length + HALO, 2 * STATE), F32),
            token_own, pltpu.VMEM((seqs, max(half - 1, 1), length, depth), BF16),
            pltpu.VMEM((2, rows_out, depth), BF16),
            pltpu.VMEM((max(pairs - 1, 1), 2, rows_out, depth), BF16),
            pltpu.SemaphoreType.DMA((64,)),
            pltpu.SemaphoreType.DMA((64,)),
            pltpu.SemaphoreType.DMA((16,)),
        ],
        out_shape=[jax.ShapeDtypeStruct(proj.shape, BF16)]
        + [jax.ShapeDtypeStruct(v, F32) for v in sums]
        + [
            jax.ShapeDtypeStruct((seqs, length, depth), BF16),
            jax.ShapeDtypeStruct((2, rows_out, depth), BF16),
        ],
        compiler_params=pltpu.CompilerParams(
            dimension_semantics=("arbitrary",), vmem_limit_bytes=56 << 20, collective_id=3,
            has_side_effects=True,
        ),
        cost_estimate=pl.CostEstimate(
            flops=steps * seqs * 2_000_000_000, transcendentals=0, bytes_accessed=16_000_000
        ),
        name="mix_backward",
    )(
        proj, proj, proj, proj, off_col, off_row, rem_col, y, grad_yn,
        stats.reshape(seqs, steps, 2, length), states, stats, mixed, part_out, consts[0], packed,
        consts[1], consts[2],
    )


class Place:
    def __init__(self, seq, fsdp):
        self.seq, self.fsdp = seq, fsdp
        self.half, self.pairs = seq // 2, fsdp // 2
        s, f = lax.axis_index("seq"), lax.axis_index("fsdp")
        self.s, self.f = s, f
        self.top, self.low = s // self.half, lax.rem(s, self.half)
        self.core, self.pair = lax.rem(f, 2), f // 2
        self.home = self.core == self.top
        self.away = self.core != self.top
        self.chunk = self.low + self.half * self.core
        self.low_bits = [1 << i for i in range(self.half.bit_length() - 1)]

    def at(self, top=0, low=0, pair=0, core=0):
        return (
            flip(self.top, top) * self.half + flip(self.low, low),
            flip(self.pair, pair) * 2 + flip(self.core, core),
        )

    def bits_for(self, q):
        return self.low_bits if q % 2 == 0 else self.low_bits[::-1]


def flip(index, bits):
    for i in range(bits.bit_length()):
        if bits >> i & 1:
            bit = lax.rem(index // (1 << i), 2)
            index = index + (1 << i) * (1 - 2 * bit)
    return index


class Copy:
    def __init__(self, make):
        self.make = make

    def start(self):
        self.make().start()
        return self

    def wait(self):
        self.make().wait()

    def wait_send(self):
        self.make().wait_send()

    def wait_recv(self):
        self.make().wait_recv()


class Links:
    def __init__(self, send, recv, near):
        self.send, self.recv, self.near = send, recv, near
        self.far_count = self.near_count = 0

    def far(self, make):
        i = self.far_count
        self.far_count += 1

        def build():
            src, dst, device = make()
            return pltpu.make_async_remote_copy(
                src_ref=src, dst_ref=dst, send_sem=self.send.at[i], recv_sem=self.recv.at[i],
                device_id=device, device_id_type=MESH,
            )

        return Copy(build)

    def local(self, make):
        i = self.near_count
        self.near_count += 1
        return Copy(lambda: pltpu.make_async_copy(*make(), self.near.at[i]))


def meet(devices):
    barrier = pltpu.get_barrier_semaphore()
    for device in devices:
        pl.semaphore_signal(barrier, inc=1, device_id=device, device_id_type=MESH)
    pl.semaphore_wait(barrier, len(devices))


def meet_pair(place):
    meet(
        [place.at(top=t, low=l, core=c) for t, l, c in peers_of(place)]
        + [place.at(pair=p) for p in range(1, place.pairs)]
    )


def peers_of(place):
    out = []
    for top in (0, 1):
        for low in range(place.half):
            for core in (0, 1):
                if (top, low, core) != (0, 0, 0):
                    out.append((top, low, core))
    return out


class TokenGather:
    def __init__(self, place, links, src, dst):
        self.place, self.src, self.dst = place, src, dst
        seqs = src.shape[0]

        def over(q):
            return links.far(
                lambda: (src.at[q], dst.at[q, place.s], place.at(top=1, core=1))
            )

        self.cross = [over(q) for q in range(seqs)]
        self.stay = links.local(lambda: (src, dst.at[:, place.s]))
        self.share = [[] for _ in range(seqs)]
        self.stages = []
        held = [[0] for _ in range(seqs)]
        for q in range(seqs):
            self.share[q].append([self.copy(links, q, low, core=1) for low in held[q]])
        for i in range(len(place.low_bits)):
            stage = []
            for q in range(seqs):
                bit = place.bits_for(q)[i]
                stage.append([self.copy(links, q, low, low_bit=bit) for low in held[q]])
                fresh = [low ^ bit for low in held[q]]
                held[q] = held[q] + fresh
                self.share[q].append([self.copy(links, q, low, core=1) for low in fresh])
            self.stages.append(stage)

    def copy(self, links, q, low, low_bit=0, core=0):
        def make():
            place = self.place
            ref = self.dst.at[q, flip(place.low, low) + place.half * place.core]
            return ref, ref, place.at(low=low_bit, core=core)

        return links.far(make)

    def begin(self):
        self.cross_over()
        self.begin_home()

    def cross_over(self):
        @pl.when(self.place.away)
        def _():
            for copy in self.cross:
                copy.start()

    def begin_home(self):
        @pl.when(self.place.home)
        def _():
            self.stay.start()
            self.stay.wait()
            self.send_stage(0)

    def arrive(self):
        @pl.when(self.place.away)
        def _():
            for copy in self.cross:
                copy.wait_recv()
            self.send_stage(0)

    def send_stage(self, i):
        for q in range(len(self.share)):
            for copy in self.stages[i][q] + self.share[q][i]:
                copy.start()

    def pass_on(self, i, role):
        @pl.when(self.place.home if role == "home" else self.place.away)
        def _():
            for q in range(len(self.share)):
                for copy in self.stages[i][q]:
                    copy.wait_recv()
                for copy in (self.stages[i + 1][q] if i + 1 < len(self.stages) else []):
                    copy.start()
                for copy in self.share[q][i + 1]:
                    copy.start()

    def finish(self):
        for share in self.share:
            for copies in share:
                for copy in copies:
                    copy.wait()
        for stage in self.stages:
            for copies in stage:
                for copy in copies:
                    copy.wait_send()

        @pl.when(self.place.away)
        def _():
            for copy in self.cross:
                copy.wait_send()


class RowGather:
    def __init__(self, place, links, src, dst):
        self.place = place
        pairs = range(1, place.pairs)

        def slot():
            return dst.at[place.pair, place.core]

        self.stay = links.local(lambda: (src, slot()))
        self.to_home = links.far(lambda: (src, slot(), place.at(core=1)))
        self.to_near = links.far(lambda: (src, slot(), place.at(top=1)))
        self.to_far = links.far(lambda: (src, slot(), place.at(top=1, core=1)))

        def forward(c, p):
            return links.far(
                lambda: (dst.at[place.pair, c], dst.at[place.pair, c], place.at(pair=p))
            )

        self.forwards = [forward(c, p) for c in (0, 1) for p in pairs]

    def begin(self):
        @pl.when(self.place.home)
        def _():
            self.stay.start()
            self.to_near.start()

        @pl.when(self.place.away)
        def _():
            self.to_home.start()
            self.to_far.start()

    def forward(self):
        @pl.when(self.place.home)
        def _():
            self.stay.wait()
            self.to_home.wait_recv()

        @pl.when(self.place.away)
        def _():
            self.to_near.wait_recv()
            self.to_far.wait_recv()

        for copy in self.forwards:
            copy.start()

    def finish(self):
        for copy in self.forwards:
            copy.wait()

        @pl.when(self.place.home)
        def _():
            self.to_near.wait_send()

        @pl.when(self.place.away)
        def _():
            self.to_home.wait_send()
            self.to_far.wait_send()


class Entry:
    def __init__(self, place, links, h_ref, zx_ref, tail_ref, seg_ref, h_v, w_v, seg_v):
        self.place = place
        cols = zx_ref.shape[2]
        self.peers = peers = peers_of(place)
        others = range(1, place.pairs)
        self.tokens = TokenGather(place, links, h_ref, h_v)

        def block(t=0, l=0, c=0):
            s, f = place.at(top=t, low=l, core=c)
            return w_v.at[s, place.pair, lax.rem(f, 2)]

        def columns(ref):
            return ref.at[:, pl.ds(0, cols)]

        def tail_of(ref):
            return ref.at[:, pl.ds(cols, TAIL)]

        def send_zx(t, l, c):
            group = flip(place.core, c) * place.half + flip(place.low, l)
            return zx_ref.at[group], columns(block()), place.at(top=t, low=l, core=c)

        self.zx = {p: links.far(functools.partial(send_zx, *p)) for p in peers}
        self.own = [
            links.local(lambda: (zx_ref.at[place.chunk], columns(block()))),
            links.local(lambda: (tail_ref, tail_of(block()))),
        ]
        self.tail_cross = links.far(lambda: (tail_ref, tail_of(block()), place.at(top=1)))
        self.near_peers = [(l, c) for t, l, c in peers if t == 0]

        def send_tail(l, c):
            return tail_ref, tail_of(block()), place.at(low=l, core=c)

        def send_other(l, c):
            return tail_of(block(1)), tail_of(block(1)), place.at(low=l, core=c)

        self.tails = {p: links.far(functools.partial(send_tail, *p)) for p in self.near_peers}
        self.tails_more = {
            p: links.far(functools.partial(send_other, *p)) for p in self.near_peers
        }
        self.seg_send = links.far(lambda: (seg_ref, seg_v, place.at(core=1)))
        self.seg_keep = links.local(lambda: (seg_ref, seg_v))

        def send_on(t, l, c, p):
            return block(t, l, c), block(t, l, c), place.at(pair=p)

        self.forwards = {
            p: [links.far(functools.partial(send_on, *p, other)) for other in others]
            for p in [(0, 0, 0)] + peers
        }

    def run(self, then):
        tokens, zx, forwards = self.tokens, self.zx, self.forwards
        stages = len(self.place.low_bits)
        far_peers = [p for p in self.peers if p[0] == 1]
        tokens.begin()
        self.tail_cross.start()
        for copy in self.own:
            copy.start()
        for p in self.near_peers:
            zx[0, *p].start()
            self.tails[p].start()

        @pl.when(self.place.home)
        def _():
            self.seg_send.start()
            self.seg_keep.start()

        for copy in self.own:
            copy.wait()
        for copy in forwards[0, 0, 0]:
            copy.start()
        self.tail_cross.wait_recv()
        for p in self.near_peers:
            self.tails_more[p].start()
        tokens.pass_on(0, "home")
        for p in self.near_peers:
            zx[0, *p].wait_recv()
            self.tails[p].wait_recv()
            for copy in forwards[0, *p]:
                copy.start()
        for p in far_peers:
            zx[p].start()
        for i in range(1, stages):
            tokens.pass_on(i, "home")
        tokens.arrive()
        for p in self.near_peers:
            self.tails_more[p].wait_recv()
        for i in range(stages):
            tokens.pass_on(i, "away")
            at, to = (len(far_peers) * k // stages for k in (i, i + 1))
            for p in far_peers[at:to]:
                zx[p].wait_recv()
                for copy in forwards[p]:
                    copy.start()
        then()

        @pl.when(self.place.home)
        def _():
            self.seg_keep.wait()
            self.seg_send.wait_send()

        @pl.when(self.place.away)
        def _():
            self.seg_send.wait_recv()

        tokens.finish()
        for p in forwards:
            for copy in forwards[p]:
                copy.wait()

    def finish(self):
        self.tail_cross.wait_send()
        for group in (self.zx, self.tails, self.tails_more):
            for copy in group.values():
                copy.wait_send()


def add_rows(out, left, right, rows=32):
    total = left.shape[0]
    step = next((size for size in (rows, 16) if total % size == 0), total)

    if step == total:
        out[...] = (left[...].astype(F32) + right[...].astype(F32)).astype(out.dtype)
        return

    @pl.loop(0, total // step)
    def _(i):
        at = pl.ds(pl.multiple_of(i * step, step), step)
        out[at] = (left[at].astype(F32) + right[at].astype(F32)).astype(out.dtype)


class TokenScatter:
    def __init__(self, place, links, src, out, own, first, later, held):
        self.place = place
        self.out, self.own, self.first, self.later = out, own, first, later
        self.seqs = src.shape[0]
        half = place.half

        def give(q):
            return links.far(lambda: (src.at[q], first.at[q], place.at(core=1)))

        self.cores = [give(q) for q in range(self.seqs)] if held == "give" else []
        self.loads = [links.local(lambda: (src, own))] if held == "halves" else []
        self.stages = [[] for _ in place.low_bits]
        for q in range(self.seqs):
            live, slot = list(range(half)), 0
            for i, bit in enumerate(place.bits_for(q)[::-1]):
                for low in [low for low in live if low & bit]:
                    self.stages[i].append((self.copy(links, q, low, slot, bit), q, low ^ bit, slot))
                    slot += 1
                live = [low for low in live if not low & bit]
        self.stay = links.local(lambda: (own.at[:, place.low], out))

    def copy(self, links, q, low, slot, bit):
        return links.far(
            lambda: (
                self.own.at[q, flip(self.place.low, low)], self.later.at[q, slot],
                self.place.at(low=bit),
            )
        )

    def begin(self):
        for copy in self.cores + self.loads:
            copy.start()

    def add_cores(self):
        for copy in self.loads:
            copy.wait()
        for q, copy in enumerate(self.cores):
            copy.wait_recv()
            for low in range(self.place.half):
                add_rows(self.own.at[q, low], self.own.at[q, low], self.first.at[q, low])

    def send_stage(self, i):
        for copy, _, _, _ in self.stages[i]:
            copy.start()

    def add_stage(self, i):
        for copy, q, low, slot in self.stages[i]:
            copy.wait_recv()
            ref = self.own.at[q, flip(self.place.low, low)]
            add_rows(ref, ref, self.later.at[q, slot])

    def store(self):
        self.stay.start()
        self.stay.wait()

    def finish(self):
        for copy in self.cores:
            copy.wait_send()
        for stage in self.stages:
            for copy, _, _, _ in stage:
                copy.wait_send()


class RowScatter:
    def __init__(self, place, links, src, out, own, first):
        self.place, self.own, self.first = place, own, first

        def over(p):
            return links.far(
                lambda: (src.at[flip(place.pair, p)], first.at[p - 1], place.at(pair=p))
            )

        def far(c):
            return links.far(
                lambda: (own.at[flip(place.core, c)], out.at[1], place.at(top=1, core=c))
            )

        self.over = [over(p) for p in range(1, place.pairs)]
        self.load = links.local(lambda: (src.at[place.pair], own))
        self.far = [far(0), far(1)]
        self.near = links.far(lambda: (own.at[1 - place.core], out.at[0], place.at(core=1)))
        self.stay = links.local(lambda: (own.at[place.core], out.at[0]))

    def begin(self):
        self.load.start()
        for copy in self.over:
            copy.start()

    def add_pairs(self):
        self.load.wait()
        for i, copy in enumerate(self.over):
            copy.wait_recv()
            for c in (0, 1):
                add_rows(self.own.at[c], self.own.at[c], self.first.at[i, c])

        @pl.when(self.place.away)
        def _():
            for copy in self.far:
                copy.start()

        @pl.when(self.place.home)
        def _():
            self.near.start()
            self.stay.start()

    def finish(self):
        for copy in self.over:
            copy.wait_send()

        @pl.when(self.place.home)
        def _():
            self.stay.wait()
            self.near.wait_send()
            self.far[0].wait_recv()

        @pl.when(self.place.away)
        def _():
            self.near.wait_recv()
            self.far[1].wait_recv()
            for copy in self.far:
                copy.wait_send()


class Deliver:
    def __init__(self, place, links, src, out):
        self.place = place
        self.cross = links.far(lambda: (src(), out, place.at(top=1, core=1)))
        self.stay = links.local(lambda: (src(), out))

    def begin(self):
        @pl.when(self.place.away)
        def _():
            self.cross.start()

        @pl.when(self.place.home)
        def _():
            self.stay.start()

    def finish(self):
        @pl.when(self.place.away)
        def _():
            self.cross.wait()

        @pl.when(self.place.home)
        def _():
            self.stay.wait()


TILE = 384
ROWS = 256


def exit_kernel(
    seq, fsdp,
    h_ref, grad_ref, w_ref, mixed_ref, gx_ref, gt_ref, gh_ref,
    dh_out, mixed_out, slots_out, vec_out,
    h_all, grads, weights, part,
    dh_give, dh_own, dh_first, dh_later, part_first, part_top, vec_val, vec_got,
    send, recv, near,
):
    place = Place(seq, fsdp)
    links = Links(send, recv, near)
    half = place.half
    others = list(range(1, place.pairs))
    seqs, _, length, depth = dh_own.shape
    rows = part.shape[3]
    width = (weights.shape[1] - TAIL) // 2
    dh = TokenScatter(
        place, links, dh_give, dh_out, dh_own, dh_first, dh_later, "give"
    )
    dh_last = Deliver(place, links, lambda: dh_own.at[:, place.low], dh_out)
    mixed = Deliver(place, links, lambda: mixed_ref, mixed_out)
    loads = [
        links.local(lambda: (h_ref, h_all)),
        links.local(lambda: (grad_ref, grads)),
        links.local(lambda: (w_ref, weights)),
    ]

    tiles = depth // 2 // TILE
    high = half // tiles

    def rows_of(top, k):
        return pl.ds(half * flip(place.top, top) + k * high, high)

    def over(top, k, p):
        return links.far(
            lambda: (
                part.at[rows_of(top, k), flip(place.pair, p)],
                part_first.at[p - 1, rows_of(top, k)],
                place.at(pair=p),
            )
        )

    def crossing(k):
        return links.far(
            lambda: (
                part.at[rows_of(1, k), place.pair], part_top.at[pl.ds(k * high, high)],
                place.at(top=1),
            )
        )

    over_pairs = [[[over(top, k, p) for p in others] for k in range(tiles)] for top in (0, 1)]
    cross = [crossing(k) for k in range(tiles)]

    def row_block(l, c):
        return part.at[
            half * place.top + flip(place.low, l), place.pair, flip(place.core, c)
        ]

    def spread(l, c):
        return links.far(
            lambda: (
                row_block(l, c), slots_out.at[place.core, place.low], place.at(low=l, core=c)
            )
        )

    near_peers = [(l, c) for t, l, c in peers_of(place) if t == 0]
    slots = {p: spread(*p) for p in near_peers}
    slots[0, 0] = links.local(lambda: (row_block(0, 0), slots_out.at[place.core, place.low]))

    hops = [dict(pair=1 << i) for i in range(place.pairs.bit_length() - 1)]
    hops += [dict(top=1)] + [dict(low=b) for b in place.low_bits] + [dict(core=1)]

    def hop(i):
        return links.far(lambda: (vec_val.at[i], vec_got.at[i], place.at(**hops[i])))

    vec = [hop(i) for i in range(len(hops))]
    vec_store = links.local(lambda: (vec_val.at[len(hops)], vec_out))
    state = {"at": 0}

    def vec_next():
        i = state["at"]
        state["at"] += 1
        if i < len(hops):
            vec[i].wait_recv()
            vec_val[i + 1] = vec_val[i] + vec_got[i]
            if i + 1 < len(hops):
                vec[i + 1].start()
            else:
                vec_store.start()

    def add_pairs(top, k):
        for i, copy in enumerate(over_pairs[top][k]):
            copy.wait_recv()
            for low in range(high):
                for c in (0, 1):
                    at = half * flip(place.top, top) + k * high + low
                    ref = part.at[at, place.pair, c]
                    add_rows(ref, ref, part_first.at[i, at, c], 16)

    blocks = TILE // rows

    def weight_rows(top, k):
        t = tiles * flip(place.top, top) + k
        lanes = pl.ds(pl.multiple_of(t * TILE, LANES), TILE)
        term = tr_mm(h_all[:, lanes], grads[...])
        for b in range(blocks):
            at = t * (blocks // fsdp) + b // fsdp
            part[at, b % fsdp // 2, b % 2] = term[b * rows : (b + 1) * rows].astype(BF16)
        sums = jnp.sum(term * weights[lanes, :].astype(F32), axis=1, keepdims=True)
        wide = jnp.broadcast_to(sums, (TILE, LANES))
        for i in range(TILE // LANES):
            vec_val[0, pl.ds(t * (TILE // LANES) + i, 1), :] = (
                wide[i * LANES : (i + 1) * LANES].T[0:1, :]
            )
        for copy in over_pairs[top][k]:
            copy.start()

    def place_sums():
        shared, group, _ = sum_rows(width, seq)
        vec_val[0] = jnp.zeros_like(vec_val[0])
        at = D // LANES
        for tap in range(KERNEL + 1):
            for j in range(2 * STATE // LANES):
                vec_val[0, at : at + 1, :] = gt_ref[
                    tap : tap + 1, j * LANES : (j + 1) * LANES
                ]
                at += 1
        at = shared + place.chunk * group
        pieces_of = [
            gx_ref[line : line + 1, j * LANES : (j + 1) * LANES]
            for line in range(KERNEL + 3)
            for j in range(lane_rows(width))
        ] + [gh_ref[0:1, :], gh_ref[1:2, :]]
        for i, piece in enumerate(pieces_of):
            vec_val[0, pl.ds(at + i, 1), :] = piece

    def token_rows(out, side):
        per_chunk = ROWS // length
        count = half // per_chunk
        for q in range(seqs):

            @pl.loop(0, count)
            def _(k):
                at = (q * seq + half * side + k * per_chunk) * length
                term = mm_tr(grads[pl.ds(pl.multiple_of(at, LANES), ROWS), :], weights[...])
                out[q, pl.ds(k * per_chunk, per_chunk)] = term.astype(BF16).reshape(
                    per_chunk, length, depth
                )

    for copy in loads:
        copy.start()
    place_sums()
    meet_pair(place)
    mixed.begin()
    for copy in loads:
        copy.wait()
    token_rows(dh_give, 1 - place.core)
    dh.begin()
    for k in range(tiles):
        weight_rows(1, k)
    token_rows(dh_own, place.core)
    dh.add_cores()
    dh.send_stage(0)
    add_pairs(1, 0)
    cross[0].start()
    for k in range(tiles):
        weight_rows(0, k)
    vec[0].start()
    for k in range(1, tiles):
        add_pairs(1, k)
        cross[k].start()
    stages = len(place.low_bits)
    for i in range(stages):
        dh.add_stage(i)
        if i + 1 < stages:
            dh.send_stage(i + 1)
        else:
            dh_last.begin()
        vec_next()
    for k in range(tiles):
        add_pairs(0, k)
    vec_next()
    for copy in cross:
        copy.wait_recv()
    for l, c in near_peers + [(0, 0)]:
        ref = row_block(l, c)
        add_rows(ref, ref, part_top.at[flip(place.low, l), flip(place.core, c)], 16)
        slots[l, c].start()
    while state["at"] < len(hops):
        vec_next()
    for copy in slots.values():
        copy.wait()
    vec_store.wait()
    mixed.finish()
    dh_last.finish()
    dh.finish()
    for copy in cross + vec + [c for top in over_pairs for tile in top for c in tile]:
        copy.wait_send()


def exit_scatter(seq, fsdp, h_all, grad_proj, w_mine, mixed, sums):
    seqs, _, length, depth = h_all.shape
    half, pairs = seq // 2, fsdp // 2
    cols = w_mine.shape[1]
    rows = depth // (seq * fsdp)
    count = seqs * seq * length
    vector = (sum_rows((cols - TAIL) // 2, seq)[2], LANES)
    bits = (half.bit_length() - 1) + (pairs.bit_length() - 1) + 2
    token_own = pltpu.VMEM((seqs, half, length, depth), BF16)
    tokens = jax.ShapeDtypeStruct((seqs, length, depth), BF16)
    return pl.pallas_call(
        functools.partial(exit_kernel, seq, fsdp),
        in_specs=[ANYWHERE] * 4 + [pl.BlockSpec(memory_space=pltpu.VMEM)] * 3,
        out_specs=[ANYWHERE] * 4,
        out_shape=[
            tokens,
            tokens,
            jax.ShapeDtypeStruct((2, half, rows, cols), BF16),
            jax.ShapeDtypeStruct(vector, F32),
        ],
        scratch_shapes=[
            pltpu.VMEM((count, depth), BF16),
            pltpu.VMEM((count, cols), BF16),
            pltpu.VMEM((depth, cols), BF16),
            pltpu.VMEM((seq, pairs, 2, rows, cols), BF16),
            token_own, token_own, token_own,
            pltpu.VMEM((seqs, max(half - 1, 1), length, depth), BF16),
            pltpu.VMEM((max(pairs - 1, 1), seq, 2, rows, cols), BF16),
            pltpu.VMEM((half, 2, rows, cols), BF16),
            pltpu.VMEM((bits + 1,) + vector, F32),
            pltpu.VMEM((bits,) + vector, F32),
            pltpu.SemaphoreType.DMA((96,)),
            pltpu.SemaphoreType.DMA((96,)),
            pltpu.SemaphoreType.DMA((16,)),
        ],
        compiler_params=pltpu.CompilerParams(
            collective_id=1, has_side_effects=True, vmem_limit_bytes=60 << 20
        ),
        cost_estimate=pl.CostEstimate(
            flops=0, transcendentals=0, bytes_accessed=200_000_000
        ),
        name="exit_scatter",
    )(h_all.reshape(count, depth), grad_proj.reshape(count, cols), w_mine, mixed, *sums)


def finish_kernel(
    seq,
    tok_ref, cot_ref, gain_ref, dh_ref, mixed_ref, slots_ref, rows_ref, vec_ref,
    mixed_out, tokens_out, gain_in_out, w_in_out, conv_w_out, conv_b_out, heads_out, gain_out_out,
    w_out_out,
):
    gain = gain_ref[...]
    for q in range(tok_ref.shape[0]):
        wide = tok_ref[q].astype(F32)
        mixed_out[q] = (wide + mixed_ref[q].astype(F32)).astype(BF16)
        scale = lax.rsqrt(jnp.mean(wide * wide, axis=-1, keepdims=True) + EPSILON)
        unit = wide * scale
        scaled = dh_ref[q].astype(F32) * gain
        tokens_out[q] = cot_ref[q].astype(F32) + scale * (
            scaled - unit * jnp.mean(scaled * unit, axis=-1, keepdims=True)
        )
    groups, _, cols = slots_ref.shape
    width = (cols - TAIL) // 2
    tail = jnp.zeros((slots_ref.shape[1], TAIL), F32)
    for g in range(groups):
        w_in_out[:, g * width : (g + 1) * width] = slots_ref[g, :, :width].astype(F32)
        w_in_out[:, INNER + g * width : INNER + (g + 1) * width] = (
            slots_ref[g, :, width : 2 * width].astype(F32)
        )
        tail = tail + slots_ref[g, :, 2 * width :].astype(F32)
    w_in_out[:, 2 * INNER :] = tail[:, : 2 * STATE + HEADS]
    w_out_out[...] = rows_ref[0].astype(F32) + rows_ref[1].astype(F32)

    shared, size, _ = sum_rows(width, seq)
    heads = HEADS // seq
    for j in range(D // LANES):
        at = slice(j * LANES, (j + 1) * LANES)
        gain_in_out[:, at] = vec_ref[j : j + 1, :] / gain_ref[:, at]
    row = D // LANES
    targets = [conv_w_out.at[k : k + 1] for k in range(KERNEL)] + [conv_b_out]
    for out in targets:
        for j in range(2 * STATE // LANES):
            out[:, INNER + j * LANES : INNER + (j + 1) * LANES] = vec_ref[row : row + 1, :]
            row += 1
    across = lane_rows(width)
    lane = iota((8, LANES), 1)
    per_head = jnp.zeros((8, LANES), F32)
    fold = expander(across * LANES)
    for g in range(groups):
        row = shared + g * size

        def lanes_of(line):
            first = row + line * across
            return jnp.concatenate(
                [vec_ref[first + j : first + j + 1, :] for j in range(across)], axis=1
            )

        at = slice(g * width, (g + 1) * width)
        for line, out in enumerate(targets):
            out[:, at] = lanes_of(line)[:, :width]
        gain_out_out[:, at] = lanes_of(KERNEL + 2)[:, :width]
        skip = mm_ones_tr(jnp.broadcast_to(lanes_of(KERNEL + 1), (8, across * LANES)), fold, 3)
        last = row + (KERNEL + 3) * across
        lines = jnp.concatenate(
            [skip[0:1, :], vec_ref[last : last + 2, :], jnp.zeros((5, LANES), F32)], axis=0
        )
        lines = jnp.where(lane < heads, lines, 0.0)
        per_head = per_head + (pltpu.roll(lines, g * heads, 1) if g else lines)
    heads_out[...] = per_head


def finish(seq, tokens, cotangent, gain_in, grad_h, mixed, slots, rows, vector, shapes):
    columns = INNER + 2 * STATE
    kinds = [
        (tokens.shape, BF16), (tokens.shape, F32), ((1, D), F32), (shapes[0], F32),
        ((KERNEL, columns), F32), ((1, columns), F32), ((8, LANES), F32), ((1, INNER), F32),
        (shapes[1], F32),
    ]
    return pl.pallas_call(
        functools.partial(finish_kernel, seq),
        out_shape=[jax.ShapeDtypeStruct(*kind) for kind in kinds],
        compiler_params=pltpu.CompilerParams(vmem_limit_bytes=32 << 20),
        name="finish",
    )(tokens, cotangent, gain_in[None], grad_h, mixed, slots, rows, vector)


def local(
    tokens, segments, gain_in, w_in, conv_w, conv_b, dt_bias, a_log, skip, gain_out, w_out,
    cotangent,
):
    steps, shards = lax.axis_size("seq"), lax.axis_size("fsdp")
    place = Place(steps, shards)
    seqs, length, _ = tokens.shape
    width = INNER // steps
    rows_in = w_in.shape[0]

    wide = tokens.astype(F32)
    scale_in = lax.rsqrt(jnp.mean(wide * wide, axis=-1, keepdims=True) + EPSILON)
    normed = (wide * scale_in * gain_in).astype(BF16)
    zx = w_in[:, : 2 * INNER].reshape(rows_in, 2, steps, width).transpose(2, 0, 1, 3)
    zx = zx.reshape(steps, rows_in, 2 * width)
    tail = jnp.pad(w_in[:, 2 * INNER :], ((0, 0), (0, LANES - HEADS)))
    columns = INNER + 2 * STATE

    def line(*arrays):
        arrays = [jnp.pad(v, (0, -v.shape[0] % LANES)) for v in arrays]
        return jnp.pad(jnp.concatenate(arrays), (0, columns - sum(v.shape[0] for v in arrays)))

    packed = jnp.concatenate(
        [
            conv_w,
            jnp.stack(
                [conv_b, line(gain_out), line(dt_bias, a_log, skip), jnp.zeros((columns,), F32)]
            ),
        ]
    )
    (
        proj, y, states, off_col, rem_col, off_row, h_all, w_mine, grad_yn, stats, mixed, part_out,
        consts,
    ) = forward_mix(normed, zx, tail, segments, cotangent, w_out, packed, steps, shards)
    grad_proj, sums_x, sums_t, sums_h, mixed, rows = backward_mix(
        proj, off_col, off_row, rem_col, y, grad_yn, stats, states, mixed, part_out,
        packed, consts, steps, shards,
    )

    grad_h, mixed, slots, vector = exit_scatter(
        steps, shards, h_all, grad_proj, w_mine, mixed, (sums_x, sums_t, sums_h)
    )
    (
        mixed, tokens_grad, gain_in_grad, w_in_grad, conv_w_grad, conv_b_grad, per_head,
        gain_out_grad, w_out_grad,
    ) = finish(
        steps, tokens, cotangent, gain_in, grad_h, mixed,
        slots.reshape(steps, rows_in, 2 * width + TAIL), rows, vector, (w_in.shape, w_out.shape),
    )
    return (
        mixed, tokens_grad, gain_in_grad[0], w_in_grad, conv_w_grad, conv_b_grad[0],
        per_head[1, :HEADS], per_head[2, :HEADS], per_head[0, :HEADS], gain_out_grad[0],
        w_out_grad,
    )


def solution(mesh):
    by_token = P("fsdp", "seq", None)
    by_row = P(("seq", "fsdp"), None)
    placed = (
        by_token, P("fsdp", None), P(), by_row, P(), P(), P(), P(), P(), P(), by_row, by_token,
    )
    return jax.shard_map(
        local,
        mesh=mesh,
        in_specs=placed,
        out_specs=(by_token, by_token, P(), by_row, P(), P(), P(), P(), P(), P(), by_row),
        check_vma=False,
    )
```

```python
import functools

import jax
import jax.numpy as jnp
import numpy as np
from jax import lax
from jax.experimental import pallas as pl
from jax.experimental.pallas import tpu as pltpu
from jax.sharding import PartitionSpec as P

D = 1536
HEADS = 48
HEAD_DIM = 64
STATE = 128
KERNEL = 4
INNER = 3072
LANES = 128
HALO = 16
EPSILON = 1e-05
TILE = 384
F32 = jnp.float32
BF16 = jnp.bfloat16


def mm(a, b):
    return jnp.dot(a.astype(BF16), b.astype(BF16), preferred_element_type=F32)


def mm_tr(a, b):
    return lax.dot_general(
        a.astype(BF16), b.astype(BF16), (((1,), (1,)), ((), ())), preferred_element_type=F32
    )


def tr_mm(a, b):
    return lax.dot_general(
        a.astype(BF16), b.astype(BF16), (((0,), (0,)), ((), ())), preferred_element_type=F32
    )


def pieces(a, count):
    out = []
    for _ in range(count - 1):
        part = a.astype(BF16)
        out.append(part)
        a = a - part.astype(F32)
    out.append(a.astype(BF16))
    return out


def ones_mm(ones, a, count):
    return sum(jnp.dot(ones, part, preferred_element_type=F32) for part in pieces(a, count))


def mm_ones(a, ones, count):
    return sum(jnp.dot(part, ones, preferred_element_type=F32) for part in pieces(a, count))


def mm_ones_tr(a, ones, count):
    return sum(
        lax.dot_general(part, ones, (((1,), (1,)), ((), ())), preferred_element_type=F32)
        for part in pieces(a, count)
    )


def iota(shape, dim):
    return lax.broadcasted_iota(jnp.int32, shape, dim)


def softplus(v):
    return jnp.maximum(v, 0.0) + jnp.log1p(jnp.exp(-jnp.abs(v)))


def sigmoid(v):
    return 1.0 / (1.0 + jnp.exp(-v))


def causal_conv(ext, current, halo, weight, bias, offset):
    length = current.shape[0]
    ext[0:HALO, :] = halo
    ext[HALO : HALO + length, :] = current
    total = bias + weight[KERNEL - 1 : KERNEL, :] * current
    for back in range(1, KERNEL):
        shifted = jnp.where(offset >= back, ext[pl.ds(HALO - back, length), :], 0.0)
        total = total + weight[KERNEL - 1 - back : KERNEL - back, :] * shifted
    return total


def head_tiles(width):
    out = []
    for start in range(0, width, LANES):
        size = min(LANES, width - start)
        heads = [start // HEAD_DIM + i for i in range(size // HEAD_DIM)]
        out.append((start, size, heads))
    return out


def masked_heads(tile, heads):
    if len(heads) == 1:
        return tile
    lane = iota(tile.shape, 1) // HEAD_DIM
    return jnp.concatenate(
        [jnp.where(lane == i, tile, jnp.zeros_like(tile)) for i in range(len(heads))], axis=0
    )


def expander(width):
    return (iota((LANES, width), 1) // HEAD_DIM == iota((LANES, width), 0)).astype(BF16)


def chunk_common(x, xh, tail, tailh, offset, params, ext_x, ext_t, width):
    wx, bx, wt, bt, heads_p, pick = params
    length = x.shape[0]
    conv_x = causal_conv(ext_x, x.astype(F32), xh.astype(F32), wx, bx, offset)
    conv_t = causal_conv(
        ext_t,
        tail[:, : 2 * STATE].astype(F32),
        tailh[:, : 2 * STATE].astype(F32),
        wt,
        bt,
        offset,
    )
    raw = jnp.dot(tail[:, 2 * STATE :], pick, preferred_element_type=F32) + heads_p[0:1, :]
    step = softplus(raw)
    decay_rate = jnp.exp(heads_p[1:2, :])
    rate = -step * decay_rate
    tril = (iota((length, length), 0) >= iota((length, length), 1)).astype(BF16)
    cumul = ones_mm(tril, rate, 3)
    spread = expander(width)
    row = iota((length, 1), 0)
    entry = jnp.where(offset > row.astype(F32), jnp.exp(cumul), 0.0)
    last_off = offset[length - 1 : length, :]
    same_last = row.astype(F32) >= (length - 1) - last_off
    to_end = jnp.where(same_last, jnp.exp(cumul[length - 1 : length, :] - cumul), 0.0)
    step_x = mm_ones(step, spread, 2)
    entry_x = mm_ones(entry, spread, 2)
    end_x = mm_ones(to_end, spread, 2)
    return conv_x, conv_t, raw, step, rate, decay_rate, cumul, spread, step_x, entry_x, end_x


def positions(segments, chunk, length):
    here = jnp.zeros((1, length), F32)
    total = segments.shape[1] // length
    rows = [segments[:, i * length : (i + 1) * length].astype(F32) for i in range(total)]
    for i in range(total):
        here = here + jnp.where(chunk == i, rows[i], 0.0)
    own = jnp.broadcast_to(here, (length, length)).T
    less = jnp.zeros((length, length), F32)
    upto = jnp.zeros((length, length), F32)
    for row in rows:
        less = less + jnp.where(row < own, 1.0, 0.0)
        upto = upto + jnp.where(row <= own, 1.0, 0.0)
    index = (chunk * length + iota((length, 1), 0)).astype(F32)
    offset = index - jnp.sum(less, axis=1, keepdims=True)
    return offset, jnp.sum(upto, axis=1, keepdims=True) - 1.0 - index


def flat_rows(ref, flat):
    rows, cols = ref.shape[-2:]
    if rows % HALO == 0:
        return ref[...].reshape(-1, cols)
    shape = ref.shape[:-2]
    for i, at in enumerate(np.ndindex(*shape)):
        flat[i * rows : (i + 1) * rows, :] = ref[at]
    return flat[...]


def pick_params(place, pack_ref, cx_ref, hp_ref, pick_ref):
    width = cx_ref.shape[1]
    heads = width // HEAD_DIM
    mine = jnp.zeros((8, width), F32)
    for g in range(INNER // width):
        mine = mine + jnp.where(place.chunk == g, pack_ref[:, g * width : (g + 1) * width], 0.0)
    lane, source = iota((LANES, LANES), 1), iota((LANES, LANES), 0)
    pick = ((lane < heads) & (source == lane + place.chunk * heads)).astype(BF16)
    pick_ref[...] = pick
    lines = [pack_ref[6:7, i * LANES : (i + 1) * LANES] for i in range(3)]
    lines = jnp.concatenate(lines + [jnp.zeros((5, LANES), F32)], axis=0)
    lines = mm_ones(lines, pick, 3)
    hp_ref[...] = lines
    cx_ref[...] = mine
    cx_ref[6:7, :] = mm_ones(lines, expander(width), 3)[2:3, :]


def forward_kernel(
    seq, fsdp,
    h_ref, zx_ref, tail_ref, seg_ref, cot_ref, ow_ref,
    pack_ref,
    proj_ref, state_ref, off_ref, rem_ref, offr_ref,
    h_out, w_out, dz_out, dy_out, stat_out, mixed_out, mixed_got, pout_out, pz_out, gain_out_ref, gain_in_ref,
    cx_ref, hp_ref, pick_ref,
    h_v, w_v, w_flat, seg_v, cot_v, ow_v, ow_flat, gated_v, sums_v, sums_got, grad_v, z_v, y_v,
    mix_give, mix_own, pout_v, pz_v, memory, ext_x, ext_t, last_rows, send, recv, near,
):
    seqs, _, length, depth = h_v.shape
    width = cx_ref.shape[1]
    step_at = pl.program_id(0)
    place = Place(seq, fsdp)
    links = Links(send, recv, near)
    peers = peers_of(place)
    near_peers = [(l, c) for t, l, c in peers if t == 0]
    entry = Entry(place, links, h_ref, zx_ref, tail_ref, seg_ref, h_v, w_v, seg_v)
    cot = TokenGather(place, links, cot_ref, cot_v)
    w_rows = RowGather(place, links, ow_ref, ow_v)
    keep = [links.local(lambda: (h_v, h_out)), links.local(lambda: (w_v, w_out))]
    stages = len(place.low_bits)

    def send_sums(i):
        l, c = near_peers[i]
        return links.far(lambda: (sums_v, sums_got.at[i], place.at(low=l, core=c)))

    sums = [send_sums(i) for i in range(len(near_peers))]

    def send_core(q):
        return links.far(lambda: (mix_give.at[q], mixed_got.at[q], place.at(core=1)))

    cores = [send_core(q) for q in range(seqs)]

    @pl.when(step_at == 0)
    def _():
        memory[...] = jnp.zeros_like(memory)
        last_rows[...] = jnp.zeros_like(last_rows)
        pick_params(place, pack_ref, cx_ref, hp_ref, pick_ref)
        meet_pair(place)
        entry.run(cot.cross_over)
        if w_v.shape[-2] % HALO:
            flat_rows(w_v, w_flat)

    @pl.when(step_at == 1)
    def _():
        for copy in keep:
            copy.start()
        cot.begin_home()
        w_rows.begin()

    for i in range(stages):

        @pl.when(step_at == min(3 + 2 * i, seq - 1))
        def _():
            cot.pass_on(i, "home")

    @pl.when(step_at == 2)
    def _():
        cot.arrive()

    for i in range(stages):

        @pl.when(step_at == min(4 + 2 * i, seq - 1))
        def _():
            cot.pass_on(i, "away")

    @pl.when(step_at == seq - 2)
    def _():
        w_rows.forward()

    @pl.when(step_at < seq)
    def _():
        weights = flat_rows(w_v, w_flat) if w_v.shape[-2] % HALO == 0 else w_flat[...]
        proj = jnp.dot(
            h_v[:, step_at].reshape(seqs * length, depth), weights, preferred_element_type=F32
        ).astype(BF16)
        proj_ref[...] = proj.reshape(proj_ref.shape)
        params = (
            cx_ref[:KERNEL, :], cx_ref[KERNEL : KERNEL + 1, :],
            pack_ref[:KERNEL, INNER:], pack_ref[KERNEL : KERNEL + 1, INNER:],
            hp_ref[...], pick_ref[...],
        )
        gain_row, skip_row = cx_ref[KERNEL + 1 : KERNEL + 2, :], cx_ref[KERNEL + 2 : KERNEL + 3, :]
        for q in range(seqs):
            offset, remain = positions(seg_v[q : q + 1, :], step_at, length)
            off_ref[q, 0] = offset
            rem_ref[q, 0] = remain
            offr_ref[q, 0] = jnp.broadcast_to(offset, (length, LANES)).T[0:1, :]
            chunk_rows = proj[q * length : (q + 1) * length]
            zx, tail = chunk_rows[:, : 2 * width], chunk_rows[:, 2 * width :]
            earlier = last_rows[q]
            z_rows = zx[:, :width]
            here = pl.ds(pl.multiple_of((q * seq + step_at) * length, length), length)
            z_v[here, :] = z_rows
            conv_x, conv_t, _, _, _, _, cumul, _, step_x, entry_x, end_x = chunk_common(
                zx[:, width:], earlier[:, width : 2 * width], tail, earlier[:, 2 * width :], offset, params,
                ext_x.at[q], ext_t.at[q], width,
            )
            xs = conv_x * sigmoid(conv_x)
            act_t = conv_t * sigmoid(conv_t)
            bs = act_t[:, :STATE].astype(BF16)
            cs = act_t[:, STATE:].astype(BF16)
            scaled = xs * step_x
            scores = mm_tr(cs, bs)
            gap = iota((length, length), 0) - iota((length, length), 1)
            same = (gap >= 0) & (gap.astype(F32) <= offset)
            cumul_t = cumul.T
            old = memory[q]
            old_low = old.astype(BF16)
            state_ref[q, 0] = old_low
            outside = mm(cs, old_low) * entry_x + skip_row * xs
            squares = jnp.zeros((length, 1), F32)
            for start, size, heads in head_tiles(width):
                mixing = []
                for head in heads:
                    spans = cumul[:, head : head + 1] - cumul_t[head : head + 1, :]
                    decays = jnp.exp(jnp.where(same, spans, -1e30))
                    mixing.append((decays * scores).astype(BF16))
                tile = masked_heads(scaled[:, start : start + size].astype(BF16), heads)
                mix = mixing[0] if len(heads) == 1 else jnp.concatenate(mixing, axis=1)
                inside = jnp.dot(mix, tile, preferred_element_type=F32)
                y_low = (inside + outside[:, start : start + size]).astype(BF16)
                y_v[here, start : start + size] = y_low
                z = zx[:, start : start + size].astype(F32)
                gated = y_low.astype(F32) * (z * sigmoid(z))
                gated_v[here, start : start + size] = (
                    gated * gain_row[:, start : start + size]
                ).astype(BF16)
                squares = squares + jnp.sum(gated * gated, axis=1, keepdims=True)
            sums_v[pl.ds(2 * (q * seq + step_at), 1), :] = jnp.broadcast_to(
                squares, (length, LANES)
            ).T[0:1, :]
            fresh = tr_mm(bs, scaled * end_x)
            memory[q] = old * entry_x[length - 1 : length, :] + fresh
            last_rows[q] = chunk_rows[length - HALO :]

    @pl.when(step_at == seq)
    def _():
        w_rows.finish()
        cot.finish()
        rows_out = flat_rows(ow_v, ow_flat)
        tile = 2 * length
        tiles = seqs * seq // 2

        @pl.loop(0, tiles)
        def _(k):
            at = pl.ds(pl.multiple_of(k * tile, tile), tile)
            cots = cot_v[k // (seq // 2), pl.ds(lax.rem(k, seq // 2) * 2, 2)].reshape(tile, depth)
            grad = mm_tr(cots, rows_out)
            grad_v[at, :] = grad
            part = jnp.sum(grad * gated_v[at, :].astype(F32), axis=1, keepdims=True)
            part = jnp.broadcast_to(part, (tile, LANES))
            for i in (0, 1):
                sums_v[pl.ds(4 * k + 2 * i + 1, 1), :] = (
                    part[i * length : (i + 1) * length].T[0:1, :]
                )

        for copy in sums:
            copy.start()

        def mixed_rows(out, side):
            per_side = seq // 2 // 2
            for q in range(seqs):

                @pl.loop(0, per_side)
                def _(k):
                    at = (q * seq + seq // 2 * side + 2 * k) * length
                    rows = gated_v[pl.ds(pl.multiple_of(at, tile), tile), :]
                    mixed = jnp.dot(rows, rows_out, preferred_element_type=F32)
                    out[q, pl.ds(2 * k, 2)] = mixed.astype(BF16).reshape(2, length, depth)

        mixed_rows(mix_give, 1 - place.core)
        for copy in cores:
            copy.start()
        mixed_rows(mix_own, place.core)
        mixed_store = links.local(lambda: (mix_own, mixed_out))
        mixed_store.start()
        for copy in sums:
            copy.wait_recv()
        total = sums_v[...]
        for i in range(len(near_peers)):
            total = total + sums_got[i]
        is_square = lax.rem(iota(total.shape, 0), 2) == 0
        scale = lax.rsqrt(total / INNER + EPSILON)
        other = pltpu.roll(scale, 1, 0)
        stat_out[...] = jnp.where(is_square, scale, total * (other * other * other / INNER))

        gain_out_ref[...] = jnp.zeros_like(gain_out_ref)
        gain_row = cx_ref[KERNEL + 1 : KERNEL + 2, :]

        @pl.loop(0, tiles)
        def _(k):
            at = pl.ds(pl.multiple_of(k * tile, tile), tile)

            def column(line):
                rows = [
                    jnp.broadcast_to(stat_out[pl.ds(4 * k + 2 * i + line, 1), :], (LANES, length))
                    for i in (0, 1)
                ]
                return jnp.concatenate([row.T[:, 0:1] for row in rows], axis=0)

            scale, slope = column(0), column(1)
            gated_v[at, :] = (gated_v[at, :].astype(F32) * scale).astype(BF16)
            z = z_v[at, :].astype(F32)
            y = y_v[at, :].astype(F32)
            sig = sigmoid(z)
            silu_z = z * sig
            gated = y * silu_z
            scaled = grad_v[at, :] * scale
            gain_out_ref[0:1, :width] += jnp.sum(scaled * gated, axis=0, keepdims=True)
            grad_gated = gain_row * scaled - gated * slope
            y_v[at, :] = (grad_gated * silu_z).astype(BF16)
            z_v[at, :] = (grad_gated * y * (sig + silu_z * (1.0 - sig))).astype(BF16)

        dz_store = links.local(lambda: (z_v, dz_out))
        dy_store = links.local(lambda: (y_v, dy_out))
        dz_store.start()
        dy_store.start()

        rows_in = w_v.shape[3]
        blocks = TILE // rows_in
        high = blocks // fsdp
        h_flat = h_v[...].reshape(-1, depth)
        for t in range(depth // TILE):
            term = tr_mm(h_flat[:, t * TILE : (t + 1) * TILE], z_v[...])
            for i in range(blocks):
                pz_v[t * high + i // fsdp, i % fsdp // 2, i % 2] = term[
                    i * rows_in : (i + 1) * rows_in
                ].astype(BF16)
            if rows_in % HALO:
                some = w_flat[t * TILE : (t + 1) * TILE, :width]
            else:
                some = w_v[t * high : (t + 1) * high, :, :, :, :width].reshape(TILE, width)
            line = jnp.sum(term * some.astype(F32), axis=1, keepdims=True)
            wide = jnp.broadcast_to(line, (TILE, LANES))
            for i in range(TILE // LANES):
                row = t * (TILE // LANES) + i
                gain_in_ref[row : row + 1, :] = wide[i * LANES : (i + 1) * LANES].T[0:1, :]
        pz_store = links.local(lambda: (pz_v, pz_out))
        pz_store.start()
        pout_v[...] = tr_mm(gated_v[...], cot_v[...].reshape(-1, depth)).astype(BF16)
        pout_store = links.local(lambda: (pout_v, pout_out))
        pout_store.start()
        for copy in [dz_store, dy_store, pz_store, mixed_store, pout_store] + keep:
            copy.wait()
        for copy in cores:
            copy.wait()
        for copy in sums:
            copy.wait_send()
        entry.finish()


def backward_kernel(
    seq, fsdp,
    x_ref, xh_ref, tail_ref, tailh_ref, off_ref, offr_ref, rem_ref, dy_ref, dz_ref, state_ref,
    w_ref,    all_stat_ref, mixed_ref, got_ref, pout_ref, pz_ref,
    cx_ref, ct_ref, hp_ref, pick_ref,
    out_ref, gx_ref, gt_ref, gh_ref, mixed_out, rows_out, slots_out, dh_out,
    memory, ext_x, ext_t, next_x, next_t,
    mix_own, mix_first, mix_later, pout_own, pout_first, pz_own, pz_first, pz_top,
    dh_give, dh_own, dh_first, send, recv, near,
):
    seqs, _, length, width = dy_ref.shape
    x_at = x_ref.shape[3] - width
    step_at = pl.program_id(0)

    place = Place(seq, fsdp)
    links = Links(send, recv, near)
    mixed = TokenScatter(
        place, links, (mixed_ref, got_ref), mixed_out, mix_own, mix_first, mix_later, "halves"
    )
    w_rows = RowScatter(place, links, pout_ref, rows_out, pout_own, pout_first)
    z_part = PartScatter(
        place, links, pz_ref, lambda s, c: pz_own.at[s, c], pz_first, pz_top, slots_out, 1
    )
    pz_load = links.local(lambda: (pz_ref.at[:, place.pair], pz_own))
    half = seq // 2

    def give_chunk(low):
        return links.far(
            lambda: (dh_give.at[:, low], dh_first.at[:, low], place.at(core=1))
        )

    dh_chunks = [give_chunk(low) for low in range(half)]
    dh_store = links.local(lambda: (dh_own, dh_out))
    stages = len(place.low_bits)

    @pl.when(step_at == 0)
    def _():
        mixed.begin()
        pz_load.start()
        meet_pair(place)
        z_part.send_pairs(1, 0)

    @pl.when(step_at == 1)
    def _():
        mixed.add_cores()
        mixed.send_stage(0)
        z_part.send_pairs(0, 0)

    @pl.when(step_at == 2)
    def _():
        pz_load.wait()
        z_part.add_pairs(1, 0)
        z_part.send_cross(0)
        w_rows.begin()

    @pl.when(step_at == 4)
    def _():
        z_part.add_pairs(0, 0)

    @pl.when(step_at == 5)
    def _():
        w_rows.add_pairs()

    @pl.when(step_at == pl.num_programs(0) - 1)
    def _():
        z_part.spread()

    @pl.when(step_at == pl.num_programs(0) - 3)
    def _():
        mixed.add_stage(0)
        if stages > 1:
            mixed.send_stage(1)

    @pl.when(pl.program_id(0) == 0)
    def _():
        memory[...] = jnp.zeros_like(memory)
        gx_ref[...] = jnp.zeros_like(gx_ref)
        gt_ref[...] = jnp.zeros_like(gt_ref)
        gh_ref[...] = jnp.zeros_like(gh_ref)
        next_x[:, length:, :] = jnp.zeros_like(next_x[:, length:, :])
        next_t[:, length:, :] = jnp.zeros_like(next_t[:, length:, :])

    params = (
        cx_ref[:KERNEL, :], cx_ref[KERNEL : KERNEL + 1, :],
        ct_ref[:KERNEL, :], ct_ref[KERNEL : KERNEL + 1, :],
        hp_ref[...], pick_ref[...],
    )
    skip_row = cx_ref[KERNEL + 2 : KERNEL + 3, :]
    for q in range(seqs):
        offset = off_ref[q, 0]
        conv_x, conv_t, raw, step, rate, decay_rate, cumul, spread, step_x, entry_x, end_x = (
            chunk_common(
                x_ref[q, 0, :, x_at:], xh_ref[q, 0, :, x_at:], tail_ref[q, 0], tailh_ref[q, 0], offset,
                params, ext_x.at[q], ext_t.at[q], width,
            )
        )
        dy_low = dy_ref[q, 0]
        dy = dy_low.astype(F32)

        sig_x = sigmoid(conv_x)
        xs = conv_x * sig_x
        slope_x = sig_x + xs * (1.0 - sig_x)
        sig_t = sigmoid(conv_t)
        act_t = conv_t * sig_t
        slope_t = sig_t + act_t * (1.0 - sig_t)
        bs = act_t[:, :STATE].astype(BF16)
        cs = act_t[:, STATE:].astype(BF16)
        scaled = xs * step_x
        scaled_low = scaled.astype(BF16)
        scores = mm_tr(bs, cs)
        rows, cols = iota((length, length), 0), iota((length, length), 1)
        gap = cols - rows
        same = (gap >= 0) & (gap.astype(F32) <= offr_ref[q, 0])
        strict = gap > 0
        upper = (rows >= cols).astype(BF16)
        cumul_t = cumul.T
        old = state_ref[q, 0]
        grad_state = memory[q]
        state_low = grad_state.astype(BF16)
        grad_scores = jnp.zeros((length, length), F32)
        grad_scaled = []
        inside_rows = []
        for start, size, heads in head_tiles(width):
            dy_tile = masked_heads(dy_low[:, start : start + size], heads)
            grad_mix = mm_tr(scaled_low[:, start : start + size], dy_tile)
            mixing = []
            for i, head in enumerate(heads):
                spans = cumul_t[head : head + 1, :] - cumul[:, head : head + 1]
                decays = jnp.exp(jnp.where(same, spans, -1e30))
                weighted = grad_mix[:, i * length : (i + 1) * length] * decays
                grad_scores = grad_scores + weighted
                mixing.append((decays * scores).astype(BF16))
                terms = jnp.where(strict, weighted * scores, 0.0).astype(BF16)
                sums = jnp.dot(terms, upper, preferred_element_type=F32)
                inside_rows.append(
                    jnp.sum(jnp.where(strict, sums, 0.0), axis=0, keepdims=True)
                )
            mix = mixing[0] if len(heads) == 1 else jnp.concatenate(mixing, axis=1)
            grad_scaled.append(jnp.dot(mix, dy_tile, preferred_element_type=F32))
        inside_rows.append(jnp.zeros((LANES - len(inside_rows), length), F32))
        inside = jnp.concatenate(inside_rows, axis=0).T
        from_end = mm(bs, state_low) * end_x
        grad_scaled = jnp.concatenate(grad_scaled, axis=1) + from_end
        entry_dy = dy * entry_x
        entry_dy_low = entry_dy.astype(BF16)
        out_terms = mm(cs, old) * entry_dy
        end_terms = scaled * from_end
        grad_step = mm_ones_tr(xs * grad_scaled, spread, 2)
        out_terms = mm_ones_tr(out_terms, spread, 2)
        end_terms = mm_ones_tr(end_terms, spread, 2)
        keep_row = entry_x[length - 1 : length, :]
        carried = jnp.sum(grad_state * old.astype(F32), axis=0, keepdims=True) * keep_row
        carried = mm_ones_tr(jnp.broadcast_to(carried, (8, width)), spread, 2)[0:1, :]
        triu = (cols >= rows).astype(BF16)
        below = (rows > cols).astype(BF16)
        grad_rate = inside + ones_mm(triu, out_terms, 2) + ones_mm(below, end_terms, 2) + carried
        grad_step = grad_step - decay_rate * grad_rate
        grad_raw = grad_step * sigmoid(raw)
        grad_scores_low = grad_scores.astype(BF16)
        grad_b = mm(grad_scores_low, cs) + mm_tr(scaled * end_x, state_low)
        grad_c = tr_mm(grad_scores_low, bs) + mm_tr(entry_dy_low, old)
        memory[q] = grad_state * keep_row + tr_mm(cs, entry_dy_low)
        conv_grad_x = (skip_row * dy + step_x * grad_scaled) * slope_x
        conv_grad_t = jnp.concatenate([grad_b, grad_c], axis=1) * slope_t

        remain = rem_ref[q, 0]
        results = []
        for grad, ext, nxt, weight, sums in (
            (conv_grad_x, ext_x.at[q], next_x.at[q], params[0], gx_ref),
            (conv_grad_t, ext_t.at[q], next_t.at[q], params[2], gt_ref),
        ):
            columns = grad.shape[1]
            current = ext[pl.ds(HALO, length), :]
            sums[KERNEL : KERNEL + 1, :columns] += jnp.sum(grad, axis=0, keepdims=True)
            sums[KERNEL - 1 : KERNEL, :columns] += jnp.sum(grad * current, axis=0, keepdims=True)
            nxt[0:length, :] = grad
            total = weight[KERNEL - 1 : KERNEL, :] * grad
            for back in range(1, KERNEL):
                tap = KERNEL - 1 - back
                shifted = jnp.where(offset >= back, ext[pl.ds(HALO - back, length), :], 0.0)
                sums[tap : tap + 1, :columns] += jnp.sum(grad * shifted, axis=0, keepdims=True)
                ahead = jnp.where(remain >= back, nxt[pl.ds(back, length), :], 0.0)
                total = total + weight[tap : tap + 1, :] * ahead
            nxt[length:, :] = grad[0:HALO, :]
            results.append(total.astype(BF16))
        results.append(mm_tr(grad_raw, params[5]).astype(BF16))
        gx_ref[KERNEL + 1 : KERNEL + 2, :width] += jnp.sum(dy * xs, axis=0, keepdims=True)
        gh_ref[0:1, :] += jnp.sum(grad_raw, axis=0, keepdims=True)
        gh_ref[1:2, :] += jnp.sum(grad_rate * rate, axis=0, keepdims=True)
        out_ref[q, 0] = jnp.concatenate(results, axis=1)

    depth = w_ref.shape[0]
    grad_h = mm_tr(dz_ref[...].reshape(seqs * length, width), w_ref[:, :width])
    grad_h = grad_h + mm_tr(
        out_ref[...].reshape(seqs * length, out_ref.shape[3]), w_ref[:, width:]
    )
    grad_h = grad_h.astype(BF16).reshape(seqs, length, depth)
    for i in range(seq):
        chunk = seq - 1 - i

        @pl.when((step_at == i) & (place.core == chunk // half))
        def _():
            dh_own[:, chunk % half] = grad_h

        @pl.when((step_at == i) & (place.core != chunk // half))
        def _():
            dh_give[:, chunk % half] = grad_h
            dh_chunks[chunk % half].start()

    @pl.when(step_at == pl.num_programs(0) - 1)
    def _():
        for stage in range(1, stages):
            mixed.add_stage(stage)
            if stage + 1 < stages:
                mixed.send_stage(stage + 1)
        for q in range(seqs):
            row = all_stat_ref[pl.ds(2 * (q * seq + place.chunk), 1), :]
            column = jnp.broadcast_to(row, (LANES, length)).T[:, 0:1]
            done = mix_own.at[q, place.low]
            done[...] = (done[...].astype(F32) * column).astype(BF16)
        mixed.store()
        z_part.finish()
        for copy in dh_chunks:
            copy.wait()
        for q in range(seqs):
            for low in range(half):
                add_rows(dh_own.at[q, low], dh_own.at[q, low], dh_first.at[q, low])
        dh_store.start()
        dh_store.wait()
        w_rows.finish()
        mixed.finish()


TAIL = 2 * STATE + LANES
AXES = ("seq", "fsdp")
MESH = pl.DeviceIdType.MESH
ANYWHERE = pl.BlockSpec(memory_space=pl.ANY)


def lane_rows(width):
    return -(-width // LANES)


def sum_rows(width):
    shared = D // LANES
    group = shared + (KERNEL + 1) * 2 * STATE // LANES
    return shared, group, -(-(group + (KERNEL + 3) * lane_rows(width) + 2) // 8) * 8


def whole_spec(shape):
    return pl.BlockSpec(shape, lambda i: (0,) * len(shape))


def chunk_specs(seqs, steps, length, reverse):
    def place(i):
        return steps - 1 - i if reverse else i

    def block(cols, column=0, rows=length):
        return pl.BlockSpec((seqs, 1, rows, cols), lambda i: (0, place(i), 0, column))

    def before(cols, column=0):
        return pl.BlockSpec(
            (seqs, 1, HALO, cols),
            lambda i: (0, jnp.maximum(place(i) - 1, 0), length // HALO - 1, column),
        )

    return block, before


def forward_mix(normed, zx, tail, segments, cotangent, out_w, packed, seq, fsdp):
    seqs, length, depth = normed.shape
    rows = tail.shape[0]
    cols = zx.shape[2] + TAIL
    width = zx.shape[2] // 2
    pairs = fsdp // 2
    count = seqs * seq * length

    def block(columns, height=length):
        return pl.BlockSpec(
            (seqs, 1, height, columns), lambda i: (0, jnp.minimum(i, seq - 1), 0, 0)
        )

    def blocks(columns, kind, height=length):
        return jax.ShapeDtypeStruct((seqs, seq, height, columns), kind)

    w_shape = (seq, pairs, 2, rows, cols)
    out_shape = (pairs, 2) + out_w.shape
    sums = (seqs * seq * 2, length)
    flat = 8 if rows % HALO == 0 else depth
    flat_out = 8 if out_w.shape[0] % HALO == 0 else width
    outs = pl.pallas_call(
        functools.partial(forward_kernel, seq, fsdp),
        grid=(seq + 1,),
        in_specs=[ANYWHERE] * 6 + [whole_spec(packed.shape)],
        out_specs=[
            block(cols), block(width, STATE), block(1), block(1), block(length, 1),
            ANYWHERE, ANYWHERE, ANYWHERE, ANYWHERE, whole_spec(sums), ANYWHERE, ANYWHERE, ANYWHERE, ANYWHERE,
            whole_spec((8, lane_rows(width) * LANES)), whole_spec((depth // LANES, LANES)),
            whole_spec((8, width)), whole_spec((8, LANES)), whole_spec((LANES, LANES)),
        ],
        out_shape=[
            blocks(cols, BF16), blocks(width, BF16, STATE),
            blocks(1, F32), blocks(1, F32), blocks(length, F32, 1),
            blocks(depth, BF16),
            jax.ShapeDtypeStruct(w_shape, BF16),
            jax.ShapeDtypeStruct((count, width), BF16),
            jax.ShapeDtypeStruct((count, width), BF16),
            jax.ShapeDtypeStruct(sums, F32),
            jax.ShapeDtypeStruct((seqs, seq // 2, length, depth), BF16),
            jax.ShapeDtypeStruct((seqs, seq // 2, length, depth), BF16),
            jax.ShapeDtypeStruct((width, depth), BF16),
            jax.ShapeDtypeStruct(w_shape[:4] + (width,), BF16),
            jax.ShapeDtypeStruct((8, lane_rows(width) * LANES), F32),
            jax.ShapeDtypeStruct((depth // LANES, LANES), F32),
            jax.ShapeDtypeStruct((8, width), F32),
            jax.ShapeDtypeStruct((8, LANES), F32),
            jax.ShapeDtypeStruct((LANES, LANES), BF16),
        ],
        scratch_shapes=[
            pltpu.VMEM((seqs, seq, length, depth), BF16),
            pltpu.VMEM(w_shape, BF16),
            pltpu.VMEM((flat, cols), BF16),
            pltpu.VMEM(segments.shape, segments.dtype),
            pltpu.VMEM((seqs, seq, length, depth), BF16),
            pltpu.VMEM(out_shape, BF16),
            pltpu.VMEM((flat_out, depth), BF16),
            pltpu.VMEM((count, width), BF16),
            pltpu.VMEM(sums, F32),
            pltpu.VMEM((seq - 1,) + sums, F32),
            pltpu.VMEM((count, width), F32),
            pltpu.VMEM((count, width), BF16),
            pltpu.VMEM((count, width), BF16),
            pltpu.VMEM((seqs, seq // 2, length, depth), BF16),
            pltpu.VMEM((seqs, seq // 2, length, depth), BF16),
            pltpu.VMEM((width, depth), BF16),
            pltpu.VMEM(w_shape[:4] + (width,), BF16),
            pltpu.VMEM((seqs, STATE, width), F32),
            pltpu.VMEM((seqs, HALO + length, width), F32),
            pltpu.VMEM((seqs, HALO + length, 2 * STATE), F32),
            pltpu.VMEM((seqs, HALO, cols), BF16),
            pltpu.SemaphoreType.DMA((320,)),
            pltpu.SemaphoreType.DMA((320,)),
            pltpu.SemaphoreType.DMA((24,)),
        ],
        compiler_params=pltpu.CompilerParams(
            dimension_semantics=("arbitrary",), vmem_limit_bytes=63 << 20, collective_id=0,
            has_side_effects=True,
        ),
        cost_estimate=pl.CostEstimate(
            flops=30_000_000_000, transcendentals=0, bytes_accessed=60_000_000
        ),
        name="mix_forward",
    )(normed, zx, tail, segments, cotangent, out_w, packed)
    (
        proj, states, off_col, rem_col, off_row, h_all, w_mine, dz, dy, stats, mixed, got, part,
        part_z, gain_out, gain_in,
    ) = outs[:16]
    return (
        proj, states, off_col, rem_col, off_row, h_all, w_mine.reshape(depth, cols), dz,
        dy.reshape(seqs, seq, length, width), stats, (mixed, got), part.reshape(out_shape),
        part_z, (gain_in, gain_out), outs[16:],
    )


def backward_mix(
    proj, off_col, off_row, rem_col, dy, dz, w_mine, stats, states, mixed, part_out, part_z, packed, consts, seq, fsdp
):
    seqs, steps, length, cols = proj.shape
    depth = mixed[0].shape[3]
    width = (cols - TAIL) // 2
    block, before = chunk_specs(seqs, steps, length, True)
    tail_at = 2 * width // TAIL
    x_cols, x_at = (width, 1) if width % LANES == 0 else (2 * width, 0)
    rows_in = part_z.shape[3]
    half, pairs = seq // 2, fsdp // 2
    rows_out = part_out.shape[2]
    sums = [(8, lane_rows(width) * LANES), (8, 2 * STATE), (8, LANES)]
    token_own = pltpu.VMEM((seqs, half, length, depth), BF16)
    return pl.pallas_call(
        functools.partial(backward_kernel, seq, fsdp),
        grid=(steps,),
        in_specs=[
            block(x_cols, x_at), before(x_cols, x_at),
            block(TAIL, tail_at), before(TAIL, tail_at),
            block(1), block(length, 0, 1), block(1), block(width), block(width),
            block(width, 0, STATE),
            pl.BlockSpec(w_mine.shape, lambda i: (0, 0), pipeline_mode=pl.Buffered(1)),
            whole_spec(stats.shape), ANYWHERE, ANYWHERE,
            ANYWHERE, ANYWHERE, whole_spec(consts[0].shape),
            pl.BlockSpec((8, 2 * STATE), lambda i: (0, INNER // (2 * STATE))),
            whole_spec(consts[1].shape), whole_spec(consts[2].shape),
        ],
        out_specs=[block(width + TAIL)] + [whole_spec(v) for v in sums] + [ANYWHERE] * 4,
        scratch_shapes=[
            pltpu.VMEM((seqs, STATE, width), F32),
            pltpu.VMEM((seqs, HALO + length, width), F32),
            pltpu.VMEM((seqs, HALO + length, 2 * STATE), F32),
            pltpu.VMEM((seqs, length + HALO, width), F32),
            pltpu.VMEM((seqs, length + HALO, 2 * STATE), F32),
            token_own, token_own, pltpu.VMEM((seqs, max(half - 1, 1), length, depth), BF16),
            pltpu.VMEM((2, rows_out, depth), BF16),
            pltpu.VMEM((max(pairs - 1, 1), 2, rows_out, depth), BF16),
            pltpu.VMEM((seq, 2, rows_in, width), BF16),
            pltpu.VMEM((max(pairs - 1, 1), seq, 2, rows_in, width), BF16),
            pltpu.VMEM((half, 2, rows_in, width), BF16),
            token_own, token_own, token_own,
            pltpu.SemaphoreType.DMA((128,)),
            pltpu.SemaphoreType.DMA((128,)),
            pltpu.SemaphoreType.DMA((16,)),
        ],
        out_shape=[jax.ShapeDtypeStruct(proj.shape[:3] + (width + TAIL,), BF16)]
        + [jax.ShapeDtypeStruct(v, F32) for v in sums]
        + [
            jax.ShapeDtypeStruct((seqs, length, depth), BF16),
            jax.ShapeDtypeStruct((2, rows_out, depth), BF16),
            jax.ShapeDtypeStruct((2, half, rows_in, width), BF16),
            jax.ShapeDtypeStruct((seqs, half, length, depth), BF16),
        ],
        compiler_params=pltpu.CompilerParams(
            dimension_semantics=("arbitrary",), vmem_limit_bytes=56 << 20, collective_id=3,
            has_side_effects=True,
        ),
        cost_estimate=pl.CostEstimate(
            flops=steps * seqs * 2_000_000_000, transcendentals=0, bytes_accessed=16_000_000
        ),
        name="mix_backward",
    )(
        proj, proj, proj, proj, off_col, off_row, rem_col, dy, dz.reshape(dy.shape), states,
        w_mine, stats, *mixed, part_out,
        part_z, consts[0], packed, consts[1], consts[2],
    )


class Place:
    def __init__(self, seq, fsdp):
        self.seq, self.fsdp = seq, fsdp
        self.half, self.pairs = seq // 2, fsdp // 2
        s, f = lax.axis_index("seq"), lax.axis_index("fsdp")
        self.s, self.f = s, f
        self.top, self.low = s // self.half, lax.rem(s, self.half)
        self.core, self.pair = lax.rem(f, 2), f // 2
        self.home = self.core == self.top
        self.away = self.core != self.top
        self.chunk = self.low + self.half * self.core
        self.low_bits = [1 << i for i in range(self.half.bit_length() - 1)]

    def at(self, top=0, low=0, pair=0, core=0):
        return (
            flip(self.top, top) * self.half + flip(self.low, low),
            flip(self.pair, pair) * 2 + flip(self.core, core),
        )

    def bits_for(self, q):
        return self.low_bits if q % 2 == 0 else self.low_bits[::-1]


def flip(index, bits):
    for i in range(bits.bit_length()):
        if bits >> i & 1:
            bit = lax.rem(index // (1 << i), 2)
            index = index + (1 << i) * (1 - 2 * bit)
    return index


class Copy:
    def __init__(self, make):
        self.make = make

    def start(self):
        self.make().start()
        return self

    def wait(self):
        self.make().wait()

    def wait_send(self):
        self.make().wait_send()

    def wait_recv(self):
        self.make().wait_recv()


class Links:
    def __init__(self, send, recv, near):
        self.send, self.recv, self.near = send, recv, near
        self.far_count = self.near_count = 0

    def far(self, make):
        i = self.far_count
        self.far_count += 1

        def build():
            src, dst, device = make()
            return pltpu.make_async_remote_copy(
                src_ref=src, dst_ref=dst, send_sem=self.send.at[i], recv_sem=self.recv.at[i],
                device_id=device, device_id_type=MESH,
            )

        return Copy(build)

    def local(self, make):
        i = self.near_count
        self.near_count += 1
        return Copy(lambda: pltpu.make_async_copy(*make(), self.near.at[i]))


def meet(devices):
    barrier = pltpu.get_barrier_semaphore()
    for device in devices:
        pl.semaphore_signal(barrier, inc=1, device_id=device, device_id_type=MESH)
    pl.semaphore_wait(barrier, len(devices))


def meet_pair(place):
    meet(
        [place.at(top=t, low=l, core=c) for t, l, c in peers_of(place)]
        + [place.at(pair=p) for p in range(1, place.pairs)]
    )


def peers_of(place):
    out = []
    for top in (0, 1):
        for low in range(place.half):
            for core in (0, 1):
                if (top, low, core) != (0, 0, 0):
                    out.append((top, low, core))
    return out


class TokenGather:
    def __init__(self, place, links, src, dst):
        self.place, self.src, self.dst = place, src, dst
        seqs = src.shape[0]

        def over(q):
            return links.far(
                lambda: (src.at[q], dst.at[q, place.s], place.at(top=1, core=1))
            )

        self.cross = [over(q) for q in range(seqs)]
        self.stay = links.local(lambda: (src, dst.at[:, place.s]))
        self.share = [[] for _ in range(seqs)]
        self.stages = []
        held = [[0] for _ in range(seqs)]
        for q in range(seqs):
            self.share[q].append([self.copy(links, q, low, core=1) for low in held[q]])
        for i in range(len(place.low_bits)):
            stage = []
            for q in range(seqs):
                bit = place.bits_for(q)[i]
                stage.append([self.copy(links, q, low, low_bit=bit) for low in held[q]])
                fresh = [low ^ bit for low in held[q]]
                held[q] = held[q] + fresh
                self.share[q].append([self.copy(links, q, low, core=1) for low in fresh])
            self.stages.append(stage)

    def copy(self, links, q, low, low_bit=0, core=0):
        def make():
            place = self.place
            ref = self.dst.at[q, flip(place.low, low) + place.half * place.core]
            return ref, ref, place.at(low=low_bit, core=core)

        return links.far(make)

    def begin(self):
        self.cross_over()
        self.begin_home()

    def cross_over(self):
        @pl.when(self.place.away)
        def _():
            for copy in self.cross:
                copy.start()

    def begin_home(self):
        @pl.when(self.place.home)
        def _():
            self.stay.start()
            self.stay.wait()
            self.send_stage(0)

    def arrive(self):
        @pl.when(self.place.away)
        def _():
            for copy in self.cross:
                copy.wait_recv()
            self.send_stage(0)

    def send_stage(self, i):
        for q in range(len(self.share)):
            for copy in self.stages[i][q] + self.share[q][i]:
                copy.start()

    def pass_on(self, i, role):
        @pl.when(self.place.home if role == "home" else self.place.away)
        def _():
            for q in range(len(self.share)):
                for copy in self.stages[i][q]:
                    copy.wait_recv()
                for copy in (self.stages[i + 1][q] if i + 1 < len(self.stages) else []):
                    copy.start()
                for copy in self.share[q][i + 1]:
                    copy.start()

    def finish(self):
        for share in self.share:
            for copies in share:
                for copy in copies:
                    copy.wait()
        for stage in self.stages:
            for copies in stage:
                for copy in copies:
                    copy.wait_send()

        @pl.when(self.place.away)
        def _():
            for copy in self.cross:
                copy.wait_send()


class RowGather:
    def __init__(self, place, links, src, dst):
        self.place = place
        pairs = range(1, place.pairs)

        def slot():
            return dst.at[place.pair, place.core]

        self.stay = links.local(lambda: (src, slot()))
        self.to_home = links.far(lambda: (src, slot(), place.at(core=1)))
        self.to_near = links.far(lambda: (src, slot(), place.at(top=1)))
        self.to_far = links.far(lambda: (src, slot(), place.at(top=1, core=1)))

        def forward(c, p):
            return links.far(
                lambda: (dst.at[place.pair, c], dst.at[place.pair, c], place.at(pair=p))
            )

        self.forwards = [forward(c, p) for c in (0, 1) for p in pairs]

    def begin(self):
        @pl.when(self.place.home)
        def _():
            self.stay.start()
            self.to_near.start()

        @pl.when(self.place.away)
        def _():
            self.to_home.start()
            self.to_far.start()

    def forward(self):
        @pl.when(self.place.home)
        def _():
            self.stay.wait()
            self.to_home.wait_recv()

        @pl.when(self.place.away)
        def _():
            self.to_near.wait_recv()
            self.to_far.wait_recv()

        for copy in self.forwards:
            copy.start()

    def finish(self):
        for copy in self.forwards:
            copy.wait()

        @pl.when(self.place.home)
        def _():
            self.to_near.wait_send()

        @pl.when(self.place.away)
        def _():
            self.to_home.wait_send()
            self.to_far.wait_send()


class Entry:
    def __init__(self, place, links, h_ref, zx_ref, tail_ref, seg_ref, h_v, w_v, seg_v):
        self.place = place
        cols = zx_ref.shape[2]
        self.peers = peers = peers_of(place)
        others = range(1, place.pairs)
        self.tokens = TokenGather(place, links, h_ref, h_v)

        def block(t=0, l=0, c=0):
            s, f = place.at(top=t, low=l, core=c)
            return w_v.at[s, place.pair, lax.rem(f, 2)]

        def columns(ref):
            return ref.at[:, pl.ds(0, cols)]

        def tail_of(ref):
            return ref.at[:, pl.ds(cols, TAIL)]

        def send_zx(t, l, c):
            group = flip(place.core, c) * place.half + flip(place.low, l)
            return zx_ref.at[group], columns(block()), place.at(top=t, low=l, core=c)

        self.zx = {p: links.far(functools.partial(send_zx, *p)) for p in peers}
        self.own = [
            links.local(lambda: (zx_ref.at[place.chunk], columns(block()))),
            links.local(lambda: (tail_ref, tail_of(block()))),
        ]
        self.tail_cross = links.far(lambda: (tail_ref, tail_of(block()), place.at(top=1)))
        self.near_peers = [(l, c) for t, l, c in peers if t == 0]

        def send_tail(l, c):
            return tail_ref, tail_of(block()), place.at(low=l, core=c)

        def send_other(l, c):
            return tail_of(block(1)), tail_of(block(1)), place.at(low=l, core=c)

        self.tails = {p: links.far(functools.partial(send_tail, *p)) for p in self.near_peers}
        self.tails_more = {
            p: links.far(functools.partial(send_other, *p)) for p in self.near_peers
        }
        self.seg_send = links.far(lambda: (seg_ref, seg_v, place.at(core=1)))
        self.seg_keep = links.local(lambda: (seg_ref, seg_v))

        def send_on(t, l, c, p):
            return block(t, l, c), block(t, l, c), place.at(pair=p)

        self.forwards = {
            p: [links.far(functools.partial(send_on, *p, other)) for other in others]
            for p in [(0, 0, 0)] + peers
        }

    def run(self, then):
        tokens, zx, forwards = self.tokens, self.zx, self.forwards
        stages = len(self.place.low_bits)
        far_peers = [p for p in self.peers if p[0] == 1]
        tokens.begin()
        self.tail_cross.start()
        for copy in self.own:
            copy.start()
        for p in self.near_peers:
            zx[0, *p].start()
            self.tails[p].start()

        @pl.when(self.place.home)
        def _():
            self.seg_send.start()
            self.seg_keep.start()

        for copy in self.own:
            copy.wait()
        for copy in forwards[0, 0, 0]:
            copy.start()
        self.tail_cross.wait_recv()
        for p in self.near_peers:
            self.tails_more[p].start()
        tokens.pass_on(0, "home")
        for p in self.near_peers:
            zx[0, *p].wait_recv()
            self.tails[p].wait_recv()
            for copy in forwards[0, *p]:
                copy.start()
        for p in far_peers:
            zx[p].start()
        for i in range(1, stages):
            tokens.pass_on(i, "home")
        tokens.arrive()
        for p in self.near_peers:
            self.tails_more[p].wait_recv()
        for i in range(stages):
            tokens.pass_on(i, "away")
            at, to = (len(far_peers) * k // stages for k in (i, i + 1))
            for p in far_peers[at:to]:
                zx[p].wait_recv()
                for copy in forwards[p]:
                    copy.start()
        then()

        @pl.when(self.place.home)
        def _():
            self.seg_keep.wait()
            self.seg_send.wait_send()

        @pl.when(self.place.away)
        def _():
            self.seg_send.wait_recv()

        tokens.finish()
        for p in forwards:
            for copy in forwards[p]:
                copy.wait()

    def finish(self):
        self.tail_cross.wait_send()
        for group in (self.zx, self.tails, self.tails_more):
            for copy in group.values():
                copy.wait_send()


def add_rows(out, left, right, rows=32):
    total = left.shape[0]
    step = next((size for size in (rows, 16) if total % size == 0), total)

    if step == total:
        out[...] = (left[...].astype(F32) + right[...].astype(F32)).astype(out.dtype)
        return

    @pl.loop(0, total // step)
    def _(i):
        at = pl.ds(pl.multiple_of(i * step, step), step)
        out[at] = (left[at].astype(F32) + right[at].astype(F32)).astype(out.dtype)


class TokenScatter:
    def __init__(self, place, links, src, out, own, first, later, held):
        self.place = place
        self.out, self.own, self.first, self.later = out, own, first, later
        self.seqs = own.shape[0]
        half = place.half
        self.loads = []
        if held == "sums":
            self.loads = [links.local(lambda: (src, own))]
        if held == "halves":
            self.loads = [
                links.local(lambda: (src[0], own)), links.local(lambda: (src[1], first)),
            ]
        self.stages = [[] for _ in place.low_bits]
        for q in range(self.seqs):
            live, slot = list(range(half)), 0
            for i, bit in enumerate(place.bits_for(q)[::-1]):
                for low in [low for low in live if low & bit]:
                    self.stages[i].append((self.copy(links, q, low, slot, bit), q, low ^ bit, slot))
                    slot += 1
                live = [low for low in live if not low & bit]
        self.stay = links.local(lambda: (own.at[:, place.low], out))

    def copy(self, links, q, low, slot, bit):
        return links.far(
            lambda: (
                self.own.at[q, flip(self.place.low, low)], self.later.at[q, slot],
                self.place.at(low=bit),
            )
        )

    def begin(self):
        for copy in self.loads:
            copy.start()

    def add_cores(self):
        for copy in self.loads:
            copy.wait()
        for q in range(self.seqs if self.first is not None else 0):
            for low in range(self.place.half):
                add_rows(self.own.at[q, low], self.own.at[q, low], self.first.at[q, low])

    def send_stage(self, i):
        for copy, _, _, _ in self.stages[i]:
            copy.start()

    def add_stage(self, i):
        for copy, q, low, slot in self.stages[i]:
            copy.wait_recv()
            ref = self.own.at[q, flip(self.place.low, low)]
            add_rows(ref, ref, self.later.at[q, slot])

    def store(self):
        self.stay.start()
        self.stay.wait()

    def finish(self):
        for stage in self.stages:
            for copy, _, _, _ in stage:
                copy.wait_send()


class RowScatter:
    def __init__(self, place, links, src, out, own, first):
        self.place, self.own, self.first = place, own, first

        def over(p):
            return links.far(
                lambda: (src.at[flip(place.pair, p)], first.at[p - 1], place.at(pair=p))
            )

        def far(c):
            return links.far(
                lambda: (own.at[flip(place.core, c)], out.at[1], place.at(top=1, core=c))
            )

        self.over = [over(p) for p in range(1, place.pairs)]
        self.load = links.local(lambda: (src.at[place.pair], own))
        self.far = [far(0), far(1)]
        self.near = links.far(lambda: (own.at[1 - place.core], out.at[0], place.at(core=1)))
        self.stay = links.local(lambda: (own.at[place.core], out.at[0]))

    def begin(self):
        self.load.start()
        for copy in self.over:
            copy.start()

    def add_pairs(self):
        self.load.wait()
        for i, copy in enumerate(self.over):
            copy.wait_recv()
            for c in (0, 1):
                add_rows(self.own.at[c], self.own.at[c], self.first.at[i, c])

        @pl.when(self.place.away)
        def _():
            for copy in self.far:
                copy.start()

        @pl.when(self.place.home)
        def _():
            self.near.start()
            self.stay.start()

    def finish(self):
        for copy in self.over:
            copy.wait_send()

        @pl.when(self.place.home)
        def _():
            self.stay.wait()
            self.near.wait_send()
            self.far[0].wait_recv()

        @pl.when(self.place.away)
        def _():
            self.near.wait_recv()
            self.far[1].wait_recv()
            for copy in self.far:
                copy.wait_send()


class PartScatter:
    def __init__(self, place, links, src, own, first, other, slots, tiles):
        self.place, self.own, self.first, self.other = place, own, first, other
        self.high = high = place.half // tiles
        pairs = range(1, place.pairs)

        def rows(top, k):
            return pl.ds(place.half * flip(place.top, top) + k * high, high)

        def over(top, k, p):
            return links.far(
                lambda: (
                    src.at[rows(top, k), flip(place.pair, p)], first.at[p - 1, rows(top, k)],
                    place.at(pair=p),
                )
            )

        def cross(i, c):
            def make():
                at = place.half * flip(place.top, 1) + i
                return own(at, c), other.at[i, c], place.at(top=1)

            return links.far(make)

        def spread(l, c):
            return links.far(
                lambda: (
                    self.block(l, c), slots.at[place.core, place.low], place.at(low=l, core=c)
                )
            )

        self.over = [[[over(top, k, p) for p in pairs] for k in range(tiles)] for top in (0, 1)]
        self.cross = [
            [cross(k * high + i, c) for i in range(high) for c in (0, 1)] for k in range(tiles)
        ]
        self.near = [(l, c) for t, l, c in peers_of(place) if t == 0]
        self.slots = {p: spread(*p) for p in self.near}
        self.slots[0, 0] = links.local(
            lambda: (self.block(0, 0), slots.at[place.core, place.low])
        )

    def block(self, l, c):
        place = self.place
        return self.own(place.half * place.top + flip(place.low, l), flip(place.core, c))

    def send_pairs(self, top, k):
        for copy in self.over[top][k]:
            copy.start()

    def add_pairs(self, top, k):
        for i, copy in enumerate(self.over[top][k]):
            copy.wait_recv()
            for low in range(self.high):
                for c in (0, 1):
                    at = self.place.half * flip(self.place.top, top) + k * self.high + low
                    ref = self.own(at, c)
                    add_rows(ref, ref, self.first.at[i, at, c], 16)

    def send_cross(self, k):
        for copy in self.cross[k]:
            copy.start()

    def wait_cross(self, k):
        for copy in self.cross[k]:
            copy.wait_recv()

    def spread(self, waits=True):
        if waits:
            for k in range(len(self.cross)):
                self.wait_cross(k)
        place = self.place
        for l, c in self.near + [(0, 0)]:
            ref = self.block(l, c)
            add_rows(ref, ref, self.other.at[flip(place.low, l), flip(place.core, c)], 16)
            self.slots[l, c].start()

    def finish(self):
        for copy in self.slots.values():
            copy.wait()
        for copies in self.cross + [c for top in self.over for c in top]:
            for copy in copies:
                copy.wait_send()


class Deliver:
    def __init__(self, place, links, src, out):
        self.place = place
        self.cross = links.far(lambda: (src(), out, place.at(top=1, core=1)))
        self.stay = links.local(lambda: (src(), out))

    def begin(self):
        @pl.when(self.place.away)
        def _():
            self.cross.start()

        @pl.when(self.place.home)
        def _():
            self.stay.start()

    def finish(self):
        @pl.when(self.place.away)
        def _():
            self.cross.wait()

        @pl.when(self.place.home)
        def _():
            self.stay.wait()


def exit_kernel(
    seq, fsdp,
    h_ref, dh_ref, grad_ref, w_ref, mixed_ref, gain_in_ref, gain_out_ref, gx_ref, gt_ref, gh_ref,
    dh_out, mixed_out, slots_out, vec_out,
    h_all, grads, weights, part, dh_own, dh_later, part_first, part_top, vec_val, vec_got,
    send, recv, near,
):
    place = Place(seq, fsdp)
    links = Links(send, recv, near)
    half = place.half
    others = list(range(1, place.pairs))
    seqs, _, length, depth = dh_own.shape
    rows = part.shape[3]
    width = weights.shape[1] - grads.shape[1]
    dh = TokenScatter(
        place, links, dh_ref, dh_out, dh_own, None, dh_later, "sums"
    )
    dh_last = Deliver(place, links, lambda: dh_own.at[:, place.low], dh_out)
    mixed = Deliver(place, links, lambda: mixed_ref, mixed_out)
    loads = [
        links.local(lambda: (h_ref, h_all)),
        links.local(lambda: (grad_ref, grads)),
        links.local(lambda: (w_ref, weights)),
    ]

    tiles = depth // 2 // TILE
    rest = PartScatter(
        place, links, part, lambda s, c: part.at[s, place.pair, c], part_first, part_top, slots_out,
        tiles,
    )

    hops = [dict(pair=1 << i) for i in range(place.pairs.bit_length() - 1)] + [dict(top=1)]

    def hop(i):
        return links.far(lambda: (vec_val.at[i], vec_got.at[i], place.at(**hops[i])))

    def share(l, c):
        return links.far(
            lambda: (
                vec_val.at[len(hops)], vec_out.at[place.core, place.low],
                place.at(low=l, core=c),
            )
        )

    vec = [hop(i) for i in range(len(hops))]
    vec_shares = [share(l, c) for t, l, c in peers_of(place) if t == 0]
    vec_shares.append(
        links.local(lambda: (vec_val.at[len(hops)], vec_out.at[place.core, place.low]))
    )

    def vec_next(i):
        vec[i].wait_recv()
        vec_val[i + 1] = vec_val[i] + vec_got[i]
        for copy in vec[i + 1 : i + 2] if i + 1 < len(hops) else vec_shares:
            copy.start()

    blocks = TILE // rows

    def weight_rows(top, k):
        t = tiles * flip(place.top, top) + k
        lanes = pl.ds(pl.multiple_of(t * TILE, LANES), TILE)
        term = tr_mm(h_all[:, lanes], grads[...])
        for b in range(blocks):
            at = t * (blocks // fsdp) + b // fsdp
            part[at, b % fsdp // 2, b % 2] = term[b * rows : (b + 1) * rows].astype(BF16)
        sums = jnp.sum(term * weights[lanes, width:].astype(F32), axis=1, keepdims=True)
        wide = jnp.broadcast_to(sums, (TILE, LANES))
        for i in range(TILE // LANES):
            row = pl.ds(t * (TILE // LANES) + i, 1)
            vec_val[0, row, :] = gain_in_ref[row, :] + wide[i * LANES : (i + 1) * LANES].T[0:1, :]
        rest.send_pairs(top, k)

    def place_sums():
        at, group, _ = sum_rows(width)
        vec_val[0] = jnp.zeros_like(vec_val[0])
        for tap in range(KERNEL + 1):
            for j in range(2 * STATE // LANES):
                vec_val[0, at : at + 1, :] = gt_ref[
                    tap : tap + 1, j * LANES : (j + 1) * LANES
                ]
                at += 1
        pieces_of = [
            ref[line : line + 1, j * LANES : (j + 1) * LANES]
            for ref, line in [(gx_ref, i) for i in range(KERNEL + 2)] + [(gain_out_ref, 0)]
            for j in range(lane_rows(width))
        ] + [gh_ref[0:1, :], gh_ref[1:2, :]]
        for i, piece in enumerate(pieces_of):
            vec_val[0, group + i : group + i + 1, :] = piece

    dh.begin()
    for copy in loads:
        copy.start()
    meet_pair(place)
    dh.add_cores()
    dh.send_stage(0)
    mixed.begin()
    place_sums()
    for copy in loads:
        copy.wait()
    for k in range(tiles):
        weight_rows(1, k)
    for k in range(tiles):
        weight_rows(0, k)
    vec[0].start()
    for k in range(tiles):
        rest.add_pairs(1, k)
        rest.send_cross(k)
    stages = len(place.low_bits)
    for i in range(stages):
        dh.add_stage(i)
        if i + 1 < stages:
            dh.send_stage(i + 1)
        else:
            dh_last.begin()
        if i < len(hops):
            vec_next(i)
    for i in range(stages, len(hops)):
        vec_next(i)
    for k in range(tiles):
        rest.add_pairs(0, k)
    rest.spread()
    for copy in vec_shares:
        copy.wait()
    rest.finish()
    mixed.finish()
    dh_last.finish()
    dh.finish()
    for copy in vec:
        copy.wait_send()


def exit_scatter(seq, fsdp, h_all, grad_h, grad_proj, w_mine, mixed, sums):
    seqs, _, length, depth = h_all.shape
    half, pairs = seq // 2, fsdp // 2
    cols = w_mine.shape[1]
    rest = grad_proj.shape[3]
    width = cols - rest
    rows = depth // (seq * fsdp)
    count = seqs * seq * length
    vector = (sum_rows(width)[2], LANES)
    hops = pairs.bit_length()
    token_own = pltpu.VMEM((seqs, half, length, depth), BF16)
    tokens = jax.ShapeDtypeStruct((seqs, length, depth), BF16)
    return pl.pallas_call(
        functools.partial(exit_kernel, seq, fsdp),
        in_specs=[ANYWHERE] * 5 + [pl.BlockSpec(memory_space=pltpu.VMEM)] * 5,
        out_specs=[ANYWHERE] * 4,
        out_shape=[
            tokens,
            tokens,
            jax.ShapeDtypeStruct((2, half, rows, rest), BF16),
            jax.ShapeDtypeStruct((2, half) + vector, F32),
        ],
        scratch_shapes=[
            pltpu.VMEM((count, depth), BF16),
            pltpu.VMEM((count, rest), BF16),
            pltpu.VMEM((depth, cols), BF16),
            pltpu.VMEM((seq, pairs, 2, rows, rest), BF16),
            token_own,
            pltpu.VMEM((seqs, max(half - 1, 1), length, depth), BF16),
            pltpu.VMEM((max(pairs - 1, 1), seq, 2, rows, rest), BF16),
            pltpu.VMEM((half, 2, rows, rest), BF16),
            pltpu.VMEM((hops + 1,) + vector, F32),
            pltpu.VMEM((hops,) + vector, F32),
            pltpu.SemaphoreType.DMA((96,)),
            pltpu.SemaphoreType.DMA((96,)),
            pltpu.SemaphoreType.DMA((16,)),
        ],
        compiler_params=pltpu.CompilerParams(
            collective_id=1, has_side_effects=True, vmem_limit_bytes=60 << 20
        ),
        cost_estimate=pl.CostEstimate(
            flops=0, transcendentals=0, bytes_accessed=200_000_000
        ),
        name="exit_scatter",
    )(
        h_all.reshape(count, depth), grad_h, grad_proj.reshape(count, rest), w_mine, mixed, *sums
    )


def finish_kernel(
    seq,
    tok_ref, cot_ref, gain_ref, dh_ref, mixed_ref, slots_z_ref, slots_ref, rows_ref, vec_ref,
    mixed_out, tokens_out, gain_in_out, w_in_out, conv_w_out, conv_b_out, heads_out, gain_out_out,
    w_out_out,
):
    gain = gain_ref[...]
    for q in range(tok_ref.shape[0]):
        wide = tok_ref[q].astype(F32)
        mixed_out[q] = (wide + mixed_ref[q].astype(F32)).astype(BF16)
        scale = lax.rsqrt(jnp.mean(wide * wide, axis=-1, keepdims=True) + EPSILON)
        unit = wide * scale
        scaled = dh_ref[q].astype(F32) * gain
        tokens_out[q] = cot_ref[q].astype(F32) + scale * (
            scaled - unit * jnp.mean(scaled * unit, axis=-1, keepdims=True)
        )
    groups, _, cols = slots_ref.shape
    width = cols - TAIL
    tail = jnp.zeros((slots_ref.shape[1], TAIL), F32)
    for g in range(groups):
        w_in_out[:, g * width : (g + 1) * width] = slots_z_ref[g].astype(F32)
        w_in_out[:, INNER + g * width : INNER + (g + 1) * width] = (
            slots_ref[g, :, :width].astype(F32)
        )
        tail = tail + slots_ref[g, :, width:].astype(F32)
    w_in_out[:, 2 * INNER :] = tail[:, : 2 * STATE + HEADS]
    w_out_out[...] = rows_ref[0].astype(F32) + rows_ref[1].astype(F32)

    row, group, _ = sum_rows(width)
    heads = HEADS // seq
    common = vec_ref[0, :group]
    for g in range(1, groups):
        common = common + vec_ref[g, :group]
    for j in range(D // LANES):
        at = slice(j * LANES, (j + 1) * LANES)
        gain_in_out[:, at] = common[j : j + 1] / gain_ref[:, at]
    targets = [conv_w_out.at[k : k + 1] for k in range(KERNEL)] + [conv_b_out]
    for out in targets:
        for j in range(2 * STATE // LANES):
            out[:, INNER + j * LANES : INNER + (j + 1) * LANES] = common[row : row + 1]
            row += 1
    across = lane_rows(width)
    lane = iota((8, LANES), 1)
    per_head = jnp.zeros((8, LANES), F32)
    fold = expander(across * LANES)
    for g in range(groups):
        def lanes_of(line):
            first = group + line * across
            return jnp.concatenate(
                [vec_ref[g, first + j : first + j + 1, :] for j in range(across)], axis=1
            )

        at = slice(g * width, (g + 1) * width)
        for line, out in enumerate(targets):
            out[:, at] = lanes_of(line)[:, :width]
        gain_out_out[:, at] = lanes_of(KERNEL + 2)[:, :width]
        skip = mm_ones_tr(jnp.broadcast_to(lanes_of(KERNEL + 1), (8, across * LANES)), fold, 3)
        last = group + (KERNEL + 3) * across
        lines = jnp.concatenate(
            [skip[0:1, :], vec_ref[g, last : last + 2, :], jnp.zeros((5, LANES), F32)], axis=0
        )
        lines = jnp.where(lane < heads, lines, 0.0)
        per_head = per_head + (pltpu.roll(lines, g * heads, 1) if g else lines)
    heads_out[...] = per_head


def finish(seq, tokens, cotangent, gain_in, grad_h, mixed, slots_z, slots, rows, vector, shapes):
    columns = INNER + 2 * STATE
    kinds = [
        (tokens.shape, BF16), (tokens.shape, F32), ((1, D), F32), (shapes[0], F32),
        ((KERNEL, columns), F32), ((1, columns), F32), ((8, LANES), F32), ((1, INNER), F32),
        (shapes[1], F32),
    ]
    return pl.pallas_call(
        functools.partial(finish_kernel, seq),
        out_shape=[jax.ShapeDtypeStruct(*kind) for kind in kinds],
        compiler_params=pltpu.CompilerParams(vmem_limit_bytes=32 << 20),
        name="finish",
    )(tokens, cotangent, gain_in[None], grad_h, mixed, slots_z, slots, rows, vector)


def local(
    tokens, segments, gain_in, w_in, conv_w, conv_b, dt_bias, a_log, skip, gain_out, w_out,
    cotangent,
):
    steps, shards = lax.axis_size("seq"), lax.axis_size("fsdp")
    place = Place(steps, shards)
    seqs, length, _ = tokens.shape
    width = INNER // steps
    rows_in = w_in.shape[0]

    wide = tokens.astype(F32)
    scale_in = lax.rsqrt(jnp.mean(wide * wide, axis=-1, keepdims=True) + EPSILON)
    normed = (wide * scale_in * gain_in).astype(BF16)
    zx = w_in[:, : 2 * INNER].reshape(rows_in, 2, steps, width).transpose(2, 0, 1, 3)
    zx = zx.reshape(steps, rows_in, 2 * width)
    tail = jnp.pad(w_in[:, 2 * INNER :], ((0, 0), (0, LANES - HEADS)))
    columns = INNER + 2 * STATE

    def line(*arrays):
        arrays = [jnp.pad(v, (0, -v.shape[0] % LANES)) for v in arrays]
        return jnp.pad(jnp.concatenate(arrays), (0, columns - sum(v.shape[0] for v in arrays)))

    packed = jnp.concatenate(
        [
            conv_w,
            jnp.stack(
                [conv_b, line(gain_out), line(dt_bias, a_log, skip), jnp.zeros((columns,), F32)]
            ),
        ]
    )
    (
        proj, states, off_col, rem_col, off_row, h_all, w_mine, dz, dy, stats, mixed, part_out,
        part_z, gains, consts,
    ) = forward_mix(normed, zx, tail, segments, cotangent, w_out, packed, steps, shards)
    grad_proj, sums_x, sums_t, sums_h, mixed, rows, slots_z, grad_h = backward_mix(
        proj, off_col, off_row, rem_col, dy, dz, w_mine, stats, states, mixed,
        part_out, part_z, packed, consts, steps, shards,
    )
    grad_h, mixed, slots, vector = exit_scatter(
        steps, shards, h_all, grad_h, grad_proj, w_mine, mixed, gains + (sums_x, sums_t, sums_h)
    )
    (
        mixed, tokens_grad, gain_in_grad, w_in_grad, conv_w_grad, conv_b_grad, per_head,
        gain_out_grad, w_out_grad,
    ) = finish(
        steps, tokens, cotangent, gain_in, grad_h, mixed,
        slots_z.reshape(steps, rows_in, width), slots.reshape(steps, rows_in, width + TAIL), rows,
        vector.reshape((steps,) + vector.shape[2:]), (w_in.shape, w_out.shape),
    )
    return (
        mixed, tokens_grad, gain_in_grad[0], w_in_grad, conv_w_grad, conv_b_grad[0],
        per_head[1, :HEADS], per_head[2, :HEADS], per_head[0, :HEADS], gain_out_grad[0],
        w_out_grad,
    )


def solution(mesh):
    by_token = P("fsdp", "seq", None)
    by_row = P(("seq", "fsdp"), None)
    placed = (
        by_token, P("fsdp", None), P(), by_row, P(), P(), P(), P(), P(), P(), by_row, by_token,
    )
    return jax.shard_map(
        local,
        mesh=mesh,
        in_specs=placed,
        out_specs=(by_token, by_token, P(), by_row, P(), P(), P(), P(), P(), P(), by_row),
        check_vma=False,
    )
```

```python
import functools

import jax
import jax.numpy as jnp
import numpy as np
from jax import lax
from jax.experimental import pallas as pl
from jax.experimental.pallas import tpu as pltpu
from jax.sharding import PartitionSpec as P

D = 1536
HEADS = 48
HEAD_DIM = 64
STATE = 128
KERNEL = 4
INNER = 3072
LANES = 128
HALO = 16
EPSILON = 1e-05
TILE = 384
F32 = jnp.float32
BF16 = jnp.bfloat16


def mm(a, b):
    return jnp.dot(a.astype(BF16), b.astype(BF16), preferred_element_type=F32)


def mm_tr(a, b):
    return lax.dot_general(
        a.astype(BF16), b.astype(BF16), (((1,), (1,)), ((), ())), preferred_element_type=F32
    )


def tr_mm(a, b):
    return lax.dot_general(
        a.astype(BF16), b.astype(BF16), (((0,), (0,)), ((), ())), preferred_element_type=F32
    )


def pieces(a, count):
    out = []
    for _ in range(count - 1):
        part = a.astype(BF16)
        out.append(part)
        a = a - part.astype(F32)
    out.append(a.astype(BF16))
    return out


def ones_mm(ones, a, count):
    return sum(jnp.dot(ones, part, preferred_element_type=F32) for part in pieces(a, count))


def mm_ones(a, ones, count):
    return sum(jnp.dot(part, ones, preferred_element_type=F32) for part in pieces(a, count))


def mm_ones_tr(a, ones, count):
    return sum(
        lax.dot_general(part, ones, (((1,), (1,)), ((), ())), preferred_element_type=F32)
        for part in pieces(a, count)
    )


def iota(shape, dim):
    return lax.broadcasted_iota(jnp.int32, shape, dim)


def softplus(v):
    return jnp.maximum(v, 0.0) + jnp.log1p(jnp.exp(-jnp.abs(v)))


def sigmoid(v):
    return 1.0 / (1.0 + jnp.exp(-v))


def causal_conv(ext, current, halo, weight, bias, offset):
    length = current.shape[0]
    ext[0:HALO, :] = halo
    ext[HALO : HALO + length, :] = current
    total = bias + weight[KERNEL - 1 : KERNEL, :] * current
    for back in range(1, KERNEL):
        shifted = jnp.where(offset >= back, ext[pl.ds(HALO - back, length), :], 0.0)
        total = total + weight[KERNEL - 1 - back : KERNEL - back, :] * shifted
    return total


def head_tiles(width):
    out = []
    for start in range(0, width, LANES):
        size = min(LANES, width - start)
        heads = [start // HEAD_DIM + i for i in range(size // HEAD_DIM)]
        out.append((start, size, heads))
    return out


def masked_heads(tile, heads):
    if len(heads) == 1:
        return tile
    lane = iota(tile.shape, 1) // HEAD_DIM
    return jnp.concatenate(
        [jnp.where(lane == i, tile, jnp.zeros_like(tile)) for i in range(len(heads))], axis=0
    )


def expander(width):
    return (iota((LANES, width), 1) // HEAD_DIM == iota((LANES, width), 0)).astype(BF16)


def chunk_common(x, xh, tail, tailh, offset, params, ext_x, ext_t, width):
    wx, bx, wt, bt, heads_p, pick = params
    length = x.shape[0]
    conv_x = causal_conv(ext_x, x.astype(F32), xh.astype(F32), wx, bx, offset)
    conv_t = causal_conv(
        ext_t,
        tail[:, : 2 * STATE].astype(F32),
        tailh[:, : 2 * STATE].astype(F32),
        wt,
        bt,
        offset,
    )
    raw = jnp.dot(tail[:, 2 * STATE :], pick, preferred_element_type=F32) + heads_p[0:1, :]
    step = softplus(raw)
    decay_rate = jnp.exp(heads_p[1:2, :])
    rate = -step * decay_rate
    tril = (iota((length, length), 0) >= iota((length, length), 1)).astype(BF16)
    cumul = ones_mm(tril, rate, 3)
    spread = expander(width)
    row = iota((length, 1), 0)
    entry = jnp.where(offset > row.astype(F32), jnp.exp(cumul), 0.0)
    last_off = offset[length - 1 : length, :]
    same_last = row.astype(F32) >= (length - 1) - last_off
    to_end = jnp.where(same_last, jnp.exp(cumul[length - 1 : length, :] - cumul), 0.0)
    step_x = mm_ones(step, spread, 2)
    entry_x = mm_ones(entry, spread, 2)
    end_x = mm_ones(to_end, spread, 2)
    return conv_x, conv_t, raw, step, rate, decay_rate, cumul, spread, step_x, entry_x, end_x


def positions(segments, chunk, length):
    here = jnp.zeros((1, length), F32)
    total = segments.shape[1] // length
    rows = [segments[:, i * length : (i + 1) * length].astype(F32) for i in range(total)]
    for i in range(total):
        here = here + jnp.where(chunk == i, rows[i], 0.0)
    own = jnp.broadcast_to(here, (length, length)).T
    less = jnp.zeros((length, length), F32)
    upto = jnp.zeros((length, length), F32)
    for row in rows:
        less = less + jnp.where(row < own, 1.0, 0.0)
        upto = upto + jnp.where(row <= own, 1.0, 0.0)
    index = (chunk * length + iota((length, 1), 0)).astype(F32)
    offset = index - jnp.sum(less, axis=1, keepdims=True)
    return offset, jnp.sum(upto, axis=1, keepdims=True) - 1.0 - index


def flat_rows(ref, flat):
    rows, cols = ref.shape[-2:]
    if rows % HALO == 0:
        return ref[...].reshape(-1, cols)
    shape = ref.shape[:-2]
    for i, at in enumerate(np.ndindex(*shape)):
        flat[i * rows : (i + 1) * rows, :] = ref[at]
    return flat[...]


def pick_params(place, pack_ref, cx_ref, hp_ref, pick_ref):
    width = cx_ref.shape[1]
    heads = width // HEAD_DIM
    mine = jnp.zeros((8, width), F32)
    for g in range(INNER // width):
        mine = mine + jnp.where(place.chunk == g, pack_ref[:, g * width : (g + 1) * width], 0.0)
    lane, source = iota((LANES, LANES), 1), iota((LANES, LANES), 0)
    pick = ((lane < heads) & (source == lane + place.chunk * heads)).astype(BF16)
    pick_ref[...] = pick
    lines = [pack_ref[6:7, i * LANES : (i + 1) * LANES] for i in range(3)]
    lines = jnp.concatenate(lines + [jnp.zeros((5, LANES), F32)], axis=0)
    lines = mm_ones(lines, pick, 3)
    hp_ref[...] = lines
    cx_ref[...] = mine
    cx_ref[6:7, :] = mm_ones(lines, expander(width), 3)[2:3, :]


def forward_kernel(
    seq, fsdp,
    h_ref, zx_ref, tail_ref, seg_ref, cot_ref, ow_ref,
    pack_ref,
    proj_ref, state_ref, off_ref, rem_ref, offr_ref,
    h_out, w_out, dz_out, dy_out, stat_out, mixed_out, mixed_got, pout_out, pz_out, gain_out_ref, gain_in_ref,
    cx_ref, hp_ref, pick_ref,
    h_v, w_v, w_flat, seg_v, cot_v, ow_v, ow_flat, gated_v, sums_v, sums_got, grad_v, z_v, y_v,
    mix_give, mix_own, pout_v, pz_v, memory, ext_x, ext_t, last_rows, send, recv, near,
):
    seqs, _, length, depth = h_v.shape
    width = cx_ref.shape[1]
    step_at = pl.program_id(0)
    place = Place(seq, fsdp)
    links = Links(send, recv, near)
    peers = peers_of(place)
    near_peers = [(l, c) for t, l, c in peers if t == 0]
    entry = Entry(place, links, h_ref, zx_ref, tail_ref, seg_ref, h_v, w_v, seg_v)
    cot = TokenGather(place, links, cot_ref, cot_v)
    w_rows = RowGather(place, links, ow_ref, ow_v)
    keep = [links.local(lambda: (h_v, h_out)), links.local(lambda: (w_v, w_out))]
    stages = len(place.low_bits)

    def send_sums(i):
        l, c = near_peers[i]
        return links.far(lambda: (sums_v, sums_got.at[i], place.at(low=l, core=c)))

    sums = [send_sums(i) for i in range(len(near_peers))]

    def send_core(q):
        return links.far(lambda: (mix_give.at[q], mixed_got.at[q], place.at(core=1)))

    cores = [send_core(q) for q in range(seqs)]

    @pl.when(step_at == 0)
    def _():
        memory[...] = jnp.zeros_like(memory)
        last_rows[...] = jnp.zeros_like(last_rows)
        pick_params(place, pack_ref, cx_ref, hp_ref, pick_ref)
        meet_pair(place)
        entry.run(cot.cross_over)
        if w_v.shape[-2] % HALO:
            flat_rows(w_v, w_flat)

    @pl.when(step_at == 1)
    def _():
        for copy in keep:
            copy.start()
        cot.begin_home()
        w_rows.begin()

    for i in range(stages):

        @pl.when(step_at == min(3 + 2 * i, seq - 1))
        def _():
            cot.pass_on(i, "home")

    @pl.when(step_at == 2)
    def _():
        cot.arrive()

    for i in range(stages):

        @pl.when(step_at == min(4 + 2 * i, seq - 1))
        def _():
            cot.pass_on(i, "away")

    @pl.when(step_at == seq - 2)
    def _():
        w_rows.forward()

    @pl.when(step_at < seq)
    def _():
        weights = flat_rows(w_v, w_flat) if w_v.shape[-2] % HALO == 0 else w_flat[...]
        proj = jnp.dot(
            h_v[:, step_at].reshape(seqs * length, depth), weights, preferred_element_type=F32
        ).astype(BF16)
        proj_ref[...] = proj.reshape(proj_ref.shape)
        params = (
            cx_ref[:KERNEL, :], cx_ref[KERNEL : KERNEL + 1, :],
            pack_ref[:KERNEL, INNER:], pack_ref[KERNEL : KERNEL + 1, INNER:],
            hp_ref[...], pick_ref[...],
        )
        gain_row, skip_row = cx_ref[KERNEL + 1 : KERNEL + 2, :], cx_ref[KERNEL + 2 : KERNEL + 3, :]
        for q in range(seqs):
            offset, remain = positions(seg_v[q : q + 1, :], step_at, length)
            off_ref[q, 0] = offset
            rem_ref[q, 0] = remain
            offr_ref[q, 0] = jnp.broadcast_to(offset, (length, LANES)).T[0:1, :]
            chunk_rows = proj[q * length : (q + 1) * length]
            zx, tail = chunk_rows[:, : 2 * width], chunk_rows[:, 2 * width :]
            earlier = last_rows[q]
            z_rows = zx[:, :width]
            here = pl.ds(pl.multiple_of((q * seq + step_at) * length, length), length)
            z_v[here, :] = z_rows
            conv_x, conv_t, _, _, _, _, cumul, _, step_x, entry_x, end_x = chunk_common(
                zx[:, width:], earlier[:, width : 2 * width], tail, earlier[:, 2 * width :], offset, params,
                ext_x.at[q], ext_t.at[q], width,
            )
            xs = conv_x * sigmoid(conv_x)
            act_t = conv_t * sigmoid(conv_t)
            bs = act_t[:, :STATE].astype(BF16)
            cs = act_t[:, STATE:].astype(BF16)
            scaled = xs * step_x
            scores = mm_tr(cs, bs)
            gap = iota((length, length), 0) - iota((length, length), 1)
            same = (gap >= 0) & (gap.astype(F32) <= offset)
            cumul_t = cumul.T
            old = memory[q]
            old_low = old.astype(BF16)
            state_ref[q, 0] = old_low
            outside = mm(cs, old_low) * entry_x + skip_row * xs
            squares = jnp.zeros((length, 1), F32)
            for start, size, heads in head_tiles(width):
                mixing = []
                for head in heads:
                    spans = cumul[:, head : head + 1] - cumul_t[head : head + 1, :]
                    decays = jnp.exp(jnp.where(same, spans, -1e30))
                    mixing.append((decays * scores).astype(BF16))
                tile = masked_heads(scaled[:, start : start + size].astype(BF16), heads)
                mix = mixing[0] if len(heads) == 1 else jnp.concatenate(mixing, axis=1)
                inside = jnp.dot(mix, tile, preferred_element_type=F32)
                y_low = (inside + outside[:, start : start + size]).astype(BF16)
                y_v[here, start : start + size] = y_low
                z = zx[:, start : start + size].astype(F32)
                gated = y_low.astype(F32) * (z * sigmoid(z))
                gated_v[here, start : start + size] = (
                    gated * gain_row[:, start : start + size]
                ).astype(BF16)
                squares = squares + jnp.sum(gated * gated, axis=1, keepdims=True)
            sums_v[pl.ds(2 * (q * seq + step_at), 1), :] = jnp.broadcast_to(
                squares, (length, LANES)
            ).T[0:1, :]
            fresh = tr_mm(bs, scaled * end_x)
            memory[q] = old * entry_x[length - 1 : length, :] + fresh
            last_rows[q] = chunk_rows[length - HALO :]

    @pl.when(step_at == seq)
    def _():
        w_rows.finish()
        cot.finish()
        rows_out = flat_rows(ow_v, ow_flat)
        tile = 2 * length
        tiles = seqs * seq // 2

        @pl.loop(0, tiles)
        def _(k):
            at = pl.ds(pl.multiple_of(k * tile, tile), tile)
            cots = cot_v[k // (seq // 2), pl.ds(lax.rem(k, seq // 2) * 2, 2)].reshape(tile, depth)
            grad = mm_tr(cots, rows_out)
            grad_v[at, :] = grad
            part = jnp.sum(grad * gated_v[at, :].astype(F32), axis=1, keepdims=True)
            part = jnp.broadcast_to(part, (tile, LANES))
            for i in (0, 1):
                sums_v[pl.ds(4 * k + 2 * i + 1, 1), :] = (
                    part[i * length : (i + 1) * length].T[0:1, :]
                )

        for copy in sums:
            copy.start()

        def mixed_rows(out, side):
            per_side = seq // 2 // 2
            for q in range(seqs):

                @pl.loop(0, per_side)
                def _(k):
                    at = (q * seq + seq // 2 * side + 2 * k) * length
                    rows = gated_v[pl.ds(pl.multiple_of(at, tile), tile), :]
                    mixed = jnp.dot(rows, rows_out, preferred_element_type=F32)
                    out[q, pl.ds(2 * k, 2)] = mixed.astype(BF16).reshape(2, length, depth)

        mixed_rows(mix_give, 1 - place.core)
        for copy in cores:
            copy.start()
        mixed_rows(mix_own, place.core)
        mixed_store = links.local(lambda: (mix_own, mixed_out))
        mixed_store.start()
        for copy in sums:
            copy.wait_recv()
        total = sums_v[...]
        for i in range(len(near_peers)):
            total = total + sums_got[i]
        is_square = lax.rem(iota(total.shape, 0), 2) == 0
        scale = lax.rsqrt(total / INNER + EPSILON)
        other = pltpu.roll(scale, 1, 0)
        stat_out[...] = jnp.where(is_square, scale, total * (other * other * other / INNER))

        gain_out_ref[...] = jnp.zeros_like(gain_out_ref)
        gain_row = cx_ref[KERNEL + 1 : KERNEL + 2, :]

        @pl.loop(0, tiles)
        def _(k):
            at = pl.ds(pl.multiple_of(k * tile, tile), tile)

            def column(line):
                rows = [
                    jnp.broadcast_to(stat_out[pl.ds(4 * k + 2 * i + line, 1), :], (LANES, length))
                    for i in (0, 1)
                ]
                return jnp.concatenate([row.T[:, 0:1] for row in rows], axis=0)

            scale, slope = column(0), column(1)
            gated_v[at, :] = (gated_v[at, :].astype(F32) * scale).astype(BF16)
            z = z_v[at, :].astype(F32)
            y = y_v[at, :].astype(F32)
            sig = sigmoid(z)
            silu_z = z * sig
            gated = y * silu_z
            scaled = grad_v[at, :] * scale
            gain_out_ref[0:1, :width] += jnp.sum(scaled * gated, axis=0, keepdims=True)
            grad_gated = gain_row * scaled - gated * slope
            y_v[at, :] = (grad_gated * silu_z).astype(BF16)
            z_v[at, :] = (grad_gated * y * (sig + silu_z * (1.0 - sig))).astype(BF16)

        dz_store = links.local(lambda: (z_v, dz_out))
        dy_store = links.local(lambda: (y_v, dy_out))
        dz_store.start()
        dy_store.start()

        rows_in = w_v.shape[3]
        blocks = TILE // rows_in
        high = blocks // fsdp
        h_flat = h_v[...].reshape(-1, depth)
        for t in range(depth // TILE):
            term = tr_mm(h_flat[:, t * TILE : (t + 1) * TILE], z_v[...])
            for i in range(blocks):
                pz_v[t * high + i // fsdp, i % fsdp // 2, i % 2] = term[
                    i * rows_in : (i + 1) * rows_in
                ].astype(BF16)
            if rows_in % HALO:
                some = w_flat[t * TILE : (t + 1) * TILE, :width]
            else:
                some = w_v[t * high : (t + 1) * high, :, :, :, :width].reshape(TILE, width)
            line = jnp.sum(term * some.astype(F32), axis=1, keepdims=True)
            wide = jnp.broadcast_to(line, (TILE, LANES))
            for i in range(TILE // LANES):
                row = t * (TILE // LANES) + i
                gain_in_ref[row : row + 1, :] = wide[i * LANES : (i + 1) * LANES].T[0:1, :]
        pz_store = links.local(lambda: (pz_v, pz_out))
        pz_store.start()
        pout_v[...] = tr_mm(gated_v[...], cot_v[...].reshape(-1, depth)).astype(BF16)
        pout_store = links.local(lambda: (pout_v, pout_out))
        pout_store.start()
        for copy in [dz_store, dy_store, pz_store, mixed_store, pout_store] + keep:
            copy.wait()
        for copy in cores:
            copy.wait()
        for copy in sums:
            copy.wait_send()
        entry.finish()


def backward_kernel(
    seq, fsdp,
    x_ref, xh_ref, tail_ref, tailh_ref, off_ref, offr_ref, rem_ref, dy_ref, dz_ref, state_ref,
    w_ref,    all_stat_ref, mixed_ref, got_ref, pout_ref, pz_ref,
    cx_ref, ct_ref, hp_ref, pick_ref,
    out_ref, gx_ref, gt_ref, gh_ref, mixed_out, rows_out, slots_out, dh_out,
    memory, ext_x, ext_t, next_x, next_t,
    mix_own, mix_first, mix_later, pout_own, pout_first, pz_own, pz_first, pz_top,
    dh_give, dh_own, dh_first, send, recv, near,
):
    seqs, _, length, width = dy_ref.shape
    x_at = x_ref.shape[3] - width
    step_at = pl.program_id(0)

    place = Place(seq, fsdp)
    links = Links(send, recv, near)
    mixed = TokenScatter(
        place, links, (mixed_ref, got_ref), mixed_out, mix_own, mix_first, mix_later, "halves"
    )
    w_rows = RowScatter(place, links, pout_ref, rows_out, pout_own, pout_first)
    z_part = PartScatter(
        place, links, pz_ref, lambda s, c: pz_own.at[s, c], pz_first, pz_top, slots_out, 1
    )
    pz_load = links.local(lambda: (pz_ref.at[:, place.pair], pz_own))
    half = seq // 2

    def give_chunk(low):
        return links.far(
            lambda: (dh_give.at[:, low], dh_first.at[:, low], place.at(core=1))
        )

    dh_chunks = [give_chunk(low) for low in range(half)]

    def add_chunk(low):
        dh_chunks[low].wait_recv()
        for q in range(seqs):
            add_rows(dh_own.at[q, low], dh_own.at[q, low], dh_first.at[q, low])

    dh_store = links.local(lambda: (dh_own, dh_out))
    stages = len(place.low_bits)

    @pl.when(step_at == 0)
    def _():
        mixed.begin()
        pz_load.start()
        meet_pair(place)
        z_part.send_pairs(1, 0)
        mixed.add_cores()
        mixed.send_stage(0)

    @pl.when(step_at == 1)
    def _():
        z_part.send_pairs(0, 0)

    @pl.when(step_at == 2)
    def _():
        pz_load.wait()
        z_part.add_pairs(1, 0)
        z_part.send_cross(0)
        w_rows.begin()

    @pl.when(step_at == 4)
    def _():
        z_part.add_pairs(0, 0)

    @pl.when(step_at == 5)
    def _():
        w_rows.add_pairs()

    @pl.when(step_at == pl.num_programs(0) - 1)
    def _():
        z_part.spread()

    @pl.when(step_at == pl.num_programs(0) - 4)
    def _():
        mixed.add_stage(0)
        if stages > 1:
            mixed.send_stage(1)

    @pl.when(pl.program_id(0) == 0)
    def _():
        memory[...] = jnp.zeros_like(memory)
        gx_ref[...] = jnp.zeros_like(gx_ref)
        gt_ref[...] = jnp.zeros_like(gt_ref)
        gh_ref[...] = jnp.zeros_like(gh_ref)
        next_x[:, length:, :] = jnp.zeros_like(next_x[:, length:, :])
        next_t[:, length:, :] = jnp.zeros_like(next_t[:, length:, :])

    params = (
        cx_ref[:KERNEL, :], cx_ref[KERNEL : KERNEL + 1, :],
        ct_ref[:KERNEL, :], ct_ref[KERNEL : KERNEL + 1, :],
        hp_ref[...], pick_ref[...],
    )
    skip_row = cx_ref[KERNEL + 2 : KERNEL + 3, :]
    for q in range(seqs):
        offset = off_ref[q, 0]
        conv_x, conv_t, raw, step, rate, decay_rate, cumul, spread, step_x, entry_x, end_x = (
            chunk_common(
                x_ref[q, 0, :, x_at:], xh_ref[q, 0, :, x_at:], tail_ref[q, 0], tailh_ref[q, 0], offset,
                params, ext_x.at[q], ext_t.at[q], width,
            )
        )
        dy_low = dy_ref[q, 0]
        dy = dy_low.astype(F32)

        sig_x = sigmoid(conv_x)
        xs = conv_x * sig_x
        slope_x = sig_x + xs * (1.0 - sig_x)
        sig_t = sigmoid(conv_t)
        act_t = conv_t * sig_t
        slope_t = sig_t + act_t * (1.0 - sig_t)
        bs = act_t[:, :STATE].astype(BF16)
        cs = act_t[:, STATE:].astype(BF16)
        scaled = xs * step_x
        scaled_low = scaled.astype(BF16)
        scores = mm_tr(bs, cs)
        rows, cols = iota((length, length), 0), iota((length, length), 1)
        gap = cols - rows
        same = (gap >= 0) & (gap.astype(F32) <= offr_ref[q, 0])
        strict = gap > 0
        upper = (rows >= cols).astype(BF16)
        cumul_t = cumul.T
        old = state_ref[q, 0]
        grad_state = memory[q]
        state_low = grad_state.astype(BF16)
        grad_scores = jnp.zeros((length, length), F32)
        grad_scaled = []
        inside_rows = []
        for start, size, heads in head_tiles(width):
            dy_tile = masked_heads(dy_low[:, start : start + size], heads)
            grad_mix = mm_tr(scaled_low[:, start : start + size], dy_tile)
            mixing = []
            for i, head in enumerate(heads):
                spans = cumul_t[head : head + 1, :] - cumul[:, head : head + 1]
                decays = jnp.exp(jnp.where(same, spans, -1e30))
                weighted = grad_mix[:, i * length : (i + 1) * length] * decays
                grad_scores = grad_scores + weighted
                mixing.append((decays * scores).astype(BF16))
                terms = jnp.where(strict, weighted * scores, 0.0).astype(BF16)
                sums = jnp.dot(terms, upper, preferred_element_type=F32)
                inside_rows.append(
                    jnp.sum(jnp.where(strict, sums, 0.0), axis=0, keepdims=True)
                )
            mix = mixing[0] if len(heads) == 1 else jnp.concatenate(mixing, axis=1)
            grad_scaled.append(jnp.dot(mix, dy_tile, preferred_element_type=F32))
        inside_rows.append(jnp.zeros((LANES - len(inside_rows), length), F32))
        inside = jnp.concatenate(inside_rows, axis=0).T
        from_end = mm(bs, state_low) * end_x
        grad_scaled = jnp.concatenate(grad_scaled, axis=1) + from_end
        entry_dy = dy * entry_x
        entry_dy_low = entry_dy.astype(BF16)
        out_terms = mm(cs, old) * entry_dy
        end_terms = scaled * from_end
        grad_step = mm_ones_tr(xs * grad_scaled, spread, 2)
        out_terms = mm_ones_tr(out_terms, spread, 2)
        end_terms = mm_ones_tr(end_terms, spread, 2)
        keep_row = entry_x[length - 1 : length, :]
        carried = jnp.sum(grad_state * old.astype(F32), axis=0, keepdims=True) * keep_row
        carried = mm_ones_tr(jnp.broadcast_to(carried, (8, width)), spread, 2)[0:1, :]
        triu = (cols >= rows).astype(BF16)
        below = (rows > cols).astype(BF16)
        grad_rate = inside + ones_mm(triu, out_terms, 2) + ones_mm(below, end_terms, 2) + carried
        grad_step = grad_step - decay_rate * grad_rate
        grad_raw = grad_step * sigmoid(raw)
        grad_scores_low = grad_scores.astype(BF16)
        grad_b = mm(grad_scores_low, cs) + mm_tr(scaled * end_x, state_low)
        grad_c = tr_mm(grad_scores_low, bs) + mm_tr(entry_dy_low, old)
        memory[q] = grad_state * keep_row + tr_mm(cs, entry_dy_low)
        conv_grad_x = (skip_row * dy + step_x * grad_scaled) * slope_x
        conv_grad_t = jnp.concatenate([grad_b, grad_c], axis=1) * slope_t

        remain = rem_ref[q, 0]
        results = []
        for grad, ext, nxt, weight, sums in (
            (conv_grad_x, ext_x.at[q], next_x.at[q], params[0], gx_ref),
            (conv_grad_t, ext_t.at[q], next_t.at[q], params[2], gt_ref),
        ):
            columns = grad.shape[1]
            current = ext[pl.ds(HALO, length), :]
            sums[KERNEL : KERNEL + 1, :columns] += jnp.sum(grad, axis=0, keepdims=True)
            sums[KERNEL - 1 : KERNEL, :columns] += jnp.sum(grad * current, axis=0, keepdims=True)
            nxt[0:length, :] = grad
            total = weight[KERNEL - 1 : KERNEL, :] * grad
            for back in range(1, KERNEL):
                tap = KERNEL - 1 - back
                shifted = jnp.where(offset >= back, ext[pl.ds(HALO - back, length), :], 0.0)
                sums[tap : tap + 1, :columns] += jnp.sum(grad * shifted, axis=0, keepdims=True)
                ahead = jnp.where(remain >= back, nxt[pl.ds(back, length), :], 0.0)
                total = total + weight[tap : tap + 1, :] * ahead
            nxt[length:, :] = grad[0:HALO, :]
            results.append(total.astype(BF16))
        results.append(mm_tr(grad_raw, params[5]).astype(BF16))
        gx_ref[KERNEL + 1 : KERNEL + 2, :width] += jnp.sum(dy * xs, axis=0, keepdims=True)
        gh_ref[0:1, :] += jnp.sum(grad_raw, axis=0, keepdims=True)
        gh_ref[1:2, :] += jnp.sum(grad_rate * rate, axis=0, keepdims=True)
        out_ref[q, 0] = jnp.concatenate(results, axis=1)

    depth = w_ref.shape[0]
    grad_h = mm_tr(dz_ref[...].reshape(seqs * length, width), w_ref[:, :width])
    grad_h = grad_h + mm_tr(
        out_ref[...].reshape(seqs * length, out_ref.shape[3]), w_ref[:, width:]
    )
    grad_h = grad_h.astype(BF16).reshape(seqs, length, depth)
    for i in range(seq):
        chunk = seq - 1 - i

        @pl.when((step_at == i) & (place.core == chunk // half))
        def _():
            dh_own[:, chunk % half] = grad_h

        if i + 1 < seq:

            @pl.when((step_at == i + 1) & (place.core == chunk // half))
            def _():
                add_chunk(chunk % half)

        @pl.when((step_at == i) & (place.core != chunk // half))
        def _():
            dh_give[:, chunk % half] = grad_h
            dh_chunks[chunk % half].start()

    @pl.when(step_at == pl.num_programs(0) - 1)
    def _():
        for stage in range(1, stages):
            mixed.add_stage(stage)
            if stage + 1 < stages:
                mixed.send_stage(stage + 1)
        for q in range(seqs):
            row = all_stat_ref[pl.ds(2 * (q * seq + place.chunk), 1), :]
            column = jnp.broadcast_to(row, (LANES, length)).T[:, 0:1]
            done = mix_own.at[q, place.low]
            done[...] = (done[...].astype(F32) * column).astype(BF16)
        mixed.store()
        z_part.finish()

        @pl.when(place.core == 0)
        def _():
            add_chunk(0)

        for copy in dh_chunks:
            copy.wait_send()
        dh_store.start()
        dh_store.wait()
        w_rows.finish()
        mixed.finish()


TAIL = 2 * STATE + LANES
AXES = ("seq", "fsdp")
MESH = pl.DeviceIdType.MESH
ANYWHERE = pl.BlockSpec(memory_space=pl.ANY)
IN_HBM = pl.BlockSpec(memory_space=pltpu.HBM)


def lane_rows(width):
    return -(-width // LANES)


def sum_rows(width):
    shared = D // LANES
    group = shared + (KERNEL + 1) * 2 * STATE // LANES
    return shared, group, -(-(group + (KERNEL + 3) * lane_rows(width) + 2) // 8) * 8


def whole_spec(shape):
    return pl.BlockSpec(shape, lambda i: (0,) * len(shape))


def chunk_specs(seqs, steps, length, reverse):
    def place(i):
        return steps - 1 - i if reverse else i

    def block(cols, column=0, rows=length):
        return pl.BlockSpec((seqs, 1, rows, cols), lambda i: (0, place(i), 0, column))

    def before(cols, column=0):
        return pl.BlockSpec(
            (seqs, 1, HALO, cols),
            lambda i: (0, jnp.maximum(place(i) - 1, 0), length // HALO - 1, column),
        )

    return block, before


def forward_mix(normed, zx, tail, segments, cotangent, out_w, packed, seq, fsdp):
    seqs, length, depth = normed.shape
    rows = tail.shape[0]
    width = INNER // seq
    cols = 2 * width + TAIL
    pairs = fsdp // 2
    count = seqs * seq * length

    def block(columns, height=length):
        return pl.BlockSpec(
            (seqs, 1, height, columns), lambda i: (0, jnp.minimum(i, seq - 1), 0, 0)
        )

    def blocks(columns, kind, height=length):
        return jax.ShapeDtypeStruct((seqs, seq, height, columns), kind)

    w_shape = (seq, pairs, 2, rows, cols)
    out_shape = (pairs, 2) + out_w.shape
    sums = (seqs * seq * 2, length)
    flat = 8 if rows % HALO == 0 else depth
    flat_out = 8 if out_w.shape[0] % HALO == 0 else width
    outs = pl.pallas_call(
        functools.partial(forward_kernel, seq, fsdp),
        grid=(seq + 1,),
        in_specs=[ANYWHERE] * 6 + [whole_spec(packed.shape)],
        out_specs=[
            block(cols), block(width, STATE), block(1), block(1), block(length, 1),
            ANYWHERE, ANYWHERE, ANYWHERE, ANYWHERE, whole_spec(sums), ANYWHERE, ANYWHERE, ANYWHERE, ANYWHERE,
            whole_spec((8, lane_rows(width) * LANES)), whole_spec((depth // LANES, LANES)),
            whole_spec((8, width)), whole_spec((8, LANES)), whole_spec((LANES, LANES)),
        ],
        out_shape=[
            blocks(cols, BF16), blocks(width, BF16, STATE),
            blocks(1, F32), blocks(1, F32), blocks(length, F32, 1),
            blocks(depth, BF16),
            jax.ShapeDtypeStruct(w_shape, BF16),
            jax.ShapeDtypeStruct((count, width), BF16),
            jax.ShapeDtypeStruct((count, width), BF16),
            jax.ShapeDtypeStruct(sums, F32),
            jax.ShapeDtypeStruct((seqs, seq // 2, length, depth), BF16),
            jax.ShapeDtypeStruct((seqs, seq // 2, length, depth), BF16),
            jax.ShapeDtypeStruct((width, depth), BF16),
            jax.ShapeDtypeStruct(w_shape[:4] + (width,), BF16),
            jax.ShapeDtypeStruct((8, lane_rows(width) * LANES), F32),
            jax.ShapeDtypeStruct((depth // LANES, LANES), F32),
            jax.ShapeDtypeStruct((8, width), F32),
            jax.ShapeDtypeStruct((8, LANES), F32),
            jax.ShapeDtypeStruct((LANES, LANES), BF16),
        ],
        scratch_shapes=[
            pltpu.VMEM((seqs, seq, length, depth), BF16),
            pltpu.VMEM(w_shape, BF16),
            pltpu.VMEM((flat, cols), BF16),
            pltpu.VMEM(segments.shape, segments.dtype),
            pltpu.VMEM((seqs, seq, length, depth), BF16),
            pltpu.VMEM(out_shape, BF16),
            pltpu.VMEM((flat_out, depth), BF16),
            pltpu.VMEM((count, width), BF16),
            pltpu.VMEM(sums, F32),
            pltpu.VMEM((seq - 1,) + sums, F32),
            pltpu.VMEM((count, width), F32),
            pltpu.VMEM((count, width), BF16),
            pltpu.VMEM((count, width), BF16),
            pltpu.VMEM((seqs, seq // 2, length, depth), BF16),
            pltpu.VMEM((seqs, seq // 2, length, depth), BF16),
            pltpu.VMEM((width, depth), BF16),
            pltpu.VMEM(w_shape[:4] + (width,), BF16),
            pltpu.VMEM((seqs, STATE, width), F32),
            pltpu.VMEM((seqs, HALO + length, width), F32),
            pltpu.VMEM((seqs, HALO + length, 2 * STATE), F32),
            pltpu.VMEM((seqs, HALO, cols), BF16),
            pltpu.SemaphoreType.DMA((320,)),
            pltpu.SemaphoreType.DMA((320,)),
            pltpu.SemaphoreType.DMA((24,)),
        ],
        compiler_params=pltpu.CompilerParams(
            dimension_semantics=("arbitrary",), vmem_limit_bytes=63 << 20, collective_id=0,
            has_side_effects=True,
        ),
        cost_estimate=pl.CostEstimate(
            flops=30_000_000_000, transcendentals=0, bytes_accessed=60_000_000
        ),
        name="mix_forward",
    )(normed, zx, tail, segments, cotangent, out_w, packed)
    (
        proj, states, off_col, rem_col, off_row, h_all, w_mine, dz, dy, stats, mixed, got, part,
        part_z, gain_out, gain_in,
    ) = outs[:16]
    return (
        proj, states, off_col, rem_col, off_row, h_all, w_mine.reshape(depth, cols), dz,
        dy.reshape(seqs, seq, length, width), stats, (mixed, got), part.reshape(out_shape),
        part_z, (gain_in, gain_out), outs[16:],
    )


def backward_mix(
    proj, off_col, off_row, rem_col, dy, dz, w_mine, stats, states, mixed, part_out, part_z, packed, consts, seq, fsdp
):
    seqs, steps, length, cols = proj.shape
    depth = mixed[0].shape[3]
    width = (cols - TAIL) // 2
    block, before = chunk_specs(seqs, steps, length, True)
    tail_at = 2 * width // TAIL
    x_cols, x_at = (width, 1) if width % LANES == 0 else (2 * width, 0)
    rows_in = part_z.shape[3]
    half, pairs = seq // 2, fsdp // 2
    rows_out = part_out.shape[2]
    sums = [(8, lane_rows(width) * LANES), (8, 2 * STATE), (8, LANES)]
    token_own = pltpu.VMEM((seqs, half, length, depth), BF16)
    return pl.pallas_call(
        functools.partial(backward_kernel, seq, fsdp),
        grid=(steps,),
        in_specs=[
            block(x_cols, x_at), before(x_cols, x_at),
            block(TAIL, tail_at), before(TAIL, tail_at),
            block(1), block(length, 0, 1), block(1), block(width), block(width),
            block(width, 0, STATE),
            pl.BlockSpec(w_mine.shape, lambda i: (0, 0), pipeline_mode=pl.Buffered(1)),
            whole_spec(stats.shape), ANYWHERE, ANYWHERE,
            ANYWHERE, ANYWHERE, whole_spec(consts[0].shape),
            pl.BlockSpec((8, 2 * STATE), lambda i: (0, INNER // (2 * STATE))),
            whole_spec(consts[1].shape), whole_spec(consts[2].shape),
        ],
        out_specs=[block(width + TAIL)] + [whole_spec(v) for v in sums] + [ANYWHERE] * 4,
        scratch_shapes=[
            pltpu.VMEM((seqs, STATE, width), F32),
            pltpu.VMEM((seqs, HALO + length, width), F32),
            pltpu.VMEM((seqs, HALO + length, 2 * STATE), F32),
            pltpu.VMEM((seqs, length + HALO, width), F32),
            pltpu.VMEM((seqs, length + HALO, 2 * STATE), F32),
            token_own, token_own, pltpu.VMEM((seqs, max(half - 1, 1), length, depth), BF16),
            pltpu.VMEM((2, rows_out, depth), BF16),
            pltpu.VMEM((max(pairs - 1, 1), 2, rows_out, depth), BF16),
            pltpu.VMEM((seq, 2, rows_in, width), BF16),
            pltpu.VMEM((max(pairs - 1, 1), seq, 2, rows_in, width), BF16),
            pltpu.VMEM((half, 2, rows_in, width), BF16),
            token_own, token_own, token_own,
            pltpu.SemaphoreType.DMA((128,)),
            pltpu.SemaphoreType.DMA((128,)),
            pltpu.SemaphoreType.DMA((16,)),
        ],
        out_shape=[jax.ShapeDtypeStruct(proj.shape[:3] + (width + TAIL,), BF16)]
        + [jax.ShapeDtypeStruct(v, F32) for v in sums]
        + [
            jax.ShapeDtypeStruct((seqs, length, depth), BF16),
            jax.ShapeDtypeStruct((2, rows_out, depth), BF16),
            jax.ShapeDtypeStruct((2, half, rows_in, width), BF16),
            jax.ShapeDtypeStruct((seqs, half, length, depth), BF16),
        ],
        compiler_params=pltpu.CompilerParams(
            dimension_semantics=("arbitrary",), vmem_limit_bytes=56 << 20, collective_id=3,
            has_side_effects=True,
        ),
        cost_estimate=pl.CostEstimate(
            flops=steps * seqs * 2_000_000_000, transcendentals=0, bytes_accessed=16_000_000
        ),
        name="mix_backward",
    )(
        proj, proj, proj, proj, off_col, off_row, rem_col, dy, dz.reshape(dy.shape), states,
        w_mine, stats, *mixed, part_out,
        part_z, consts[0], packed, consts[1], consts[2],
    )


class Place:
    def __init__(self, seq, fsdp):
        self.seq, self.fsdp = seq, fsdp
        self.half, self.pairs = seq // 2, fsdp // 2
        s, f = lax.axis_index("seq"), lax.axis_index("fsdp")
        self.s, self.f = s, f
        self.top, self.low = s // self.half, lax.rem(s, self.half)
        self.core, self.pair = lax.rem(f, 2), f // 2
        self.home = self.core == self.top
        self.away = self.core != self.top
        self.chunk = self.low + self.half * self.core
        self.low_bits = [1 << i for i in range(self.half.bit_length() - 1)]

    def at(self, top=0, low=0, pair=0, core=0):
        return (
            flip(self.top, top) * self.half + flip(self.low, low),
            flip(self.pair, pair) * 2 + flip(self.core, core),
        )

    def bits_for(self, q):
        return self.low_bits if q % 2 == 0 else self.low_bits[::-1]


def flip(index, bits):
    for i in range(bits.bit_length()):
        if bits >> i & 1:
            bit = lax.rem(index // (1 << i), 2)
            index = index + (1 << i) * (1 - 2 * bit)
    return index


class Copy:
    def __init__(self, make):
        self.make = make

    def start(self):
        self.make().start()
        return self

    def wait(self):
        self.make().wait()

    def wait_send(self):
        self.make().wait_send()

    def wait_recv(self):
        self.make().wait_recv()


class Copies:
    def __init__(self, copies):
        self.copies = copies

    def start(self):
        for copy in self.copies:
            copy.start()

    def wait_recv(self):
        for copy in self.copies:
            copy.wait_recv()

    def wait_send(self):
        for copy in self.copies:
            copy.wait_send()


class Links:
    def __init__(self, send, recv, near):
        self.send, self.recv, self.near = send, recv, near
        self.far_count = self.near_count = 0

    def far(self, make):
        i = self.far_count
        self.far_count += 1

        def build():
            src, dst, device = make()
            return pltpu.make_async_remote_copy(
                src_ref=src, dst_ref=dst, send_sem=self.send.at[i], recv_sem=self.recv.at[i],
                device_id=device, device_id_type=MESH,
            )

        return Copy(build)

    def local(self, make):
        i = self.near_count
        self.near_count += 1
        return Copy(lambda: pltpu.make_async_copy(*make(), self.near.at[i]))


def meet(devices):
    barrier = pltpu.get_barrier_semaphore()
    for device in devices:
        pl.semaphore_signal(barrier, inc=1, device_id=device, device_id_type=MESH)
    pl.semaphore_wait(barrier, len(devices))


def meet_pair(place):
    meet(
        [place.at(top=t, low=l, core=c) for t, l, c in peers_of(place)]
        + [place.at(pair=p) for p in range(1, place.pairs)]
    )


def peers_of(place):
    out = []
    for top in (0, 1):
        for low in range(place.half):
            for core in (0, 1):
                if (top, low, core) != (0, 0, 0):
                    out.append((top, low, core))
    return out


class TokenGather:
    def __init__(self, place, links, src, dst):
        self.place, self.src, self.dst = place, src, dst
        seqs = src.shape[0]

        def over(q):
            return links.far(
                lambda: (src.at[q], dst.at[q, place.s], place.at(top=1, core=1))
            )

        self.cross = [over(q) for q in range(seqs)]
        self.stay = links.local(lambda: (src, dst.at[:, place.s]))
        self.share = [[] for _ in range(seqs)]
        self.stages = []
        held = [[0] for _ in range(seqs)]
        for q in range(seqs):
            self.share[q].append([self.copy(links, q, low, core=1) for low in held[q]])
        for i in range(len(place.low_bits)):
            stage = []
            for q in range(seqs):
                bit = place.bits_for(q)[i]
                stage.append([self.copy(links, q, low, low_bit=bit) for low in held[q]])
                fresh = [low ^ bit for low in held[q]]
                held[q] = held[q] + fresh
                self.share[q].append([self.copy(links, q, low, core=1) for low in fresh])
            self.stages.append(stage)

    def copy(self, links, q, low, low_bit=0, core=0):
        def make():
            place = self.place
            ref = self.dst.at[q, flip(place.low, low) + place.half * place.core]
            return ref, ref, place.at(low=low_bit, core=core)

        return links.far(make)

    def begin(self):
        self.cross_over()
        self.begin_home()

    def cross_over(self):
        @pl.when(self.place.away)
        def _():
            for copy in self.cross:
                copy.start()

    def begin_home(self):
        @pl.when(self.place.home)
        def _():
            self.stay.start()
            self.stay.wait()
            self.send_stage(0)

    def arrive(self):
        @pl.when(self.place.away)
        def _():
            for copy in self.cross:
                copy.wait_recv()
            self.send_stage(0)

    def send_stage(self, i):
        for q in range(len(self.share)):
            for copy in self.stages[i][q] + self.share[q][i]:
                copy.start()

    def pass_on(self, i, role):
        @pl.when(self.place.home if role == "home" else self.place.away)
        def _():
            for q in range(len(self.share)):
                for copy in self.stages[i][q]:
                    copy.wait_recv()
                for copy in (self.stages[i + 1][q] if i + 1 < len(self.stages) else []):
                    copy.start()
                for copy in self.share[q][i + 1]:
                    copy.start()

    def finish(self):
        for share in self.share:
            for copies in share:
                for copy in copies:
                    copy.wait()
        for stage in self.stages:
            for copies in stage:
                for copy in copies:
                    copy.wait_send()

        @pl.when(self.place.away)
        def _():
            for copy in self.cross:
                copy.wait_send()


class RowGather:
    def __init__(self, place, links, src, dst):
        self.place = place
        pairs = range(1, place.pairs)

        def slot():
            return dst.at[place.pair, place.core]

        self.stay = links.local(lambda: (src, slot()))
        self.to_home = links.far(lambda: (src, slot(), place.at(core=1)))
        self.to_near = links.far(lambda: (src, slot(), place.at(top=1)))
        self.to_far = links.far(lambda: (src, slot(), place.at(top=1, core=1)))

        def forward(c, p):
            return links.far(
                lambda: (dst.at[place.pair, c], dst.at[place.pair, c], place.at(pair=p))
            )

        self.forwards = [forward(c, p) for c in (0, 1) for p in pairs]

    def begin(self):
        @pl.when(self.place.home)
        def _():
            self.stay.start()
            self.to_near.start()

        @pl.when(self.place.away)
        def _():
            self.to_home.start()
            self.to_far.start()

    def forward(self):
        @pl.when(self.place.home)
        def _():
            self.stay.wait()
            self.to_home.wait_recv()

        @pl.when(self.place.away)
        def _():
            self.to_near.wait_recv()
            self.to_far.wait_recv()

        for copy in self.forwards:
            copy.start()

    def finish(self):
        for copy in self.forwards:
            copy.wait()

        @pl.when(self.place.home)
        def _():
            self.to_near.wait_send()

        @pl.when(self.place.away)
        def _():
            self.to_home.wait_send()
            self.to_far.wait_send()


class Entry:
    def __init__(self, place, links, h_ref, zx_ref, tail_ref, seg_ref, h_v, w_v, seg_v):
        self.place = place
        cols = zx_ref.shape[-1]
        self.peers = peers = peers_of(place)
        others = range(1, place.pairs)
        self.tokens = TokenGather(place, links, h_ref, h_v)

        def block(t=0, l=0, c=0):
            s, f = place.at(top=t, low=l, core=c)
            return w_v.at[s, place.pair, lax.rem(f, 2)]

        direct = len(zx_ref.shape) == 2
        if direct:
            cols = w_v.shape[4] - TAIL
        width = cols // 2

        def source(group, part):
            if direct:
                return zx_ref.at[:, pl.ds(pl.multiple_of(part * INNER + group * width, LANES), width)]
            return zx_ref.at[group]

        def columns(ref, part):
            if direct:
                return ref.at[:, pl.ds(part * width, width)]
            return ref.at[:, pl.ds(0, cols)]

        def tail_of(ref):
            return ref.at[:, pl.ds(cols, TAIL)]

        def send_zx(part, t, l, c):
            group = flip(place.core, c) * place.half + flip(place.low, l)
            return source(group, part), columns(block(), part), place.at(top=t, low=l, core=c)

        def keep_zx(part):
            return links.local(lambda: (source(place.chunk, part), columns(block(), part)))

        parts = (0, 1) if direct else (0,)
        self.zx = {
            p: Copies([links.far(functools.partial(send_zx, part, *p)) for part in parts])
            for p in peers
        }
        self.own = [keep_zx(part) for part in parts] + [
            links.local(lambda: (tail_ref, tail_of(block())))
        ]
        self.tail_cross = links.far(lambda: (tail_ref, tail_of(block()), place.at(top=1)))
        self.near_peers = [(l, c) for t, l, c in peers if t == 0]

        def send_tail(l, c):
            return tail_ref, tail_of(block()), place.at(low=l, core=c)

        def send_other(l, c):
            return tail_of(block(1)), tail_of(block(1)), place.at(low=l, core=c)

        self.tails = {p: links.far(functools.partial(send_tail, *p)) for p in self.near_peers}
        self.tails_more = {
            p: links.far(functools.partial(send_other, *p)) for p in self.near_peers
        }
        self.seg_send = links.far(lambda: (seg_ref, seg_v, place.at(core=1)))
        self.seg_keep = links.local(lambda: (seg_ref, seg_v))

        def send_on(t, l, c, p):
            return block(t, l, c), block(t, l, c), place.at(pair=p)

        self.forwards = {
            p: [links.far(functools.partial(send_on, *p, other)) for other in others]
            for p in [(0, 0, 0)] + peers
        }

    def run(self, then):
        tokens, zx, forwards = self.tokens, self.zx, self.forwards
        stages = len(self.place.low_bits)
        far_peers = [p for p in self.peers if p[0] == 1]
        tokens.begin()
        self.tail_cross.start()
        for copy in self.own:
            copy.start()
        for p in self.near_peers:
            zx[0, *p].start()
            self.tails[p].start()

        @pl.when(self.place.home)
        def _():
            self.seg_send.start()
            self.seg_keep.start()

        for copy in self.own:
            copy.wait()
        for copy in forwards[0, 0, 0]:
            copy.start()
        self.tail_cross.wait_recv()
        for p in self.near_peers:
            self.tails_more[p].start()
        tokens.pass_on(0, "home")
        for p in self.near_peers:
            zx[0, *p].wait_recv()
            self.tails[p].wait_recv()
            for copy in forwards[0, *p]:
                copy.start()
        for p in far_peers:
            zx[p].start()
        for i in range(1, stages):
            tokens.pass_on(i, "home")
        tokens.arrive()
        for p in self.near_peers:
            self.tails_more[p].wait_recv()
        for i in range(stages):
            tokens.pass_on(i, "away")
            at, to = (len(far_peers) * k // stages for k in (i, i + 1))
            for p in far_peers[at:to]:
                zx[p].wait_recv()
                for copy in forwards[p]:
                    copy.start()
        then()

        @pl.when(self.place.home)
        def _():
            self.seg_keep.wait()
            self.seg_send.wait_send()

        @pl.when(self.place.away)
        def _():
            self.seg_send.wait_recv()

        tokens.finish()
        for p in forwards:
            for copy in forwards[p]:
                copy.wait()

    def finish(self):
        self.tail_cross.wait_send()
        for group in (self.zx, self.tails, self.tails_more):
            for copy in group.values():
                copy.wait_send()


def add_rows(out, left, right, rows=32):
    total = left.shape[0]
    step = next((size for size in (rows, 16) if total % size == 0), total)

    if step == total:
        out[...] = left[...] + right[...]
        return

    @pl.loop(0, total // step)
    def _(i):
        at = pl.ds(pl.multiple_of(i * step, step), step)
        out[at] = left[at] + right[at]


class TokenScatter:
    def __init__(self, place, links, src, out, own, first, later, held):
        self.place = place
        self.out, self.own, self.first, self.later = out, own, first, later
        self.seqs = own.shape[0]
        half = place.half
        self.loads = []
        if held == "sums":
            self.loads = [links.local(lambda: (src, own))]
        if held == "halves":
            self.loads = [
                links.local(lambda: (src[0], own)), links.local(lambda: (src[1], first)),
            ]
        self.stages = [[] for _ in place.low_bits]
        for q in range(self.seqs):
            live, slot = list(range(half)), 0
            for i, bit in enumerate(place.bits_for(q)[::-1]):
                for low in [low for low in live if low & bit]:
                    self.stages[i].append((self.copy(links, q, low, slot, bit), q, low ^ bit, slot))
                    slot += 1
                live = [low for low in live if not low & bit]
        self.stay = links.local(lambda: (own.at[:, place.low], out))

    def copy(self, links, q, low, slot, bit):
        return links.far(
            lambda: (
                self.own.at[q, flip(self.place.low, low)], self.later.at[q, slot],
                self.place.at(low=bit),
            )
        )

    def begin(self):
        for copy in self.loads:
            copy.start()

    def add_cores(self):
        for copy in self.loads:
            copy.wait()
        for q in range(self.seqs if self.first is not None else 0):
            for low in range(self.place.half):
                add_rows(self.own.at[q, low], self.own.at[q, low], self.first.at[q, low])

    def send_stage(self, i):
        for copy, _, _, _ in self.stages[i]:
            copy.start()

    def add_stage(self, i):
        for copy, q, low, slot in self.stages[i]:
            copy.wait_recv()
            ref = self.own.at[q, flip(self.place.low, low)]
            add_rows(ref, ref, self.later.at[q, slot])

    def store(self):
        self.stay.start()
        self.stay.wait()

    def finish(self):
        for stage in self.stages:
            for copy, _, _, _ in stage:
                copy.wait_send()


class RowScatter:
    def __init__(self, place, links, src, out, own, first):
        self.place, self.own, self.first = place, own, first

        def over(p):
            return links.far(
                lambda: (src.at[flip(place.pair, p)], first.at[p - 1], place.at(pair=p))
            )

        def far(c):
            return links.far(
                lambda: (own.at[flip(place.core, c)], out.at[1], place.at(top=1, core=c))
            )

        self.over = [over(p) for p in range(1, place.pairs)]
        self.load = links.local(lambda: (src.at[place.pair], own))
        self.far = [far(0), far(1)]
        self.near = links.far(lambda: (own.at[1 - place.core], out.at[0], place.at(core=1)))
        self.stay = links.local(lambda: (own.at[place.core], out.at[0]))

    def begin(self):
        self.load.start()
        for copy in self.over:
            copy.start()

    def add_pairs(self):
        self.load.wait()
        for i, copy in enumerate(self.over):
            copy.wait_recv()
            for c in (0, 1):
                add_rows(self.own.at[c], self.own.at[c], self.first.at[i, c])

        @pl.when(self.place.away)
        def _():
            for copy in self.far:
                copy.start()

        @pl.when(self.place.home)
        def _():
            self.near.start()
            self.stay.start()

    def finish(self):
        for copy in self.over:
            copy.wait_send()

        @pl.when(self.place.home)
        def _():
            self.stay.wait()
            self.near.wait_send()
            self.far[0].wait_recv()

        @pl.when(self.place.away)
        def _():
            self.near.wait_recv()
            self.far[1].wait_recv()
            for copy in self.far:
                copy.wait_send()


class PartScatter:
    def __init__(self, place, links, src, own, first, other, slots, tiles):
        self.place, self.own, self.first, self.other = place, own, first, other
        self.high = high = place.half // tiles
        pairs = range(1, place.pairs)

        def rows(top, k):
            return pl.ds(place.half * flip(place.top, top) + k * high, high)

        def over(top, k, p):
            return links.far(
                lambda: (
                    src.at[rows(top, k), flip(place.pair, p)], first.at[p - 1, rows(top, k)],
                    place.at(pair=p),
                )
            )

        def cross(i, c):
            def make():
                at = place.half * flip(place.top, 1) + i
                return own(at, c), other.at[i, c], place.at(top=1)

            return links.far(make)

        def spread(l, c):
            return links.far(
                lambda: (
                    self.block(l, c), slots.at[place.core, place.low], place.at(low=l, core=c)
                )
            )

        self.over = [[[over(top, k, p) for p in pairs] for k in range(tiles)] for top in (0, 1)]
        self.cross = [
            [cross(k * high + i, c) for i in range(high) for c in (0, 1)] for k in range(tiles)
        ]
        self.near = [(l, c) for t, l, c in peers_of(place) if t == 0]
        self.slots = {p: spread(*p) for p in self.near}
        self.slots[0, 0] = links.local(
            lambda: (self.block(0, 0), slots.at[place.core, place.low])
        )

    def block(self, l, c):
        place = self.place
        return self.own(place.half * place.top + flip(place.low, l), flip(place.core, c))

    def send_pairs(self, top, k):
        for copy in self.over[top][k]:
            copy.start()

    def add_pairs(self, top, k):
        for i, copy in enumerate(self.over[top][k]):
            copy.wait_recv()
            for low in range(self.high):
                for c in (0, 1):
                    at = self.place.half * flip(self.place.top, top) + k * self.high + low
                    ref = self.own(at, c)
                    add_rows(ref, ref, self.first.at[i, at, c], 16)

    def send_cross(self, k):
        for copy in self.cross[k]:
            copy.start()

    def wait_cross(self, k):
        for copy in self.cross[k]:
            copy.wait_recv()

    def spread(self, waits=True):
        if waits:
            for k in range(len(self.cross)):
                self.wait_cross(k)
        place = self.place
        for l, c in self.near + [(0, 0)]:
            ref = self.block(l, c)
            add_rows(ref, ref, self.other.at[flip(place.low, l), flip(place.core, c)], 16)
            self.slots[l, c].start()

    def finish(self):
        for copy in self.slots.values():
            copy.wait()
        for copies in self.cross + [c for top in self.over for c in top]:
            for copy in copies:
                copy.wait_send()


class Deliver:
    def __init__(self, place, links, src, out):
        self.place = place
        self.cross = links.far(lambda: (src(), out, place.at(top=1, core=1)))
        self.stay = links.local(lambda: (src(), out))

    def begin(self):
        @pl.when(self.place.away)
        def _():
            self.cross.start()

        @pl.when(self.place.home)
        def _():
            self.stay.start()

    def finish(self):
        @pl.when(self.place.away)
        def _():
            self.cross.wait()

        @pl.when(self.place.home)
        def _():
            self.stay.wait()


def exit_kernel(
    seq, fsdp,
    h_ref, dh_ref, grad_ref, w_ref, mixed_ref, gain_in_ref, gain_out_ref, gx_ref, gt_ref, gh_ref,
    dh_out, mixed_out, slots_out, vec_out,
    h_all, grads, weights, part, dh_own, dh_later, part_first, part_top, vec_val, vec_got,
    send, recv, near,
):
    place = Place(seq, fsdp)
    links = Links(send, recv, near)
    half = place.half
    others = list(range(1, place.pairs))
    seqs, _, length, depth = dh_own.shape
    rows = part.shape[3]
    width = weights.shape[1] - grads.shape[1]
    dh = TokenScatter(
        place, links, dh_ref, dh_out, dh_own, None, dh_later, "sums"
    )
    dh_last = Deliver(place, links, lambda: dh_own.at[:, place.low], dh_out)
    mixed = Deliver(place, links, lambda: mixed_ref, mixed_out)
    loads = [
        links.local(lambda: (h_ref, h_all)),
        links.local(lambda: (grad_ref, grads)),
        links.local(lambda: (w_ref, weights)),
    ]

    tiles = depth // 2 // TILE
    rest = PartScatter(
        place, links, part, lambda s, c: part.at[s, place.pair, c], part_first, part_top, slots_out,
        tiles,
    )

    hops = [dict(pair=1 << i) for i in range(place.pairs.bit_length() - 1)] + [dict(top=1)]

    def hop(i):
        return links.far(lambda: (vec_val.at[i], vec_got.at[i], place.at(**hops[i])))

    def share(l, c):
        return links.far(
            lambda: (
                vec_val.at[len(hops)], vec_out.at[place.core, place.low],
                place.at(low=l, core=c),
            )
        )

    vec = [hop(i) for i in range(len(hops))]
    vec_shares = [share(l, c) for t, l, c in peers_of(place) if t == 0]
    vec_shares.append(
        links.local(lambda: (vec_val.at[len(hops)], vec_out.at[place.core, place.low]))
    )

    def vec_next(i):
        vec[i].wait_recv()
        vec_val[i + 1] = vec_val[i] + vec_got[i]
        for copy in vec[i + 1 : i + 2] if i + 1 < len(hops) else vec_shares:
            copy.start()

    blocks = TILE // rows

    def weight_rows(top, k):
        t = tiles * flip(place.top, top) + k
        lanes = pl.ds(pl.multiple_of(t * TILE, LANES), TILE)
        term = tr_mm(h_all[:, lanes], grads[...])
        for b in range(blocks):
            at = t * (blocks // fsdp) + b // fsdp
            part[at, b % fsdp // 2, b % 2] = term[b * rows : (b + 1) * rows].astype(BF16)
        sums = jnp.sum(term * weights[lanes, width:].astype(F32), axis=1, keepdims=True)
        wide = jnp.broadcast_to(sums, (TILE, LANES))
        for i in range(TILE // LANES):
            row = pl.ds(t * (TILE // LANES) + i, 1)
            vec_val[0, row, :] = gain_in_ref[row, :] + wide[i * LANES : (i + 1) * LANES].T[0:1, :]
        rest.send_pairs(top, k)

    def place_sums():
        at, group, _ = sum_rows(width)
        vec_val[0] = jnp.zeros_like(vec_val[0])
        for tap in range(KERNEL + 1):
            for j in range(2 * STATE // LANES):
                vec_val[0, at : at + 1, :] = gt_ref[
                    tap : tap + 1, j * LANES : (j + 1) * LANES
                ]
                at += 1
        pieces_of = [
            ref[line : line + 1, j * LANES : (j + 1) * LANES]
            for ref, line in [(gx_ref, i) for i in range(KERNEL + 2)] + [(gain_out_ref, 0)]
            for j in range(lane_rows(width))
        ] + [gh_ref[0:1, :], gh_ref[1:2, :]]
        for i, piece in enumerate(pieces_of):
            vec_val[0, group + i : group + i + 1, :] = piece

    dh.begin()
    for copy in loads:
        copy.start()
    meet_pair(place)
    dh.add_cores()
    dh.send_stage(0)
    mixed.begin()
    place_sums()
    for copy in loads:
        copy.wait()
    for k in range(tiles):
        weight_rows(1, k)
    for k in range(tiles):
        weight_rows(0, k)
    vec[0].start()
    for k in range(tiles):
        rest.add_pairs(1, k)
        rest.send_cross(k)
    stages = len(place.low_bits)
    for i in range(stages):
        dh.add_stage(i)
        if i + 1 < stages:
            dh.send_stage(i + 1)
        else:
            dh_last.begin()
        if i < len(hops):
            vec_next(i)
    for i in range(stages, len(hops)):
        vec_next(i)
    for k in range(tiles):
        rest.add_pairs(0, k)
    rest.spread()
    for copy in vec_shares:
        copy.wait()
    rest.finish()
    mixed.finish()
    dh_last.finish()
    dh.finish()
    for copy in vec:
        copy.wait_send()


def exit_scatter(seq, fsdp, h_all, grad_h, grad_proj, w_mine, mixed, sums):
    seqs, _, length, depth = h_all.shape
    half, pairs = seq // 2, fsdp // 2
    cols = w_mine.shape[1]
    rest = grad_proj.shape[3]
    width = cols - rest
    rows = depth // (seq * fsdp)
    count = seqs * seq * length
    vector = (sum_rows(width)[2], LANES)
    hops = pairs.bit_length()
    token_own = pltpu.VMEM((seqs, half, length, depth), BF16)
    tokens = jax.ShapeDtypeStruct((seqs, length, depth), BF16)
    return pl.pallas_call(
        functools.partial(exit_kernel, seq, fsdp),
        in_specs=[ANYWHERE] * 5 + [pl.BlockSpec(memory_space=pltpu.VMEM)] * 5,
        out_specs=[ANYWHERE] * 4,
        out_shape=[
            tokens,
            tokens,
            jax.ShapeDtypeStruct((2, half, rows, rest), BF16),
            jax.ShapeDtypeStruct((2, half) + vector, F32),
        ],
        scratch_shapes=[
            pltpu.VMEM((count, depth), BF16),
            pltpu.VMEM((count, rest), BF16),
            pltpu.VMEM((depth, cols), BF16),
            pltpu.VMEM((seq, pairs, 2, rows, rest), BF16),
            token_own,
            pltpu.VMEM((seqs, max(half - 1, 1), length, depth), BF16),
            pltpu.VMEM((max(pairs - 1, 1), seq, 2, rows, rest), BF16),
            pltpu.VMEM((half, 2, rows, rest), BF16),
            pltpu.VMEM((hops + 1,) + vector, F32),
            pltpu.VMEM((hops,) + vector, F32),
            pltpu.SemaphoreType.DMA((96,)),
            pltpu.SemaphoreType.DMA((96,)),
            pltpu.SemaphoreType.DMA((16,)),
        ],
        compiler_params=pltpu.CompilerParams(
            collective_id=1, has_side_effects=True, vmem_limit_bytes=60 << 20
        ),
        cost_estimate=pl.CostEstimate(
            flops=0, transcendentals=0, bytes_accessed=200_000_000
        ),
        name="exit_scatter",
    )(
        h_all.reshape(count, depth), grad_h, grad_proj.reshape(count, rest), w_mine, mixed, *sums
    )


def finish_kernel(
    seq,
    tok_in, cot_in, gain_ref, dh_in, mixed_in, slots_z_in, slots_in, rows_in, vec_in,
    mixed_out, tokens_out, gain_in_out, w_in_out, conv_w_out, conv_b_out, heads_out, gain_out_out,
    w_out_out,
    tok_ref, cot_ref, dh_ref, mixed_ref, slots_z_ref, slots_ref, rows_ref, vec_ref, near,
):
    pairs = [
        (slots_z_in, slots_z_ref), (slots_in, slots_ref), (rows_in, rows_ref), (vec_in, vec_ref),
        (tok_in, tok_ref), (dh_in, dh_ref), (mixed_in, mixed_ref), (cot_in, cot_ref),
    ]
    loads = [pltpu.make_async_copy(*pair, near.at[i]) for i, pair in enumerate(pairs)]
    for copy in loads:
        copy.start()
    gain = gain_ref[...]
    for copy in loads[:4]:
        copy.wait()
    groups, _, cols = slots_ref.shape
    width = cols - TAIL
    tail = jnp.zeros((slots_ref.shape[1], TAIL), F32)
    for g in range(groups):
        w_in_out[:, g * width : (g + 1) * width] = slots_z_ref[g].astype(F32)
        w_in_out[:, INNER + g * width : INNER + (g + 1) * width] = (
            slots_ref[g, :, :width].astype(F32)
        )
        tail = tail + slots_ref[g, :, width:].astype(F32)
    w_in_out[:, 2 * INNER :] = tail[:, : 2 * STATE + HEADS]
    w_out_out[...] = rows_ref[0].astype(F32) + rows_ref[1].astype(F32)

    row, group, _ = sum_rows(width)
    heads = HEADS // seq
    common = vec_ref[0, :group]
    for g in range(1, groups):
        common = common + vec_ref[g, :group]
    for j in range(D // LANES):
        at = slice(j * LANES, (j + 1) * LANES)
        gain_in_out[:, at] = common[j : j + 1] / gain_ref[:, at]
    targets = [conv_w_out.at[k : k + 1] for k in range(KERNEL)] + [conv_b_out]
    for out in targets:
        for j in range(2 * STATE // LANES):
            out[:, INNER + j * LANES : INNER + (j + 1) * LANES] = common[row : row + 1]
            row += 1
    across = lane_rows(width)
    lane = iota((8, LANES), 1)
    per_head = jnp.zeros((8, LANES), F32)
    fold = expander(across * LANES)
    for g in range(groups):
        def lanes_of(line):
            first = group + line * across
            return jnp.concatenate(
                [vec_ref[g, first + j : first + j + 1, :] for j in range(across)], axis=1
            )

        at = slice(g * width, (g + 1) * width)
        for line, out in enumerate(targets):
            out[:, at] = lanes_of(line)[:, :width]
        gain_out_out[:, at] = lanes_of(KERNEL + 2)[:, :width]
        skip = mm_ones_tr(jnp.broadcast_to(lanes_of(KERNEL + 1), (8, across * LANES)), fold, 3)
        last = group + (KERNEL + 3) * across
        lines = jnp.concatenate(
            [skip[0:1, :], vec_ref[g, last : last + 2, :], jnp.zeros((5, LANES), F32)], axis=0
        )
        lines = jnp.where(lane < heads, lines, 0.0)
        per_head = per_head + (pltpu.roll(lines, g * heads, 1) if g else lines)
    heads_out[...] = per_head
    for copy in loads[4:]:
        copy.wait()
    for q in range(tok_ref.shape[0]):
        wide = tok_ref[q].astype(F32)
        mixed_out[q] = (wide + mixed_ref[q].astype(F32)).astype(BF16)
        scale = lax.rsqrt(jnp.mean(wide * wide, axis=-1, keepdims=True) + EPSILON)
        unit = wide * scale
        scaled = dh_ref[q].astype(F32) * gain
        tokens_out[q] = cot_ref[q].astype(F32) + scale * (
            scaled - unit * jnp.mean(scaled * unit, axis=-1, keepdims=True)
        )


def finish(seq, tokens, cotangent, gain_in, grad_h, mixed, slots_z, slots, rows, vector, shapes):
    columns = INNER + 2 * STATE
    kinds = [
        (tokens.shape, BF16), (tokens.shape, F32), ((1, D), F32), (shapes[0], F32),
        ((KERNEL, columns), F32), ((1, columns), F32), ((8, LANES), F32), ((1, INNER), F32),
        (shapes[1], F32),
    ]
    arrays = (tokens, cotangent, grad_h, mixed, slots_z, slots, rows, vector)
    return pl.pallas_call(
        functools.partial(finish_kernel, seq),
        in_specs=[IN_HBM] * 2 + [pl.BlockSpec(memory_space=pltpu.VMEM)] + [IN_HBM] * 6,
        scratch_shapes=[pltpu.VMEM(v.shape, v.dtype) for v in arrays]
        + [pltpu.SemaphoreType.DMA((len(arrays),))],
        out_shape=[jax.ShapeDtypeStruct(*kind) for kind in kinds],
        compiler_params=pltpu.CompilerParams(vmem_limit_bytes=62 << 20),
        name="finish",
    )(tokens, cotangent, gain_in[None], grad_h, mixed, slots_z, slots, rows, vector)


def local(
    tokens, segments, gain_in, w_in, conv_w, conv_b, dt_bias, a_log, skip, gain_out, w_out,
    cotangent,
):
    steps, shards = lax.axis_size("seq"), lax.axis_size("fsdp")
    place = Place(steps, shards)
    seqs, length, _ = tokens.shape
    width = INNER // steps
    rows_in = w_in.shape[0]

    wide = tokens.astype(F32)
    scale_in = lax.rsqrt(jnp.mean(wide * wide, axis=-1, keepdims=True) + EPSILON)
    normed = (wide * scale_in * gain_in).astype(BF16)
    zx = w_in
    if width % LANES:
        zx = w_in[:, : 2 * INNER].reshape(rows_in, 2, steps, width).transpose(2, 0, 1, 3)
        zx = zx.reshape(steps, rows_in, 2 * width)
    tail = jnp.pad(w_in[:, 2 * INNER :], ((0, 0), (0, LANES - HEADS)))
    columns = INNER + 2 * STATE

    def line(*arrays):
        arrays = [jnp.pad(v, (0, -v.shape[0] % LANES)) for v in arrays]
        return jnp.pad(jnp.concatenate(arrays), (0, columns - sum(v.shape[0] for v in arrays)))

    packed = jnp.concatenate(
        [
            conv_w,
            jnp.stack(
                [conv_b, line(gain_out), line(dt_bias, a_log, skip), jnp.zeros((columns,), F32)]
            ),
        ]
    )
    (
        proj, states, off_col, rem_col, off_row, h_all, w_mine, dz, dy, stats, mixed, part_out,
        part_z, gains, consts,
    ) = forward_mix(normed, zx, tail, segments, cotangent, w_out, packed, steps, shards)
    grad_proj, sums_x, sums_t, sums_h, mixed, rows, slots_z, grad_h = backward_mix(
        proj, off_col, off_row, rem_col, dy, dz, w_mine, stats, states, mixed,
        part_out, part_z, packed, consts, steps, shards,
    )
    grad_h, mixed, slots, vector = exit_scatter(
        steps, shards, h_all, grad_h, grad_proj, w_mine, mixed, gains + (sums_x, sums_t, sums_h)
    )
    (
        mixed, tokens_grad, gain_in_grad, w_in_grad, conv_w_grad, conv_b_grad, per_head,
        gain_out_grad, w_out_grad,
    ) = finish(
        steps, tokens, cotangent, gain_in, grad_h, mixed,
        slots_z.reshape(steps, rows_in, width), slots.reshape(steps, rows_in, width + TAIL), rows,
        vector.reshape((steps,) + vector.shape[2:]), (w_in.shape, w_out.shape),
    )
    return (
        mixed, tokens_grad, gain_in_grad[0], w_in_grad, conv_w_grad, conv_b_grad[0],
        per_head[1, :HEADS], per_head[2, :HEADS], per_head[0, :HEADS], gain_out_grad[0],
        w_out_grad,
    )


def solution(mesh):
    by_token = P("fsdp", "seq", None)
    by_row = P(("seq", "fsdp"), None)
    placed = (
        by_token, P("fsdp", None), P(), by_row, P(), P(), P(), P(), P(), P(), by_row, by_token,
    )
    return jax.shard_map(
        local,
        mesh=mesh,
        in_specs=placed,
        out_specs=(by_token, by_token, P(), by_row, P(), P(), P(), P(), P(), P(), by_row),
        check_vma=False,
    )
```

```python
import functools

import jax
import jax.numpy as jnp
import numpy as np
from jax import lax
from jax.experimental import pallas as pl
from jax.experimental.pallas import tpu as pltpu
from jax.sharding import PartitionSpec as P

D = 1536
HEADS = 48
HEAD_DIM = 64
STATE = 128
KERNEL = 4
INNER = 3072
LANES = 128
HALO = 16
EPSILON = 1e-05
TILE = 384
F32 = jnp.float32
BF16 = jnp.bfloat16


def mm(a, b):
    return jnp.dot(a.astype(BF16), b.astype(BF16), preferred_element_type=F32)


def mm_tr(a, b):
    return lax.dot_general(
        a.astype(BF16), b.astype(BF16), (((1,), (1,)), ((), ())), preferred_element_type=F32
    )


def tr_mm(a, b):
    return lax.dot_general(
        a.astype(BF16), b.astype(BF16), (((0,), (0,)), ((), ())), preferred_element_type=F32
    )


def pieces(a, count):
    out = []
    for _ in range(count - 1):
        part = a.astype(BF16)
        out.append(part)
        a = a - part.astype(F32)
    out.append(a.astype(BF16))
    return out


def ones_mm(ones, a, count):
    return sum(jnp.dot(ones, part, preferred_element_type=F32) for part in pieces(a, count))


def mm_ones(a, ones, count):
    return sum(jnp.dot(part, ones, preferred_element_type=F32) for part in pieces(a, count))


def mm_ones_tr(a, ones, count):
    return sum(
        lax.dot_general(part, ones, (((1,), (1,)), ((), ())), preferred_element_type=F32)
        for part in pieces(a, count)
    )


def iota(shape, dim):
    return lax.broadcasted_iota(jnp.int32, shape, dim)


def softplus(v):
    return jnp.maximum(v, 0.0) + jnp.log1p(jnp.exp(-jnp.abs(v)))


def sigmoid(v):
    return 1.0 / (1.0 + jnp.exp(-v))


def causal_conv(ext, current, halo, weight, bias, offset):
    length = current.shape[0]
    ext[0:HALO, :] = halo
    ext[HALO : HALO + length, :] = current
    total = bias + weight[KERNEL - 1 : KERNEL, :] * current
    for back in range(1, KERNEL):
        shifted = jnp.where(offset >= back, ext[pl.ds(HALO - back, length), :], 0.0)
        total = total + weight[KERNEL - 1 - back : KERNEL - back, :] * shifted
    return total


def head_tiles(width):
    out = []
    for start in range(0, width, LANES):
        size = min(LANES, width - start)
        heads = [start // HEAD_DIM + i for i in range(size // HEAD_DIM)]
        out.append((start, size, heads))
    return out


def masked_heads(tile, heads):
    if len(heads) == 1:
        return tile
    lane = iota(tile.shape, 1) // HEAD_DIM
    return jnp.concatenate(
        [jnp.where(lane == i, tile, jnp.zeros_like(tile)) for i in range(len(heads))], axis=0
    )


def expander(width):
    return (iota((LANES, width), 1) // HEAD_DIM == iota((LANES, width), 0)).astype(BF16)


def chunk_common(x, xh, tail, tailh, offset, params, ext_x, ext_t, width):
    wx, bx, wt, bt, heads_p, pick = params
    length = x.shape[0]
    conv_x = causal_conv(ext_x, x.astype(F32), xh.astype(F32), wx, bx, offset)
    conv_t = causal_conv(
        ext_t,
        tail[:, : 2 * STATE].astype(F32),
        tailh[:, : 2 * STATE].astype(F32),
        wt,
        bt,
        offset,
    )
    raw = jnp.dot(tail[:, 2 * STATE :], pick, preferred_element_type=F32) + heads_p[0:1, :]
    step = softplus(raw)
    decay_rate = jnp.exp(heads_p[1:2, :])
    rate = -step * decay_rate
    tril = (iota((length, length), 0) >= iota((length, length), 1)).astype(BF16)
    cumul = ones_mm(tril, rate, 3)
    spread = expander(width)
    row = iota((length, 1), 0)
    entry = jnp.where(offset > row.astype(F32), jnp.exp(cumul), 0.0)
    last_off = offset[length - 1 : length, :]
    same_last = row.astype(F32) >= (length - 1) - last_off
    to_end = jnp.where(same_last, jnp.exp(cumul[length - 1 : length, :] - cumul), 0.0)
    step_x = mm_ones(step, spread, 2)
    entry_x = mm_ones(entry, spread, 2)
    end_x = mm_ones(to_end, spread, 2)
    return conv_x, conv_t, raw, step, rate, decay_rate, cumul, spread, step_x, entry_x, end_x


def positions(segments, chunk, length):
    here = jnp.zeros((1, length), F32)
    total = segments.shape[1] // length
    rows = [segments[:, i * length : (i + 1) * length].astype(F32) for i in range(total)]
    for i in range(total):
        here = here + jnp.where(chunk == i, rows[i], 0.0)
    own = jnp.broadcast_to(here, (length, length)).T
    less = jnp.zeros((length, length), F32)
    upto = jnp.zeros((length, length), F32)
    for row in rows:
        less = less + jnp.where(row < own, 1.0, 0.0)
        upto = upto + jnp.where(row <= own, 1.0, 0.0)
    index = (chunk * length + iota((length, 1), 0)).astype(F32)
    offset = index - jnp.sum(less, axis=1, keepdims=True)
    return offset, jnp.sum(upto, axis=1, keepdims=True) - 1.0 - index


def flat_rows(ref, flat):
    rows, cols = ref.shape[-2:]
    if rows % HALO == 0:
        return ref[...].reshape(-1, cols)
    shape = ref.shape[:-2]
    for i, at in enumerate(np.ndindex(*shape)):
        flat[i * rows : (i + 1) * rows, :] = ref[at]
    return flat[...]


def pick_params(place, pack_ref, cx_ref, hp_ref, pick_ref):
    width = cx_ref.shape[1]
    heads = width // HEAD_DIM
    mine = jnp.zeros((8, width), F32)
    for g in range(INNER // width):
        mine = mine + jnp.where(place.chunk == g, pack_ref[:, g * width : (g + 1) * width], 0.0)
    lane, source = iota((LANES, LANES), 1), iota((LANES, LANES), 0)
    pick = ((lane < heads) & (source == lane + place.chunk * heads)).astype(BF16)
    pick_ref[...] = pick
    lines = [pack_ref[6:7, i * LANES : (i + 1) * LANES] for i in range(3)]
    lines = jnp.concatenate(lines + [jnp.zeros((5, LANES), F32)], axis=0)
    lines = mm_ones(lines, pick, 3)
    hp_ref[...] = lines
    cx_ref[...] = mine
    cx_ref[6:7, :] = mm_ones(lines, expander(width), 3)[2:3, :]


def forward_kernel(
    seq, fsdp,
    h_ref, zx_ref, tail_ref, seg_ref, cot_ref, ow_ref,
    pack_ref,
    proj_ref, state_ref, off_ref, rem_ref, offr_ref,
    h_out, w_out, dz_out, dy_out, stat_out, mixed_out, mixed_got, pout_out, pz_out, gain_out_ref, gain_in_ref,
    cx_ref, hp_ref, pick_ref,
    h_v, w_v, w_flat, seg_v, cot_v, ow_v, ow_flat, gated_v, sums_v, sums_got, grad_v, z_v, y_v,
    mix_give, mix_own, pout_v, pz_v, memory, ext_x, ext_t, last_rows, send, recv, near,
):
    seqs, _, length, depth = h_v.shape
    width = cx_ref.shape[1]
    step_at = pl.program_id(0)
    place = Place(seq, fsdp)
    links = Links(send, recv, near)
    peers = peers_of(place)
    near_peers = [(l, c) for t, l, c in peers if t == 0]
    entry = Entry(place, links, h_ref, zx_ref, tail_ref, seg_ref, h_v, w_v, seg_v)
    cot = TokenGather(place, links, cot_ref, cot_v)
    w_rows = RowGather(place, links, ow_ref, ow_v)
    keep = [links.local(lambda: (h_v, h_out)), links.local(lambda: (w_v, w_out))]
    stages = len(place.low_bits)

    def send_sums(i):
        l, c = near_peers[i]
        return links.far(lambda: (sums_v, sums_got.at[i], place.at(low=l, core=c)))

    sums = [send_sums(i) for i in range(len(near_peers))]

    def send_core(q):
        return links.far(lambda: (mix_give.at[q], mixed_got.at[q], place.at(core=1)))

    cores = [send_core(q) for q in range(seqs)]

    @pl.when(step_at == 0)
    def _():
        memory[...] = jnp.zeros_like(memory)
        last_rows[...] = jnp.zeros_like(last_rows)
        pick_params(place, pack_ref, cx_ref, hp_ref, pick_ref)
        meet_pair(place)
        entry.run(cot.cross_over)
        if w_v.shape[-2] % HALO:
            flat_rows(w_v, w_flat)

    @pl.when(step_at == 1)
    def _():
        for copy in keep:
            copy.start()
        cot.begin_home()
        w_rows.begin()

    for i in range(stages):

        @pl.when(step_at == min(3 + 2 * i, seq - 1))
        def _():
            cot.pass_on(i, "home")

    @pl.when(step_at == 2)
    def _():
        cot.arrive()

    for i in range(stages):

        @pl.when(step_at == min(4 + 2 * i, seq - 1))
        def _():
            cot.pass_on(i, "away")

    @pl.when(step_at == seq - 3)
    def _():
        w_rows.forward()

    @pl.when(step_at < seq)
    def _():
        weights = flat_rows(w_v, w_flat) if w_v.shape[-2] % HALO == 0 else w_flat[...]
        proj = jnp.dot(
            h_v[:, step_at].reshape(seqs * length, depth), weights, preferred_element_type=F32
        ).astype(BF16)
        proj_ref[...] = proj.reshape(proj_ref.shape)
        params = (
            cx_ref[:KERNEL, :], cx_ref[KERNEL : KERNEL + 1, :],
            pack_ref[:KERNEL, INNER:], pack_ref[KERNEL : KERNEL + 1, INNER:],
            hp_ref[...], pick_ref[...],
        )
        gain_row, skip_row = cx_ref[KERNEL + 1 : KERNEL + 2, :], cx_ref[KERNEL + 2 : KERNEL + 3, :]
        for q in range(seqs):
            offset, remain = positions(seg_v[q : q + 1, :], step_at, length)
            off_ref[q, 0] = offset
            rem_ref[q, 0] = remain
            offr_ref[q, 0] = jnp.broadcast_to(offset, (length, LANES)).T[0:1, :]
            chunk_rows = proj[q * length : (q + 1) * length]
            zx, tail = chunk_rows[:, : 2 * width], chunk_rows[:, 2 * width :]
            earlier = last_rows[q]
            z_rows = zx[:, :width]
            here = pl.ds(pl.multiple_of((q * seq + step_at) * length, length), length)
            z_v[here, :] = z_rows
            conv_x, conv_t, _, _, _, _, cumul, _, step_x, entry_x, end_x = chunk_common(
                zx[:, width:], earlier[:, width : 2 * width], tail, earlier[:, 2 * width :], offset, params,
                ext_x.at[q], ext_t.at[q], width,
            )
            xs = conv_x * sigmoid(conv_x)
            act_t = conv_t * sigmoid(conv_t)
            bs = act_t[:, :STATE].astype(BF16)
            cs = act_t[:, STATE:].astype(BF16)
            scaled = xs * step_x
            scores = mm_tr(cs, bs)
            gap = iota((length, length), 0) - iota((length, length), 1)
            same = (gap >= 0) & (gap.astype(F32) <= offset)
            cumul_t = cumul.T
            old = memory[q]
            old_low = old.astype(BF16)
            state_ref[q, 0] = old_low
            outside = mm(cs, old_low) * entry_x + skip_row * xs
            squares = jnp.zeros((length, 1), F32)
            for start, size, heads in head_tiles(width):
                mixing = []
                for head in heads:
                    spans = cumul[:, head : head + 1] - cumul_t[head : head + 1, :]
                    decays = jnp.exp(jnp.where(same, spans, -1e30))
                    mixing.append((decays * scores).astype(BF16))
                tile = masked_heads(scaled[:, start : start + size].astype(BF16), heads)
                mix = mixing[0] if len(heads) == 1 else jnp.concatenate(mixing, axis=1)
                inside = jnp.dot(mix, tile, preferred_element_type=F32)
                y_low = (inside + outside[:, start : start + size]).astype(BF16)
                y_v[here, start : start + size] = y_low
                z = zx[:, start : start + size].astype(F32)
                gated = y_low.astype(F32) * (z * sigmoid(z))
                gated_v[here, start : start + size] = (
                    gated * gain_row[:, start : start + size]
                ).astype(BF16)
                squares = squares + jnp.sum(gated * gated, axis=1, keepdims=True)
            sums_v[pl.ds(2 * (q * seq + step_at), 1), :] = jnp.broadcast_to(
                squares, (length, LANES)
            ).T[0:1, :]
            fresh = tr_mm(bs, scaled * end_x)
            memory[q] = old * entry_x[length - 1 : length, :] + fresh
            last_rows[q] = chunk_rows[length - HALO :]

    @pl.when(step_at == seq)
    def _():
        w_rows.finish()
        cot.finish()
        rows_out = flat_rows(ow_v, ow_flat)
        tile = 2 * length
        tiles = seqs * seq // 2

        @pl.loop(0, tiles)
        def _(k):
            at = pl.ds(pl.multiple_of(k * tile, tile), tile)
            cots = cot_v[k // (seq // 2), pl.ds(lax.rem(k, seq // 2) * 2, 2)].reshape(tile, depth)
            grad = mm_tr(cots, rows_out)
            grad_v[at, :] = grad
            part = jnp.sum(grad * gated_v[at, :].astype(F32), axis=1, keepdims=True)
            part = jnp.broadcast_to(part, (tile, LANES))
            for i in (0, 1):
                sums_v[pl.ds(4 * k + 2 * i + 1, 1), :] = (
                    part[i * length : (i + 1) * length].T[0:1, :]
                )

        for copy in sums:
            copy.start()

        def mixed_rows(out, side):
            per_side = seq // 2 // 2
            for q in range(seqs):

                @pl.loop(0, per_side)
                def _(k):
                    at = (q * seq + seq // 2 * side + 2 * k) * length
                    rows = gated_v[pl.ds(pl.multiple_of(at, tile), tile), :]
                    mixed = jnp.dot(rows, rows_out, preferred_element_type=F32)
                    out[q, pl.ds(2 * k, 2)] = mixed.astype(BF16).reshape(2, length, depth)

        mixed_rows(mix_give, 1 - place.core)
        for copy in cores:
            copy.start()
        mixed_rows(mix_own, place.core)
        mixed_store = links.local(lambda: (mix_own, mixed_out))
        mixed_store.start()
        for copy in sums:
            copy.wait_recv()
        total = sums_v[...]
        for i in range(len(near_peers)):
            total = total + sums_got[i]
        is_square = lax.rem(iota(total.shape, 0), 2) == 0
        scale = lax.rsqrt(total / INNER + EPSILON)
        other = pltpu.roll(scale, 1, 0)
        stat_out[...] = jnp.where(is_square, scale, total * (other * other * other / INNER))

        gain_out_ref[...] = jnp.zeros_like(gain_out_ref)
        gain_row = cx_ref[KERNEL + 1 : KERNEL + 2, :]

        @pl.loop(0, tiles)
        def _(k):
            at = pl.ds(pl.multiple_of(k * tile, tile), tile)

            def column(line):
                rows = [
                    jnp.broadcast_to(stat_out[pl.ds(4 * k + 2 * i + line, 1), :], (LANES, length))
                    for i in (0, 1)
                ]
                return jnp.concatenate([row.T[:, 0:1] for row in rows], axis=0)

            scale, slope = column(0), column(1)
            gated_v[at, :] = (gated_v[at, :].astype(F32) * scale).astype(BF16)
            z = z_v[at, :].astype(F32)
            y = y_v[at, :].astype(F32)
            sig = sigmoid(z)
            silu_z = z * sig
            gated = y * silu_z
            scaled = grad_v[at, :] * scale
            gain_out_ref[0:1, :width] += jnp.sum(scaled * gated, axis=0, keepdims=True)
            grad_gated = gain_row * scaled - gated * slope
            y_v[at, :] = (grad_gated * silu_z).astype(BF16)
            z_v[at, :] = (grad_gated * y * (sig + silu_z * (1.0 - sig))).astype(BF16)

        dz_store = links.local(lambda: (z_v, dz_out))
        dy_store = links.local(lambda: (y_v, dy_out))
        dz_store.start()
        dy_store.start()

        rows_in = w_v.shape[3]
        blocks = TILE // rows_in
        high = blocks // fsdp
        h_flat = h_v[...].reshape(-1, depth)
        for t in range(depth // TILE):
            term = tr_mm(h_flat[:, t * TILE : (t + 1) * TILE], z_v[...])
            for i in range(blocks):
                pz_v[t * high + i // fsdp, i % fsdp // 2, i % 2] = term[
                    i * rows_in : (i + 1) * rows_in
                ].astype(BF16)
            if rows_in % HALO:
                some = w_flat[t * TILE : (t + 1) * TILE, :width]
            else:
                some = w_v[t * high : (t + 1) * high, :, :, :, :width].reshape(TILE, width)
            line = jnp.sum(term * some.astype(F32), axis=1, keepdims=True)
            wide = jnp.broadcast_to(line, (TILE, LANES))
            for i in range(TILE // LANES):
                row = t * (TILE // LANES) + i
                gain_in_ref[row : row + 1, :] = wide[i * LANES : (i + 1) * LANES].T[0:1, :]
        pz_store = links.local(lambda: (pz_v, pz_out))
        pz_store.start()
        pout_v[...] = tr_mm(gated_v[...], cot_v[...].reshape(-1, depth)).astype(BF16)
        pout_store = links.local(lambda: (pout_v, pout_out))
        pout_store.start()
        for copy in [dz_store, dy_store, pz_store, mixed_store, pout_store] + keep:
            copy.wait()
        for copy in cores:
            copy.wait()
        for copy in sums:
            copy.wait_send()
        entry.finish()


def backward_kernel(
    seq, fsdp,
    x_ref, xh_ref, tail_ref, tailh_ref, off_ref, offr_ref, rem_ref, dy_ref, dz_ref, state_ref,
    w_ref,    all_stat_ref, mixed_ref, got_ref, pout_ref, pz_ref,
    cx_ref, ct_ref, hp_ref, pick_ref,
    out_ref, gx_ref, gt_ref, gh_ref, mixed_out, rows_out, slots_out, dh_out,
    memory, ext_x, ext_t, next_x, next_t,
    mix_own, mix_first, mix_later, pout_own, pout_first, pz_own, pz_first, pz_top,
    dh_give, dh_own, dh_first, send, recv, near,
):
    seqs, _, length, width = dy_ref.shape
    x_at = x_ref.shape[3] - width
    step_at = pl.program_id(0)

    place = Place(seq, fsdp)
    links = Links(send, recv, near)
    mixed = TokenScatter(
        place, links, (mixed_ref, got_ref), mixed_out, mix_own, mix_first, mix_later, "halves"
    )
    w_rows = RowScatter(place, links, pout_ref, rows_out, pout_own, pout_first)
    z_part = PartScatter(
        place, links, pz_ref, lambda s, c: pz_own.at[s, c], pz_first, pz_top, slots_out, 1
    )
    pz_load = links.local(lambda: (pz_ref.at[:, place.pair], pz_own))
    half = seq // 2

    def give_chunk(low):
        return links.far(
            lambda: (dh_give.at[:, low], dh_first.at[:, low], place.at(core=1))
        )

    dh_chunks = [give_chunk(low) for low in range(half)]

    def add_chunk(low):
        dh_chunks[low].wait_recv()
        for q in range(seqs):
            add_rows(dh_own.at[q, low], dh_own.at[q, low], dh_first.at[q, low])

    dh_store = links.local(lambda: (dh_own, dh_out))
    stages = len(place.low_bits)

    @pl.when(step_at == 0)
    def _():
        mixed.begin()
        pz_load.start()
        meet_pair(place)
        z_part.send_pairs(1, 0)
        mixed.add_cores()
        mixed.send_stage(0)

    @pl.when(step_at == 1)
    def _():
        z_part.send_pairs(0, 0)

    @pl.when(step_at == 2)
    def _():
        pz_load.wait()
        z_part.add_pairs(1, 0)
        z_part.send_cross(0)
        w_rows.begin()

    @pl.when(step_at == 4)
    def _():
        z_part.add_pairs(0, 0)

    @pl.when(step_at == 5)
    def _():
        w_rows.add_pairs()

    @pl.when(step_at == pl.num_programs(0) - 1)
    def _():
        z_part.spread()

    @pl.when(step_at == pl.num_programs(0) - 4)
    def _():
        mixed.add_stage(0)
        if stages > 1:
            mixed.send_stage(1)

    @pl.when(pl.program_id(0) == 0)
    def _():
        memory[...] = jnp.zeros_like(memory)
        gx_ref[...] = jnp.zeros_like(gx_ref)
        gt_ref[...] = jnp.zeros_like(gt_ref)
        gh_ref[...] = jnp.zeros_like(gh_ref)
        next_x[:, length:, :] = jnp.zeros_like(next_x[:, length:, :])
        next_t[:, length:, :] = jnp.zeros_like(next_t[:, length:, :])

    params = (
        cx_ref[:KERNEL, :], cx_ref[KERNEL : KERNEL + 1, :],
        ct_ref[:KERNEL, :], ct_ref[KERNEL : KERNEL + 1, :],
        hp_ref[...], pick_ref[...],
    )
    skip_row = cx_ref[KERNEL + 2 : KERNEL + 3, :]
    for q in range(seqs):
        offset = off_ref[q, 0]
        conv_x, conv_t, raw, step, rate, decay_rate, cumul, spread, step_x, entry_x, end_x = (
            chunk_common(
                x_ref[q, 0, :, x_at:], xh_ref[q, 0, :, x_at:], tail_ref[q, 0], tailh_ref[q, 0], offset,
                params, ext_x.at[q], ext_t.at[q], width,
            )
        )
        dy_low = dy_ref[q, 0]
        dy = dy_low.astype(F32)

        sig_x = sigmoid(conv_x)
        xs = conv_x * sig_x
        slope_x = sig_x + xs * (1.0 - sig_x)
        sig_t = sigmoid(conv_t)
        act_t = conv_t * sig_t
        slope_t = sig_t + act_t * (1.0 - sig_t)
        bs = act_t[:, :STATE].astype(BF16)
        cs = act_t[:, STATE:].astype(BF16)
        scaled = xs * step_x
        scaled_low = scaled.astype(BF16)
        scores = mm_tr(bs, cs)
        rows, cols = iota((length, length), 0), iota((length, length), 1)
        gap = cols - rows
        same = (gap >= 0) & (gap.astype(F32) <= offr_ref[q, 0])
        strict = gap > 0
        upper = (rows >= cols).astype(BF16)
        cumul_t = cumul.T
        old = state_ref[q, 0]
        grad_state = memory[q]
        state_low = grad_state.astype(BF16)
        grad_scores = jnp.zeros((length, length), F32)
        grad_scaled = []
        inside_rows = []
        for start, size, heads in head_tiles(width):
            dy_tile = masked_heads(dy_low[:, start : start + size], heads)
            grad_mix = mm_tr(scaled_low[:, start : start + size], dy_tile)
            mixing = []
            for i, head in enumerate(heads):
                spans = cumul_t[head : head + 1, :] - cumul[:, head : head + 1]
                decays = jnp.exp(jnp.where(same, spans, -1e30))
                weighted = grad_mix[:, i * length : (i + 1) * length] * decays
                grad_scores = grad_scores + weighted
                mixing.append((decays * scores).astype(BF16))
                terms = jnp.where(strict, weighted * scores, 0.0).astype(BF16)
                sums = jnp.dot(terms, upper, preferred_element_type=F32)
                inside_rows.append(
                    jnp.sum(jnp.where(strict, sums, 0.0), axis=0, keepdims=True)
                )
            mix = mixing[0] if len(heads) == 1 else jnp.concatenate(mixing, axis=1)
            grad_scaled.append(jnp.dot(mix, dy_tile, preferred_element_type=F32))
        inside_rows.append(jnp.zeros((LANES - len(inside_rows), length), F32))
        inside = jnp.concatenate(inside_rows, axis=0).T
        from_end = mm(bs, state_low) * end_x
        grad_scaled = jnp.concatenate(grad_scaled, axis=1) + from_end
        entry_dy = dy * entry_x
        entry_dy_low = entry_dy.astype(BF16)
        out_terms = mm(cs, old) * entry_dy
        end_terms = scaled * from_end
        grad_step = mm_ones_tr(xs * grad_scaled, spread, 2)
        out_terms = mm_ones_tr(out_terms, spread, 2)
        end_terms = mm_ones_tr(end_terms, spread, 2)
        keep_row = entry_x[length - 1 : length, :]
        carried = jnp.sum(grad_state * old.astype(F32), axis=0, keepdims=True) * keep_row
        carried = mm_ones_tr(jnp.broadcast_to(carried, (8, width)), spread, 2)[0:1, :]
        triu = (cols >= rows).astype(BF16)
        below = (rows > cols).astype(BF16)
        grad_rate = inside + ones_mm(triu, out_terms, 2) + ones_mm(below, end_terms, 2) + carried
        grad_step = grad_step - decay_rate * grad_rate
        grad_raw = grad_step * sigmoid(raw)
        grad_scores_low = grad_scores.astype(BF16)
        grad_b = mm(grad_scores_low, cs) + mm_tr(scaled * end_x, state_low)
        grad_c = tr_mm(grad_scores_low, bs) + mm_tr(entry_dy_low, old)
        memory[q] = grad_state * keep_row + tr_mm(cs, entry_dy_low)
        conv_grad_x = (skip_row * dy + step_x * grad_scaled) * slope_x
        conv_grad_t = jnp.concatenate([grad_b, grad_c], axis=1) * slope_t

        remain = rem_ref[q, 0]
        results = []
        for grad, ext, nxt, weight, sums in (
            (conv_grad_x, ext_x.at[q], next_x.at[q], params[0], gx_ref),
            (conv_grad_t, ext_t.at[q], next_t.at[q], params[2], gt_ref),
        ):
            columns = grad.shape[1]
            current = ext[pl.ds(HALO, length), :]
            sums[KERNEL : KERNEL + 1, :columns] += jnp.sum(grad, axis=0, keepdims=True)
            sums[KERNEL - 1 : KERNEL, :columns] += jnp.sum(grad * current, axis=0, keepdims=True)
            nxt[0:length, :] = grad
            total = weight[KERNEL - 1 : KERNEL, :] * grad
            for back in range(1, KERNEL):
                tap = KERNEL - 1 - back
                shifted = jnp.where(offset >= back, ext[pl.ds(HALO - back, length), :], 0.0)
                sums[tap : tap + 1, :columns] += jnp.sum(grad * shifted, axis=0, keepdims=True)
                ahead = jnp.where(remain >= back, nxt[pl.ds(back, length), :], 0.0)
                total = total + weight[tap : tap + 1, :] * ahead
            nxt[length:, :] = grad[0:HALO, :]
            results.append(total.astype(BF16))
        results.append(mm_tr(grad_raw, params[5]).astype(BF16))
        gx_ref[KERNEL + 1 : KERNEL + 2, :width] += jnp.sum(dy * xs, axis=0, keepdims=True)
        gh_ref[0:1, :] += jnp.sum(grad_raw, axis=0, keepdims=True)
        gh_ref[1:2, :] += jnp.sum(grad_rate * rate, axis=0, keepdims=True)
        out_ref[q, 0] = jnp.concatenate(results, axis=1)

    depth = w_ref.shape[0]
    grad_h = mm_tr(dz_ref[...].reshape(seqs * length, width), w_ref[:, :width])
    grad_h = grad_h + mm_tr(
        out_ref[...].reshape(seqs * length, out_ref.shape[3]), w_ref[:, width:]
    )
    grad_h = grad_h.astype(BF16).reshape(seqs, length, depth)
    for i in range(seq):
        chunk = seq - 1 - i

        @pl.when((step_at == i) & (place.core == chunk // half))
        def _():
            dh_own[:, chunk % half] = grad_h

        if i + 1 < seq:

            @pl.when((step_at == i + 1) & (place.core == chunk // half))
            def _():
                add_chunk(chunk % half)

        @pl.when((step_at == i) & (place.core != chunk // half))
        def _():
            dh_give[:, chunk % half] = grad_h
            dh_chunks[chunk % half].start()

    @pl.when(step_at == pl.num_programs(0) - 1)
    def _():
        for stage in range(1, stages):
            mixed.add_stage(stage)
            if stage + 1 < stages:
                mixed.send_stage(stage + 1)
        for q in range(seqs):
            row = all_stat_ref[pl.ds(2 * (q * seq + place.chunk), 1), :]
            column = jnp.broadcast_to(row, (LANES, length)).T[:, 0:1]
            done = mix_own.at[q, place.low]
            done[...] = (done[...].astype(F32) * column).astype(BF16)
        mixed.store()
        z_part.finish()

        @pl.when(place.core == 0)
        def _():
            add_chunk(0)

        for copy in dh_chunks:
            copy.wait_send()
        dh_store.start()
        dh_store.wait()
        w_rows.finish()
        mixed.finish()


TAIL = 2 * STATE + LANES
AXES = ("seq", "fsdp")
MESH = pl.DeviceIdType.MESH
ANYWHERE = pl.BlockSpec(memory_space=pl.ANY)
IN_HBM = pl.BlockSpec(memory_space=pltpu.HBM)


def lane_rows(width):
    return -(-width // LANES)


def sum_rows(width):
    shared = D // LANES
    group = shared + (KERNEL + 1) * 2 * STATE // LANES
    return shared, group, -(-(group + (KERNEL + 3) * lane_rows(width) + 2) // 8) * 8


def whole_spec(shape):
    return pl.BlockSpec(shape, lambda i: (0,) * len(shape))


def chunk_specs(seqs, steps, length, reverse):
    def place(i):
        return steps - 1 - i if reverse else i

    def block(cols, column=0, rows=length):
        return pl.BlockSpec((seqs, 1, rows, cols), lambda i: (0, place(i), 0, column))

    def before(cols, column=0):
        return pl.BlockSpec(
            (seqs, 1, HALO, cols),
            lambda i: (0, jnp.maximum(place(i) - 1, 0), length // HALO - 1, column),
        )

    return block, before


def forward_mix(normed, zx, tail, segments, cotangent, out_w, packed, seq, fsdp):
    seqs, length, depth = normed.shape
    rows = tail.shape[0]
    width = INNER // seq
    cols = 2 * width + TAIL
    pairs = fsdp // 2
    count = seqs * seq * length

    def block(columns, height=length):
        return pl.BlockSpec(
            (seqs, 1, height, columns), lambda i: (0, jnp.minimum(i, seq - 1), 0, 0)
        )

    def blocks(columns, kind, height=length):
        return jax.ShapeDtypeStruct((seqs, seq, height, columns), kind)

    w_shape = (seq, pairs, 2, rows, cols)
    out_shape = (pairs, 2) + out_w.shape
    sums = (seqs * seq * 2, length)
    flat = 8 if rows % HALO == 0 else depth
    flat_out = 8 if out_w.shape[0] % HALO == 0 else width
    outs = pl.pallas_call(
        functools.partial(forward_kernel, seq, fsdp),
        grid=(seq + 1,),
        in_specs=[ANYWHERE] * 6 + [whole_spec(packed.shape)],
        out_specs=[
            block(cols), block(width, STATE), block(1), block(1), block(length, 1),
            ANYWHERE, ANYWHERE, ANYWHERE, ANYWHERE, whole_spec(sums), ANYWHERE, ANYWHERE, ANYWHERE, ANYWHERE,
            whole_spec((8, lane_rows(width) * LANES)), whole_spec((depth // LANES, LANES)),
            whole_spec((8, width)), whole_spec((8, LANES)), whole_spec((LANES, LANES)),
        ],
        out_shape=[
            blocks(cols, BF16), blocks(width, BF16, STATE),
            blocks(1, F32), blocks(1, F32), blocks(length, F32, 1),
            blocks(depth, BF16),
            jax.ShapeDtypeStruct(w_shape, BF16),
            jax.ShapeDtypeStruct((count, width), BF16),
            jax.ShapeDtypeStruct((count, width), BF16),
            jax.ShapeDtypeStruct(sums, F32),
            jax.ShapeDtypeStruct((seqs, seq // 2, length, depth), BF16),
            jax.ShapeDtypeStruct((seqs, seq // 2, length, depth), BF16),
            jax.ShapeDtypeStruct((width, depth), BF16),
            jax.ShapeDtypeStruct(w_shape[:4] + (width,), BF16),
            jax.ShapeDtypeStruct((8, lane_rows(width) * LANES), F32),
            jax.ShapeDtypeStruct((depth // LANES, LANES), F32),
            jax.ShapeDtypeStruct((8, width), F32),
            jax.ShapeDtypeStruct((8, LANES), F32),
            jax.ShapeDtypeStruct((LANES, LANES), BF16),
        ],
        scratch_shapes=[
            pltpu.VMEM((seqs, seq, length, depth), BF16),
            pltpu.VMEM(w_shape, BF16),
            pltpu.VMEM((flat, cols), BF16),
            pltpu.VMEM(segments.shape, segments.dtype),
            pltpu.VMEM((seqs, seq, length, depth), BF16),
            pltpu.VMEM(out_shape, BF16),
            pltpu.VMEM((flat_out, depth), BF16),
            pltpu.VMEM((count, width), BF16),
            pltpu.VMEM(sums, F32),
            pltpu.VMEM((seq - 1,) + sums, F32),
            pltpu.VMEM((count, width), F32),
            pltpu.VMEM((count, width), BF16),
            pltpu.VMEM((count, width), BF16),
            pltpu.VMEM((seqs, seq // 2, length, depth), BF16),
            pltpu.VMEM((seqs, seq // 2, length, depth), BF16),
            pltpu.VMEM((width, depth), BF16),
            pltpu.VMEM(w_shape[:4] + (width,), BF16),
            pltpu.VMEM((seqs, STATE, width), F32),
            pltpu.VMEM((seqs, HALO + length, width), F32),
            pltpu.VMEM((seqs, HALO + length, 2 * STATE), F32),
            pltpu.VMEM((seqs, HALO, cols), BF16),
            pltpu.SemaphoreType.DMA((320,)),
            pltpu.SemaphoreType.DMA((320,)),
            pltpu.SemaphoreType.DMA((24,)),
        ],
        compiler_params=pltpu.CompilerParams(
            dimension_semantics=("arbitrary",), vmem_limit_bytes=63 << 20, collective_id=0,
            has_side_effects=True,
        ),
        cost_estimate=pl.CostEstimate(
            flops=30_000_000_000, transcendentals=0, bytes_accessed=60_000_000
        ),
        name="mix_forward",
    )(normed, zx, tail, segments, cotangent, out_w, packed)
    (
        proj, states, off_col, rem_col, off_row, h_all, w_mine, dz, dy, stats, mixed, got, part,
        part_z, gain_out, gain_in,
    ) = outs[:16]
    return (
        proj, states, off_col, rem_col, off_row, h_all, w_mine.reshape(depth, cols), dz,
        dy.reshape(seqs, seq, length, width), stats, (mixed, got), part.reshape(out_shape),
        part_z, (gain_in, gain_out), outs[16:],
    )


def backward_mix(
    proj, off_col, off_row, rem_col, dy, dz, w_mine, stats, states, mixed, part_out, part_z, packed, consts, seq, fsdp
):
    seqs, steps, length, cols = proj.shape
    depth = mixed[0].shape[3]
    width = (cols - TAIL) // 2
    block, before = chunk_specs(seqs, steps, length, True)
    tail_at = 2 * width // TAIL
    x_cols, x_at = (width, 1) if width % LANES == 0 else (2 * width, 0)
    rows_in = part_z.shape[3]
    half, pairs = seq // 2, fsdp // 2
    rows_out = part_out.shape[2]
    sums = [(8, lane_rows(width) * LANES), (8, 2 * STATE), (8, LANES)]
    token_own = pltpu.VMEM((seqs, half, length, depth), BF16)
    return pl.pallas_call(
        functools.partial(backward_kernel, seq, fsdp),
        grid=(steps,),
        in_specs=[
            block(x_cols, x_at), before(x_cols, x_at),
            block(TAIL, tail_at), before(TAIL, tail_at),
            block(1), block(length, 0, 1), block(1), block(width), block(width),
            block(width, 0, STATE),
            pl.BlockSpec(w_mine.shape, lambda i: (0, 0), pipeline_mode=pl.Buffered(1)),
            whole_spec(stats.shape), ANYWHERE, ANYWHERE,
            ANYWHERE, ANYWHERE, whole_spec(consts[0].shape),
            pl.BlockSpec((8, 2 * STATE), lambda i: (0, INNER // (2 * STATE))),
            whole_spec(consts[1].shape), whole_spec(consts[2].shape),
        ],
        out_specs=[block(width + TAIL)] + [whole_spec(v) for v in sums] + [ANYWHERE] * 4,
        scratch_shapes=[
            pltpu.VMEM((seqs, STATE, width), F32),
            pltpu.VMEM((seqs, HALO + length, width), F32),
            pltpu.VMEM((seqs, HALO + length, 2 * STATE), F32),
            pltpu.VMEM((seqs, length + HALO, width), F32),
            pltpu.VMEM((seqs, length + HALO, 2 * STATE), F32),
            token_own, token_own, pltpu.VMEM((seqs, max(half - 1, 1), length, depth), BF16),
            pltpu.VMEM((2, rows_out, depth), BF16),
            pltpu.VMEM((max(pairs - 1, 1), 2, rows_out, depth), BF16),
            pltpu.VMEM((seq, 2, rows_in, width), BF16),
            pltpu.VMEM((max(pairs - 1, 1), seq, 2, rows_in, width), BF16),
            pltpu.VMEM((half, 2, rows_in, width), BF16),
            token_own, token_own, token_own,
            pltpu.SemaphoreType.DMA((128,)),
            pltpu.SemaphoreType.DMA((128,)),
            pltpu.SemaphoreType.DMA((16,)),
        ],
        out_shape=[jax.ShapeDtypeStruct(proj.shape[:3] + (width + TAIL,), BF16)]
        + [jax.ShapeDtypeStruct(v, F32) for v in sums]
        + [
            jax.ShapeDtypeStruct((seqs, length, depth), BF16),
            jax.ShapeDtypeStruct((2, rows_out, depth), BF16),
            jax.ShapeDtypeStruct((2, half, rows_in, width), BF16),
            jax.ShapeDtypeStruct((seqs, half, length, depth), BF16),
        ],
        compiler_params=pltpu.CompilerParams(
            dimension_semantics=("arbitrary",), vmem_limit_bytes=56 << 20, collective_id=3,
            has_side_effects=True,
        ),
        cost_estimate=pl.CostEstimate(
            flops=steps * seqs * 2_000_000_000, transcendentals=0, bytes_accessed=16_000_000
        ),
        name="mix_backward",
    )(
        proj, proj, proj, proj, off_col, off_row, rem_col, dy, dz.reshape(dy.shape), states,
        w_mine, stats, *mixed, part_out,
        part_z, consts[0], packed, consts[1], consts[2],
    )


class Place:
    def __init__(self, seq, fsdp):
        self.seq, self.fsdp = seq, fsdp
        self.half, self.pairs = seq // 2, fsdp // 2
        s, f = lax.axis_index("seq"), lax.axis_index("fsdp")
        self.s, self.f = s, f
        self.top, self.low = s // self.half, lax.rem(s, self.half)
        self.core, self.pair = lax.rem(f, 2), f // 2
        self.home = self.core == self.top
        self.away = self.core != self.top
        self.chunk = self.low + self.half * self.core
        self.low_bits = [1 << i for i in range(self.half.bit_length() - 1)]

    def at(self, top=0, low=0, pair=0, core=0):
        return (
            flip(self.top, top) * self.half + flip(self.low, low),
            flip(self.pair, pair) * 2 + flip(self.core, core),
        )

    def bits_for(self, q):
        return self.low_bits if q % 2 == 0 else self.low_bits[::-1]


def flip(index, bits):
    for i in range(bits.bit_length()):
        if bits >> i & 1:
            bit = lax.rem(index // (1 << i), 2)
            index = index + (1 << i) * (1 - 2 * bit)
    return index


class Copy:
    def __init__(self, make):
        self.make = make

    def start(self):
        self.make().start()
        return self

    def wait(self):
        self.make().wait()

    def wait_send(self):
        self.make().wait_send()

    def wait_recv(self):
        self.make().wait_recv()


class Copies:
    def __init__(self, copies):
        self.copies = copies

    def start(self):
        for copy in self.copies:
            copy.start()

    def wait_recv(self):
        for copy in self.copies:
            copy.wait_recv()

    def wait_send(self):
        for copy in self.copies:
            copy.wait_send()


class Links:
    def __init__(self, send, recv, near):
        self.send, self.recv, self.near = send, recv, near
        self.far_count = self.near_count = 0

    def far(self, make):
        i = self.far_count
        self.far_count += 1

        def build():
            src, dst, device = make()
            return pltpu.make_async_remote_copy(
                src_ref=src, dst_ref=dst, send_sem=self.send.at[i], recv_sem=self.recv.at[i],
                device_id=device, device_id_type=MESH,
            )

        return Copy(build)

    def local(self, make):
        i = self.near_count
        self.near_count += 1
        return Copy(lambda: pltpu.make_async_copy(*make(), self.near.at[i]))


def meet(devices):
    barrier = pltpu.get_barrier_semaphore()
    for device in devices:
        pl.semaphore_signal(barrier, inc=1, device_id=device, device_id_type=MESH)
    pl.semaphore_wait(barrier, len(devices))


def meet_pair(place):
    meet(
        [place.at(top=t, low=l, core=c) for t, l, c in peers_of(place)]
        + [place.at(pair=p) for p in range(1, place.pairs)]
    )


def peers_of(place):
    out = []
    for top in (0, 1):
        for low in range(place.half):
            for core in (0, 1):
                if (top, low, core) != (0, 0, 0):
                    out.append((top, low, core))
    return out


class TokenGather:
    def __init__(self, place, links, src, dst):
        self.place, self.src, self.dst = place, src, dst
        seqs = src.shape[0]

        def over(q):
            return links.far(
                lambda: (src.at[q], dst.at[q, place.s], place.at(top=1, core=1))
            )

        self.cross = [over(q) for q in range(seqs)]
        self.stay = links.local(lambda: (src, dst.at[:, place.s]))
        self.share = [[] for _ in range(seqs)]
        self.stages = []
        held = [[0] for _ in range(seqs)]
        for q in range(seqs):
            self.share[q].append([self.copy(links, q, low, core=1) for low in held[q]])
        for i in range(len(place.low_bits)):
            stage = []
            for q in range(seqs):
                bit = place.bits_for(q)[i]
                stage.append([self.copy(links, q, low, low_bit=bit) for low in held[q]])
                fresh = [low ^ bit for low in held[q]]
                held[q] = held[q] + fresh
                self.share[q].append([self.copy(links, q, low, core=1) for low in fresh])
            self.stages.append(stage)

    def copy(self, links, q, low, low_bit=0, core=0):
        def make():
            place = self.place
            ref = self.dst.at[q, flip(place.low, low) + place.half * place.core]
            return ref, ref, place.at(low=low_bit, core=core)

        return links.far(make)

    def begin(self):
        self.cross_over()
        self.begin_home()

    def cross_over(self):
        @pl.when(self.place.away)
        def _():
            for copy in self.cross:
                copy.start()

    def begin_home(self):
        @pl.when(self.place.home)
        def _():
            self.stay.start()
            self.stay.wait()
            self.send_stage(0)

    def arrive(self):
        @pl.when(self.place.away)
        def _():
            for copy in self.cross:
                copy.wait_recv()
            self.send_stage(0)

    def send_stage(self, i):
        for q in range(len(self.share)):
            for copy in self.stages[i][q] + self.share[q][i]:
                copy.start()

    def pass_on(self, i, role):
        @pl.when(self.place.home if role == "home" else self.place.away)
        def _():
            for q in range(len(self.share)):
                for copy in self.stages[i][q]:
                    copy.wait_recv()
                for copy in (self.stages[i + 1][q] if i + 1 < len(self.stages) else []):
                    copy.start()
                for copy in self.share[q][i + 1]:
                    copy.start()

    def finish(self):
        for share in self.share:
            for copies in share:
                for copy in copies:
                    copy.wait()
        for stage in self.stages:
            for copies in stage:
                for copy in copies:
                    copy.wait_send()

        @pl.when(self.place.away)
        def _():
            for copy in self.cross:
                copy.wait_send()


class RowGather:
    def __init__(self, place, links, src, dst):
        self.place = place
        pairs = range(1, place.pairs)

        def slot():
            return dst.at[place.pair, place.core]

        self.stay = links.local(lambda: (src, slot()))
        self.to_home = links.far(lambda: (src, slot(), place.at(core=1)))
        self.to_near = links.far(lambda: (src, slot(), place.at(top=1)))
        self.to_far = links.far(lambda: (src, slot(), place.at(top=1, core=1)))

        def forward(c, p):
            return links.far(
                lambda: (dst.at[place.pair, c], dst.at[place.pair, c], place.at(pair=p))
            )

        self.forwards = [forward(c, p) for c in (0, 1) for p in pairs]

    def begin(self):
        @pl.when(self.place.home)
        def _():
            self.stay.start()
            self.to_near.start()

        @pl.when(self.place.away)
        def _():
            self.to_home.start()
            self.to_far.start()

    def forward(self):
        @pl.when(self.place.home)
        def _():
            self.stay.wait()
            self.to_home.wait_recv()

        @pl.when(self.place.away)
        def _():
            self.to_near.wait_recv()
            self.to_far.wait_recv()

        for copy in self.forwards:
            copy.start()

    def finish(self):
        for copy in self.forwards:
            copy.wait()

        @pl.when(self.place.home)
        def _():
            self.to_near.wait_send()

        @pl.when(self.place.away)
        def _():
            self.to_home.wait_send()
            self.to_far.wait_send()


class Entry:
    def __init__(self, place, links, h_ref, zx_ref, tail_ref, seg_ref, h_v, w_v, seg_v):
        self.place = place
        cols = zx_ref.shape[-1]
        self.peers = peers = peers_of(place)
        others = range(1, place.pairs)
        self.tokens = TokenGather(place, links, h_ref, h_v)

        def block(t=0, l=0, c=0):
            s, f = place.at(top=t, low=l, core=c)
            return w_v.at[s, place.pair, lax.rem(f, 2)]

        direct = len(zx_ref.shape) == 2
        if direct:
            cols = w_v.shape[4] - TAIL
        width = cols // 2

        def source(group, part):
            if direct:
                return zx_ref.at[:, pl.ds(pl.multiple_of(part * INNER + group * width, LANES), width)]
            return zx_ref.at[group]

        def columns(ref, part):
            if direct:
                return ref.at[:, pl.ds(part * width, width)]
            return ref.at[:, pl.ds(0, cols)]

        def tail_of(ref):
            return ref.at[:, pl.ds(cols, TAIL)]

        def send_zx(part, t, l, c):
            group = flip(place.core, c) * place.half + flip(place.low, l)
            return source(group, part), columns(block(), part), place.at(top=t, low=l, core=c)

        def keep_zx(part):
            return links.local(lambda: (source(place.chunk, part), columns(block(), part)))

        parts = (0, 1) if direct else (0,)
        self.zx = {
            p: Copies([links.far(functools.partial(send_zx, part, *p)) for part in parts])
            for p in peers
        }
        self.own = [keep_zx(part) for part in parts] + [
            links.local(lambda: (tail_ref, tail_of(block())))
        ]
        self.tail_cross = links.far(lambda: (tail_ref, tail_of(block()), place.at(top=1)))
        self.near_peers = [(l, c) for t, l, c in peers if t == 0]

        def send_tail(l, c):
            return tail_ref, tail_of(block()), place.at(low=l, core=c)

        def send_other(l, c):
            return tail_of(block(1)), tail_of(block(1)), place.at(low=l, core=c)

        self.tails = {p: links.far(functools.partial(send_tail, *p)) for p in self.near_peers}
        self.tails_more = {
            p: links.far(functools.partial(send_other, *p)) for p in self.near_peers
        }
        self.seg_send = links.far(lambda: (seg_ref, seg_v, place.at(core=1)))
        self.seg_keep = links.local(lambda: (seg_ref, seg_v))

        def send_on(t, l, c, p):
            return block(t, l, c), block(t, l, c), place.at(pair=p)

        self.forwards = {
            p: [links.far(functools.partial(send_on, *p, other)) for other in others]
            for p in [(0, 0, 0)] + peers
        }

    def run(self, then):
        tokens, zx, forwards = self.tokens, self.zx, self.forwards
        stages = len(self.place.low_bits)
        far_peers = [p for p in self.peers if p[0] == 1]
        tokens.begin()
        self.tail_cross.start()
        for copy in self.own:
            copy.start()
        for p in self.near_peers:
            zx[0, *p].start()
            self.tails[p].start()

        @pl.when(self.place.home)
        def _():
            self.seg_send.start()
            self.seg_keep.start()

        for copy in self.own:
            copy.wait()
        for copy in forwards[0, 0, 0]:
            copy.start()
        self.tail_cross.wait_recv()
        for p in self.near_peers:
            self.tails_more[p].start()
        tokens.pass_on(0, "home")
        for p in self.near_peers:
            zx[0, *p].wait_recv()
            self.tails[p].wait_recv()
            for copy in forwards[0, *p]:
                copy.start()
        for p in far_peers:
            zx[p].start()
        for i in range(1, stages):
            tokens.pass_on(i, "home")
        tokens.arrive()
        for p in self.near_peers:
            self.tails_more[p].wait_recv()
        for i in range(stages):
            tokens.pass_on(i, "away")
            at, to = (len(far_peers) * k // stages for k in (i, i + 1))
            for p in far_peers[at:to]:
                zx[p].wait_recv()
                for copy in forwards[p]:
                    copy.start()
        then()

        @pl.when(self.place.home)
        def _():
            self.seg_keep.wait()
            self.seg_send.wait_send()

        @pl.when(self.place.away)
        def _():
            self.seg_send.wait_recv()

        tokens.finish()
        for p in forwards:
            for copy in forwards[p]:
                copy.wait()

    def finish(self):
        self.tail_cross.wait_send()
        for group in (self.zx, self.tails, self.tails_more):
            for copy in group.values():
                copy.wait_send()


def add_rows(out, left, right, rows=32):
    total = left.shape[0]
    step = next((size for size in (rows, 16) if total % size == 0), total)

    if step == total:
        out[...] = left[...] + right[...]
        return

    @pl.loop(0, total // step)
    def _(i):
        at = pl.ds(pl.multiple_of(i * step, step), step)
        out[at] = left[at] + right[at]


class TokenScatter:
    def __init__(self, place, links, src, out, own, first, later, held):
        self.place = place
        self.out, self.own, self.first, self.later = out, own, first, later
        self.seqs = own.shape[0]
        half = place.half
        self.loads = []
        if held == "sums":
            self.loads = [links.local(lambda: (src, own))]
        if held == "halves":
            self.loads = [
                links.local(lambda: (src[0], own)), links.local(lambda: (src[1], first)),
            ]
        self.stages = [[] for _ in place.low_bits]
        for q in range(self.seqs):
            live, slot = list(range(half)), 0
            for i, bit in enumerate(place.bits_for(q)[::-1]):
                for low in [low for low in live if low & bit]:
                    self.stages[i].append((self.copy(links, q, low, slot, bit), q, low ^ bit, slot))
                    slot += 1
                live = [low for low in live if not low & bit]
        self.stay = links.local(lambda: (own.at[:, place.low], out))

    def copy(self, links, q, low, slot, bit):
        return links.far(
            lambda: (
                self.own.at[q, flip(self.place.low, low)], self.later.at[q, slot],
                self.place.at(low=bit),
            )
        )

    def begin(self):
        for copy in self.loads:
            copy.start()

    def add_cores(self):
        for copy in self.loads:
            copy.wait()
        for q in range(self.seqs if self.first is not None else 0):
            for low in range(self.place.half):
                add_rows(self.own.at[q, low], self.own.at[q, low], self.first.at[q, low])

    def send_stage(self, i):
        for copy, _, _, _ in self.stages[i]:
            copy.start()

    def add_stage(self, i):
        for copy, q, low, slot in self.stages[i]:
            copy.wait_recv()
            ref = self.own.at[q, flip(self.place.low, low)]
            add_rows(ref, ref, self.later.at[q, slot])

    def store(self):
        self.stay.start()
        self.stay.wait()

    def finish(self):
        for stage in self.stages:
            for copy, _, _, _ in stage:
                copy.wait_send()


class RowScatter:
    def __init__(self, place, links, src, out, own, first):
        self.place, self.own, self.first = place, own, first

        def over(p):
            return links.far(
                lambda: (src.at[flip(place.pair, p)], first.at[p - 1], place.at(pair=p))
            )

        def far(c):
            return links.far(
                lambda: (own.at[flip(place.core, c)], out.at[1], place.at(top=1, core=c))
            )

        self.over = [over(p) for p in range(1, place.pairs)]
        self.load = links.local(lambda: (src.at[place.pair], own))
        self.far = [far(0), far(1)]
        self.near = links.far(lambda: (own.at[1 - place.core], out.at[0], place.at(core=1)))
        self.stay = links.local(lambda: (own.at[place.core], out.at[0]))

    def begin(self):
        self.load.start()
        for copy in self.over:
            copy.start()

    def add_pairs(self):
        self.load.wait()
        for i, copy in enumerate(self.over):
            copy.wait_recv()
            for c in (0, 1):
                add_rows(self.own.at[c], self.own.at[c], self.first.at[i, c])

        @pl.when(self.place.away)
        def _():
            for copy in self.far:
                copy.start()

        @pl.when(self.place.home)
        def _():
            self.near.start()
            self.stay.start()

    def finish(self):
        for copy in self.over:
            copy.wait_send()

        @pl.when(self.place.home)
        def _():
            self.stay.wait()
            self.near.wait_send()
            self.far[0].wait_recv()

        @pl.when(self.place.away)
        def _():
            self.near.wait_recv()
            self.far[1].wait_recv()
            for copy in self.far:
                copy.wait_send()


class PartScatter:
    def __init__(self, place, links, src, own, first, other, slots, tiles):
        self.place, self.own, self.first, self.other = place, own, first, other
        self.high = high = place.half // tiles
        pairs = range(1, place.pairs)

        def rows(top, k):
            return pl.ds(place.half * flip(place.top, top) + k * high, high)

        def over(top, k, p):
            return links.far(
                lambda: (
                    src.at[rows(top, k), flip(place.pair, p)], first.at[p - 1, rows(top, k)],
                    place.at(pair=p),
                )
            )

        def cross(i, c):
            def make():
                at = place.half * flip(place.top, 1) + i
                return own(at, c), other.at[i, c], place.at(top=1)

            return links.far(make)

        def spread(l, c):
            return links.far(
                lambda: (
                    self.block(l, c), slots.at[place.core, place.low], place.at(low=l, core=c)
                )
            )

        self.over = [[[over(top, k, p) for p in pairs] for k in range(tiles)] for top in (0, 1)]
        self.cross = [
            [cross(k * high + i, c) for i in range(high) for c in (0, 1)] for k in range(tiles)
        ]
        self.near = [(l, c) for t, l, c in peers_of(place) if t == 0]
        self.slots = {p: spread(*p) for p in self.near}
        self.slots[0, 0] = links.local(
            lambda: (self.block(0, 0), slots.at[place.core, place.low])
        )

    def block(self, l, c):
        place = self.place
        return self.own(place.half * place.top + flip(place.low, l), flip(place.core, c))

    def send_pairs(self, top, k):
        for copy in self.over[top][k]:
            copy.start()

    def add_pairs(self, top, k):
        for i, copy in enumerate(self.over[top][k]):
            copy.wait_recv()
            for low in range(self.high):
                for c in (0, 1):
                    at = self.place.half * flip(self.place.top, top) + k * self.high + low
                    ref = self.own(at, c)
                    add_rows(ref, ref, self.first.at[i, at, c], 16)

    def send_cross(self, k):
        for copy in self.cross[k]:
            copy.start()

    def wait_cross(self, k):
        for copy in self.cross[k]:
            copy.wait_recv()

    def spread(self, waits=True):
        if waits:
            for k in range(len(self.cross)):
                self.wait_cross(k)
        place = self.place
        for l, c in self.near + [(0, 0)]:
            ref = self.block(l, c)
            add_rows(ref, ref, self.other.at[flip(place.low, l), flip(place.core, c)], 16)
            self.slots[l, c].start()

    def finish(self):
        for copy in self.slots.values():
            copy.wait()
        for copies in self.cross + [c for top in self.over for c in top]:
            for copy in copies:
                copy.wait_send()


class Deliver:
    def __init__(self, place, links, src, out):
        self.place = place
        self.cross = links.far(lambda: (src(), out, place.at(top=1, core=1)))
        self.stay = links.local(lambda: (src(), out))

    def begin(self):
        @pl.when(self.place.away)
        def _():
            self.cross.start()

        @pl.when(self.place.home)
        def _():
            self.stay.start()

    def finish(self):
        @pl.when(self.place.away)
        def _():
            self.cross.wait()

        @pl.when(self.place.home)
        def _():
            self.stay.wait()


def exit_kernel(
    seq, fsdp,
    h_ref, dh_ref, grad_ref, w_ref, mixed_ref, gain_in_ref, gain_out_ref, gx_ref, gt_ref, gh_ref,
    dh_out, mixed_out, slots_out, vec_out,
    h_all, grads, weights, part, dh_own, dh_later, part_first, part_top, vec_val, vec_got,
    send, recv, near,
):
    place = Place(seq, fsdp)
    links = Links(send, recv, near)
    half = place.half
    others = list(range(1, place.pairs))
    seqs, _, length, depth = dh_own.shape
    rows = part.shape[3]
    width = weights.shape[1] - grads.shape[1]
    dh = TokenScatter(
        place, links, dh_ref, dh_out, dh_own, None, dh_later, "sums"
    )
    dh_last = Deliver(place, links, lambda: dh_own.at[:, place.low], dh_out)
    mixed = Deliver(place, links, lambda: mixed_ref, mixed_out)
    loads = [
        links.local(lambda: (h_ref, h_all)),
        links.local(lambda: (grad_ref, grads)),
        links.local(lambda: (w_ref, weights)),
    ]

    tiles = depth // 2 // TILE
    rest = PartScatter(
        place, links, part, lambda s, c: part.at[s, place.pair, c], part_first, part_top, slots_out,
        tiles,
    )

    hops = [dict(pair=1 << i) for i in range(place.pairs.bit_length() - 1)] + [dict(top=1)]

    def hop(i):
        return links.far(lambda: (vec_val.at[i], vec_got.at[i], place.at(**hops[i])))

    def share(l, c):
        return links.far(
            lambda: (
                vec_val.at[len(hops)], vec_out.at[place.core, place.low],
                place.at(low=l, core=c),
            )
        )

    vec = [hop(i) for i in range(len(hops))]
    vec_shares = [share(l, c) for t, l, c in peers_of(place) if t == 0]
    vec_shares.append(
        links.local(lambda: (vec_val.at[len(hops)], vec_out.at[place.core, place.low]))
    )

    def vec_next(i):
        vec[i].wait_recv()
        vec_val[i + 1] = vec_val[i] + vec_got[i]
        for copy in vec[i + 1 : i + 2] if i + 1 < len(hops) else vec_shares:
            copy.start()

    blocks = TILE // rows

    def weight_rows(top, k):
        t = tiles * flip(place.top, top) + k
        lanes = pl.ds(pl.multiple_of(t * TILE, LANES), TILE)
        term = tr_mm(h_all[:, lanes], grads[...])
        for b in range(blocks):
            at = t * (blocks // fsdp) + b // fsdp
            part[at, b % fsdp // 2, b % 2] = term[b * rows : (b + 1) * rows].astype(BF16)
        sums = jnp.sum(term * weights[lanes, width:].astype(F32), axis=1, keepdims=True)
        wide = jnp.broadcast_to(sums, (TILE, LANES))
        for i in range(TILE // LANES):
            row = pl.ds(t * (TILE // LANES) + i, 1)
            vec_val[0, row, :] = gain_in_ref[row, :] + wide[i * LANES : (i + 1) * LANES].T[0:1, :]
        rest.send_pairs(top, k)

    def place_sums():
        at, group, _ = sum_rows(width)
        vec_val[0] = jnp.zeros_like(vec_val[0])
        for tap in range(KERNEL + 1):
            for j in range(2 * STATE // LANES):
                vec_val[0, at : at + 1, :] = gt_ref[
                    tap : tap + 1, j * LANES : (j + 1) * LANES
                ]
                at += 1
        pieces_of = [
            ref[line : line + 1, j * LANES : (j + 1) * LANES]
            for ref, line in [(gx_ref, i) for i in range(KERNEL + 2)] + [(gain_out_ref, 0)]
            for j in range(lane_rows(width))
        ] + [gh_ref[0:1, :], gh_ref[1:2, :]]
        for i, piece in enumerate(pieces_of):
            vec_val[0, group + i : group + i + 1, :] = piece

    dh.begin()
    for copy in loads:
        copy.start()
    meet_pair(place)
    dh.add_cores()
    dh.send_stage(0)
    mixed.begin()
    place_sums()
    for copy in loads:
        copy.wait()
    for k in range(tiles):
        weight_rows(1, k)
    for k in range(tiles):
        weight_rows(0, k)
    vec[0].start()
    for k in range(tiles):
        rest.add_pairs(1, k)
        rest.send_cross(k)
    stages = len(place.low_bits)
    for i in range(stages):
        dh.add_stage(i)
        if i + 1 < stages:
            dh.send_stage(i + 1)
        else:
            dh_last.begin()
        if i < len(hops):
            vec_next(i)
    for i in range(stages, len(hops)):
        vec_next(i)
    for k in range(tiles):
        rest.add_pairs(0, k)
    rest.spread()
    for copy in vec_shares:
        copy.wait()
    rest.finish()
    mixed.finish()
    dh_last.finish()
    dh.finish()
    for copy in vec:
        copy.wait_send()


def exit_scatter(seq, fsdp, h_all, grad_h, grad_proj, w_mine, mixed, sums):
    seqs, _, length, depth = h_all.shape
    half, pairs = seq // 2, fsdp // 2
    cols = w_mine.shape[1]
    rest = grad_proj.shape[3]
    width = cols - rest
    rows = depth // (seq * fsdp)
    count = seqs * seq * length
    vector = (sum_rows(width)[2], LANES)
    hops = pairs.bit_length()
    token_own = pltpu.VMEM((seqs, half, length, depth), BF16)
    tokens = jax.ShapeDtypeStruct((seqs, length, depth), BF16)
    return pl.pallas_call(
        functools.partial(exit_kernel, seq, fsdp),
        in_specs=[ANYWHERE] * 5 + [pl.BlockSpec(memory_space=pltpu.VMEM)] * 5,
        out_specs=[ANYWHERE] * 4,
        out_shape=[
            tokens,
            tokens,
            jax.ShapeDtypeStruct((2, half, rows, rest), BF16),
            jax.ShapeDtypeStruct((2, half) + vector, F32),
        ],
        scratch_shapes=[
            pltpu.VMEM((count, depth), BF16),
            pltpu.VMEM((count, rest), BF16),
            pltpu.VMEM((depth, cols), BF16),
            pltpu.VMEM((seq, pairs, 2, rows, rest), BF16),
            token_own,
            pltpu.VMEM((seqs, max(half - 1, 1), length, depth), BF16),
            pltpu.VMEM((max(pairs - 1, 1), seq, 2, rows, rest), BF16),
            pltpu.VMEM((half, 2, rows, rest), BF16),
            pltpu.VMEM((hops + 1,) + vector, F32),
            pltpu.VMEM((hops,) + vector, F32),
            pltpu.SemaphoreType.DMA((96,)),
            pltpu.SemaphoreType.DMA((96,)),
            pltpu.SemaphoreType.DMA((16,)),
        ],
        compiler_params=pltpu.CompilerParams(
            collective_id=1, has_side_effects=True, vmem_limit_bytes=60 << 20
        ),
        cost_estimate=pl.CostEstimate(
            flops=0, transcendentals=0, bytes_accessed=200_000_000
        ),
        name="exit_scatter",
    )(
        h_all.reshape(count, depth), grad_h, grad_proj.reshape(count, rest), w_mine, mixed, *sums
    )


def finish_kernel(
    seq,
    tok_in, cot_in, gain_ref, dh_in, mixed_in, slots_z_in, slots_in, rows_in, vec_in,
    mixed_out, tokens_out, gain_in_out, w_in_out, conv_w_out, conv_b_out, heads_out, gain_out_out,
    w_out_out,
    tok_ref, cot_ref, dh_ref, mixed_ref, slots_z_ref, slots_ref, rows_ref, vec_ref, near,
):
    pairs = [
        (slots_z_in, slots_z_ref), (slots_in, slots_ref), (rows_in, rows_ref), (vec_in, vec_ref),
        (tok_in, tok_ref), (dh_in, dh_ref), (mixed_in, mixed_ref), (cot_in, cot_ref),
    ]
    loads = [pltpu.make_async_copy(*pair, near.at[i]) for i, pair in enumerate(pairs)]
    for copy in loads:
        copy.start()
    gain = gain_ref[...]
    for copy in loads[:4]:
        copy.wait()
    groups, _, cols = slots_ref.shape
    width = cols - TAIL
    tail = jnp.zeros((slots_ref.shape[1], TAIL), F32)
    for g in range(groups):
        w_in_out[:, g * width : (g + 1) * width] = slots_z_ref[g].astype(F32)
        w_in_out[:, INNER + g * width : INNER + (g + 1) * width] = (
            slots_ref[g, :, :width].astype(F32)
        )
        tail = tail + slots_ref[g, :, width:].astype(F32)
    w_in_out[:, 2 * INNER :] = tail[:, : 2 * STATE + HEADS]
    w_out_out[...] = rows_ref[0].astype(F32) + rows_ref[1].astype(F32)

    row, group, _ = sum_rows(width)
    heads = HEADS // seq
    common = vec_ref[0, :group]
    for g in range(1, groups):
        common = common + vec_ref[g, :group]
    for j in range(D // LANES):
        at = slice(j * LANES, (j + 1) * LANES)
        gain_in_out[:, at] = common[j : j + 1] / gain_ref[:, at]
    targets = [conv_w_out.at[k : k + 1] for k in range(KERNEL)] + [conv_b_out]
    for out in targets:
        for j in range(2 * STATE // LANES):
            out[:, INNER + j * LANES : INNER + (j + 1) * LANES] = common[row : row + 1]
            row += 1
    across = lane_rows(width)
    lane = iota((8, LANES), 1)
    per_head = jnp.zeros((8, LANES), F32)
    fold = expander(across * LANES)
    for g in range(groups):
        def lanes_of(line):
            first = group + line * across
            return jnp.concatenate(
                [vec_ref[g, first + j : first + j + 1, :] for j in range(across)], axis=1
            )

        at = slice(g * width, (g + 1) * width)
        for line, out in enumerate(targets):
            out[:, at] = lanes_of(line)[:, :width]
        gain_out_out[:, at] = lanes_of(KERNEL + 2)[:, :width]
        skip = mm_ones_tr(jnp.broadcast_to(lanes_of(KERNEL + 1), (8, across * LANES)), fold, 3)
        last = group + (KERNEL + 3) * across
        lines = jnp.concatenate(
            [skip[0:1, :], vec_ref[g, last : last + 2, :], jnp.zeros((5, LANES), F32)], axis=0
        )
        lines = jnp.where(lane < heads, lines, 0.0)
        per_head = per_head + (pltpu.roll(lines, g * heads, 1) if g else lines)
    heads_out[...] = per_head
    for copy in loads[4:]:
        copy.wait()
    for q in range(tok_ref.shape[0]):
        wide = tok_ref[q].astype(F32)
        mixed_out[q] = (wide + mixed_ref[q].astype(F32)).astype(BF16)
        scale = lax.rsqrt(jnp.mean(wide * wide, axis=-1, keepdims=True) + EPSILON)
        unit = wide * scale
        scaled = dh_ref[q].astype(F32) * gain
        tokens_out[q] = cot_ref[q].astype(F32) + scale * (
            scaled - unit * jnp.mean(scaled * unit, axis=-1, keepdims=True)
        )


def finish(seq, tokens, cotangent, gain_in, grad_h, mixed, slots_z, slots, rows, vector, shapes):
    columns = INNER + 2 * STATE
    kinds = [
        (tokens.shape, BF16), (tokens.shape, F32), ((1, D), F32), (shapes[0], F32),
        ((KERNEL, columns), F32), ((1, columns), F32), ((8, LANES), F32), ((1, INNER), F32),
        (shapes[1], F32),
    ]
    arrays = (tokens, cotangent, grad_h, mixed, slots_z, slots, rows, vector)
    return pl.pallas_call(
        functools.partial(finish_kernel, seq),
        in_specs=[IN_HBM] * 2 + [pl.BlockSpec(memory_space=pltpu.VMEM)] + [IN_HBM] * 6,
        scratch_shapes=[pltpu.VMEM(v.shape, v.dtype) for v in arrays]
        + [pltpu.SemaphoreType.DMA((len(arrays),))],
        out_shape=[jax.ShapeDtypeStruct(*kind) for kind in kinds],
        compiler_params=pltpu.CompilerParams(vmem_limit_bytes=62 << 20),
        name="finish",
    )(tokens, cotangent, gain_in[None], grad_h, mixed, slots_z, slots, rows, vector)


def local(
    tokens, segments, gain_in, w_in, conv_w, conv_b, dt_bias, a_log, skip, gain_out, w_out,
    cotangent,
):
    steps, shards = lax.axis_size("seq"), lax.axis_size("fsdp")
    place = Place(steps, shards)
    seqs, length, _ = tokens.shape
    width = INNER // steps
    rows_in = w_in.shape[0]

    wide = tokens.astype(F32)
    scale_in = lax.rsqrt(jnp.mean(wide * wide, axis=-1, keepdims=True) + EPSILON)
    normed = (wide * scale_in * gain_in).astype(BF16)
    zx = w_in
    if width % LANES:
        zx = w_in[:, : 2 * INNER].reshape(rows_in, 2, steps, width).transpose(2, 0, 1, 3)
        zx = zx.reshape(steps, rows_in, 2 * width)
    tail = jnp.pad(w_in[:, 2 * INNER :], ((0, 0), (0, LANES - HEADS)))
    columns = INNER + 2 * STATE

    def line(*arrays):
        arrays = [jnp.pad(v, (0, -v.shape[0] % LANES)) for v in arrays]
        return jnp.pad(jnp.concatenate(arrays), (0, columns - sum(v.shape[0] for v in arrays)))

    packed = jnp.concatenate(
        [
            conv_w,
            jnp.stack(
                [conv_b, line(gain_out), line(dt_bias, a_log, skip), jnp.zeros((columns,), F32)]
            ),
        ]
    )
    (
        proj, states, off_col, rem_col, off_row, h_all, w_mine, dz, dy, stats, mixed, part_out,
        part_z, gains, consts,
    ) = forward_mix(normed, zx, tail, segments, cotangent, w_out, packed, steps, shards)
    grad_proj, sums_x, sums_t, sums_h, mixed, rows, slots_z, grad_h = backward_mix(
        proj, off_col, off_row, rem_col, dy, dz, w_mine, stats, states, mixed,
        part_out, part_z, packed, consts, steps, shards,
    )
    grad_h, mixed, slots, vector = exit_scatter(
        steps, shards, h_all, grad_h, grad_proj, w_mine, mixed, gains + (sums_x, sums_t, sums_h)
    )
    (
        mixed, tokens_grad, gain_in_grad, w_in_grad, conv_w_grad, conv_b_grad, per_head,
        gain_out_grad, w_out_grad,
    ) = finish(
        steps, tokens, cotangent, gain_in, grad_h, mixed,
        slots_z.reshape(steps, rows_in, width), slots.reshape(steps, rows_in, width + TAIL), rows,
        vector.reshape((steps,) + vector.shape[2:]), (w_in.shape, w_out.shape),
    )
    return (
        mixed, tokens_grad, gain_in_grad[0], w_in_grad, conv_w_grad, conv_b_grad[0],
        per_head[1, :HEADS], per_head[2, :HEADS], per_head[0, :HEADS], gain_out_grad[0],
        w_out_grad,
    )


def solution(mesh):
    by_token = P("fsdp", "seq", None)
    by_row = P(("seq", "fsdp"), None)
    placed = (
        by_token, P("fsdp", None), P(), by_row, P(), P(), P(), P(), P(), P(), by_row, by_token,
    )
    return jax.shard_map(
        local,
        mesh=mesh,
        in_specs=placed,
        out_specs=(by_token, by_token, P(), by_row, P(), P(), P(), P(), P(), P(), by_row),
        check_vma=False,
    )
```

```python
import functools

import jax
import jax.numpy as jnp
import numpy as np
from jax import lax
from jax.experimental import pallas as pl
from jax.experimental.pallas import tpu as pltpu
from jax.sharding import PartitionSpec as P

D = 1536
HEADS = 48
HEAD_DIM = 64
STATE = 128
KERNEL = 4
INNER = 3072
LANES = 128
HALO = 16
EPSILON = 1e-05
TILE = 384
F32 = jnp.float32
BF16 = jnp.bfloat16


def mm(a, b):
    return jnp.dot(a.astype(BF16), b.astype(BF16), preferred_element_type=F32)


def mm_tr(a, b):
    return lax.dot_general(
        a.astype(BF16), b.astype(BF16), (((1,), (1,)), ((), ())), preferred_element_type=F32
    )


def tr_mm(a, b):
    return lax.dot_general(
        a.astype(BF16), b.astype(BF16), (((0,), (0,)), ((), ())), preferred_element_type=F32
    )


def pieces(a, count):
    out = []
    for _ in range(count - 1):
        part = a.astype(BF16)
        out.append(part)
        a = a - part.astype(F32)
    out.append(a.astype(BF16))
    return out


def ones_mm(ones, a, count):
    return sum(jnp.dot(ones, part, preferred_element_type=F32) for part in pieces(a, count))


def mm_ones(a, ones, count):
    return sum(jnp.dot(part, ones, preferred_element_type=F32) for part in pieces(a, count))


def mm_ones_tr(a, ones, count):
    return sum(
        lax.dot_general(part, ones, (((1,), (1,)), ((), ())), preferred_element_type=F32)
        for part in pieces(a, count)
    )


def iota(shape, dim):
    return lax.broadcasted_iota(jnp.int32, shape, dim)


def softplus(v):
    return jnp.maximum(v, 0.0) + jnp.log1p(jnp.exp(-jnp.abs(v)))


def sigmoid(v):
    return 1.0 / (1.0 + jnp.exp(-v))


def causal_conv(ext, current, halo, weight, bias, offset):
    length = current.shape[0]
    ext[0:HALO, :] = halo
    ext[HALO : HALO + length, :] = current
    total = bias + weight[KERNEL - 1 : KERNEL, :] * current
    for back in range(1, KERNEL):
        shifted = jnp.where(offset >= back, ext[pl.ds(HALO - back, length), :], 0.0)
        total = total + weight[KERNEL - 1 - back : KERNEL - back, :] * shifted
    return total


def head_tiles(width):
    out = []
    for start in range(0, width, LANES):
        size = min(LANES, width - start)
        heads = [start // HEAD_DIM + i for i in range(size // HEAD_DIM)]
        out.append((start, size, heads))
    return out


def masked_heads(tile, heads):
    if len(heads) == 1:
        return tile
    lane = iota(tile.shape, 1) // HEAD_DIM
    return jnp.concatenate(
        [jnp.where(lane == i, tile, jnp.zeros_like(tile)) for i in range(len(heads))], axis=0
    )


def expander(width):
    return (iota((LANES, width), 1) // HEAD_DIM == iota((LANES, width), 0)).astype(BF16)


def chunk_common(x, xh, tail, tailh, offset, params, ext_x, ext_t, width):
    wx, bx, wt, bt, heads_p, pick = params
    length = x.shape[0]
    conv_x = causal_conv(ext_x, x.astype(F32), xh.astype(F32), wx, bx, offset)
    conv_t = causal_conv(
        ext_t,
        tail[:, : 2 * STATE].astype(F32),
        tailh[:, : 2 * STATE].astype(F32),
        wt,
        bt,
        offset,
    )
    raw = jnp.dot(tail[:, 2 * STATE :], pick, preferred_element_type=F32) + heads_p[0:1, :]
    step = softplus(raw)
    decay_rate = jnp.exp(heads_p[1:2, :])
    rate = -step * decay_rate
    tril = (iota((length, length), 0) >= iota((length, length), 1)).astype(BF16)
    cumul = ones_mm(tril, rate, 3)
    spread = expander(width)
    row = iota((length, 1), 0)
    entry = jnp.where(offset > row.astype(F32), jnp.exp(cumul), 0.0)
    last_off = offset[length - 1 : length, :]
    same_last = row.astype(F32) >= (length - 1) - last_off
    to_end = jnp.where(same_last, jnp.exp(cumul[length - 1 : length, :] - cumul), 0.0)
    step_x = mm_ones(step, spread, 2)
    entry_x = mm_ones(entry, spread, 2)
    end_x = mm_ones(to_end, spread, 2)
    return conv_x, conv_t, raw, step, rate, decay_rate, cumul, spread, step_x, entry_x, end_x


def positions(segments, chunk, length):
    here = jnp.zeros((1, length), F32)
    total = segments.shape[1] // length
    rows = [segments[:, i * length : (i + 1) * length].astype(F32) for i in range(total)]
    for i in range(total):
        here = here + jnp.where(chunk == i, rows[i], 0.0)
    own = jnp.broadcast_to(here, (length, length)).T
    less = jnp.zeros((length, length), F32)
    upto = jnp.zeros((length, length), F32)
    for row in rows:
        less = less + jnp.where(row < own, 1.0, 0.0)
        upto = upto + jnp.where(row <= own, 1.0, 0.0)
    index = (chunk * length + iota((length, 1), 0)).astype(F32)
    offset = index - jnp.sum(less, axis=1, keepdims=True)
    return offset, jnp.sum(upto, axis=1, keepdims=True) - 1.0 - index


def flat_rows(ref, flat):
    rows, cols = ref.shape[-2:]
    if rows % HALO == 0:
        return ref[...].reshape(-1, cols)
    shape = ref.shape[:-2]
    for i, at in enumerate(np.ndindex(*shape)):
        flat[i * rows : (i + 1) * rows, :] = ref[at]
    return flat[...]


def pick_params(place, pack_ref, cx_ref, hp_ref, pick_ref):
    width = cx_ref.shape[1]
    heads = width // HEAD_DIM
    mine = jnp.zeros((8, width), F32)
    for g in range(INNER // width):
        mine = mine + jnp.where(place.chunk == g, pack_ref[:, g * width : (g + 1) * width], 0.0)
    lane, source = iota((LANES, LANES), 1), iota((LANES, LANES), 0)
    pick = ((lane < heads) & (source == lane + place.chunk * heads)).astype(BF16)
    pick_ref[...] = pick
    lines = [pack_ref[6:7, i * LANES : (i + 1) * LANES] for i in range(3)]
    lines = jnp.concatenate(lines + [jnp.zeros((5, LANES), F32)], axis=0)
    lines = mm_ones(lines, pick, 3)
    hp_ref[...] = lines
    cx_ref[...] = mine
    cx_ref[6:7, :] = mm_ones(lines, expander(width), 3)[2:3, :]


def forward_kernel(
    seq, fsdp,
    h_ref, zx_ref, tail_ref, seg_ref, cot_ref, ow_ref,
    pack_ref,
    proj_ref, state_ref, off_ref, rem_ref, offr_ref,
    h_out, w_out, dz_out, dy_out, stat_out, mixed_out, mixed_got, pout_out, pz_out, gain_out_ref, gain_in_ref,
    cx_ref, hp_ref, pick_ref,
    h_v, w_v, w_flat, seg_v, cot_v, ow_v, ow_flat, gated_v, sums_v, sums_got, grad_v, z_v, y_v,
    mix_give, mix_own, pout_v, pz_v, memory, ext_x, ext_t, last_rows, send, recv, near,
):
    seqs, _, length, depth = h_v.shape
    width = cx_ref.shape[1]
    step_at = pl.program_id(0)
    place = Place(seq, fsdp)
    links = Links(send, recv, near)
    peers = peers_of(place)
    near_peers = [(l, c) for t, l, c in peers if t == 0]
    entry = Entry(place, links, h_ref, zx_ref, tail_ref, seg_ref, h_v, w_v, seg_v)
    cot = TokenGather(place, links, cot_ref, cot_v)
    w_rows = RowGather(place, links, ow_ref, ow_v)
    keep = [links.local(lambda: (h_v, h_out)), links.local(lambda: (w_v, w_out))]
    stages = len(place.low_bits)

    def send_sums(i):
        l, c = near_peers[i]
        return links.far(lambda: (sums_v, sums_got.at[i], place.at(low=l, core=c)))

    sums = [send_sums(i) for i in range(len(near_peers))]

    def send_core(q):
        return links.far(lambda: (mix_give.at[q], mixed_got.at[q], place.at(core=1)))

    cores = [send_core(q) for q in range(seqs)]

    @pl.when(step_at == 0)
    def _():
        memory[...] = jnp.zeros_like(memory)
        last_rows[...] = jnp.zeros_like(last_rows)
        pick_params(place, pack_ref, cx_ref, hp_ref, pick_ref)
        meet_pair(place)
        entry.run(cot.cross_over)
        if w_v.shape[-2] % HALO:
            flat_rows(w_v, w_flat)

    @pl.when(step_at == 1)
    def _():
        for copy in keep:
            copy.start()
        cot.begin_home()
        w_rows.begin()

    for i in range(stages):

        @pl.when(step_at == min(3 + 2 * i, seq - 1))
        def _():
            cot.pass_on(i, "home")

    @pl.when(step_at == 2)
    def _():
        cot.arrive()

    for i in range(stages):

        @pl.when(step_at == min(4 + 2 * i, seq - 1))
        def _():
            cot.pass_on(i, "away")

    @pl.when(step_at == seq - 3)
    def _():
        w_rows.forward()

    @pl.when(step_at < seq)
    def _():
        weights = flat_rows(w_v, w_flat) if w_v.shape[-2] % HALO == 0 else w_flat[...]
        proj = jnp.dot(
            h_v[:, step_at].reshape(seqs * length, depth), weights, preferred_element_type=F32
        ).astype(BF16)
        proj_ref[...] = proj.reshape(proj_ref.shape)
        params = (
            cx_ref[:KERNEL, :], cx_ref[KERNEL : KERNEL + 1, :],
            pack_ref[:KERNEL, INNER:], pack_ref[KERNEL : KERNEL + 1, INNER:],
            hp_ref[...], pick_ref[...],
        )
        gain_row, skip_row = cx_ref[KERNEL + 1 : KERNEL + 2, :], cx_ref[KERNEL + 2 : KERNEL + 3, :]
        for q in range(seqs):
            offset, remain = positions(seg_v[q : q + 1, :], step_at, length)
            off_ref[q, 0] = offset
            rem_ref[q, 0] = remain
            offr_ref[q, 0] = jnp.broadcast_to(offset, (length, LANES)).T[0:1, :]
            chunk_rows = proj[q * length : (q + 1) * length]
            zx, tail = chunk_rows[:, : 2 * width], chunk_rows[:, 2 * width :]
            earlier = last_rows[q]
            z_rows = zx[:, :width]
            here = pl.ds(pl.multiple_of((q * seq + step_at) * length, length), length)
            z_v[here, :] = z_rows
            conv_x, conv_t, _, _, _, _, cumul, _, step_x, entry_x, end_x = chunk_common(
                zx[:, width:], earlier[:, width : 2 * width], tail, earlier[:, 2 * width :], offset, params,
                ext_x.at[q], ext_t.at[q], width,
            )
            xs = conv_x * sigmoid(conv_x)
            act_t = conv_t * sigmoid(conv_t)
            bs = act_t[:, :STATE].astype(BF16)
            cs = act_t[:, STATE:].astype(BF16)
            scaled = xs * step_x
            scores = mm_tr(cs, bs)
            gap = iota((length, length), 0) - iota((length, length), 1)
            same = (gap >= 0) & (gap.astype(F32) <= offset)
            cumul_t = cumul.T
            old = memory[q]
            old_low = old.astype(BF16)
            state_ref[q, 0] = old_low
            outside = mm(cs, old_low) * entry_x + skip_row * xs
            squares = jnp.zeros((length, 1), F32)
            for start, size, heads in head_tiles(width):
                mixing = []
                for head in heads:
                    spans = cumul[:, head : head + 1] - cumul_t[head : head + 1, :]
                    decays = jnp.exp(jnp.where(same, spans, -1e30))
                    mixing.append((decays * scores).astype(BF16))
                tile = masked_heads(scaled[:, start : start + size].astype(BF16), heads)
                mix = mixing[0] if len(heads) == 1 else jnp.concatenate(mixing, axis=1)
                inside = jnp.dot(mix, tile, preferred_element_type=F32)
                y_low = (inside + outside[:, start : start + size]).astype(BF16)
                y_v[here, start : start + size] = y_low
                z = zx[:, start : start + size].astype(F32)
                gated = y_low.astype(F32) * (z * sigmoid(z))
                gated_v[here, start : start + size] = (
                    gated * gain_row[:, start : start + size]
                ).astype(BF16)
                squares = squares + jnp.sum(gated * gated, axis=1, keepdims=True)
            sums_v[pl.ds(2 * (q * seq + step_at), 1), :] = jnp.broadcast_to(
                squares, (length, LANES)
            ).T[0:1, :]
            fresh = tr_mm(bs, scaled * end_x)
            memory[q] = old * entry_x[length - 1 : length, :] + fresh
            last_rows[q] = chunk_rows[length - HALO :]

    @pl.when(step_at == seq)
    def _():
        w_rows.finish()
        cot.finish()
        rows_out = flat_rows(ow_v, ow_flat)
        tile = 2 * length
        tiles = seqs * seq // 2

        @pl.loop(0, tiles)
        def _(k):
            at = pl.ds(pl.multiple_of(k * tile, tile), tile)
            cots = cot_v[k // (seq // 2), pl.ds(lax.rem(k, seq // 2) * 2, 2)].reshape(tile, depth)
            grad = mm_tr(cots, rows_out)
            grad_v[at, :] = grad
            part = jnp.sum(grad * gated_v[at, :].astype(F32), axis=1, keepdims=True)
            part = jnp.broadcast_to(part, (tile, LANES))
            for i in (0, 1):
                sums_v[pl.ds(4 * k + 2 * i + 1, 1), :] = (
                    part[i * length : (i + 1) * length].T[0:1, :]
                )

        for copy in sums:
            copy.start()

        def mixed_rows(out, side):
            per_side = seq // 2 // 2
            for q in range(seqs):

                @pl.loop(0, per_side)
                def _(k):
                    at = (q * seq + seq // 2 * side + 2 * k) * length
                    rows = gated_v[pl.ds(pl.multiple_of(at, tile), tile), :]
                    mixed = jnp.dot(rows, rows_out, preferred_element_type=F32)
                    out[q, pl.ds(2 * k, 2)] = mixed.astype(BF16).reshape(2, length, depth)

        mixed_rows(mix_give, 1 - place.core)
        for copy in cores:
            copy.start()
        mixed_rows(mix_own, place.core)
        mixed_store = links.local(lambda: (mix_own, mixed_out))
        mixed_store.start()
        for copy in sums:
            copy.wait_recv()
        total = sums_v[...]
        for i in range(len(near_peers)):
            total = total + sums_got[i]
        is_square = lax.rem(iota(total.shape, 0), 2) == 0
        scale = lax.rsqrt(total / INNER + EPSILON)
        other = pltpu.roll(scale, 1, 0)
        stat_out[...] = jnp.where(is_square, scale, total * (other * other * other / INNER))

        gain_out_ref[...] = jnp.zeros_like(gain_out_ref)
        gain_row = cx_ref[KERNEL + 1 : KERNEL + 2, :]

        @pl.loop(0, tiles)
        def _(k):
            at = pl.ds(pl.multiple_of(k * tile, tile), tile)

            def column(line):
                rows = [
                    jnp.broadcast_to(stat_out[pl.ds(4 * k + 2 * i + line, 1), :], (LANES, length))
                    for i in (0, 1)
                ]
                return jnp.concatenate([row.T[:, 0:1] for row in rows], axis=0)

            scale, slope = column(0), column(1)
            gated_v[at, :] = (gated_v[at, :].astype(F32) * scale).astype(BF16)
            z = z_v[at, :].astype(F32)
            y = y_v[at, :].astype(F32)
            sig = sigmoid(z)
            silu_z = z * sig
            gated = y * silu_z
            scaled = grad_v[at, :] * scale
            gain_out_ref[0:1, :width] += jnp.sum(scaled * gated, axis=0, keepdims=True)
            grad_gated = gain_row * scaled - gated * slope
            y_v[at, :] = (grad_gated * silu_z).astype(BF16)
            z_v[at, :] = (grad_gated * y * (sig + silu_z * (1.0 - sig))).astype(BF16)

        dz_store = links.local(lambda: (z_v, dz_out))
        dy_store = links.local(lambda: (y_v, dy_out))
        dz_store.start()
        dy_store.start()

        rows_in = w_v.shape[3]
        blocks = TILE // rows_in
        high = blocks // fsdp
        h_flat = h_v[...].reshape(-1, depth)
        for t in range(depth // TILE):
            term = tr_mm(h_flat[:, t * TILE : (t + 1) * TILE], z_v[...])
            for i in range(blocks):
                pz_v[t * high + i // fsdp, i % fsdp // 2, i % 2] = term[
                    i * rows_in : (i + 1) * rows_in
                ].astype(BF16)
            if rows_in % HALO:
                some = w_flat[t * TILE : (t + 1) * TILE, :width]
            else:
                some = w_v[t * high : (t + 1) * high, :, :, :, :width].reshape(TILE, width)
            line = jnp.sum(term * some.astype(F32), axis=1, keepdims=True)
            wide = jnp.broadcast_to(line, (TILE, LANES))
            for i in range(TILE // LANES):
                row = t * (TILE // LANES) + i
                gain_in_ref[row : row + 1, :] = wide[i * LANES : (i + 1) * LANES].T[0:1, :]
        pz_store = links.local(lambda: (pz_v, pz_out))
        pz_store.start()
        pout_v[...] = tr_mm(gated_v[...], cot_v[...].reshape(-1, depth)).astype(BF16)
        pout_store = links.local(lambda: (pout_v, pout_out))
        pout_store.start()
        for copy in [dz_store, dy_store, pz_store, mixed_store, pout_store] + keep:
            copy.wait()
        for copy in cores:
            copy.wait()
        for copy in sums:
            copy.wait_send()
        entry.finish()


def backward_kernel(
    seq, fsdp,
    x_ref, xh_ref, tail_ref, tailh_ref, off_ref, offr_ref, rem_ref, dy_ref, dz_ref, state_ref,
    w_ref,    all_stat_ref, mixed_ref, got_ref, pout_ref, pz_ref,
    cx_ref, ct_ref, hp_ref, pick_ref,
    out_ref, gx_ref, gt_ref, gh_ref, mixed_out, rows_out, slots_out, dh_out,
    memory, ext_x, ext_t, next_x, next_t,
    mix_own, mix_first, mix_later, pout_own, pout_first, pz_own, pz_first, pz_top,
    dh_give, dh_own, dh_first, send, recv, near,
):
    seqs, _, length, width = dy_ref.shape
    x_at = x_ref.shape[3] - width
    step_at = pl.program_id(0)

    place = Place(seq, fsdp)
    links = Links(send, recv, near)
    mixed = TokenScatter(
        place, links, (mixed_ref, got_ref), mixed_out, mix_own, mix_first, mix_later, "halves"
    )
    w_rows = RowScatter(place, links, pout_ref, rows_out, pout_own, pout_first)
    z_part = PartScatter(
        place, links, pz_ref, lambda s, c: pz_own.at[s, c], pz_first, pz_top, slots_out, 1
    )
    pz_load = links.local(lambda: (pz_ref.at[:, place.pair], pz_own))
    half = seq // 2

    def give_chunk(low):
        return links.far(
            lambda: (dh_give.at[:, low], dh_first.at[:, low], place.at(core=1))
        )

    dh_chunks = [give_chunk(low) for low in range(half)]

    def add_chunk(low):
        dh_chunks[low].wait_recv()
        for q in range(seqs):
            add_rows(dh_own.at[q, low], dh_own.at[q, low], dh_first.at[q, low])

    dh_store = links.local(lambda: (dh_own, dh_out))
    stages = len(place.low_bits)

    @pl.when(step_at == 0)
    def _():
        mixed.begin()
        pz_load.start()
        meet_pair(place)
        z_part.send_pairs(1, 0)
        mixed.add_cores()
        mixed.send_stage(0)

    @pl.when(step_at == 1)
    def _():
        z_part.send_pairs(0, 0)

    @pl.when(step_at == 2)
    def _():
        pz_load.wait()
        z_part.add_pairs(1, 0)
        z_part.send_cross(0)
        w_rows.begin()

    @pl.when(step_at == 4)
    def _():
        z_part.add_pairs(0, 0)

    @pl.when(step_at == 4)
    def _():
        w_rows.add_pairs()

    @pl.when(step_at == pl.num_programs(0) - 1)
    def _():
        z_part.spread()

    @pl.when(step_at == pl.num_programs(0) - 4)
    def _():
        mixed.add_stage(0)
        if stages > 1:
            mixed.send_stage(1)

    @pl.when(pl.program_id(0) == 0)
    def _():
        memory[...] = jnp.zeros_like(memory)
        gx_ref[...] = jnp.zeros_like(gx_ref)
        gt_ref[...] = jnp.zeros_like(gt_ref)
        gh_ref[...] = jnp.zeros_like(gh_ref)
        next_x[:, length:, :] = jnp.zeros_like(next_x[:, length:, :])
        next_t[:, length:, :] = jnp.zeros_like(next_t[:, length:, :])

    params = (
        cx_ref[:KERNEL, :], cx_ref[KERNEL : KERNEL + 1, :],
        ct_ref[:KERNEL, :], ct_ref[KERNEL : KERNEL + 1, :],
        hp_ref[...], pick_ref[...],
    )
    skip_row = cx_ref[KERNEL + 2 : KERNEL + 3, :]
    for q in range(seqs):
        offset = off_ref[q, 0]
        conv_x, conv_t, raw, step, rate, decay_rate, cumul, spread, step_x, entry_x, end_x = (
            chunk_common(
                x_ref[q, 0, :, x_at:], xh_ref[q, 0, :, x_at:], tail_ref[q, 0], tailh_ref[q, 0], offset,
                params, ext_x.at[q], ext_t.at[q], width,
            )
        )
        dy_low = dy_ref[q, 0]
        dy = dy_low.astype(F32)

        sig_x = sigmoid(conv_x)
        xs = conv_x * sig_x
        slope_x = sig_x + xs * (1.0 - sig_x)
        sig_t = sigmoid(conv_t)
        act_t = conv_t * sig_t
        slope_t = sig_t + act_t * (1.0 - sig_t)
        bs = act_t[:, :STATE].astype(BF16)
        cs = act_t[:, STATE:].astype(BF16)
        scaled = xs * step_x
        scaled_low = scaled.astype(BF16)
        scores = mm_tr(bs, cs)
        rows, cols = iota((length, length), 0), iota((length, length), 1)
        gap = cols - rows
        same = (gap >= 0) & (gap.astype(F32) <= offr_ref[q, 0])
        strict = gap > 0
        upper = (rows >= cols).astype(BF16)
        cumul_t = cumul.T
        old = state_ref[q, 0]
        grad_state = memory[q]
        state_low = grad_state.astype(BF16)
        grad_scores = jnp.zeros((length, length), F32)
        grad_scaled = []
        inside_rows = []
        for start, size, heads in head_tiles(width):
            dy_tile = masked_heads(dy_low[:, start : start + size], heads)
            grad_mix = mm_tr(scaled_low[:, start : start + size], dy_tile)
            mixing = []
            for i, head in enumerate(heads):
                spans = cumul_t[head : head + 1, :] - cumul[:, head : head + 1]
                decays = jnp.exp(jnp.where(same, spans, -1e30))
                weighted = grad_mix[:, i * length : (i + 1) * length] * decays
                grad_scores = grad_scores + weighted
                mixing.append((decays * scores).astype(BF16))
                terms = jnp.where(strict, weighted * scores, 0.0).astype(BF16)
                sums = jnp.dot(terms, upper, preferred_element_type=F32)
                inside_rows.append(
                    jnp.sum(jnp.where(strict, sums, 0.0), axis=0, keepdims=True)
                )
            mix = mixing[0] if len(heads) == 1 else jnp.concatenate(mixing, axis=1)
            grad_scaled.append(jnp.dot(mix, dy_tile, preferred_element_type=F32))
        inside_rows.append(jnp.zeros((LANES - len(inside_rows), length), F32))
        inside = jnp.concatenate(inside_rows, axis=0).T
        from_end = mm(bs, state_low) * end_x
        grad_scaled = jnp.concatenate(grad_scaled, axis=1) + from_end
        entry_dy = dy * entry_x
        entry_dy_low = entry_dy.astype(BF16)
        out_terms = mm(cs, old) * entry_dy
        end_terms = scaled * from_end
        grad_step = mm_ones_tr(xs * grad_scaled, spread, 2)
        out_terms = mm_ones_tr(out_terms, spread, 2)
        end_terms = mm_ones_tr(end_terms, spread, 2)
        keep_row = entry_x[length - 1 : length, :]
        carried = jnp.sum(grad_state * old.astype(F32), axis=0, keepdims=True) * keep_row
        carried = mm_ones_tr(jnp.broadcast_to(carried, (8, width)), spread, 2)[0:1, :]
        triu = (cols >= rows).astype(BF16)
        below = (rows > cols).astype(BF16)
        grad_rate = inside + ones_mm(triu, out_terms, 2) + ones_mm(below, end_terms, 2) + carried
        grad_step = grad_step - decay_rate * grad_rate
        grad_raw = grad_step * sigmoid(raw)
        grad_scores_low = grad_scores.astype(BF16)
        grad_b = mm(grad_scores_low, cs) + mm_tr(scaled * end_x, state_low)
        grad_c = tr_mm(grad_scores_low, bs) + mm_tr(entry_dy_low, old)
        memory[q] = grad_state * keep_row + tr_mm(cs, entry_dy_low)
        conv_grad_x = (skip_row * dy + step_x * grad_scaled) * slope_x
        conv_grad_t = jnp.concatenate([grad_b, grad_c], axis=1) * slope_t

        remain = rem_ref[q, 0]
        results = []
        for grad, ext, nxt, weight, sums in (
            (conv_grad_x, ext_x.at[q], next_x.at[q], params[0], gx_ref),
            (conv_grad_t, ext_t.at[q], next_t.at[q], params[2], gt_ref),
        ):
            columns = grad.shape[1]
            current = ext[pl.ds(HALO, length), :]
            sums[KERNEL : KERNEL + 1, :columns] += jnp.sum(grad, axis=0, keepdims=True)
            sums[KERNEL - 1 : KERNEL, :columns] += jnp.sum(grad * current, axis=0, keepdims=True)
            nxt[0:length, :] = grad
            total = weight[KERNEL - 1 : KERNEL, :] * grad
            for back in range(1, KERNEL):
                tap = KERNEL - 1 - back
                shifted = jnp.where(offset >= back, ext[pl.ds(HALO - back, length), :], 0.0)
                sums[tap : tap + 1, :columns] += jnp.sum(grad * shifted, axis=0, keepdims=True)
                ahead = jnp.where(remain >= back, nxt[pl.ds(back, length), :], 0.0)
                total = total + weight[tap : tap + 1, :] * ahead
            nxt[length:, :] = grad[0:HALO, :]
            results.append(total.astype(BF16))
        results.append(mm_tr(grad_raw, params[5]).astype(BF16))
        gx_ref[KERNEL + 1 : KERNEL + 2, :width] += jnp.sum(dy * xs, axis=0, keepdims=True)
        gh_ref[0:1, :] += jnp.sum(grad_raw, axis=0, keepdims=True)
        gh_ref[1:2, :] += jnp.sum(grad_rate * rate, axis=0, keepdims=True)
        out_ref[q, 0] = jnp.concatenate(results, axis=1)

    depth = w_ref.shape[0]
    grad_h = mm_tr(dz_ref[...].reshape(seqs * length, width), w_ref[:, :width])
    grad_h = grad_h + mm_tr(
        out_ref[...].reshape(seqs * length, out_ref.shape[3]), w_ref[:, width:]
    )
    grad_h = grad_h.astype(BF16).reshape(seqs, length, depth)
    for i in range(seq):
        chunk = seq - 1 - i

        @pl.when((step_at == i) & (place.core == chunk // half))
        def _():
            dh_own[:, chunk % half] = grad_h

        if i + 1 < seq:

            @pl.when((step_at == i + 1) & (place.core == chunk // half))
            def _():
                add_chunk(chunk % half)

        @pl.when((step_at == i) & (place.core != chunk // half))
        def _():
            dh_give[:, chunk % half] = grad_h
            dh_chunks[chunk % half].start()

    @pl.when(step_at == pl.num_programs(0) - 1)
    def _():
        for stage in range(1, stages):
            mixed.add_stage(stage)
            if stage + 1 < stages:
                mixed.send_stage(stage + 1)
        for q in range(seqs):
            row = all_stat_ref[pl.ds(2 * (q * seq + place.chunk), 1), :]
            column = jnp.broadcast_to(row, (LANES, length)).T[:, 0:1]
            done = mix_own.at[q, place.low]
            done[...] = (done[...].astype(F32) * column).astype(BF16)
        mixed.store()
        z_part.finish()

        @pl.when(place.core == 0)
        def _():
            add_chunk(0)

        for copy in dh_chunks:
            copy.wait_send()
        dh_store.start()
        dh_store.wait()
        w_rows.finish()
        mixed.finish()


TAIL = 2 * STATE + LANES
AXES = ("seq", "fsdp")
MESH = pl.DeviceIdType.MESH
ANYWHERE = pl.BlockSpec(memory_space=pl.ANY)
IN_HBM = pl.BlockSpec(memory_space=pltpu.HBM)


def lane_rows(width):
    return -(-width // LANES)


def sum_rows(width):
    shared = D // LANES
    group = shared + (KERNEL + 1) * 2 * STATE // LANES
    return shared, group, -(-(group + (KERNEL + 3) * lane_rows(width) + 2) // 8) * 8


def whole_spec(shape):
    return pl.BlockSpec(shape, lambda i: (0,) * len(shape))


def chunk_specs(seqs, steps, length, reverse):
    def place(i):
        return steps - 1 - i if reverse else i

    def block(cols, column=0, rows=length):
        return pl.BlockSpec((seqs, 1, rows, cols), lambda i: (0, place(i), 0, column))

    def before(cols, column=0):
        return pl.BlockSpec(
            (seqs, 1, HALO, cols),
            lambda i: (0, jnp.maximum(place(i) - 1, 0), length // HALO - 1, column),
        )

    return block, before


def forward_mix(normed, zx, tail, segments, cotangent, out_w, packed, seq, fsdp):
    seqs, length, depth = normed.shape
    rows = tail.shape[0]
    width = INNER // seq
    cols = 2 * width + TAIL
    pairs = fsdp // 2
    count = seqs * seq * length

    def block(columns, height=length):
        return pl.BlockSpec(
            (seqs, 1, height, columns), lambda i: (0, jnp.minimum(i, seq - 1), 0, 0)
        )

    def blocks(columns, kind, height=length):
        return jax.ShapeDtypeStruct((seqs, seq, height, columns), kind)

    w_shape = (seq, pairs, 2, rows, cols)
    out_shape = (pairs, 2) + out_w.shape
    sums = (seqs * seq * 2, length)
    flat = 8 if rows % HALO == 0 else depth
    flat_out = 8 if out_w.shape[0] % HALO == 0 else width
    outs = pl.pallas_call(
        functools.partial(forward_kernel, seq, fsdp),
        grid=(seq + 1,),
        in_specs=[ANYWHERE] * 6 + [whole_spec(packed.shape)],
        out_specs=[
            block(cols), block(width, STATE), block(1), block(1), block(length, 1),
            ANYWHERE, ANYWHERE, ANYWHERE, ANYWHERE, whole_spec(sums), ANYWHERE, ANYWHERE, ANYWHERE, ANYWHERE,
            whole_spec((8, lane_rows(width) * LANES)), whole_spec((depth // LANES, LANES)),
            whole_spec((8, width)), whole_spec((8, LANES)), whole_spec((LANES, LANES)),
        ],
        out_shape=[
            blocks(cols, BF16), blocks(width, BF16, STATE),
            blocks(1, F32), blocks(1, F32), blocks(length, F32, 1),
            blocks(depth, BF16),
            jax.ShapeDtypeStruct(w_shape, BF16),
            jax.ShapeDtypeStruct((count, width), BF16),
            jax.ShapeDtypeStruct((count, width), BF16),
            jax.ShapeDtypeStruct(sums, F32),
            jax.ShapeDtypeStruct((seqs, seq // 2, length, depth), BF16),
            jax.ShapeDtypeStruct((seqs, seq // 2, length, depth), BF16),
            jax.ShapeDtypeStruct((width, depth), BF16),
            jax.ShapeDtypeStruct(w_shape[:4] + (width,), BF16),
            jax.ShapeDtypeStruct((8, lane_rows(width) * LANES), F32),
            jax.ShapeDtypeStruct((depth // LANES, LANES), F32),
            jax.ShapeDtypeStruct((8, width), F32),
            jax.ShapeDtypeStruct((8, LANES), F32),
            jax.ShapeDtypeStruct((LANES, LANES), BF16),
        ],
        scratch_shapes=[
            pltpu.VMEM((seqs, seq, length, depth), BF16),
            pltpu.VMEM(w_shape, BF16),
            pltpu.VMEM((flat, cols), BF16),
            pltpu.VMEM(segments.shape, segments.dtype),
            pltpu.VMEM((seqs, seq, length, depth), BF16),
            pltpu.VMEM(out_shape, BF16),
            pltpu.VMEM((flat_out, depth), BF16),
            pltpu.VMEM((count, width), BF16),
            pltpu.VMEM(sums, F32),
            pltpu.VMEM((seq - 1,) + sums, F32),
            pltpu.VMEM((count, width), F32),
            pltpu.VMEM((count, width), BF16),
            pltpu.VMEM((count, width), BF16),
            pltpu.VMEM((seqs, seq // 2, length, depth), BF16),
            pltpu.VMEM((seqs, seq // 2, length, depth), BF16),
            pltpu.VMEM((width, depth), BF16),
            pltpu.VMEM(w_shape[:4] + (width,), BF16),
            pltpu.VMEM((seqs, STATE, width), F32),
            pltpu.VMEM((seqs, HALO + length, width), F32),
            pltpu.VMEM((seqs, HALO + length, 2 * STATE), F32),
            pltpu.VMEM((seqs, HALO, cols), BF16),
            pltpu.SemaphoreType.DMA((320,)),
            pltpu.SemaphoreType.DMA((320,)),
            pltpu.SemaphoreType.DMA((24,)),
        ],
        compiler_params=pltpu.CompilerParams(
            dimension_semantics=("arbitrary",), vmem_limit_bytes=63 << 20, collective_id=0,
            has_side_effects=True,
        ),
        cost_estimate=pl.CostEstimate(
            flops=30_000_000_000, transcendentals=0, bytes_accessed=60_000_000
        ),
        name="mix_forward",
    )(normed, zx, tail, segments, cotangent, out_w, packed)
    (
        proj, states, off_col, rem_col, off_row, h_all, w_mine, dz, dy, stats, mixed, got, part,
        part_z, gain_out, gain_in,
    ) = outs[:16]
    return (
        proj, states, off_col, rem_col, off_row, h_all, w_mine.reshape(depth, cols), dz,
        dy.reshape(seqs, seq, length, width), stats, (mixed, got), part.reshape(out_shape),
        part_z, (gain_in, gain_out), outs[16:],
    )


def backward_mix(
    proj, off_col, off_row, rem_col, dy, dz, w_mine, stats, states, mixed, part_out, part_z, packed, consts, seq, fsdp
):
    seqs, steps, length, cols = proj.shape
    depth = mixed[0].shape[3]
    width = (cols - TAIL) // 2
    block, before = chunk_specs(seqs, steps, length, True)
    tail_at = 2 * width // TAIL
    x_cols, x_at = (width, 1) if width % LANES == 0 else (2 * width, 0)
    rows_in = part_z.shape[3]
    half, pairs = seq // 2, fsdp // 2
    rows_out = part_out.shape[2]
    sums = [(8, lane_rows(width) * LANES), (8, 2 * STATE), (8, LANES)]
    token_own = pltpu.VMEM((seqs, half, length, depth), BF16)
    return pl.pallas_call(
        functools.partial(backward_kernel, seq, fsdp),
        grid=(steps,),
        in_specs=[
            block(x_cols, x_at), before(x_cols, x_at),
            block(TAIL, tail_at), before(TAIL, tail_at),
            block(1), block(length, 0, 1), block(1), block(width), block(width),
            block(width, 0, STATE),
            pl.BlockSpec(w_mine.shape, lambda i: (0, 0), pipeline_mode=pl.Buffered(1)),
            whole_spec(stats.shape), ANYWHERE, ANYWHERE,
            ANYWHERE, ANYWHERE, whole_spec(consts[0].shape),
            pl.BlockSpec((8, 2 * STATE), lambda i: (0, INNER // (2 * STATE))),
            whole_spec(consts[1].shape), whole_spec(consts[2].shape),
        ],
        out_specs=[block(width + TAIL)] + [whole_spec(v) for v in sums] + [ANYWHERE] * 4,
        scratch_shapes=[
            pltpu.VMEM((seqs, STATE, width), F32),
            pltpu.VMEM((seqs, HALO + length, width), F32),
            pltpu.VMEM((seqs, HALO + length, 2 * STATE), F32),
            pltpu.VMEM((seqs, length + HALO, width), F32),
            pltpu.VMEM((seqs, length + HALO, 2 * STATE), F32),
            token_own, token_own, pltpu.VMEM((seqs, max(half - 1, 1), length, depth), BF16),
            pltpu.VMEM((2, rows_out, depth), BF16),
            pltpu.VMEM((max(pairs - 1, 1), 2, rows_out, depth), BF16),
            pltpu.VMEM((seq, 2, rows_in, width), BF16),
            pltpu.VMEM((max(pairs - 1, 1), seq, 2, rows_in, width), BF16),
            pltpu.VMEM((half, 2, rows_in, width), BF16),
            token_own, token_own, token_own,
            pltpu.SemaphoreType.DMA((128,)),
            pltpu.SemaphoreType.DMA((128,)),
            pltpu.SemaphoreType.DMA((16,)),
        ],
        out_shape=[jax.ShapeDtypeStruct(proj.shape[:3] + (width + TAIL,), BF16)]
        + [jax.ShapeDtypeStruct(v, F32) for v in sums]
        + [
            jax.ShapeDtypeStruct((seqs, length, depth), BF16),
            jax.ShapeDtypeStruct((2, rows_out, depth), BF16),
            jax.ShapeDtypeStruct((2, half, rows_in, width), BF16),
            jax.ShapeDtypeStruct((seqs, half, length, depth), BF16),
        ],
        compiler_params=pltpu.CompilerParams(
            dimension_semantics=("arbitrary",), vmem_limit_bytes=56 << 20, collective_id=3,
            has_side_effects=True,
        ),
        cost_estimate=pl.CostEstimate(
            flops=steps * seqs * 2_000_000_000, transcendentals=0, bytes_accessed=16_000_000
        ),
        name="mix_backward",
    )(
        proj, proj, proj, proj, off_col, off_row, rem_col, dy, dz.reshape(dy.shape), states,
        w_mine, stats, *mixed, part_out,
        part_z, consts[0], packed, consts[1], consts[2],
    )


class Place:
    def __init__(self, seq, fsdp):
        self.seq, self.fsdp = seq, fsdp
        self.half, self.pairs = seq // 2, fsdp // 2
        s, f = lax.axis_index("seq"), lax.axis_index("fsdp")
        self.s, self.f = s, f
        self.top, self.low = s // self.half, lax.rem(s, self.half)
        self.core, self.pair = lax.rem(f, 2), f // 2
        self.home = self.core == self.top
        self.away = self.core != self.top
        self.chunk = self.low + self.half * self.core
        self.low_bits = [1 << i for i in range(self.half.bit_length() - 1)]

    def at(self, top=0, low=0, pair=0, core=0):
        return (
            flip(self.top, top) * self.half + flip(self.low, low),
            flip(self.pair, pair) * 2 + flip(self.core, core),
        )

    def bits_for(self, q):
        return self.low_bits if q % 2 == 0 else self.low_bits[::-1]


def flip(index, bits):
    for i in range(bits.bit_length()):
        if bits >> i & 1:
            bit = lax.rem(index // (1 << i), 2)
            index = index + (1 << i) * (1 - 2 * bit)
    return index


class Copy:
    def __init__(self, make):
        self.make = make

    def start(self):
        self.make().start()
        return self

    def wait(self):
        self.make().wait()

    def wait_send(self):
        self.make().wait_send()

    def wait_recv(self):
        self.make().wait_recv()


class Copies:
    def __init__(self, copies):
        self.copies = copies

    def start(self):
        for copy in self.copies:
            copy.start()

    def wait_recv(self):
        for copy in self.copies:
            copy.wait_recv()

    def wait_send(self):
        for copy in self.copies:
            copy.wait_send()


class Links:
    def __init__(self, send, recv, near):
        self.send, self.recv, self.near = send, recv, near
        self.far_count = self.near_count = 0

    def far(self, make):
        i = self.far_count
        self.far_count += 1

        def build():
            src, dst, device = make()
            return pltpu.make_async_remote_copy(
                src_ref=src, dst_ref=dst, send_sem=self.send.at[i], recv_sem=self.recv.at[i],
                device_id=device, device_id_type=MESH,
            )

        return Copy(build)

    def local(self, make):
        i = self.near_count
        self.near_count += 1
        return Copy(lambda: pltpu.make_async_copy(*make(), self.near.at[i]))


def meet(devices):
    barrier = pltpu.get_barrier_semaphore()
    for device in devices:
        pl.semaphore_signal(barrier, inc=1, device_id=device, device_id_type=MESH)
    pl.semaphore_wait(barrier, len(devices))


def meet_pair(place):
    meet(
        [place.at(top=t, low=l, core=c) for t, l, c in peers_of(place)]
        + [place.at(pair=p) for p in range(1, place.pairs)]
    )


def peers_of(place):
    out = []
    for top in (0, 1):
        for low in range(place.half):
            for core in (0, 1):
                if (top, low, core) != (0, 0, 0):
                    out.append((top, low, core))
    return out


class TokenGather:
    def __init__(self, place, links, src, dst):
        self.place, self.src, self.dst = place, src, dst
        seqs = src.shape[0]

        def over(q):
            return links.far(
                lambda: (src.at[q], dst.at[q, place.s], place.at(top=1, core=1))
            )

        self.cross = [over(q) for q in range(seqs)]
        self.stay = links.local(lambda: (src, dst.at[:, place.s]))
        self.share = [[] for _ in range(seqs)]
        self.stages = []
        held = [[0] for _ in range(seqs)]
        for q in range(seqs):
            self.share[q].append([self.copy(links, q, low, core=1) for low in held[q]])
        for i in range(len(place.low_bits)):
            stage = []
            for q in range(seqs):
                bit = place.bits_for(q)[i]
                stage.append([self.copy(links, q, low, low_bit=bit) for low in held[q]])
                fresh = [low ^ bit for low in held[q]]
                held[q] = held[q] + fresh
                self.share[q].append([self.copy(links, q, low, core=1) for low in fresh])
            self.stages.append(stage)

    def copy(self, links, q, low, low_bit=0, core=0):
        def make():
            place = self.place
            ref = self.dst.at[q, flip(place.low, low) + place.half * place.core]
            return ref, ref, place.at(low=low_bit, core=core)

        return links.far(make)

    def begin(self):
        self.cross_over()
        self.begin_home()

    def cross_over(self):
        @pl.when(self.place.away)
        def _():
            for copy in self.cross:
                copy.start()

    def begin_home(self):
        @pl.when(self.place.home)
        def _():
            self.stay.start()
            self.stay.wait()
            self.send_stage(0)

    def arrive(self):
        @pl.when(self.place.away)
        def _():
            for copy in self.cross:
                copy.wait_recv()
            self.send_stage(0)

    def send_stage(self, i):
        for q in range(len(self.share)):
            for copy in self.stages[i][q] + self.share[q][i]:
                copy.start()

    def pass_on(self, i, role):
        @pl.when(self.place.home if role == "home" else self.place.away)
        def _():
            for q in range(len(self.share)):
                for copy in self.stages[i][q]:
                    copy.wait_recv()
                for copy in (self.stages[i + 1][q] if i + 1 < len(self.stages) else []):
                    copy.start()
                for copy in self.share[q][i + 1]:
                    copy.start()

    def finish(self):
        for share in self.share:
            for copies in share:
                for copy in copies:
                    copy.wait()
        for stage in self.stages:
            for copies in stage:
                for copy in copies:
                    copy.wait_send()

        @pl.when(self.place.away)
        def _():
            for copy in self.cross:
                copy.wait_send()


class RowGather:
    def __init__(self, place, links, src, dst):
        self.place = place
        pairs = range(1, place.pairs)

        def slot():
            return dst.at[place.pair, place.core]

        self.stay = links.local(lambda: (src, slot()))
        self.to_home = links.far(lambda: (src, slot(), place.at(core=1)))
        self.to_near = links.far(lambda: (src, slot(), place.at(top=1)))
        self.to_far = links.far(lambda: (src, slot(), place.at(top=1, core=1)))

        def forward(c, p):
            return links.far(
                lambda: (dst.at[place.pair, c], dst.at[place.pair, c], place.at(pair=p))
            )

        self.forwards = [forward(c, p) for c in (0, 1) for p in pairs]

    def begin(self):
        @pl.when(self.place.home)
        def _():
            self.stay.start()
            self.to_near.start()

        @pl.when(self.place.away)
        def _():
            self.to_home.start()
            self.to_far.start()

    def forward(self):
        @pl.when(self.place.home)
        def _():
            self.stay.wait()
            self.to_home.wait_recv()

        @pl.when(self.place.away)
        def _():
            self.to_near.wait_recv()
            self.to_far.wait_recv()

        for copy in self.forwards:
            copy.start()

    def finish(self):
        for copy in self.forwards:
            copy.wait()

        @pl.when(self.place.home)
        def _():
            self.to_near.wait_send()

        @pl.when(self.place.away)
        def _():
            self.to_home.wait_send()
            self.to_far.wait_send()


class Entry:
    def __init__(self, place, links, h_ref, zx_ref, tail_ref, seg_ref, h_v, w_v, seg_v):
        self.place = place
        cols = zx_ref.shape[-1]
        self.peers = peers = peers_of(place)
        others = range(1, place.pairs)
        self.tokens = TokenGather(place, links, h_ref, h_v)

        def block(t=0, l=0, c=0):
            s, f = place.at(top=t, low=l, core=c)
            return w_v.at[s, place.pair, lax.rem(f, 2)]

        direct = len(zx_ref.shape) == 2
        if direct:
            cols = w_v.shape[4] - TAIL
        width = cols // 2

        def source(group, part):
            if direct:
                return zx_ref.at[:, pl.ds(pl.multiple_of(part * INNER + group * width, LANES), width)]
            return zx_ref.at[group]

        def columns(ref, part):
            if direct:
                return ref.at[:, pl.ds(part * width, width)]
            return ref.at[:, pl.ds(0, cols)]

        def tail_of(ref):
            return ref.at[:, pl.ds(cols, TAIL)]

        def send_zx(part, t, l, c):
            group = flip(place.core, c) * place.half + flip(place.low, l)
            return source(group, part), columns(block(), part), place.at(top=t, low=l, core=c)

        def keep_zx(part):
            return links.local(lambda: (source(place.chunk, part), columns(block(), part)))

        parts = (0, 1) if direct else (0,)
        self.zx = {
            p: Copies([links.far(functools.partial(send_zx, part, *p)) for part in parts])
            for p in peers
        }
        self.own = [keep_zx(part) for part in parts] + [
            links.local(lambda: (tail_ref, tail_of(block())))
        ]
        self.tail_cross = links.far(lambda: (tail_ref, tail_of(block()), place.at(top=1)))
        self.near_peers = [(l, c) for t, l, c in peers if t == 0]

        def send_tail(l, c):
            return tail_ref, tail_of(block()), place.at(low=l, core=c)

        def send_other(l, c):
            return tail_of(block(1)), tail_of(block(1)), place.at(low=l, core=c)

        self.tails = {p: links.far(functools.partial(send_tail, *p)) for p in self.near_peers}
        self.tails_more = {
            p: links.far(functools.partial(send_other, *p)) for p in self.near_peers
        }
        self.seg_send = links.far(lambda: (seg_ref, seg_v, place.at(core=1)))
        self.seg_keep = links.local(lambda: (seg_ref, seg_v))

        def send_on(t, l, c, p):
            return block(t, l, c), block(t, l, c), place.at(pair=p)

        self.forwards = {
            p: [links.far(functools.partial(send_on, *p, other)) for other in others]
            for p in [(0, 0, 0)] + peers
        }

    def run(self, then):
        tokens, zx, forwards = self.tokens, self.zx, self.forwards
        stages = len(self.place.low_bits)
        far_peers = [p for p in self.peers if p[0] == 1]
        tokens.begin()
        self.tail_cross.start()
        for copy in self.own:
            copy.start()
        for p in self.near_peers:
            zx[0, *p].start()
            self.tails[p].start()

        @pl.when(self.place.home)
        def _():
            self.seg_send.start()
            self.seg_keep.start()

        for copy in self.own:
            copy.wait()
        for copy in forwards[0, 0, 0]:
            copy.start()
        self.tail_cross.wait_recv()
        for p in self.near_peers:
            self.tails_more[p].start()
        tokens.pass_on(0, "home")
        for p in self.near_peers:
            zx[0, *p].wait_recv()
            self.tails[p].wait_recv()
            for copy in forwards[0, *p]:
                copy.start()
        for p in far_peers:
            zx[p].start()
        for i in range(1, stages):
            tokens.pass_on(i, "home")
        tokens.arrive()
        for p in self.near_peers:
            self.tails_more[p].wait_recv()
        for i in range(stages):
            tokens.pass_on(i, "away")
            at, to = (len(far_peers) * k // stages for k in (i, i + 1))
            for p in far_peers[at:to]:
                zx[p].wait_recv()
                for copy in forwards[p]:
                    copy.start()
        then()

        @pl.when(self.place.home)
        def _():
            self.seg_keep.wait()
            self.seg_send.wait_send()

        @pl.when(self.place.away)
        def _():
            self.seg_send.wait_recv()

        tokens.finish()
        for p in forwards:
            for copy in forwards[p]:
                copy.wait()

    def finish(self):
        self.tail_cross.wait_send()
        for group in (self.zx, self.tails, self.tails_more):
            for copy in group.values():
                copy.wait_send()


def add_rows(out, left, right, rows=32):
    total = left.shape[0]
    step = next((size for size in (rows, 16) if total % size == 0), total)

    if step == total:
        out[...] = left[...] + right[...]
        return

    @pl.loop(0, total // step)
    def _(i):
        at = pl.ds(pl.multiple_of(i * step, step), step)
        out[at] = left[at] + right[at]


class TokenScatter:
    def __init__(self, place, links, src, out, own, first, later, held):
        self.place = place
        self.out, self.own, self.first, self.later = out, own, first, later
        self.seqs = own.shape[0]
        half = place.half
        self.loads = []
        if held == "sums":
            self.loads = [links.local(lambda: (src, own))]
        if held == "halves":
            self.loads = [
                links.local(lambda: (src[0], own)), links.local(lambda: (src[1], first)),
            ]
        self.stages = [[] for _ in place.low_bits]
        for q in range(self.seqs):
            live, slot = list(range(half)), 0
            for i, bit in enumerate(place.bits_for(q)[::-1]):
                for low in [low for low in live if low & bit]:
                    self.stages[i].append((self.copy(links, q, low, slot, bit), q, low ^ bit, slot))
                    slot += 1
                live = [low for low in live if not low & bit]
        self.stay = links.local(lambda: (own.at[:, place.low], out))

    def copy(self, links, q, low, slot, bit):
        return links.far(
            lambda: (
                self.own.at[q, flip(self.place.low, low)], self.later.at[q, slot],
                self.place.at(low=bit),
            )
        )

    def begin(self):
        for copy in self.loads:
            copy.start()

    def add_cores(self):
        for copy in self.loads:
            copy.wait()
        for q in range(self.seqs if self.first is not None else 0):
            for low in range(self.place.half):
                add_rows(self.own.at[q, low], self.own.at[q, low], self.first.at[q, low])

    def send_stage(self, i):
        for copy, _, _, _ in self.stages[i]:
            copy.start()

    def add_stage(self, i):
        for copy, q, low, slot in self.stages[i]:
            copy.wait_recv()
            ref = self.own.at[q, flip(self.place.low, low)]
            add_rows(ref, ref, self.later.at[q, slot])

    def store(self):
        self.stay.start()
        self.stay.wait()

    def finish(self):
        for stage in self.stages:
            for copy, _, _, _ in stage:
                copy.wait_send()


class RowScatter:
    def __init__(self, place, links, src, out, own, first):
        self.place, self.own, self.first = place, own, first

        def over(p):
            return links.far(
                lambda: (src.at[flip(place.pair, p)], first.at[p - 1], place.at(pair=p))
            )

        def far(c):
            return links.far(
                lambda: (own.at[flip(place.core, c)], out.at[1], place.at(top=1, core=c))
            )

        self.over = [over(p) for p in range(1, place.pairs)]
        self.load = links.local(lambda: (src.at[place.pair], own))
        self.far = [far(0), far(1)]
        self.near = links.far(lambda: (own.at[1 - place.core], out.at[0], place.at(core=1)))
        self.stay = links.local(lambda: (own.at[place.core], out.at[0]))

    def begin(self):
        self.load.start()
        for copy in self.over:
            copy.start()

    def add_pairs(self):
        self.load.wait()
        for i, copy in enumerate(self.over):
            copy.wait_recv()
            for c in (0, 1):
                add_rows(self.own.at[c], self.own.at[c], self.first.at[i, c])

        @pl.when(self.place.away)
        def _():
            for copy in self.far:
                copy.start()

        @pl.when(self.place.home)
        def _():
            self.near.start()
            self.stay.start()

    def finish(self):
        for copy in self.over:
            copy.wait_send()

        @pl.when(self.place.home)
        def _():
            self.stay.wait()
            self.near.wait_send()
            self.far[0].wait_recv()

        @pl.when(self.place.away)
        def _():
            self.near.wait_recv()
            self.far[1].wait_recv()
            for copy in self.far:
                copy.wait_send()


class PartScatter:
    def __init__(self, place, links, src, own, first, other, slots, tiles):
        self.place, self.own, self.first, self.other = place, own, first, other
        self.high = high = place.half // tiles
        pairs = range(1, place.pairs)

        def rows(top, k):
            return pl.ds(place.half * flip(place.top, top) + k * high, high)

        def over(top, k, p):
            return links.far(
                lambda: (
                    src.at[rows(top, k), flip(place.pair, p)], first.at[p - 1, rows(top, k)],
                    place.at(pair=p),
                )
            )

        def cross(i, c):
            def make():
                at = place.half * flip(place.top, 1) + i
                return own(at, c), other.at[i, c], place.at(top=1)

            return links.far(make)

        def spread(l, c):
            return links.far(
                lambda: (
                    self.block(l, c), slots.at[place.core, place.low], place.at(low=l, core=c)
                )
            )

        self.over = [[[over(top, k, p) for p in pairs] for k in range(tiles)] for top in (0, 1)]
        self.cross = [
            [cross(k * high + i, c) for i in range(high) for c in (0, 1)] for k in range(tiles)
        ]
        self.near = [(l, c) for t, l, c in peers_of(place) if t == 0]
        self.slots = {p: spread(*p) for p in self.near}
        self.slots[0, 0] = links.local(
            lambda: (self.block(0, 0), slots.at[place.core, place.low])
        )

    def block(self, l, c):
        place = self.place
        return self.own(place.half * place.top + flip(place.low, l), flip(place.core, c))

    def send_pairs(self, top, k):
        for copy in self.over[top][k]:
            copy.start()

    def add_pairs(self, top, k):
        for i, copy in enumerate(self.over[top][k]):
            copy.wait_recv()
            for low in range(self.high):
                for c in (0, 1):
                    at = self.place.half * flip(self.place.top, top) + k * self.high + low
                    ref = self.own(at, c)
                    add_rows(ref, ref, self.first.at[i, at, c], 16)

    def send_cross(self, k):
        for copy in self.cross[k]:
            copy.start()

    def wait_cross(self, k):
        for copy in self.cross[k]:
            copy.wait_recv()

    def spread(self, waits=True):
        if waits:
            for k in range(len(self.cross)):
                self.wait_cross(k)
        place = self.place
        for l, c in self.near + [(0, 0)]:
            ref = self.block(l, c)
            add_rows(ref, ref, self.other.at[flip(place.low, l), flip(place.core, c)], 16)
            self.slots[l, c].start()

    def finish(self):
        for copy in self.slots.values():
            copy.wait()
        for copies in self.cross + [c for top in self.over for c in top]:
            for copy in copies:
                copy.wait_send()


class Deliver:
    def __init__(self, place, links, src, out):
        self.place = place
        self.cross = links.far(lambda: (src(), out, place.at(top=1, core=1)))
        self.stay = links.local(lambda: (src(), out))

    def begin(self):
        @pl.when(self.place.away)
        def _():
            self.cross.start()

        @pl.when(self.place.home)
        def _():
            self.stay.start()

    def finish(self):
        @pl.when(self.place.away)
        def _():
            self.cross.wait()

        @pl.when(self.place.home)
        def _():
            self.stay.wait()


def exit_kernel(
    seq, fsdp,
    h_ref, dh_ref, grad_ref, w_ref, mixed_ref, gain_in_ref, gain_out_ref, gx_ref, gt_ref, gh_ref,
    dh_out, mixed_out, slots_out, vec_out,
    h_all, grads, weights, part, dh_own, dh_later, part_first, part_top, vec_val, vec_got,
    send, recv, near,
):
    place = Place(seq, fsdp)
    links = Links(send, recv, near)
    half = place.half
    others = list(range(1, place.pairs))
    seqs, _, length, depth = dh_own.shape
    rows = part.shape[3]
    width = weights.shape[1] - grads.shape[1]
    dh = TokenScatter(
        place, links, dh_ref, dh_out, dh_own, None, dh_later, "sums"
    )
    dh_last = Deliver(place, links, lambda: dh_own.at[:, place.low], dh_out)
    mixed = Deliver(place, links, lambda: mixed_ref, mixed_out)
    loads = [
        links.local(lambda: (h_ref, h_all)),
        links.local(lambda: (grad_ref, grads)),
        links.local(lambda: (w_ref, weights)),
    ]

    tiles = depth // 2 // TILE
    rest = PartScatter(
        place, links, part, lambda s, c: part.at[s, place.pair, c], part_first, part_top, slots_out,
        tiles,
    )

    hops = [dict(pair=1 << i) for i in range(place.pairs.bit_length() - 1)] + [dict(top=1)]

    def hop(i):
        return links.far(lambda: (vec_val.at[i], vec_got.at[i], place.at(**hops[i])))

    def share(l, c):
        return links.far(
            lambda: (
                vec_val.at[len(hops)], vec_out.at[place.core, place.low],
                place.at(low=l, core=c),
            )
        )

    vec = [hop(i) for i in range(len(hops))]
    vec_shares = [share(l, c) for t, l, c in peers_of(place) if t == 0]
    vec_shares.append(
        links.local(lambda: (vec_val.at[len(hops)], vec_out.at[place.core, place.low]))
    )

    def vec_next(i):
        vec[i].wait_recv()
        vec_val[i + 1] = vec_val[i] + vec_got[i]
        for copy in vec[i + 1 : i + 2] if i + 1 < len(hops) else vec_shares:
            copy.start()

    blocks = TILE // rows

    def weight_rows(top, k):
        t = tiles * flip(place.top, top) + k
        lanes = pl.ds(pl.multiple_of(t * TILE, LANES), TILE)
        term = tr_mm(h_all[:, lanes], grads[...])
        for b in range(blocks):
            at = t * (blocks // fsdp) + b // fsdp
            part[at, b % fsdp // 2, b % 2] = term[b * rows : (b + 1) * rows].astype(BF16)
        sums = jnp.sum(term * weights[lanes, width:].astype(F32), axis=1, keepdims=True)
        wide = jnp.broadcast_to(sums, (TILE, LANES))
        for i in range(TILE // LANES):
            row = pl.ds(t * (TILE // LANES) + i, 1)
            vec_val[0, row, :] = gain_in_ref[row, :] + wide[i * LANES : (i + 1) * LANES].T[0:1, :]
        rest.send_pairs(top, k)

    def place_sums():
        at, group, _ = sum_rows(width)
        vec_val[0] = jnp.zeros_like(vec_val[0])
        for tap in range(KERNEL + 1):
            for j in range(2 * STATE // LANES):
                vec_val[0, at : at + 1, :] = gt_ref[
                    tap : tap + 1, j * LANES : (j + 1) * LANES
                ]
                at += 1
        pieces_of = [
            ref[line : line + 1, j * LANES : (j + 1) * LANES]
            for ref, line in [(gx_ref, i) for i in range(KERNEL + 2)] + [(gain_out_ref, 0)]
            for j in range(lane_rows(width))
        ] + [gh_ref[0:1, :], gh_ref[1:2, :]]
        for i, piece in enumerate(pieces_of):
            vec_val[0, group + i : group + i + 1, :] = piece

    dh.begin()
    for copy in loads:
        copy.start()
    meet_pair(place)
    dh.add_cores()
    dh.send_stage(0)
    mixed.begin()
    place_sums()
    for copy in loads:
        copy.wait()
    for k in range(tiles):
        weight_rows(1, k)
    for k in range(tiles):
        weight_rows(0, k)
    vec[0].start()
    for k in range(tiles):
        rest.add_pairs(1, k)
        rest.send_cross(k)
    stages = len(place.low_bits)
    for i in range(stages):
        dh.add_stage(i)
        if i + 1 < stages:
            dh.send_stage(i + 1)
        else:
            dh_last.begin()
        if i < len(hops):
            vec_next(i)
    for i in range(stages, len(hops)):
        vec_next(i)
    for k in range(tiles):
        rest.add_pairs(0, k)
    rest.spread()
    for copy in vec_shares:
        copy.wait()
    rest.finish()
    mixed.finish()
    dh_last.finish()
    dh.finish()
    for copy in vec:
        copy.wait_send()


def exit_scatter(seq, fsdp, h_all, grad_h, grad_proj, w_mine, mixed, sums):
    seqs, _, length, depth = h_all.shape
    half, pairs = seq // 2, fsdp // 2
    cols = w_mine.shape[1]
    rest = grad_proj.shape[3]
    width = cols - rest
    rows = depth // (seq * fsdp)
    count = seqs * seq * length
    vector = (sum_rows(width)[2], LANES)
    hops = pairs.bit_length()
    token_own = pltpu.VMEM((seqs, half, length, depth), BF16)
    tokens = jax.ShapeDtypeStruct((seqs, length, depth), BF16)
    return pl.pallas_call(
        functools.partial(exit_kernel, seq, fsdp),
        in_specs=[ANYWHERE] * 5 + [pl.BlockSpec(memory_space=pltpu.VMEM)] * 5,
        out_specs=[ANYWHERE] * 4,
        out_shape=[
            tokens,
            tokens,
            jax.ShapeDtypeStruct((2, half, rows, rest), BF16),
            jax.ShapeDtypeStruct((2, half) + vector, F32),
        ],
        scratch_shapes=[
            pltpu.VMEM((count, depth), BF16),
            pltpu.VMEM((count, rest), BF16),
            pltpu.VMEM((depth, cols), BF16),
            pltpu.VMEM((seq, pairs, 2, rows, rest), BF16),
            token_own,
            pltpu.VMEM((seqs, max(half - 1, 1), length, depth), BF16),
            pltpu.VMEM((max(pairs - 1, 1), seq, 2, rows, rest), BF16),
            pltpu.VMEM((half, 2, rows, rest), BF16),
            pltpu.VMEM((hops + 1,) + vector, F32),
            pltpu.VMEM((hops,) + vector, F32),
            pltpu.SemaphoreType.DMA((96,)),
            pltpu.SemaphoreType.DMA((96,)),
            pltpu.SemaphoreType.DMA((16,)),
        ],
        compiler_params=pltpu.CompilerParams(
            collective_id=1, has_side_effects=True, vmem_limit_bytes=60 << 20
        ),
        cost_estimate=pl.CostEstimate(
            flops=0, transcendentals=0, bytes_accessed=200_000_000
        ),
        name="exit_scatter",
    )(
        h_all.reshape(count, depth), grad_h, grad_proj.reshape(count, rest), w_mine, mixed, *sums
    )


def finish_kernel(
    seq,
    tok_in, cot_in, gain_ref, dh_in, mixed_in, slots_z_in, slots_in, rows_in, vec_in,
    mixed_out, tokens_out, gain_in_out, w_in_out, conv_w_out, conv_b_out, heads_out, gain_out_out,
    w_out_out,
    tok_ref, cot_ref, dh_ref, mixed_ref, slots_z_ref, slots_ref, rows_ref, vec_ref, near,
):
    pairs = [
        (slots_z_in, slots_z_ref), (slots_in, slots_ref), (rows_in, rows_ref), (vec_in, vec_ref),
        (tok_in, tok_ref), (dh_in, dh_ref), (mixed_in, mixed_ref), (cot_in, cot_ref),
    ]
    loads = [pltpu.make_async_copy(*pair, near.at[i]) for i, pair in enumerate(pairs)]
    for copy in loads:
        copy.start()
    gain = gain_ref[...]
    for copy in loads[:4]:
        copy.wait()
    groups, _, cols = slots_ref.shape
    width = cols - TAIL
    tail = jnp.zeros((slots_ref.shape[1], TAIL), F32)
    for g in range(groups):
        w_in_out[:, g * width : (g + 1) * width] = slots_z_ref[g].astype(F32)
        w_in_out[:, INNER + g * width : INNER + (g + 1) * width] = (
            slots_ref[g, :, :width].astype(F32)
        )
        tail = tail + slots_ref[g, :, width:].astype(F32)
    w_in_out[:, 2 * INNER :] = tail[:, : 2 * STATE + HEADS]
    w_out_out[...] = rows_ref[0].astype(F32) + rows_ref[1].astype(F32)

    row, group, _ = sum_rows(width)
    heads = HEADS // seq
    common = vec_ref[0, :group]
    for g in range(1, groups):
        common = common + vec_ref[g, :group]
    for j in range(D // LANES):
        at = slice(j * LANES, (j + 1) * LANES)
        gain_in_out[:, at] = common[j : j + 1] / gain_ref[:, at]
    targets = [conv_w_out.at[k : k + 1] for k in range(KERNEL)] + [conv_b_out]
    for out in targets:
        for j in range(2 * STATE // LANES):
            out[:, INNER + j * LANES : INNER + (j + 1) * LANES] = common[row : row + 1]
            row += 1
    across = lane_rows(width)
    lane = iota((8, LANES), 1)
    per_head = jnp.zeros((8, LANES), F32)
    fold = expander(across * LANES)
    for g in range(groups):
        def lanes_of(line):
            first = group + line * across
            return jnp.concatenate(
                [vec_ref[g, first + j : first + j + 1, :] for j in range(across)], axis=1
            )

        at = slice(g * width, (g + 1) * width)
        for line, out in enumerate(targets):
            out[:, at] = lanes_of(line)[:, :width]
        gain_out_out[:, at] = lanes_of(KERNEL + 2)[:, :width]
        skip = mm_ones_tr(jnp.broadcast_to(lanes_of(KERNEL + 1), (8, across * LANES)), fold, 3)
        last = group + (KERNEL + 3) * across
        lines = jnp.concatenate(
            [skip[0:1, :], vec_ref[g, last : last + 2, :], jnp.zeros((5, LANES), F32)], axis=0
        )
        lines = jnp.where(lane < heads, lines, 0.0)
        per_head = per_head + (pltpu.roll(lines, g * heads, 1) if g else lines)
    heads_out[...] = per_head
    for copy in loads[4:]:
        copy.wait()
    for q in range(tok_ref.shape[0]):
        wide = tok_ref[q].astype(F32)
        mixed_out[q] = (wide + mixed_ref[q].astype(F32)).astype(BF16)
        scale = lax.rsqrt(jnp.mean(wide * wide, axis=-1, keepdims=True) + EPSILON)
        unit = wide * scale
        scaled = dh_ref[q].astype(F32) * gain
        tokens_out[q] = cot_ref[q].astype(F32) + scale * (
            scaled - unit * jnp.mean(scaled * unit, axis=-1, keepdims=True)
        )


def finish(seq, tokens, cotangent, gain_in, grad_h, mixed, slots_z, slots, rows, vector, shapes):
    columns = INNER + 2 * STATE
    kinds = [
        (tokens.shape, BF16), (tokens.shape, F32), ((1, D), F32), (shapes[0], F32),
        ((KERNEL, columns), F32), ((1, columns), F32), ((8, LANES), F32), ((1, INNER), F32),
        (shapes[1], F32),
    ]
    arrays = (tokens, cotangent, grad_h, mixed, slots_z, slots, rows, vector)
    return pl.pallas_call(
        functools.partial(finish_kernel, seq),
        in_specs=[IN_HBM] * 2 + [pl.BlockSpec(memory_space=pltpu.VMEM)] + [IN_HBM] * 6,
        scratch_shapes=[pltpu.VMEM(v.shape, v.dtype) for v in arrays]
        + [pltpu.SemaphoreType.DMA((len(arrays),))],
        out_shape=[jax.ShapeDtypeStruct(*kind) for kind in kinds],
        compiler_params=pltpu.CompilerParams(vmem_limit_bytes=62 << 20),
        name="finish",
    )(tokens, cotangent, gain_in[None], grad_h, mixed, slots_z, slots, rows, vector)


def local(
    tokens, segments, gain_in, w_in, conv_w, conv_b, dt_bias, a_log, skip, gain_out, w_out,
    cotangent,
):
    steps, shards = lax.axis_size("seq"), lax.axis_size("fsdp")
    place = Place(steps, shards)
    seqs, length, _ = tokens.shape
    width = INNER // steps
    rows_in = w_in.shape[0]

    wide = tokens.astype(F32)
    scale_in = lax.rsqrt(jnp.mean(wide * wide, axis=-1, keepdims=True) + EPSILON)
    normed = (wide * scale_in * gain_in).astype(BF16)
    zx = w_in
    if width % LANES:
        zx = w_in[:, : 2 * INNER].reshape(rows_in, 2, steps, width).transpose(2, 0, 1, 3)
        zx = zx.reshape(steps, rows_in, 2 * width)
    tail = jnp.pad(w_in[:, 2 * INNER :], ((0, 0), (0, LANES - HEADS)))
    columns = INNER + 2 * STATE

    def line(*arrays):
        arrays = [jnp.pad(v, (0, -v.shape[0] % LANES)) for v in arrays]
        return jnp.pad(jnp.concatenate(arrays), (0, columns - sum(v.shape[0] for v in arrays)))

    packed = jnp.concatenate(
        [
            conv_w,
            jnp.stack(
                [conv_b, line(gain_out), line(dt_bias, a_log, skip), jnp.zeros((columns,), F32)]
            ),
        ]
    )
    (
        proj, states, off_col, rem_col, off_row, h_all, w_mine, dz, dy, stats, mixed, part_out,
        part_z, gains, consts,
    ) = forward_mix(normed, zx, tail, segments, cotangent, w_out, packed, steps, shards)
    grad_proj, sums_x, sums_t, sums_h, mixed, rows, slots_z, grad_h = backward_mix(
        proj, off_col, off_row, rem_col, dy, dz, w_mine, stats, states, mixed,
        part_out, part_z, packed, consts, steps, shards,
    )
    grad_h, mixed, slots, vector = exit_scatter(
        steps, shards, h_all, grad_h, grad_proj, w_mine, mixed, gains + (sums_x, sums_t, sums_h)
    )
    (
        mixed, tokens_grad, gain_in_grad, w_in_grad, conv_w_grad, conv_b_grad, per_head,
        gain_out_grad, w_out_grad,
    ) = finish(
        steps, tokens, cotangent, gain_in, grad_h, mixed,
        slots_z.reshape(steps, rows_in, width), slots.reshape(steps, rows_in, width + TAIL), rows,
        vector.reshape((steps,) + vector.shape[2:]), (w_in.shape, w_out.shape),
    )
    return (
        mixed, tokens_grad, gain_in_grad[0], w_in_grad, conv_w_grad, conv_b_grad[0],
        per_head[1, :HEADS], per_head[2, :HEADS], per_head[0, :HEADS], gain_out_grad[0],
        w_out_grad,
    )


def solution(mesh):
    by_token = P("fsdp", "seq", None)
    by_row = P(("seq", "fsdp"), None)
    placed = (
        by_token, P("fsdp", None), P(), by_row, P(), P(), P(), P(), P(), P(), by_row, by_token,
    )
    return jax.shard_map(
        local,
        mesh=mesh,
        in_specs=placed,
        out_specs=(by_token, by_token, P(), by_row, P(), P(), P(), P(), P(), P(), by_row),
        check_vma=False,
    )
```
